32 devices in a mesh: tm: 4 (over z), row: 2 (over core), col: 4 (over y, x).
Axes of the slice: x: 2, y: 2, z: 4, core: 2. Of those that a mesh axis runs over, the one named last changes fastest.
Arguments:
- features: bfloat16 [8, 32, 128, 128], P('tm', 'row', 'col'), may hold values from -65 to 65
- conv_first: bfloat16 [3, 3, 3, 128, 128], replicated, may hold values from -0.109375 to 0.109375
- conv_second: bfloat16 [3, 3, 3, 128, 128], replicated, may hold values from -0.109375 to 0.109375
- out_grad: bfloat16 [8, 32, 128, 128], P('tm', 'row', 'col'), may hold values from -6 to 6
Outputs:
- result: bfloat16 [8, 32, 128, 128], P('tm', 'row', 'col')
- feature_grad: bfloat16 [8, 32, 128, 128], P('tm', 'row', 'col')
- first_grad: bfloat16 [3, 3, 3, 128, 128], replicated
- second_grad: bfloat16 [3, 3, 3, 128, 128], replicated
The draws below stay inside these ranges and needn't reach their ends.
All inputs are finite; a program needn't handle non-finite values.
Results may differ from the reference program's by a relative error of at most 0.0068.
Values may be sent and summed in bfloat16 or wider, within the bound.
No kernel may reach another device: no remote copies, remote signals or barrier semaphores. Data moves between devices by JAX's collectives and lax.ppermute only.
A program may use at most 64 MiB of HBM per device.

```python
import math
import jax
import jax.numpy as jnp
from jax import lax

C = 128
GROUPS = 32
NT = 8
NH = 32
NW = 128


def draw_features(key, part):
    sample_key, cell_key, chan_key = jax.random.split(key, 3)
    sample = jnp.clip(jax.random.normal(sample_key, (NT, NH, NW, C), jnp.float32), -4.0, 4.0)
    cell_scale = jnp.exp(jax.random.uniform(cell_key, (NT, NH, NW, 1), jnp.float32, math.log(0.3), math.log(3.0)))
    chan_scale = jnp.exp(jax.random.uniform(chan_key, (C,), jnp.float32, math.log(0.3), math.log(3.0)))
    rise_rows = jnp.arange(NH, dtype=jnp.float32) / max(NH - 1, 1)
    rise_cols = jnp.arange(NW, dtype=jnp.float32) / max(NW - 1, 1)
    position = 0.6 * jnp.exp(math.log(3.0) * 0.5 * (rise_rows[:, None] + rise_cols[None, :]))
    return (sample * cell_scale * chan_scale * position[None, :, :, None]).astype(jnp.bfloat16)


def levels(rng, extent, pieces, smallest, high):
    loudness = 1.0
    for axis_at, blocks in pieces:
        steps = jax.random.uniform(jax.random.fold_in(jax.random.fold_in(rng, 6), axis_at), (blocks,), jnp.float32, smallest / len(pieces), high / len(pieces))
        loudness = loudness * jnp.repeat(jnp.exp(steps), extent[axis_at] // blocks).reshape((-1,) + (1,) * (len(extent) - 1 - axis_at))
    return loudness


def normal_values(own_key, dims, width, bound, cuts=(), held_as=jnp.bfloat16):
    values = width * jax.random.normal(own_key, dims, jnp.float32)
    if cuts:
        values = values * levels(own_key, dims, cuts, -0.22, 0.18)
    return jnp.clip(values, -bound, bound).astype(held_as)


def setup_inputs(seed: int = 0) -> dict:
    key_of = jax.random.split(jax.random.key(seed), 5)
    features = draw_features(jax.random.fold_in(key_of[4], 71), 0)
    conv_first = normal_values(key_of[1], (3, 3, 3, C, C), (27 * C) ** -0.5, 0.109375)
    conv_second = normal_values(key_of[2], (3, 3, 3, C, C), (27 * C) ** -0.5, 0.109375)
    out_grad = normal_values(key_of[3], (NT, NH, NW, C), 1.0, 6.0, ((0, 4), (1, 2), (2, 4)))
    return dict(features=features, conv_first=conv_first, conv_second=conv_second, out_grad=out_grad)


EPSILON = 1e-06
NUMBERS = ('NDHWC', 'DHWIO', 'NDHWC')

def conv_valid(window, kernel):
    return lax.conv_general_dilated(window[None], kernel, (1, 1, 1), 'VALID', dimension_numbers=NUMBERS, preferred_element_type=jnp.float32)[0]

def flipped(kernel):
    return jnp.transpose(jnp.flip(kernel, (0, 1, 2)), (0, 1, 2, 4, 3))

def group_sum(values):
    per_group = values.shape[3] // GROUPS
    return values.sum((1, 2)).reshape(values.shape[0], GROUPS, per_group).sum(2)

def widen(stat):
    return jnp.repeat(stat, C // GROUPS, axis=1)[:, None, None, :]

def norm_act(raw):
    values = raw.astype(jnp.float32)
    count = values.shape[1] * values.shape[2] * (C // GROUPS)
    group_mean = group_sum(values) / count
    centred = values - widen(group_mean)
    spread = group_sum(centred * centred) / count
    inv_std = widen(lax.rsqrt(spread + EPSILON))
    normed = centred * inv_std
    return ((normed * jax.nn.sigmoid(normed)).astype(jnp.bfloat16), normed, inv_std)

def norm_back(grad_act, normed, inv_std):
    count = normed.shape[1] * normed.shape[2] * (C // GROUPS)
    sigmoid_z = jax.nn.sigmoid(normed)
    grad_norm = grad_act * sigmoid_z * (1.0 + normed * (1.0 - sigmoid_z))
    first_mean = widen(group_sum(grad_norm) / count)
    second_mean = widen(group_sum(grad_norm * normed) / count)
    return inv_std * (grad_norm - first_mean - normed * second_mean)

def weight_grad(padded, grad):
    flat_grad = grad.reshape(-1, C)
    terms = []
    for depth in range(3):
        for height in range(3):
            for column in range(3):
                piece = padded[depth:depth + NT, height:height + NH, column:column + NW].reshape(-1, C)
                terms.append(lax.dot_general(piece, flat_grad, (((0,), (0,)), ((), ())), preferred_element_type=jnp.float32))
    return jnp.stack(terms, 0).reshape(3, 3, 3, C, C)

def reference(features, conv_first, conv_second, out_grad):
    past = ((2, 0), (1, 1), (1, 1), (0, 0))
    future = ((0, 2), (1, 1), (1, 1), (0, 0))
    act_first, norm_first, std_first = norm_act(features)
    pad_first = jnp.pad(act_first, past)
    hidden = conv_valid(pad_first, conv_first).astype(jnp.bfloat16)
    act_second, norm_second, std_second = norm_act(hidden)
    pad_second = jnp.pad(act_second, past)
    branch = conv_valid(pad_second, conv_second)
    result = (features.astype(jnp.float32) + branch).astype(jnp.bfloat16)
    grad_act2 = conv_valid(jnp.pad(out_grad, future), flipped(conv_second))
    hidden_grad = norm_back(grad_act2, norm_second, std_second).astype(jnp.bfloat16)
    grad_act1 = conv_valid(jnp.pad(hidden_grad, future), flipped(conv_first))
    feature_grad = (out_grad.astype(jnp.float32) + norm_back(grad_act1, norm_first, std_first)).astype(jnp.bfloat16)
    factor = 1.0 / math.sqrt(NT * NH * NW)
    first_grad = (weight_grad(pad_first, hidden_grad) * factor).astype(jnp.bfloat16)
    second_grad = (weight_grad(pad_second, out_grad) * factor).astype(jnp.bfloat16)
    return (result, feature_grad, first_grad, second_grad)
```

```python
import math

import jax
import jax.numpy as jnp
from jax import lax
from jax.sharding import PartitionSpec as P

GROUPS = 32


EPSILON = 1e-06
NUMBERS = ("NDHWC", "DHWIO", "NDHWC")
SWAPPED = ("CDHWN", "DHWIO", "CDHWN")


def conv_valid(window, kernel):
    return lax.conv_general_dilated(
        window[None],
        kernel,
        (1, 1, 1),
        "VALID",
        dimension_numbers=NUMBERS,
        preferred_element_type=jnp.float32,
    )[0]


def flipped(kernel):
    return jnp.transpose(jnp.flip(kernel, (0, 1, 2)), (0, 1, 2, 4, 3))


def weight_grad(padded, grad):
    summed = lax.conv_general_dilated(
        padded[None],
        grad[:, :, :, None, :],
        (1, 1, 1),
        "VALID",
        dimension_numbers=SWAPPED,
        preferred_element_type=jnp.float32,
    )
    return jnp.transpose(summed, (1, 2, 3, 4, 0))


def split3(stat):
    high = lax.reduce_precision(stat, 8, 7)
    rest = stat - high
    middle = lax.reduce_precision(rest, 8, 7)
    return jnp.stack([high, middle, rest - middle]).astype(jnp.bfloat16)


def join3(parts):
    terms = parts.astype(jnp.float32)
    return terms[0] + (terms[1] + terms[2])


def group_total(stat):
    chans = stat.shape[-1]
    per_group = chans // GROUPS
    ids = jnp.arange(chans) // per_group
    same = (ids[:, None] == ids[None, :]).astype(jnp.float32)
    flat = stat.reshape(-1, chans)
    return jnp.dot(flat, same, precision=lax.Precision.HIGHEST).reshape(stat.shape)


def local_stats(values):
    mean = values.mean((1, 2))
    centred = values - mean[:, None, None, :]
    return jnp.stack([mean, (centred * centred).sum((1, 2))])


def rows_of(*pieces):
    return jnp.concatenate([p.reshape(-1, p.shape[-1]) for p in pieces], 0)


def unrows(flat, shapes):
    out, at = [], 0
    for shape in shapes:
        count = math.prod(shape[:-1])
        out.append(flat[at : at + count].reshape(shape))
        at += count
    return out


def row_swap(values):
    return lax.ppermute(values, "row", [(0, 1), (1, 0)])


def exchange(arrays, rims, stats, cells):
    upper = lax.axis_index("row") == 0
    edges = [
        jnp.where(upper, a[:, a.shape[1] - rim :], a[:, :rim]) for a, rim in zip(arrays, rims)
    ]
    parts = split3(stats)
    got = unrows(row_swap(rows_of(*edges, parts)), [e.shape for e in edges] + [parts.shape])
    arrays = [
        jnp.concatenate(
            [
                jnp.where(upper, jnp.zeros_like(rim), rim),
                a,
                jnp.where(upper, rim, jnp.zeros_like(rim)),
            ],
            1,
        )
        for a, rim in zip(arrays, got)
    ]
    other = join3(got[-1])
    delta = stats[0] - other[0]
    stats = jnp.stack(
        [0.5 * (stats[0] + other[0]), stats[1] + other[1] + (0.5 * cells) * delta * delta]
    )

    count = lax.axis_size("col")
    here = lax.axis_index("col")
    heads = [a[:, :, :rim] for a, rim in zip(arrays, rims)]
    tails = [a[:, :, a.shape[2] - rim :] for a, rim in zip(arrays, rims)]
    shapes = [h.shape for h in heads]
    head, tail = rows_of(*heads), rows_of(*tails)
    parts = split3(stats)
    target = jnp.arange(count)[:, None, None]
    nothing = jnp.zeros_like(head)
    slots = jnp.where(target == here + 1, tail, jnp.where(target == here - 1, head, nothing))
    flat_parts = rows_of(parts)
    slots = jnp.concatenate(
        [slots, jnp.broadcast_to(flat_parts[None], (count,) + flat_parts.shape)], 1
    )
    got = lax.all_to_all(slots, "col", 0, 0)
    edge = head.shape[0]
    left = lax.dynamic_index_in_dim(got, jnp.maximum(here - 1, 0), 0, False)[:edge]
    right = lax.dynamic_index_in_dim(got, jnp.minimum(here + 1, count - 1), 0, False)[:edge]
    left = unrows(jnp.where(here > 0, left, nothing), shapes)
    right = unrows(jnp.where(here < count - 1, right, nothing), shapes)
    arrays = [jnp.concatenate([lo, a, hi], 2) for lo, a, hi in zip(left, arrays, right)]

    terms = got[:, edge:].reshape((count,) + parts.shape).astype(jnp.float32)
    means, squares = jnp.moveaxis(terms[:, 0] + (terms[:, 1] + terms[:, 2]), 1, 0)
    per_group = stats.shape[-1] // GROUPS
    pieces = count * per_group
    mean = group_total(means.sum(0)) / pieces
    off = means - mean[None]
    spread = group_total((squares + (2.0 * cells) * off * off).sum(0)) / (2.0 * cells * pieces)
    return arrays, mean[:, None, None, :], lax.rsqrt(spread + EPSILON)[:, None, None, :]


def inside(frame, rim):
    high, wide = frame.shape[1] - 2 * rim, frame.shape[2] - 2 * rim
    rows = lax.axis_index("row") * high + jnp.arange(-rim, high + rim)
    cols = lax.axis_index("col") * wide + jnp.arange(-rim, wide + rim)
    in_rows = (rows >= 0) & (rows < high * lax.axis_size("row"))
    in_cols = (cols >= 0) & (cols < wide * lax.axis_size("col"))
    return (in_rows[:, None] & in_cols[None, :])[None, :, :, None]


def frame_means(sums, cells):
    peers = lax.axis_size("row") * lax.axis_size("col")
    slots = jnp.broadcast_to(sums[None], (peers,) + sums.shape)
    total = lax.all_to_all(slots, ("row", "col"), 0, 0).sum(0)
    return group_total(total) / (cells * peers * (sums.shape[-1] // GROUPS))


def later(values, by):
    peers = lax.axis_size("tm")
    pairs = [(i, i + by) for i in range(peers) if 0 <= i + by < peers]
    return lax.ppermute(values, "tm", pairs)


def back_sums(act_grad, normed):
    sigmoid_z = jax.nn.sigmoid(normed)
    return act_grad * sigmoid_z * (1.0 + normed * (1.0 - sigmoid_z))


def scatter_sum(values, axis):
    peers = lax.axis_size(axis)
    share = -(-values.shape[0] // peers)
    values = jnp.pad(values, ((0, share * peers - values.shape[0]), (0, 0)))
    slots = values.reshape(peers, share, values.shape[1]).astype(jnp.bfloat16)
    return lax.all_to_all(slots, axis, 0, 0).astype(jnp.float32).sum(0)


def gather_shares(share, axis, rows):
    peers = lax.axis_size(axis)
    slots = jnp.broadcast_to(share[None], (peers,) + share.shape)
    return lax.all_to_all(slots, axis, 0, 0).reshape(-1, share.shape[1])[:rows]


def summed_kernels(first_term, second_term, factor):
    shape = first_term.shape
    chans = shape[-1]
    first_term, second_term = first_term.reshape(-1, chans), second_term.reshape(-1, chans)
    upper = lax.axis_index("row") == 0
    keep = jnp.where(upper, first_term, second_term)
    give = jnp.where(upper, second_term, first_term).astype(jnp.bfloat16)
    keep = keep + row_swap(give).astype(jnp.float32)
    by_col = scatter_sum(keep, "col")
    by_tm = scatter_sum(by_col, "tm")
    done = (by_tm * factor).astype(jnp.bfloat16)
    done = gather_shares(done, "tm", by_col.shape[0])
    done = gather_shares(done, "col", keep.shape[0])
    other = row_swap(done)
    return (
        jnp.where(upper, done, other).reshape(shape),
        jnp.where(upper, other, done).reshape(shape),
    )


def on_device(features, conv_first, conv_second, out_grad):
    frames, high, wide, _ = features.shape
    cells = high * wide
    every = cells * frames * lax.axis_size("tm") * lax.axis_size("row") * lax.axis_size("col")
    factor = 1.0 / math.sqrt(every)

    stats = local_stats(features.astype(jnp.float32))
    (wide_features, wide_grad), mean_first, std_first = exchange(
        [features, out_grad], [1, 2], stats, cells
    )
    normed = (wide_features.astype(jnp.float32) - mean_first) * std_first
    act_first = normed * jax.nn.sigmoid(normed)
    rim_ok = inside(act_first, 1)
    act_first = jnp.where(rim_ok, act_first, 0.0).astype(jnp.bfloat16)
    pad_first = jnp.concatenate([later(act_first[-2:], 1), act_first], 0)
    grad_window = jnp.concatenate([wide_grad, later(wide_grad[:2], -1)], 0)

    hidden = conv_valid(pad_first, conv_first).astype(jnp.bfloat16)
    grad_act2 = conv_valid(grad_window, flipped(conv_second))
    stats = local_stats(hidden.astype(jnp.float32))
    (wide_hidden,), mean_second, std_second = exchange([hidden], [1], stats, cells)
    normed = (wide_hidden.astype(jnp.float32) - mean_second) * std_second
    act_second = normed * jax.nn.sigmoid(normed)
    act_second = jnp.where(rim_ok, act_second, 0.0).astype(jnp.bfloat16)
    core = (slice(None), slice(1, -1), slice(1, -1))

    q = back_sums(grad_act2, normed)
    sums = jnp.stack([q[core].sum((1, 2)), (q * normed)[core].sum((1, 2))])
    means = frame_means(sums, cells)[:, :, None, None, :]
    hidden_grad = std_second * (q - means[0] - normed * means[1])
    hidden_grad = jnp.where(rim_ok, hidden_grad, 0.0).astype(jnp.bfloat16)

    hidden_window = jnp.concatenate([hidden_grad, later(hidden_grad[:2], -1)], 0)
    pad_second = jnp.concatenate([later(act_second[-2:], 1), act_second], 0)
    first_term = weight_grad(pad_first, hidden_grad[core])
    second_term = jnp.flip(weight_grad(grad_window[core], act_second[core]), (0, 1, 2))
    second_term = jnp.swapaxes(second_term, 3, 4)

    branch = conv_valid(pad_second, conv_second)
    result = (features.astype(jnp.float32) + branch).astype(jnp.bfloat16)

    grad_act1 = conv_valid(hidden_window, flipped(conv_first))
    normed = (features.astype(jnp.float32) - mean_first) * std_first
    q = back_sums(grad_act1, normed)
    means = frame_means(jnp.stack([q.sum((1, 2)), (q * normed).sum((1, 2))]), cells)
    means = means[:, :, None, None, :]
    feature_grad = std_first * (q - means[0] - normed * means[1])
    feature_grad = (out_grad.astype(jnp.float32) + feature_grad).astype(jnp.bfloat16)

    first_grad, second_grad = summed_kernels(first_term, second_term, factor)
    return (result, feature_grad, first_grad, second_grad)


def solution(mesh):
    in_specs = (P("tm", "row", "col", None), P(), P(), P("tm", "row", "col", None))
    out_specs = (P("tm", "row", "col", None), P("tm", "row", "col", None), P(), P())
    return jax.shard_map(
        on_device, mesh=mesh, in_specs=in_specs, out_specs=out_specs, check_vma=False
    )
```

```python
import math

import jax
import jax.numpy as jnp
from jax import lax
from jax.sharding import PartitionSpec as P

GROUPS = 32


EPSILON = 1e-06
NUMBERS = ("NDHWC", "DHWIO", "NDHWC")
SWAPPED = ("CDHWN", "DHWIO", "CDHWN")


def conv_valid(window, kernel):
    return lax.conv_general_dilated(
        window[None],
        kernel,
        (1, 1, 1),
        "VALID",
        dimension_numbers=NUMBERS,
        preferred_element_type=jnp.float32,
    )[0]


def flipped(kernel):
    return jnp.transpose(jnp.flip(kernel, (0, 1, 2)), (0, 1, 2, 4, 3))


def weight_grad(padded, grad):
    summed = lax.conv_general_dilated(
        padded[None],
        grad[:, :, :, None, :],
        (1, 1, 1),
        "VALID",
        dimension_numbers=SWAPPED,
        preferred_element_type=jnp.float32,
    )
    return jnp.transpose(summed, (1, 2, 3, 4, 0))


def split3(stat):
    high = lax.reduce_precision(stat, 8, 7)
    rest = stat - high
    middle = lax.reduce_precision(rest, 8, 7)
    return jnp.stack([high, middle, rest - middle]).astype(jnp.bfloat16)


def join3(parts):
    terms = parts.astype(jnp.float32)
    return terms[0] + (terms[1] + terms[2])


def group_total(stat):
    chans = stat.shape[-1]
    per_group = chans // GROUPS
    ids = jnp.arange(chans) // per_group
    same = (ids[:, None] == ids[None, :]).astype(jnp.float32)
    flat = stat.reshape(-1, chans)
    return jnp.dot(flat, same, precision=lax.Precision.HIGHEST).reshape(stat.shape)


def local_stats(values):
    mean = values.mean((1, 2))
    centred = values - mean[:, None, None, :]
    return jnp.stack([mean, (centred * centred).sum((1, 2))])


def rows_of(*pieces):
    return jnp.concatenate([p.reshape(-1, p.shape[-1]) for p in pieces], 0)


def unrows(flat, shapes):
    out, at = [], 0
    for shape in shapes:
        count = math.prod(shape[:-1])
        out.append(flat[at : at + count].reshape(shape))
        at += count
    return out


def row_swap(values):
    return lax.ppermute(values, "row", [(0, 1), (1, 0)])


def exchange(arrays, rims, stats, cells):
    upper = lax.axis_index("row") == 0
    edges = [
        jnp.where(upper, a[:, a.shape[1] - rim :], a[:, :rim]) for a, rim in zip(arrays, rims)
    ]
    parts = split3(stats)
    got = unrows(row_swap(rows_of(*edges, parts)), [e.shape for e in edges] + [parts.shape])
    arrays = [
        jnp.concatenate(
            [
                jnp.where(upper, jnp.zeros_like(rim), rim),
                a,
                jnp.where(upper, rim, jnp.zeros_like(rim)),
            ],
            1,
        )
        for a, rim in zip(arrays, got)
    ]
    other = join3(got[-1])
    delta = stats[0] - other[0]
    stats = jnp.stack(
        [0.5 * (stats[0] + other[0]), stats[1] + other[1] + (0.5 * cells) * delta * delta]
    )

    count = lax.axis_size("col")
    here = lax.axis_index("col")
    heads = [a[:, :, :rim] for a, rim in zip(arrays, rims)]
    tails = [a[:, :, a.shape[2] - rim :] for a, rim in zip(arrays, rims)]
    shapes = [h.shape for h in heads]
    head, tail = rows_of(*heads), rows_of(*tails)
    parts = split3(stats)
    target = jnp.arange(count)[:, None, None]
    nothing = jnp.zeros_like(head)
    slots = jnp.where(target == here + 1, tail, jnp.where(target == here - 1, head, nothing))
    flat_parts = rows_of(parts)
    slots = jnp.concatenate(
        [slots, jnp.broadcast_to(flat_parts[None], (count,) + flat_parts.shape)], 1
    )
    got = lax.all_to_all(slots, "col", 0, 0)
    edge = head.shape[0]
    left = lax.dynamic_index_in_dim(got, jnp.maximum(here - 1, 0), 0, False)[:edge]
    right = lax.dynamic_index_in_dim(got, jnp.minimum(here + 1, count - 1), 0, False)[:edge]
    left = unrows(jnp.where(here > 0, left, nothing), shapes)
    right = unrows(jnp.where(here < count - 1, right, nothing), shapes)
    arrays = [jnp.concatenate([lo, a, hi], 2) for lo, a, hi in zip(left, arrays, right)]

    terms = got[:, edge:].reshape((count,) + parts.shape).astype(jnp.float32)
    means, squares = jnp.moveaxis(terms[:, 0] + (terms[:, 1] + terms[:, 2]), 1, 0)
    per_group = stats.shape[-1] // GROUPS
    pieces = count * per_group
    mean = group_total(means.sum(0)) / pieces
    off = means - mean[None]
    spread = group_total((squares + (2.0 * cells) * off * off).sum(0)) / (2.0 * cells * pieces)
    return arrays, mean[:, None, None, :], lax.rsqrt(spread + EPSILON)[:, None, None, :]


def inside(frame, rim):
    high, wide = frame.shape[1] - 2 * rim, frame.shape[2] - 2 * rim
    rows = lax.axis_index("row") * high + jnp.arange(-rim, high + rim)
    cols = lax.axis_index("col") * wide + jnp.arange(-rim, wide + rim)
    in_rows = (rows >= 0) & (rows < high * lax.axis_size("row"))
    in_cols = (cols >= 0) & (cols < wide * lax.axis_size("col"))
    return (in_rows[:, None] & in_cols[None, :])[None, :, :, None]


def frame_means(sums, cells):
    peers = lax.axis_size("row") * lax.axis_size("col")
    slots = jnp.broadcast_to(sums[None], (peers,) + sums.shape)
    total = lax.all_to_all(slots, ("row", "col"), 0, 0).sum(0)
    return group_total(total) / (cells * peers * (sums.shape[-1] // GROUPS))


def later(values, by):
    peers = lax.axis_size("tm")
    pairs = [(i, i + by) for i in range(peers) if 0 <= i + by < peers]
    return lax.ppermute(values, "tm", pairs)


def back_sums(act_grad, normed):
    sigmoid_z = jax.nn.sigmoid(normed)
    return act_grad * sigmoid_z * (1.0 + normed * (1.0 - sigmoid_z))


def summed_kernel(term, factor):
    shape = term.shape
    term = term.reshape(-1, shape[-1])
    half = term.shape[0] // 2
    peers = lax.axis_size("tm") * lax.axis_size("col")
    share = -(-half // peers)
    upper = lax.axis_index("row") == 0
    keep = jnp.where(upper, term[:half], term[half:])
    give = jnp.where(upper, term[half:], term[:half]).astype(jnp.bfloat16)
    keep = keep + row_swap(give).astype(jnp.float32)
    keep = jnp.pad(keep, ((0, share * peers - half), (0, 0))).astype(jnp.bfloat16)
    slots = keep.reshape(peers, share, shape[-1])
    total = lax.all_to_all(slots, ("tm", "col"), 0, 0).astype(jnp.float32).sum(0)
    done = (total * factor).astype(jnp.bfloat16)
    slots = jnp.broadcast_to(done[None], (peers,) + done.shape)
    done = lax.all_to_all(slots, ("tm", "col"), 0, 0).reshape(-1, shape[-1])[:half]
    other = row_swap(done)
    low = jnp.where(upper, done, other)
    top = jnp.where(upper, other, done)
    return jnp.concatenate([low, top], 0).reshape(shape)


def on_device(features, conv_first, conv_second, out_grad):
    frames, high, wide, _ = features.shape
    cells = high * wide
    every = cells * frames * lax.axis_size("tm") * lax.axis_size("row") * lax.axis_size("col")
    factor = 1.0 / math.sqrt(every)

    stats = local_stats(features.astype(jnp.float32))
    (wide_features, wide_grad), mean_first, std_first = exchange(
        [features, out_grad], [1, 2], stats, cells
    )
    normed = (wide_features.astype(jnp.float32) - mean_first) * std_first
    act_first = normed * jax.nn.sigmoid(normed)
    rim_ok = inside(act_first, 1)
    act_first = jnp.where(rim_ok, act_first, 0.0).astype(jnp.bfloat16)
    pad_first = jnp.concatenate([later(act_first[-2:], 1), act_first], 0)
    grad_window = jnp.concatenate([wide_grad, later(wide_grad[:2], -1)], 0)

    hidden = conv_valid(pad_first, conv_first).astype(jnp.bfloat16)
    hidden, grad_window = lax.optimization_barrier((hidden, grad_window))
    grad_act2 = conv_valid(grad_window, flipped(conv_second))
    stats = local_stats(hidden.astype(jnp.float32))
    (wide_hidden,), mean_second, std_second = exchange([hidden], [1], stats, cells)
    normed = (wide_hidden.astype(jnp.float32) - mean_second) * std_second
    act_second = normed * jax.nn.sigmoid(normed)
    act_second = jnp.where(rim_ok, act_second, 0.0).astype(jnp.bfloat16)
    core = (slice(None), slice(1, -1), slice(1, -1))

    q = back_sums(grad_act2, normed)
    sums = jnp.stack([q[core].sum((1, 2)), (q * normed)[core].sum((1, 2))])
    means = frame_means(sums, cells)[:, :, None, None, :]
    hidden_grad = std_second * (q - means[0] - normed * means[1])
    hidden_grad = jnp.where(rim_ok, hidden_grad, 0.0).astype(jnp.bfloat16)

    hidden_window = jnp.concatenate([hidden_grad, later(hidden_grad[:2], -1)], 0)
    pad_second = jnp.concatenate([later(act_second[-2:], 1), act_second], 0)
    first_term = weight_grad(pad_first, hidden_grad[core])
    second_term = jnp.flip(weight_grad(grad_window[core], act_second[core]), (0, 1, 2))
    second_term = jnp.swapaxes(second_term, 3, 4)

    branch = conv_valid(pad_second, conv_second)
    result = (features.astype(jnp.float32) + branch).astype(jnp.bfloat16)

    grad_act1 = conv_valid(hidden_window, flipped(conv_first))
    normed = (features.astype(jnp.float32) - mean_first) * std_first
    q = back_sums(grad_act1, normed)
    means = frame_means(jnp.stack([q.sum((1, 2)), (q * normed).sum((1, 2))]), cells)
    means = means[:, :, None, None, :]
    feature_grad = std_first * (q - means[0] - normed * means[1])
    feature_grad = (out_grad.astype(jnp.float32) + feature_grad).astype(jnp.bfloat16)

    first_grad = summed_kernel(first_term, factor)
    second_grad = summed_kernel(second_term, factor)
    return (result, feature_grad, first_grad, second_grad)


def solution(mesh):
    in_specs = (P("tm", "row", "col", None), P(), P(), P("tm", "row", "col", None))
    out_specs = (P("tm", "row", "col", None), P("tm", "row", "col", None), P(), P())
    return jax.shard_map(
        on_device, mesh=mesh, in_specs=in_specs, out_specs=out_specs, check_vma=False
    )
```

```python
import math

import jax
import jax.numpy as jnp
from jax import lax
from jax.sharding import PartitionSpec as P

GROUPS = 32


EPSILON = 1e-06
NUMBERS = ("NDHWC", "DHWIO", "NDHWC")
SWAPPED = ("CDHWN", "DHWIO", "CDHWN")


def conv_valid(window, kernel):
    return lax.conv_general_dilated(
        window[None],
        kernel,
        (1, 1, 1),
        "VALID",
        dimension_numbers=NUMBERS,
        preferred_element_type=jnp.float32,
    )[0]


def flipped(kernel):
    return jnp.transpose(jnp.flip(kernel, (0, 1, 2)), (0, 1, 2, 4, 3))


def weight_grad(padded, grad):
    summed = lax.conv_general_dilated(
        padded[None],
        grad[:, :, :, None, :],
        (1, 1, 1),
        "VALID",
        dimension_numbers=SWAPPED,
        preferred_element_type=jnp.float32,
    )
    return jnp.transpose(summed, (1, 2, 3, 4, 0))


def split3(stat):
    high = lax.reduce_precision(stat, 8, 7)
    rest = stat - high
    middle = lax.reduce_precision(rest, 8, 7)
    return jnp.stack([high, middle, rest - middle]).astype(jnp.bfloat16)


def join3(parts):
    terms = parts.astype(jnp.float32)
    return terms[0] + (terms[1] + terms[2])


def group_total(stat):
    chans = stat.shape[-1]
    per_group = chans // GROUPS
    ids = jnp.arange(chans) // per_group
    same = (ids[:, None] == ids[None, :]).astype(jnp.float32)
    flat = stat.reshape(-1, chans)
    return jnp.dot(flat, same, precision=lax.Precision.HIGHEST).reshape(stat.shape)


def local_stats(values):
    mean = values.mean((1, 2))
    centred = values - mean[:, None, None, :]
    return jnp.stack([mean, (centred * centred).sum((1, 2))])


def rows_of(*pieces):
    return jnp.concatenate([p.reshape(-1, p.shape[-1]) for p in pieces], 0)


def unrows(flat, shapes):
    out, at = [], 0
    for shape in shapes:
        count = math.prod(shape[:-1])
        out.append(flat[at : at + count].reshape(shape))
        at += count
    return out


def row_swap(values):
    return lax.ppermute(values, "row", [(0, 1), (1, 0)])


def exchange(arrays, rims, stats, cells):
    upper = lax.axis_index("row") == 0
    edges = [
        jnp.where(upper, a[:, a.shape[1] - rim :], a[:, :rim]) for a, rim in zip(arrays, rims)
    ]
    parts = split3(stats)
    got = unrows(row_swap(rows_of(*edges, parts)), [e.shape for e in edges] + [parts.shape])
    arrays = [
        jnp.concatenate(
            [
                jnp.where(upper, jnp.zeros_like(rim), rim),
                a,
                jnp.where(upper, rim, jnp.zeros_like(rim)),
            ],
            1,
        )
        for a, rim in zip(arrays, got)
    ]
    other = join3(got[-1])
    delta = stats[0] - other[0]
    stats = jnp.stack(
        [0.5 * (stats[0] + other[0]), stats[1] + other[1] + (0.5 * cells) * delta * delta]
    )

    count = lax.axis_size("col")
    here = lax.axis_index("col")
    heads = [a[:, :, :rim] for a, rim in zip(arrays, rims)]
    tails = [a[:, :, a.shape[2] - rim :] for a, rim in zip(arrays, rims)]
    shapes = [h.shape for h in heads]
    head, tail = rows_of(*heads), rows_of(*tails)
    parts = split3(stats)
    target = jnp.arange(count)[:, None, None]
    nothing = jnp.zeros_like(head)
    slots = jnp.where(target == here + 1, tail, jnp.where(target == here - 1, head, nothing))
    flat_parts = rows_of(parts)
    slots = jnp.concatenate(
        [slots, jnp.broadcast_to(flat_parts[None], (count,) + flat_parts.shape)], 1
    )
    got = lax.all_to_all(slots, "col", 0, 0)
    edge = head.shape[0]
    left = lax.dynamic_index_in_dim(got, jnp.maximum(here - 1, 0), 0, False)[:edge]
    right = lax.dynamic_index_in_dim(got, jnp.minimum(here + 1, count - 1), 0, False)[:edge]
    left = unrows(jnp.where(here > 0, left, nothing), shapes)
    right = unrows(jnp.where(here < count - 1, right, nothing), shapes)
    arrays = [jnp.concatenate([lo, a, hi], 2) for lo, a, hi in zip(left, arrays, right)]

    terms = got[:, edge:].reshape((count,) + parts.shape).astype(jnp.float32)
    means, squares = jnp.moveaxis(terms[:, 0] + (terms[:, 1] + terms[:, 2]), 1, 0)
    per_group = stats.shape[-1] // GROUPS
    pieces = count * per_group
    mean = group_total(means.sum(0)) / pieces
    off = means - mean[None]
    spread = group_total((squares + (2.0 * cells) * off * off).sum(0)) / (2.0 * cells * pieces)
    return arrays, mean[:, None, None, :], lax.rsqrt(spread + EPSILON)[:, None, None, :]


def inside(frame, rim):
    high, wide = frame.shape[1] - 2 * rim, frame.shape[2] - 2 * rim
    rows = lax.axis_index("row") * high + jnp.arange(-rim, high + rim)
    cols = lax.axis_index("col") * wide + jnp.arange(-rim, wide + rim)
    in_rows = (rows >= 0) & (rows < high * lax.axis_size("row"))
    in_cols = (cols >= 0) & (cols < wide * lax.axis_size("col"))
    return (in_rows[:, None] & in_cols[None, :])[None, :, :, None]


def frame_means(sums, cells):
    peers = lax.axis_size("row") * lax.axis_size("col")
    slots = jnp.broadcast_to(sums[None], (peers,) + sums.shape)
    total = lax.all_to_all(slots, ("row", "col"), 0, 0).sum(0)
    return group_total(total) / (cells * peers * (sums.shape[-1] // GROUPS))


def later(values, by):
    peers = lax.axis_size("tm")
    pairs = [(i, i + by) for i in range(peers) if 0 <= i + by < peers]
    return lax.ppermute(values, "tm", pairs)


def back_sums(act_grad, normed):
    sigmoid_z = jax.nn.sigmoid(normed)
    return act_grad * sigmoid_z * (1.0 + normed * (1.0 - sigmoid_z))


def tiled(count, peers):
    return -(-count // (16 * peers)) * 16


def scatter_sum(values, axis):
    peers = lax.axis_size(axis)
    share = tiled(values.shape[0], peers)
    values = jnp.pad(values, ((0, share * peers - values.shape[0]), (0, 0)))
    slots = values.reshape(peers, share, values.shape[1]).astype(jnp.bfloat16)
    return lax.all_to_all(slots, axis, 0, 0).astype(jnp.float32).sum(0)


def gather_shares(share, axis):
    peers = lax.axis_size(axis)
    slots = jnp.broadcast_to(share[None], (peers,) + share.shape)
    return lax.all_to_all(slots, axis, 0, 0)


def summed_kernels(first_term, second_term, sums, factor):
    shape = first_term.shape
    chans = shape[-1]
    first_term, second_term = first_term.reshape(-1, chans), second_term.reshape(-1, chans)
    rows = first_term.shape[0]
    upper = lax.axis_index("row") == 0
    keep = jnp.where(upper, first_term, second_term)
    give = jnp.where(upper, second_term, first_term).astype(jnp.bfloat16)
    keep = keep + row_swap(give).astype(jnp.float32)
    by_col = scatter_sum(keep, "col")
    by_tm = scatter_sum(by_col, "tm")
    done = (by_tm * factor).astype(jnp.bfloat16)
    done = gather_shares(done, "tm").reshape(-1, chans)[: by_col.shape[0]]
    parts = split3(sums + row_swap(sums)).reshape(-1, chans)
    spare = -parts.shape[0] % 16
    done = jnp.concatenate([done, jnp.pad(parts, ((0, spare), (0, 0)))], 0)
    done = gather_shares(done, "col")
    terms = done[:, by_col.shape[0] : done.shape[1] - spare].astype(jnp.float32)
    total = terms.sum(0).reshape((3,) + sums.shape)
    total = total[0] + (total[1] + total[2])
    done = done[:, : by_col.shape[0]].reshape(-1, chans)[:rows]
    other = row_swap(done)
    return (
        jnp.where(upper, done, other).reshape(shape),
        jnp.where(upper, other, done).reshape(shape),
        total,
    )


def on_device(features, conv_first, conv_second, out_grad):
    frames, high, wide, _ = features.shape
    cells = high * wide
    every = cells * frames * lax.axis_size("tm") * lax.axis_size("row") * lax.axis_size("col")
    factor = 1.0 / math.sqrt(every)
    peers = lax.axis_size("row") * lax.axis_size("col")

    stats = local_stats(features.astype(jnp.float32))
    (wide_features, wide_grad), mean_first, std_first = exchange(
        [features, out_grad], [1, 2], stats, cells
    )
    normed = (wide_features.astype(jnp.float32) - mean_first) * std_first
    act_first = normed * jax.nn.sigmoid(normed)
    rim_ok = inside(act_first, 1)
    act_first = jnp.where(rim_ok, act_first, 0.0).astype(jnp.bfloat16)
    pad_first = jnp.concatenate([later(act_first[-2:], 1), act_first], 0)
    grad_window = jnp.concatenate([wide_grad, later(wide_grad[:2], -1)], 0)

    hidden = conv_valid(pad_first, conv_first).astype(jnp.bfloat16)
    hidden, grad_window = lax.optimization_barrier((hidden, grad_window))
    grad_act2 = conv_valid(grad_window, flipped(conv_second))
    stats = local_stats(hidden.astype(jnp.float32))
    (wide_hidden,), mean_second, std_second = exchange([hidden], [1], stats, cells)
    normed = (wide_hidden.astype(jnp.float32) - mean_second) * std_second
    act_second = normed * jax.nn.sigmoid(normed)
    act_second = jnp.where(rim_ok, act_second, 0.0).astype(jnp.bfloat16)
    core = (slice(None), slice(1, -1), slice(1, -1))

    q = back_sums(grad_act2, normed)
    sums = jnp.stack([q[core].sum((1, 2)), (q * normed)[core].sum((1, 2))])
    means = frame_means(sums, cells)[:, :, None, None, :]
    hidden_grad = std_second * (q - means[0] - normed * means[1])
    hidden_grad = jnp.where(rim_ok, hidden_grad, 0.0).astype(jnp.bfloat16)

    pad_second = jnp.concatenate([later(act_second[-2:], 1), act_second], 0)
    hidden_grad, pad_second = lax.optimization_barrier((hidden_grad, pad_second))
    hidden_window = jnp.concatenate([hidden_grad, later(hidden_grad[:2], -1)], 0)
    first_term = weight_grad(pad_first, hidden_grad[core])
    second_term = jnp.flip(weight_grad(grad_window[core], act_second[core]), (0, 1, 2))
    second_term = jnp.swapaxes(second_term, 3, 4)
    first_term, hidden_window = lax.optimization_barrier((first_term, hidden_window))

    branch = conv_valid(pad_second, conv_second)
    result = (features.astype(jnp.float32) + branch).astype(jnp.bfloat16)

    grad_act1 = conv_valid(hidden_window, flipped(conv_first))
    normed = (features.astype(jnp.float32) - mean_first) * std_first
    q = back_sums(grad_act1, normed)
    sums = jnp.stack([q.sum((1, 2)), (q * normed).sum((1, 2))])
    first_grad, second_grad, total = summed_kernels(first_term, second_term, sums, factor)
    means = group_total(total) / (cells * peers * (sums.shape[-1] // GROUPS))
    means = means[:, :, None, None, :]
    feature_grad = std_first * (q - means[0] - normed * means[1])
    feature_grad = (out_grad.astype(jnp.float32) + feature_grad).astype(jnp.bfloat16)
    return (result, feature_grad, first_grad, second_grad)


def solution(mesh):
    in_specs = (P("tm", "row", "col", None), P(), P(), P("tm", "row", "col", None))
    out_specs = (P("tm", "row", "col", None), P("tm", "row", "col", None), P(), P())
    return jax.shard_map(
        on_device, mesh=mesh, in_specs=in_specs, out_specs=out_specs, check_vma=False
    )
```

```python
import functools
import math

import jax
import jax.numpy as jnp
from jax import lax
from jax.experimental import pallas as pl
from jax.experimental.pallas import tpu as pltpu
from jax.sharding import PartitionSpec as P

GROUPS = 32
EPSILON = 1e-06
F32 = jnp.float32
BF16 = jnp.bfloat16
LANES = 128
FRAMES = 2
STATS = 8
PARTS = 3 * STATS


def up(count, step):
    return -(-count // step) * step


class Sizes:
    def __init__(self, high, wide):
        self.high, self.wide = high, wide
        self.cells = high * wide

    def stride(self, rim):
        return up(self.high + 2 * rim, 8)

    def main(self, rim):
        return FRAMES * (self.high + 2 * rim) * self.wide

    def rows(self, rim):
        return up(self.main(rim) + 2 * rim * FRAMES * self.stride(rim), 16)

    def tall(self):
        return self.high + 2

    def broad(self):
        return up(self.wide + 2, 8)


def call(body, outs, args, scratch=(), smem=0, mib=16, flops=0):
    specs = [pl.BlockSpec(memory_space=pltpu.SMEM)] * smem
    specs += [pl.BlockSpec(memory_space=pltpu.VMEM)] * (len(args) - smem)
    shapes = [jax.ShapeDtypeStruct(shape, dtype) for shape, dtype in outs]
    moved = sum(math.prod(a.shape) * a.dtype.itemsize for a in [*args, *shapes])
    return pl.pallas_call(
        body,
        out_shape=shapes,
        in_specs=specs,
        out_specs=[pl.BlockSpec(memory_space=pltpu.VMEM)] * len(outs),
        scratch_shapes=[pltpu.VMEM(shape, dtype) for shape, dtype in scratch],
        cost_estimate=pl.CostEstimate(flops=flops, bytes_accessed=moved, transcendentals=0),
        compiler_params=pltpu.CompilerParams(vmem_limit_bytes=mib << 20),
    )(*args)


def lane_totals(stat):
    lane = lax.broadcasted_iota(jnp.int32, stat.shape, 1)
    step = 1
    while step < LANES // GROUPS:
        ahead = pltpu.roll(stat, LANES - step, 1)
        behind = pltpu.roll(stat, step, 1)
        stat = stat + jnp.where((lane // step) % 2 == 0, ahead, behind)
        step *= 2
    return stat


def split3(stat):
    high = stat.astype(BF16).astype(F32)
    rest = stat - high
    middle = rest.astype(BF16).astype(F32)
    return jnp.concatenate([high, middle, rest - middle], 0)


def join3(parts):
    parts = parts.astype(F32)
    return parts[:STATS] + (parts[STATS : 2 * STATS] + parts[2 * STATS : PARTS])


def stat_block(first, second):
    rest = jnp.zeros((STATS - 2 * FRAMES, LANES), F32)
    return jnp.concatenate([*first, *second, rest], 0)


def measured(frames):
    means, squares = [], []
    for frame in frames:
        mean = jnp.sum(frame, 0, keepdims=True) / frame.shape[0]
        centred = frame - mean
        means.append(mean)
        squares.append(jnp.sum(centred * centred, 0, keepdims=True))
    return stat_block(means, squares)


def merged(one, two, cells):
    delta = one - two
    extra = (0.5 * cells) * delta * delta
    mean = 0.5 * (one[:FRAMES] + two[:FRAMES])
    square = one[FRAMES : 2 * FRAMES] + two[FRAMES : 2 * FRAMES] + extra[:FRAMES]
    return jnp.concatenate([mean, square, jnp.zeros((STATS - 2 * FRAMES, LANES), F32)], 0)


def concluded(blocks, cells):
    per_group = LANES // GROUPS
    mean = sum(blocks[1:], blocks[0])[:FRAMES]
    mean = lane_totals(mean) / (len(blocks) * per_group)
    total = jnp.zeros((FRAMES, LANES), F32)
    for block in blocks:
        off = block[:FRAMES] - mean
        total = total + block[FRAMES : 2 * FRAMES] + cells * off * off
    spread = lane_totals(total) / (cells * len(blocks) * per_group)
    rest = jnp.zeros((STATS - 2 * FRAMES, LANES), F32)
    return jnp.concatenate([mean, lax.rsqrt(spread + EPSILON), rest], 0)


def rim_rows(place, got):
    upper = place[0] == 0
    nothing = jnp.zeros_like(got)
    return jnp.where(upper, nothing, got), jnp.where(upper, got, nothing)


def in_frame(shape, place, across, size, rim):
    row = lax.broadcasted_iota(jnp.int32, shape, 0)
    col = lax.broadcasted_iota(jnp.int32, shape, 1)
    top = jnp.where(place[0] == 0, rim, 0)
    bottom = jnp.where(place[0] == 0, size.high + 2 * rim, size.high + rim)
    left = jnp.where(place[1] == 0, rim, 0)
    right = jnp.where(place[1] == across - 1, size.wide + rim, size.wide + 2 * rim)
    return (row >= top) & (row < bottom) & (col >= left) & (col < right)


def start_body(size, place, features, out_grad, pay, stats):
    high, wide = size.high, size.wide
    upper = place[0] == 0
    at = 0
    for frame in range(FRAMES):
        pay[at : at + wide] = jnp.where(upper, features[frame, high - 1], features[frame, 0])
        at += wide
    for frame in range(FRAMES):
        for row in range(2):
            edge = jnp.where(upper, out_grad[frame, high - 2 + row], out_grad[frame, row])
            pay[at : at + wide] = edge
            at += wide
    found = measured([features[f].astype(F32).reshape(size.cells, LANES) for f in range(FRAMES)])
    stats[...] = found
    fill = jnp.zeros((pay.shape[0] - at - PARTS, LANES), F32)
    pay[at:] = jnp.concatenate([split3(found), fill], 0).astype(BF16)


def columns(own, top, bottom, col):
    return jnp.concatenate([*[r[col : col + 1] for r in top], own[:, col], *[r[col : col + 1] for r in bottom]], 0)


def slots_first_body(size, across, place, features, out_grad, got, stats, slots, flat):
    wide, high = size.wide, size.high
    edge = got.shape[0]
    flat[...] = jnp.zeros_like(flat)
    at = 0
    cols = {0: [], 1: []}
    for frame in range(FRAMES):
        rim = got[frame * wide : (frame + 1) * wide].astype(F32)
        top, bottom = rim_rows(place, rim)
        own = features[frame].astype(F32)
        for side, col in ((0, 0), (1, wide - 1)):
            flat[side, at : at + high + 2] = columns(own, [top], [bottom], col)
        at += size.stride(1)
    base = FRAMES * wide
    for j in range(2):
        for frame in range(FRAMES):
            tops, bottoms = [], []
            for row in range(2):
                first = base + (frame * 2 + row) * wide
                top, bottom = rim_rows(place, got[first : first + wide].astype(F32))
                tops.append(top)
                bottoms.append(bottom)
            own = out_grad[frame].astype(F32)
            for side, col in ((0, j), (1, wide - 2 + j)):
                flat[side, at : at + high + 4] = columns(own, tops, bottoms, col)
            at += size.stride(2)
    first = 3 * FRAMES * wide
    both = merged(stats[...], join3(got[first : first + PARTS]), size.cells)
    parts = split3(both)
    flat[0, at : at + PARTS] = parts
    flat[1, at : at + PARTS] = parts
    for peer in range(across):
        slots[peer] = jnp.where(peer > place[1], flat[1], flat[0]).astype(BF16)


def sides(place, across, got, first, count):
    left = got[jnp.maximum(place[1] - 1, 0), first : first + count].astype(F32)
    right = got[jnp.minimum(place[1] + 1, across - 1), first : first + count].astype(F32)
    nothing = jnp.zeros_like(left)
    left = jnp.where(place[1] > 0, left, nothing)
    right = jnp.where(place[1] < across - 1, right, nothing)
    return left, right


def padded_frame(size, own, top, bottom, left, right, frame):
    high, wide = size.high, size.wide
    frame[1 : high + 1, 1 : wide + 1] = own
    frame[0:1, 1 : wide + 1] = top[None]
    frame[high + 1 : high + 2, 1 : wide + 1] = bottom[None]
    tall = high + 2
    frame[:, 0:1] = left[:tall].reshape(tall, 1, LANES)
    frame[:, wide + 1 : wide + 2] = right[:tall].reshape(tall, 1, LANES)


def put_frame(size, frame, index, out):
    wide, tall, step = size.wide, size.tall(), size.stride(1)
    flat = frame[:, 1 : wide + 1].reshape(tall * wide, LANES)
    out[index * tall * wide : (index + 1) * tall * wide] = flat.astype(BF16)
    fill = jnp.zeros((step - tall, LANES), F32)
    left = frame[:, 0:1].reshape(tall, LANES)
    right = frame[:, wide + 1 : wide + 2].reshape(tall, LANES)
    return jnp.concatenate([left, fill], 0), jnp.concatenate([right, fill], 0)


def put_sides(out, first, blocks):
    fill = out.shape[0] - first - sum(b.shape[0] for b in blocks)
    if fill:
        blocks = [*blocks, jnp.zeros((fill, LANES), F32)]
    out[first:] = jnp.concatenate(blocks, 0).astype(BF16)


def act_first_body(
    size, across, place, features, out_grad, row_got, col_got, act, grad, norm, frame
):
    high, wide = size.high, size.wide
    at = FRAMES * size.stride(1) + 2 * FRAMES * size.stride(2)
    blocks = [join3(col_got[peer, at : at + PARTS]) for peer in range(across)]
    found = concluded(blocks, 2 * size.cells)
    norm[...] = found
    step = size.stride(1)
    left_all, right_all = sides(place, across, col_got, 0, FRAMES * step)
    ok = in_frame((size.tall(), size.broad(), LANES), place, across, size, 1)
    lefts, rights = [], []
    frame[...] = jnp.zeros_like(frame)
    for f in range(FRAMES):
        top, bottom = rim_rows(place, row_got[f * wide : (f + 1) * wide].astype(F32))
        padded_frame(
            size,
            features[f].astype(F32),
            top,
            bottom,
            left_all[f * step : (f + 1) * step],
            right_all[f * step : (f + 1) * step],
            frame,
        )
        normed = (frame[...] - found[f : f + 1][None]) * found[FRAMES + f : FRAMES + f + 1][None]
        frame[...] = jnp.where(ok, normed * jax.nn.sigmoid(normed), 0.0)
        left, right = put_frame(size, frame, f, act)
        lefts.append(left)
        rights.append(right)
    put_sides(act, size.main(1), lefts + rights)

    tall = high + 4
    for f in range(FRAMES):
        start = f * tall * wide
        for row in range(2):
            first = FRAMES * wide + (f * 2 + row) * wide
            top, bottom = rim_rows(place, row_got[first : first + wide])
            grad[start + row * wide : start + (row + 1) * wide] = top
            below = start + (high + 2 + row) * wide
            grad[below : below + wide] = bottom
        grad[start + 2 * wide : start + (high + 2) * wide] = out_grad[f].reshape(
            size.cells, LANES
        )
    left, right = sides(
        place, across, col_got, FRAMES * step, 2 * FRAMES * size.stride(2)
    )
    put_sides(grad, size.main(2), [left, right])


def spread_columns(size, rim, trim, wo, block, index, dst, at, frame):
    wide, high = size.wide, size.high
    tall, step = high + 2 * rim, size.stride(rim)
    main = block[index * tall * wide : (index + 1) * tall * wide].astype(F32)
    main = main.reshape(tall, wide, LANES)
    cut = rim - trim
    tall_out = tall - 2 * cut
    frame[:, trim : trim + wide] = main[cut : cut + tall_out]
    first = size.main(rim)
    edges = block[first:].astype(F32)
    for j in range(2 * rim):
        col = j - cut if j < rim else j - rim + trim + wide
        if j < cut or (j >= rim and j - rim >= trim):
            continue
        start = (j * FRAMES + index) * step
        edge = edges[start + cut : start + cut + tall_out]
        frame[:, col : col + 1] = edge.reshape(tall_out, 1, LANES)
    for c in range(3):
        dst[at, :, :, c * LANES : (c + 1) * LANES] = frame[:, c : c + wo].astype(BF16)


def spread_all(size, rim, trim, wo, near, far, dst, frame):
    filled = size.wide + 2 * trim
    if frame.shape[1] > filled:
        frame[:, filled:] = jnp.zeros((frame.shape[0], frame.shape[1] - filled, LANES), F32)
    for f in range(2 * FRAMES):
        block = near if f < FRAMES else far
        spread_columns(size, rim, trim, wo, block, f % FRAMES, dst, f, frame)


def convolved(x, kernel, turned):
    tall, wo = x.shape[1], x.shape[2]
    ho = tall - 2
    count = ho * wo
    span = 9 * LANES

    def cells(f):
        return jnp.concatenate(
            [x[f, b : b + ho].reshape(count, 3 * LANES) for b in range(3)], 1
        )

    def taps(a):
        if not turned:
            return kernel[a * span : (a + 1) * span]
        last = (3 - a) * 9 - 1
        return jnp.concatenate(
            [kernel[(last - k) * LANES : (last - k + 1) * LANES] for k in range(9)], 1
        )

    dims = (((1,), (1 if turned else 0,)), ((), ()))

    def dot(one, two):
        return lax.dot_general(one, two, dims, preferred_element_type=F32)

    def pair(one, two):
        return jnp.concatenate([one, two], 0 if turned else 1)

    both = dot(cells(1), pair(taps(1), taps(0))) + dot(cells(2), pair(taps(2), taps(1)))
    first = both[:, :LANES] + dot(cells(0), taps(0))
    second = both[:, LANES:] + dot(cells(3), taps(2))
    return first, second


def conv_scratch(size, trim, wo):
    tall = size.high + 2 * trim
    return [((2 * FRAMES, tall, wo, 3 * LANES), BF16), ((tall, up(wo + 2, 8), LANES), F32)]


def hidden_body(size, place, near, far, kernel, hidden, pay, stats, x, frame):
    high, wide = size.high, size.wide
    spread_all(size, 1, 1, wide, near, far, x, frame)
    sums = convolved(x, kernel, False)
    upper = place[0] == 0
    rounded = [s.astype(BF16) for s in sums]
    for f in range(FRAMES):
        hidden[f] = rounded[f].reshape(high, wide, LANES)
        edge = jnp.where(upper, rounded[f][size.cells - wide :], rounded[f][:wide])
        pay[f * wide : (f + 1) * wide] = edge
    found = measured([r.astype(F32) for r in rounded])
    stats[...] = found
    at = FRAMES * wide
    fill = jnp.zeros((pay.shape[0] - at - PARTS, LANES), F32)
    pay[at:] = jnp.concatenate([split3(found), fill], 0).astype(BF16)


def grad_act_body(size, near, far, kernel, out, x, frame):
    wo = x.shape[2]
    spread_all(size, 2, 2, wo, near, far, x, frame)
    sums = convolved(x, kernel, True)
    for f in range(FRAMES):
        out[f] = sums[f].reshape(size.tall(), wo, LANES)[:, : size.broad()]


def slots_second_body(size, across, place, hidden, got, stats, slots, flat):
    wide, high = size.wide, size.high
    flat[...] = jnp.zeros_like(flat)
    at = 0
    for frame in range(FRAMES):
        top, bottom = rim_rows(place, got[frame * wide : (frame + 1) * wide].astype(F32))
        own = hidden[frame].astype(F32)
        for side, col in ((0, 0), (1, wide - 1)):
            flat[side, at : at + high + 2] = columns(own, [top], [bottom], col)
        at += size.stride(1)
    first = FRAMES * wide
    parts = split3(merged(stats[...], join3(got[first : first + PARTS]), size.cells))
    flat[0, at : at + PARTS] = parts
    flat[1, at : at + PARTS] = parts
    for peer in range(across):
        slots[peer] = jnp.where(peer > place[1], flat[1], flat[0]).astype(BF16)


def act_second_body(
    size, across, place, hidden, row_got, col_got, grad_act, act, q, z, norm, slots, frame
):
    high, wide = size.high, size.wide
    step = size.stride(1)
    at = FRAMES * step
    found = concluded(
        [join3(col_got[peer, at : at + PARTS]) for peer in range(across)], 2 * size.cells
    )
    norm[...] = found
    left_all, right_all = sides(place, across, col_got, 0, FRAMES * step)
    ok = in_frame((size.tall(), size.broad(), LANES), place, across, size, 1)
    lefts, rights, firsts, seconds = [], [], [], []
    frame[...] = jnp.zeros_like(frame)
    for f in range(FRAMES):
        top, bottom = rim_rows(place, row_got[f * wide : (f + 1) * wide].astype(F32))
        padded_frame(
            size,
            hidden[f].astype(F32),
            top,
            bottom,
            left_all[f * step : (f + 1) * step],
            right_all[f * step : (f + 1) * step],
            frame,
        )
        normed = (frame[...] - found[f : f + 1][None]) * found[FRAMES + f : FRAMES + f + 1][None]
        sigmoid = jax.nn.sigmoid(normed)
        frame[...] = jnp.where(ok, normed * sigmoid, 0.0)
        left, right = put_frame(size, frame, f, act)
        lefts.append(left)
        rights.append(right)
        grad = grad_act[f] * sigmoid * (1.0 + normed * (1.0 - sigmoid))
        z[f] = normed
        q[f] = grad
        row = lax.broadcasted_iota(jnp.int32, grad.shape, 0)
        col = lax.broadcasted_iota(jnp.int32, grad.shape, 1)
        own = (row > 0) & (row <= high) & (col > 0) & (col <= wide)
        inner = jnp.where(own, grad, 0.0)
        firsts.append(jnp.sum(jnp.sum(inner, 0), 0, keepdims=True))
        seconds.append(jnp.sum(jnp.sum(inner * normed, 0), 0, keepdims=True))
    put_sides(act, size.main(1), lefts + rights)
    sums = stat_block(firsts, seconds)
    for peer in range(slots.shape[0]):
        slots[peer] = sums


def hidden_grad_body(size, across, place, q, z, got, norm, out, frame):
    peers = got.shape[0]
    total = got[0]
    for peer in range(1, peers):
        total = total + got[peer]
    means = lane_totals(total) / (size.cells * peers * (LANES // GROUPS))
    ok = in_frame((size.tall(), size.broad(), LANES), place, across, size, 1)
    lefts, rights = [], []
    for f in range(FRAMES):
        first, second = means[f : f + 1][None], means[FRAMES + f : FRAMES + f + 1][None]
        inv = norm[FRAMES + f : FRAMES + f + 1][None]
        frame[...] = jnp.where(ok, inv * (q[f] - first - z[f] * second), 0.0)
        left, right = put_frame(size, frame, f, out)
        lefts.append(left)
        rights.append(right)
    put_sides(out, size.main(1), lefts + rights)


def own_cells(size, block, f):
    start = (f * size.tall() + 1) * size.wide
    return block[start : start + size.cells]


def turned_cells(size, block, out):
    for f in range(FRAMES):
        cells = own_cells(size, block, f).astype(F32).T.astype(BF16)
        out[f * LANES : (f + 1) * LANES] = cells


def tap_sums(x, turned, b):
    ho, wo = x.shape[1] - 2, x.shape[2]

    def cells(f):
        return x[f, b : b + ho].reshape(ho * wo, 3 * LANES)

    def dot(one, two):
        return jnp.dot(one, two, preferred_element_type=F32)

    low = dot(turned[...], cells(1))
    high = dot(turned[...], cells(2))
    return (
        dot(turned[:LANES], cells(0)) + low[LANES:],
        low[:LANES] + high[LANES:],
        high[:LANES] + dot(turned[LANES:], cells(3)),
    )


def second_term_body(size, near, far, act, out, x, frame, turned):
    spread_all(size, 2, 1, size.wide, near, far, x, frame)
    turned_cells(size, act, turned)
    for b in range(3):
        for a, total in enumerate(tap_sums(x, turned, b)):
            for c in range(3):
                tap = ((2 - a) * 3 + 2 - b) * 3 + 2 - c
                out[tap * LANES : (tap + 1) * LANES] = total[:, c * LANES : (c + 1) * LANES]


def first_term_body(size, place, near, far, grad, second, keep, give, x, frame, turned, both):
    spread_all(size, 1, 1, size.wide, near, far, x, frame)
    turned_cells(size, grad, turned)
    for b in range(3):
        for a, total in enumerate(tap_sums(x, turned, b)):
            first = (a * 3 + b) * 3 * LANES
            both[first : first + 3 * LANES] = total.T
    upper = place[0] == 0
    keep[...] = jnp.where(upper, both[...], second[...])
    give[...] = jnp.where(upper, second[...], both[...]).astype(BF16)


def result_body(size, near, far, kernel, features, out, x, frame):
    spread_all(size, 1, 1, size.wide, near, far, x, frame)
    sums = convolved(x, kernel, False)
    for f in range(FRAMES):
        total = features[f].astype(F32) + sums[f].reshape(size.high, size.wide, LANES)
        out[f] = total.astype(BF16)


def back_first_body(size, near, far, kernel, features, norm, q, sums, x, frame):
    spread_all(size, 1, 1, size.wide, near, far, x, frame)
    grads = convolved(x, kernel, True)
    firsts, seconds = [], []
    for f in range(FRAMES):
        values = features[f].astype(F32).reshape(size.cells, LANES)
        normed = (values - norm[f : f + 1]) * norm[FRAMES + f : FRAMES + f + 1]
        sigmoid = jax.nn.sigmoid(normed)
        grad = grads[f] * sigmoid * (1.0 + normed * (1.0 - sigmoid))
        q[f] = grad
        firsts.append(jnp.sum(grad, 0, keepdims=True))
        seconds.append(jnp.sum(grad * normed, 0, keepdims=True))
    sums[...] = stat_block(firsts, seconds)


def feature_grad_body(size, peers, features, out_grad, norm, q, got, out):
    total = join3(got[0])
    for peer in range(1, got.shape[0]):
        total = total + join3(got[peer])
    means = lane_totals(total) / (size.cells * peers * (LANES // GROUPS))
    for f in range(FRAMES):
        values = features[f].astype(F32).reshape(size.cells, LANES)
        inv = norm[FRAMES + f : FRAMES + f + 1]
        normed = (values - norm[f : f + 1]) * inv
        grad = inv * (q[f] - means[f : f + 1] - normed * means[FRAMES + f : FRAMES + f + 1])
        grad = out_grad[f].astype(F32) + grad.reshape(size.high, size.wide, LANES)
        out[f] = grad.astype(BF16)


def row_swap(values):
    return lax.ppermute(values, "row", [(0, 1), (1, 0)])


def later(values, by):
    peers = lax.axis_size("tm")
    pairs = [(i, i + by) for i in range(peers) if 0 <= i + by < peers]
    return lax.ppermute(values, "tm", pairs)


def scatter_sum(values, axis):
    peers = lax.axis_size(axis)
    share = up(values.shape[0], 16 * peers) // peers
    values = jnp.pad(values, ((0, share * peers - values.shape[0]), (0, 0)))
    slots = values.reshape(peers, share, LANES).astype(BF16)
    return lax.all_to_all(slots, axis, 0, 0).astype(F32).sum(0)


def gather_shares(share, axis):
    peers = lax.axis_size(axis)
    slots = jnp.broadcast_to(share[None], (peers,) + share.shape)
    return lax.all_to_all(slots, axis, 0, 0)


def sum_parts(stat):
    high = lax.reduce_precision(stat, 8, 7)
    rest = stat - high
    middle = lax.reduce_precision(rest, 8, 7)
    return jnp.concatenate([high, middle, rest - middle], 0).astype(BF16)


def summed_kernels(keep, give, sums, factor):
    rows = keep.shape[0]
    upper = lax.axis_index("row") == 0
    keep = keep + row_swap(give).astype(F32)
    by_col = scatter_sum(keep, "col")
    by_tm = scatter_sum(by_col, "tm")
    done = (by_tm * factor).astype(BF16)
    done = gather_shares(done, "tm").reshape(-1, LANES)[: by_col.shape[0]]
    parts = sum_parts(sums + row_swap(sums))
    spare = -parts.shape[0] % 16
    done = jnp.concatenate([done, jnp.pad(parts, ((0, spare), (0, 0)))], 0)
    done = gather_shares(done, "col")
    terms = done[:, by_col.shape[0] :]
    done = done[:, : by_col.shape[0]].reshape(-1, LANES)[:rows]
    other = row_swap(done)
    return jnp.where(upper, done, other), jnp.where(upper, other, done), terms


def on_device(features, conv_first, conv_second, out_grad):
    frames, high, wide, chans = features.shape
    assert frames == FRAMES and chans == LANES and lax.axis_size("row") == 2
    size = Sizes(high, wide)
    across = lax.axis_size("col")
    peers = 2 * across
    factor = 1.0 / math.sqrt(size.cells * FRAMES * lax.axis_size("tm") * peers)
    place = jnp.stack([lax.axis_index("row"), lax.axis_index("col")]).astype(jnp.int32)
    taps = conv_first.shape
    first = conv_first.reshape(-1, LANES)
    second = conv_second.reshape(-1, LANES)
    work = 2 * first.size * size.cells * FRAMES
    part = functools.partial
    stat = ((STATS, LANES), F32)
    tall, broad = size.tall(), size.broad()
    frame = ((tall, broad, LANES), F32)

    edge = up(3 * FRAMES * wide + PARTS, 16)
    pay, stats = call(
        part(start_body, size), [((edge, LANES), BF16), stat], [place, features, out_grad], smem=1
    )
    row_got = row_swap(pay)
    lines = up(FRAMES * size.stride(1) + 2 * FRAMES * size.stride(2) + PARTS, 16)
    (slots,) = call(
        part(slots_first_body, size, across),
        [((across, lines, LANES), BF16)],
        [place, features, out_grad, row_got, stats],
        [((2, lines, LANES), F32)],
        smem=1,
    )
    col_got = lax.all_to_all(slots, "col", 0, 0)
    block = ((size.rows(1), LANES), BF16)
    act_first, grad, norm_first = call(
        part(act_first_body, size, across),
        [block, ((size.rows(2), LANES), BF16), stat],
        [place, features, out_grad, row_got, col_got],
        [frame],
        smem=1,
    )
    act_before = later(act_first, 1)
    grad_after = later(grad, -1)

    edge = up(FRAMES * wide + PARTS, 16)
    hidden, pay, stats = call(
        part(hidden_body, size),
        [(features.shape, BF16), ((edge, LANES), BF16), stat],
        [place, act_before, act_first, first],
        conv_scratch(size, 1, wide),
        smem=1,
        mib=24,
        flops=work,
    )
    pay, grad_after = lax.optimization_barrier((pay, grad_after))
    row_got = row_swap(pay)
    lines = up(FRAMES * size.stride(1) + PARTS, 16)
    (slots,) = call(
        part(slots_second_body, size, across),
        [((across, lines, LANES), BF16)],
        [place, hidden, row_got, stats],
        [((2, lines, LANES), F32)],
        smem=1,
    )
    col_got = lax.all_to_all(slots, "col", 0, 0)
    (grad_act,) = call(
        part(grad_act_body, size),
        [((FRAMES, tall, broad, LANES), F32)],
        [grad, grad_after, second],
        conv_scratch(size, 2, up(wide + 2, 16)),
        mib=32,
        flops=2 * work,
    )
    field = ((FRAMES, tall, broad, LANES), F32)
    act_second, q, z, norm_second, slots = call(
        part(act_second_body, size, across),
        [block, field, field, stat, ((peers, STATS, LANES), F32)],
        [place, hidden, row_got, col_got, grad_act],
        [frame],
        smem=1,
    )
    got = lax.all_to_all(slots, ("row", "col"), 0, 0)
    act_second_before = later(act_second, 1)
    turned = ((FRAMES * LANES, size.cells), BF16)
    (second_term,) = call(
        part(second_term_body, size),
        [(first.shape, F32)],
        [grad, grad_after, act_second],
        [*conv_scratch(size, 1, wide), turned],
        mib=24,
        flops=work,
    )
    (hidden_grad,) = call(
        part(hidden_grad_body, size, across),
        [block],
        [place, q, z, got, norm_second],
        [frame],
        smem=1,
    )
    hidden_grad, act_second_before = lax.optimization_barrier((hidden_grad, act_second_before))
    hidden_after = later(hidden_grad, -1)
    keep, give = call(
        part(first_term_body, size),
        [(first.shape, F32), (first.shape, BF16)],
        [place, act_before, act_first, hidden_grad, second_term],
        [*conv_scratch(size, 1, wide), turned, (first.shape, F32)],
        smem=1,
        mib=24,
        flops=work,
    )
    (result,) = call(
        part(result_body, size),
        [(features.shape, BF16)],
        [act_second_before, act_second, second, features],
        conv_scratch(size, 1, wide),
        mib=24,
        flops=work,
    )
    q, sums = call(
        part(back_first_body, size),
        [((FRAMES, size.cells, LANES), F32), stat],
        [hidden_grad, hidden_after, first, features, norm_first],
        conv_scratch(size, 1, wide),
        mib=24,
        flops=work,
    )
    first_grad, second_grad, terms = summed_kernels(keep, give, sums, factor)
    (feature_grad,) = call(
        part(feature_grad_body, size, peers),
        [(features.shape, BF16)],
        [features, out_grad, norm_first, q, terms],
    )
    return (result, feature_grad, first_grad.reshape(taps), second_grad.reshape(taps))


def solution(mesh):
    in_specs = (P("tm", "row", "col", None), P(), P(), P("tm", "row", "col", None))
    out_specs = (P("tm", "row", "col", None), P("tm", "row", "col", None), P(), P())
    return jax.shard_map(
        on_device, mesh=mesh, in_specs=in_specs, out_specs=out_specs, check_vma=False
    )
```

```python
import functools
import math

import jax
import jax.numpy as jnp
from jax import lax
from jax.experimental import pallas as pl
from jax.experimental.pallas import tpu as pltpu
from jax.sharding import PartitionSpec as P

GROUPS = 32
EPSILON = 1e-06
F32 = jnp.float32
BF16 = jnp.bfloat16
LANES = 128
FRAMES = 2
STATS = 8
PARTS = 3 * STATS


def up(count, step):
    return -(-count // step) * step


class Sizes:
    def __init__(self, high, wide):
        self.high, self.wide = high, wide
        self.cells = high * wide

    def stride(self, rim):
        return up(self.high + 2 * rim, 8)

    def main(self, rim):
        return FRAMES * (self.high + 2 * rim) * self.wide

    def rows(self, rim):
        return up(self.main(rim) + 2 * rim * FRAMES * self.stride(rim), 16)

    def tall(self):
        return self.high + 2

    def broad(self):
        return up(self.wide + 2, 8)


def call(body, outs, args, scratch=(), smem=0, mib=8, flops=0):
    specs = [pl.BlockSpec(memory_space=pltpu.SMEM)] * smem
    specs += [pl.BlockSpec(memory_space=pltpu.VMEM)] * (len(args) - smem)
    shapes = [jax.ShapeDtypeStruct(shape, dtype) for shape, dtype in outs]
    moved = sum(math.prod(a.shape) * a.dtype.itemsize for a in [*args, *shapes])
    return pl.pallas_call(
        body,
        out_shape=shapes,
        in_specs=specs,
        out_specs=[pl.BlockSpec(memory_space=pltpu.VMEM)] * len(outs),
        scratch_shapes=[pltpu.VMEM(shape, dtype) for shape, dtype in scratch],
        cost_estimate=pl.CostEstimate(flops=flops, bytes_accessed=moved, transcendentals=0),
        compiler_params=pltpu.CompilerParams(vmem_limit_bytes=mib << 20),
    )(*args)


def lane_totals(stat):
    lane = lax.broadcasted_iota(jnp.int32, stat.shape, 1)
    step = 1
    while step < LANES // GROUPS:
        ahead = pltpu.roll(stat, LANES - step, 1)
        behind = pltpu.roll(stat, step, 1)
        stat = stat + jnp.where((lane // step) % 2 == 0, ahead, behind)
        step *= 2
    return stat


def split3(stat):
    high = stat.astype(BF16).astype(F32)
    rest = stat - high
    middle = rest.astype(BF16).astype(F32)
    return jnp.concatenate([high, middle, rest - middle], 0)


def join3(parts):
    parts = parts.astype(F32)
    return parts[:STATS] + (parts[STATS : 2 * STATS] + parts[2 * STATS : PARTS])


def stat_block(first, second):
    rest = jnp.zeros((STATS - 2 * FRAMES, LANES), F32)
    return jnp.concatenate([*first, *second, rest], 0)


def measured(frames):
    means, squares = [], []
    for frame in frames:
        mean = jnp.sum(frame, 0, keepdims=True) / frame.shape[0]
        centred = frame - mean
        means.append(mean)
        squares.append(jnp.sum(centred * centred, 0, keepdims=True))
    return stat_block(means, squares)


def merged(one, two, cells):
    delta = one - two
    extra = (0.5 * cells) * delta * delta
    mean = 0.5 * (one[:FRAMES] + two[:FRAMES])
    square = one[FRAMES : 2 * FRAMES] + two[FRAMES : 2 * FRAMES] + extra[:FRAMES]
    return jnp.concatenate([mean, square, jnp.zeros((STATS - 2 * FRAMES, LANES), F32)], 0)


def concluded(blocks, cells):
    per_group = LANES // GROUPS
    mean = sum(blocks[1:], blocks[0])[:FRAMES]
    mean = lane_totals(mean) / (len(blocks) * per_group)
    total = jnp.zeros((FRAMES, LANES), F32)
    for block in blocks:
        off = block[:FRAMES] - mean
        total = total + block[FRAMES : 2 * FRAMES] + cells * off * off
    spread = lane_totals(total) / (cells * len(blocks) * per_group)
    rest = jnp.zeros((STATS - 2 * FRAMES, LANES), F32)
    return jnp.concatenate([mean, lax.rsqrt(spread + EPSILON), rest], 0)


def rim_rows(place, got):
    upper = place[0] == 0
    nothing = jnp.zeros_like(got)
    return jnp.where(upper, nothing, got), jnp.where(upper, got, nothing)


def in_frame(shape, place, across, size, rim):
    row = lax.broadcasted_iota(jnp.int32, shape, 0)
    col = lax.broadcasted_iota(jnp.int32, shape, 1)
    top = jnp.where(place[0] == 0, rim, 0)
    bottom = jnp.where(place[0] == 0, size.high + 2 * rim, size.high + rim)
    left = jnp.where(place[1] == 0, rim, 0)
    right = jnp.where(place[1] == across - 1, size.wide + rim, size.wide + 2 * rim)
    return (row >= top) & (row < bottom) & (col >= left) & (col < right)


def start_body(size, place, features, out_grad, pay, stats):
    high, wide = size.high, size.wide
    upper = place[0] == 0
    at = 0
    for frame in range(FRAMES):
        pay[at : at + wide] = jnp.where(upper, features[frame, high - 1], features[frame, 0])
        at += wide
    for frame in range(FRAMES):
        for row in range(2):
            edge = jnp.where(upper, out_grad[frame, high - 2 + row], out_grad[frame, row])
            pay[at : at + wide] = edge
            at += wide
    found = measured([features[f].astype(F32).reshape(size.cells, LANES) for f in range(FRAMES)])
    stats[...] = found
    fill = jnp.zeros((pay.shape[0] - at - PARTS, LANES), F32)
    pay[at:] = jnp.concatenate([split3(found), fill], 0).astype(BF16)


def columns(own, top, bottom, col):
    return jnp.concatenate([*[r[col : col + 1] for r in top], own[:, col], *[r[col : col + 1] for r in bottom]], 0)


def slots_first_body(size, across, place, features, out_grad, got, stats, slots, flat):
    wide, high = size.wide, size.high
    edge = got.shape[0]
    flat[...] = jnp.zeros_like(flat)
    at = 0
    cols = {0: [], 1: []}
    for frame in range(FRAMES):
        rim = got[frame * wide : (frame + 1) * wide].astype(F32)
        top, bottom = rim_rows(place, rim)
        own = features[frame].astype(F32)
        for side, col in ((0, 0), (1, wide - 1)):
            flat[side, at : at + high + 2] = columns(own, [top], [bottom], col)
        at += size.stride(1)
    base = FRAMES * wide
    for j in range(2):
        for frame in range(FRAMES):
            tops, bottoms = [], []
            for row in range(2):
                first = base + (frame * 2 + row) * wide
                top, bottom = rim_rows(place, got[first : first + wide].astype(F32))
                tops.append(top)
                bottoms.append(bottom)
            own = out_grad[frame].astype(F32)
            for side, col in ((0, j), (1, wide - 2 + j)):
                flat[side, at : at + high + 4] = columns(own, tops, bottoms, col)
            at += size.stride(2)
    first = 3 * FRAMES * wide
    both = merged(stats[...], join3(got[first : first + PARTS]), size.cells)
    parts = split3(both)
    flat[0, at : at + PARTS] = parts
    flat[1, at : at + PARTS] = parts
    for peer in range(across):
        slots[peer] = jnp.where(peer > place[1], flat[1], flat[0]).astype(BF16)


def sides(place, across, got, first, count):
    left = got[jnp.maximum(place[1] - 1, 0), first : first + count].astype(F32)
    right = got[jnp.minimum(place[1] + 1, across - 1), first : first + count].astype(F32)
    nothing = jnp.zeros_like(left)
    left = jnp.where(place[1] > 0, left, nothing)
    right = jnp.where(place[1] < across - 1, right, nothing)
    return left, right


def padded_frame(size, own, top, bottom, left, right, frame):
    high, wide = size.high, size.wide
    frame[1 : high + 1, 1 : wide + 1] = own
    frame[0:1, 1 : wide + 1] = top[None]
    frame[high + 1 : high + 2, 1 : wide + 1] = bottom[None]
    tall = high + 2
    frame[:, 0:1] = left[:tall].reshape(tall, 1, LANES)
    frame[:, wide + 1 : wide + 2] = right[:tall].reshape(tall, 1, LANES)


def put_frame(size, frame, index, out):
    wide, tall, step = size.wide, size.tall(), size.stride(1)
    flat = frame[:, 1 : wide + 1].reshape(tall * wide, LANES)
    out[index * tall * wide : (index + 1) * tall * wide] = flat.astype(BF16)
    fill = jnp.zeros((step - tall, LANES), F32)
    left = frame[:, 0:1].reshape(tall, LANES)
    right = frame[:, wide + 1 : wide + 2].reshape(tall, LANES)
    return jnp.concatenate([left, fill], 0), jnp.concatenate([right, fill], 0)


def put_sides(out, first, blocks):
    fill = out.shape[0] - first - sum(b.shape[0] for b in blocks)
    if fill:
        blocks = [*blocks, jnp.zeros((fill, LANES), F32)]
    out[first:] = jnp.concatenate(blocks, 0).astype(BF16)


def act_first_body(
    size, across, place, features, out_grad, row_got, col_got, act, grad, norm, frame
):
    high, wide = size.high, size.wide
    at = FRAMES * size.stride(1) + 2 * FRAMES * size.stride(2)
    blocks = [join3(col_got[peer, at : at + PARTS]) for peer in range(across)]
    found = concluded(blocks, 2 * size.cells)
    norm[...] = found
    step = size.stride(1)
    left_all, right_all = sides(place, across, col_got, 0, FRAMES * step)
    ok = in_frame((size.tall(), size.broad(), LANES), place, across, size, 1)
    lefts, rights = [], []
    frame[...] = jnp.zeros_like(frame)
    for f in range(FRAMES):
        top, bottom = rim_rows(place, row_got[f * wide : (f + 1) * wide].astype(F32))
        padded_frame(
            size,
            features[f].astype(F32),
            top,
            bottom,
            left_all[f * step : (f + 1) * step],
            right_all[f * step : (f + 1) * step],
            frame,
        )
        normed = (frame[...] - found[f : f + 1][None]) * found[FRAMES + f : FRAMES + f + 1][None]
        frame[...] = jnp.where(ok, normed * jax.nn.sigmoid(normed), 0.0)
        left, right = put_frame(size, frame, f, act)
        lefts.append(left)
        rights.append(right)
    put_sides(act, size.main(1), lefts + rights)

    tall = high + 4
    for f in range(FRAMES):
        start = f * tall * wide
        for row in range(2):
            first = FRAMES * wide + (f * 2 + row) * wide
            top, bottom = rim_rows(place, row_got[first : first + wide])
            grad[start + row * wide : start + (row + 1) * wide] = top
            below = start + (high + 2 + row) * wide
            grad[below : below + wide] = bottom
        grad[start + 2 * wide : start + (high + 2) * wide] = out_grad[f].reshape(
            size.cells, LANES
        )
    left, right = sides(
        place, across, col_got, FRAMES * step, 2 * FRAMES * size.stride(2)
    )
    put_sides(grad, size.main(2), [left, right])


def spread_columns(size, rim, trim, wo, block, index, dst, at, frame):
    wide, high = size.wide, size.high
    tall, step = high + 2 * rim, size.stride(rim)
    main = block[index * tall * wide : (index + 1) * tall * wide].astype(F32)
    main = main.reshape(tall, wide, LANES)
    cut = rim - trim
    tall_out = tall - 2 * cut
    frame[:, trim : trim + wide] = main[cut : cut + tall_out]
    first = size.main(rim)
    edges = block[first:].astype(F32)
    for j in range(2 * rim):
        col = j - cut if j < rim else j - rim + trim + wide
        if j < cut or (j >= rim and j - rim >= trim):
            continue
        start = (j * FRAMES + index) * step
        edge = edges[start + cut : start + cut + tall_out]
        frame[:, col : col + 1] = edge.reshape(tall_out, 1, LANES)
    for c in range(3):
        dst[at, :, :, c * LANES : (c + 1) * LANES] = frame[:, c : c + wo].astype(BF16)


def spread_all(size, rim, trim, wo, near, far, dst, frame):
    filled = size.wide + 2 * trim
    if frame.shape[1] > filled:
        frame[:, filled:] = jnp.zeros((frame.shape[0], frame.shape[1] - filled, LANES), F32)
    for f in range(2 * FRAMES):
        block = near if f < FRAMES else far
        spread_columns(size, rim, trim, wo, block, f % FRAMES, dst, f, frame)


def convolved(x, kernel, turned):
    tall, wo = x.shape[1], x.shape[2]
    ho = tall - 2
    count = ho * wo
    span = 9 * LANES

    def cells(f):
        return jnp.concatenate(
            [x[f, b : b + ho].reshape(count, 3 * LANES) for b in range(3)], 1
        )

    def taps(a):
        if not turned:
            return kernel[a * span : (a + 1) * span]
        last = (3 - a) * 9 - 1
        return jnp.concatenate(
            [kernel[(last - k) * LANES : (last - k + 1) * LANES] for k in range(9)], 1
        )

    dims = (((1,), (1 if turned else 0,)), ((), ()))

    def dot(one, two):
        return lax.dot_general(one, two, dims, preferred_element_type=F32)

    def pair(one, two):
        return jnp.concatenate([one, two], 0 if turned else 1)

    both = dot(cells(1), pair(taps(1), taps(0))) + dot(cells(2), pair(taps(2), taps(1)))
    first = both[:, :LANES] + dot(cells(0), taps(0))
    second = both[:, LANES:] + dot(cells(3), taps(2))
    return first, second


def conv_scratch(size, trim, wo):
    tall = size.high + 2 * trim
    return [((2 * FRAMES, tall, wo, 3 * LANES), BF16), ((tall, up(wo + 2, 8), LANES), F32)]


def hidden_body(size, place, near, far, kernel, hidden, pay, stats, x, frame):
    high, wide = size.high, size.wide
    spread_all(size, 1, 1, wide, near, far, x, frame)
    sums = convolved(x, kernel, False)
    upper = place[0] == 0
    rounded = [s.astype(BF16) for s in sums]
    for f in range(FRAMES):
        hidden[f] = rounded[f].reshape(high, wide, LANES)
        edge = jnp.where(upper, rounded[f][size.cells - wide :], rounded[f][:wide])
        pay[f * wide : (f + 1) * wide] = edge
    found = measured([r.astype(F32) for r in rounded])
    stats[...] = found
    at = FRAMES * wide
    fill = jnp.zeros((pay.shape[0] - at - PARTS, LANES), F32)
    pay[at:] = jnp.concatenate([split3(found), fill], 0).astype(BF16)


def grad_act_body(size, near, far, kernel, out, x, frame):
    wo = x.shape[2]
    spread_all(size, 2, 2, wo, near, far, x, frame)
    sums = convolved(x, kernel, True)
    for f in range(FRAMES):
        out[f] = sums[f].reshape(size.tall(), wo, LANES)[:, : size.broad()]


def slots_second_body(size, across, place, hidden, got, stats, slots, flat):
    wide, high = size.wide, size.high
    flat[...] = jnp.zeros_like(flat)
    at = 0
    for frame in range(FRAMES):
        top, bottom = rim_rows(place, got[frame * wide : (frame + 1) * wide].astype(F32))
        own = hidden[frame].astype(F32)
        for side, col in ((0, 0), (1, wide - 1)):
            flat[side, at : at + high + 2] = columns(own, [top], [bottom], col)
        at += size.stride(1)
    first = FRAMES * wide
    parts = split3(merged(stats[...], join3(got[first : first + PARTS]), size.cells))
    flat[0, at : at + PARTS] = parts
    flat[1, at : at + PARTS] = parts
    for peer in range(across):
        slots[peer] = jnp.where(peer > place[1], flat[1], flat[0]).astype(BF16)


def act_second_body(
    size, across, place, hidden, row_got, col_got, grad_act, act, q, z, norm, slots, frame
):
    high, wide = size.high, size.wide
    step = size.stride(1)
    at = FRAMES * step
    found = concluded(
        [join3(col_got[peer, at : at + PARTS]) for peer in range(across)], 2 * size.cells
    )
    norm[...] = found
    left_all, right_all = sides(place, across, col_got, 0, FRAMES * step)
    ok = in_frame((size.tall(), size.broad(), LANES), place, across, size, 1)
    lefts, rights, firsts, seconds = [], [], [], []
    frame[...] = jnp.zeros_like(frame)
    for f in range(FRAMES):
        top, bottom = rim_rows(place, row_got[f * wide : (f + 1) * wide].astype(F32))
        padded_frame(
            size,
            hidden[f].astype(F32),
            top,
            bottom,
            left_all[f * step : (f + 1) * step],
            right_all[f * step : (f + 1) * step],
            frame,
        )
        normed = (frame[...] - found[f : f + 1][None]) * found[FRAMES + f : FRAMES + f + 1][None]
        sigmoid = jax.nn.sigmoid(normed)
        frame[...] = jnp.where(ok, normed * sigmoid, 0.0)
        left, right = put_frame(size, frame, f, act)
        lefts.append(left)
        rights.append(right)
        grad = grad_act[f] * sigmoid * (1.0 + normed * (1.0 - sigmoid))
        z[f] = normed
        q[f] = grad
        row = lax.broadcasted_iota(jnp.int32, grad.shape, 0)
        col = lax.broadcasted_iota(jnp.int32, grad.shape, 1)
        own = (row > 0) & (row <= high) & (col > 0) & (col <= wide)
        inner = jnp.where(own, grad, 0.0)
        firsts.append(jnp.sum(jnp.sum(inner, 0), 0, keepdims=True))
        seconds.append(jnp.sum(jnp.sum(inner * normed, 0), 0, keepdims=True))
    put_sides(act, size.main(1), lefts + rights)
    sums = stat_block(firsts, seconds)
    for peer in range(slots.shape[0]):
        slots[peer] = sums


def hidden_grad_body(size, across, place, q, z, got, norm, out, frame):
    peers = got.shape[0]
    total = got[0]
    for peer in range(1, peers):
        total = total + got[peer]
    means = lane_totals(total) / (size.cells * peers * (LANES // GROUPS))
    ok = in_frame((size.tall(), size.broad(), LANES), place, across, size, 1)
    lefts, rights = [], []
    for f in range(FRAMES):
        first, second = means[f : f + 1][None], means[FRAMES + f : FRAMES + f + 1][None]
        inv = norm[FRAMES + f : FRAMES + f + 1][None]
        frame[...] = jnp.where(ok, inv * (q[f] - first - z[f] * second), 0.0)
        left, right = put_frame(size, frame, f, out)
        lefts.append(left)
        rights.append(right)
    put_sides(out, size.main(1), lefts + rights)


def own_cells(size, block, f):
    start = (f * size.tall() + 1) * size.wide
    return block[start : start + size.cells]


def turned_cells(size, block, out):
    for f in range(FRAMES):
        cells = own_cells(size, block, f).astype(F32).T.astype(BF16)
        out[f * LANES : (f + 1) * LANES] = cells


def tap_sums(x, turned, b):
    ho, wo = x.shape[1] - 2, x.shape[2]

    def cells(f):
        return x[f, b : b + ho].reshape(ho * wo, 3 * LANES)

    def dot(one, two):
        return jnp.dot(one, two, preferred_element_type=F32)

    low = dot(turned[...], cells(1))
    high = dot(turned[...], cells(2))
    return (
        dot(turned[:LANES], cells(0)) + low[LANES:],
        low[:LANES] + high[LANES:],
        high[:LANES] + dot(turned[LANES:], cells(3)),
    )


def second_term_body(size, near, far, act, out, x, frame, turned):
    spread_all(size, 2, 1, size.wide, near, far, x, frame)
    turned_cells(size, act, turned)
    for b in range(3):
        for a, total in enumerate(tap_sums(x, turned, b)):
            for c in range(3):
                tap = ((2 - a) * 3 + 2 - b) * 3 + 2 - c
                out[tap * LANES : (tap + 1) * LANES] = total[:, c * LANES : (c + 1) * LANES]


def first_term_body(size, place, near, far, grad, second, keep, give, x, frame, turned, both):
    spread_all(size, 1, 1, size.wide, near, far, x, frame)
    turned_cells(size, grad, turned)
    for b in range(3):
        for a, total in enumerate(tap_sums(x, turned, b)):
            first = (a * 3 + b) * 3 * LANES
            both[first : first + 3 * LANES] = total.T
    upper = place[0] == 0
    keep[...] = jnp.where(upper, both[...], second[...])
    give[...] = jnp.where(upper, second[...], both[...]).astype(BF16)


def result_body(size, near, far, kernel, features, out, x, frame):
    spread_all(size, 1, 1, size.wide, near, far, x, frame)
    sums = convolved(x, kernel, False)
    for f in range(FRAMES):
        total = features[f].astype(F32) + sums[f].reshape(size.high, size.wide, LANES)
        out[f] = total.astype(BF16)


def back_first_body(size, near, far, kernel, features, norm, q, sums, x, frame):
    spread_all(size, 1, 1, size.wide, near, far, x, frame)
    grads = convolved(x, kernel, True)
    firsts, seconds = [], []
    for f in range(FRAMES):
        values = features[f].astype(F32).reshape(size.cells, LANES)
        normed = (values - norm[f : f + 1]) * norm[FRAMES + f : FRAMES + f + 1]
        sigmoid = jax.nn.sigmoid(normed)
        grad = grads[f] * sigmoid * (1.0 + normed * (1.0 - sigmoid))
        q[f] = grad
        firsts.append(jnp.sum(grad, 0, keepdims=True))
        seconds.append(jnp.sum(grad * normed, 0, keepdims=True))
    sums[...] = stat_block(firsts, seconds)


def feature_grad_body(size, peers, features, out_grad, norm, q, got, out):
    total = join3(got[0])
    for peer in range(1, got.shape[0]):
        total = total + join3(got[peer])
    means = lane_totals(total) / (size.cells * peers * (LANES // GROUPS))
    for f in range(FRAMES):
        values = features[f].astype(F32).reshape(size.cells, LANES)
        inv = norm[FRAMES + f : FRAMES + f + 1]
        normed = (values - norm[f : f + 1]) * inv
        grad = inv * (q[f] - means[f : f + 1] - normed * means[FRAMES + f : FRAMES + f + 1])
        grad = out_grad[f].astype(F32) + grad.reshape(size.high, size.wide, LANES)
        out[f] = grad.astype(BF16)


def row_swap(values):
    return lax.ppermute(values, "row", [(0, 1), (1, 0)])


def later(values, by):
    peers = lax.axis_size("tm")
    pairs = [(i, i + by) for i in range(peers) if 0 <= i + by < peers]
    return lax.ppermute(values, "tm", pairs)


def sum_parts(stat):
    high = lax.reduce_precision(stat, 8, 7)
    rest = stat - high
    middle = lax.reduce_precision(rest, 8, 7)
    return jnp.concatenate([high, middle, rest - middle], 0).astype(BF16)


def total_of(got):
    total = got[0].astype(F32)
    for peer in range(1, got.shape[0]):
        total = total + got[peer].astype(F32)
    return total


def shared_body(got, out, flat):
    rows, share = got.shape[1], out.shape[1]
    if flat.shape[0] > rows:
        flat[rows:] = jnp.zeros((flat.shape[0] - rows, LANES), F32)
    flat[:rows] = total_of(got)
    for peer in range(out.shape[0]):
        out[peer] = flat[peer * share : (peer + 1) * share].astype(BF16)


def finished_body(factor, got, out):
    total = (total_of(got) * factor).astype(BF16)
    for peer in range(out.shape[0]):
        out[peer] = total


def placed_body(rows, place, mine, theirs, first, second, sems):
    def move(one, two):
        copies = []
        for peer in range(mine.shape[0]):
            for k, (source, target) in enumerate(((mine, one), (theirs, two))):
                copies.append(
                    pltpu.make_async_copy(
                        source.at[peer, pl.ds(0, rows)],
                        target.at[pl.ds(peer * rows, rows)],
                        sems.at[k, peer],
                    )
                )
        for copy in copies:
            copy.start()
        for copy in copies:
            copy.wait()

    @pl.when(place[0] == 0)
    def _():
        move(first, second)

    @pl.when(place[0] != 0)
    def _():
        move(second, first)


def placed(place, mine, theirs, rows, count):
    anywhere = pl.BlockSpec(memory_space=pl.ANY)
    return pl.pallas_call(
        functools.partial(placed_body, rows),
        out_shape=[jax.ShapeDtypeStruct((count, LANES), BF16)] * 2,
        in_specs=[pl.BlockSpec(memory_space=pltpu.SMEM), anywhere, anywhere],
        out_specs=[anywhere, anywhere],
        scratch_shapes=[pltpu.SemaphoreType.DMA((2, mine.shape[0]))],
        compiler_params=pltpu.CompilerParams(vmem_limit_bytes=1 << 20),
    )(place, mine, theirs)


def on_device(features, conv_first, conv_second, out_grad):
    frames, high, wide, chans = features.shape
    assert frames == FRAMES and chans == LANES and lax.axis_size("row") == 2
    size = Sizes(high, wide)
    across = lax.axis_size("col")
    peers = 2 * across
    factor = 1.0 / math.sqrt(size.cells * FRAMES * lax.axis_size("tm") * peers)
    place = jnp.stack([lax.axis_index("row"), lax.axis_index("col")]).astype(jnp.int32)
    taps = conv_first.shape
    first = conv_first.reshape(-1, LANES)
    second = conv_second.reshape(-1, LANES)
    work = 2 * first.size * size.cells * FRAMES
    part = functools.partial
    stat = ((STATS, LANES), F32)
    tall, broad = size.tall(), size.broad()
    frame = ((tall, broad, LANES), F32)

    edge = up(3 * FRAMES * wide + PARTS, 16)
    pay, stats = call(
        part(start_body, size), [((edge, LANES), BF16), stat], [place, features, out_grad], smem=1
    )
    row_got = row_swap(pay)
    lines = up(FRAMES * size.stride(1) + 2 * FRAMES * size.stride(2) + PARTS, 16)
    (slots,) = call(
        part(slots_first_body, size, across),
        [((across, lines, LANES), BF16)],
        [place, features, out_grad, row_got, stats],
        [((2, lines, LANES), F32)],
        smem=1,
    )
    col_got = lax.all_to_all(slots, "col", 0, 0)
    block = ((size.rows(1), LANES), BF16)
    act_first, grad, norm_first = call(
        part(act_first_body, size, across),
        [block, ((size.rows(2), LANES), BF16), stat],
        [place, features, out_grad, row_got, col_got],
        [frame],
        smem=1,
    )
    act_before = later(act_first, 1)
    grad_after = later(grad, -1)

    edge = up(FRAMES * wide + PARTS, 16)
    hidden, pay, stats = call(
        part(hidden_body, size),
        [(features.shape, BF16), ((edge, LANES), BF16), stat],
        [place, act_before, act_first, first],
        conv_scratch(size, 1, wide),
        smem=1,
        mib=14,
        flops=work,
    )
    row_got = row_swap(pay)
    lines = up(FRAMES * size.stride(1) + PARTS, 16)
    (slots,) = call(
        part(slots_second_body, size, across),
        [((across, lines, LANES), BF16)],
        [place, hidden, row_got, stats],
        [((2, lines, LANES), F32)],
        smem=1,
    )
    slots, grad_after = lax.optimization_barrier((slots, grad_after))
    col_got = lax.all_to_all(slots, "col", 0, 0)
    (grad_act,) = call(
        part(grad_act_body, size),
        [((FRAMES, tall, broad, LANES), F32)],
        [grad, grad_after, second],
        conv_scratch(size, 2, up(wide + 2, 16)),
        mib=16,
        flops=2 * work,
    )
    field = ((FRAMES, tall, broad, LANES), F32)
    act_second, q, z, norm_second, slots = call(
        part(act_second_body, size, across),
        [block, field, field, stat, ((peers, STATS, LANES), F32)],
        [place, hidden, row_got, col_got, grad_act],
        [frame],
        smem=1,
    )
    got = lax.all_to_all(slots, ("row", "col"), 0, 0)
    turned = ((FRAMES * LANES, size.cells), BF16)
    (second_term,) = call(
        part(second_term_body, size),
        [(first.shape, F32)],
        [grad, grad_after, act_second],
        [*conv_scratch(size, 1, wide), turned],
        mib=14,
        flops=work,
    )
    (hidden_grad,) = call(
        part(hidden_grad_body, size, across),
        [block],
        [place, q, z, got, norm_second],
        [frame],
        smem=1,
    )
    keep, give = call(
        part(first_term_body, size),
        [(first.shape, F32), (first.shape, BF16)],
        [place, act_before, act_first, hidden_grad, second_term],
        [*conv_scratch(size, 1, wide), turned, (first.shape, F32)],
        smem=1,
        mib=20,
        flops=work,
    )
    give, late_grad, late_act = lax.optimization_barrier((give, hidden_grad, act_second))
    hidden_after = later(late_grad, -1)
    act_before = later(late_act, 1)

    along = lax.axis_size("tm")
    rows = first.shape[0]
    keep = keep + row_swap(give).astype(F32)
    by_col = rows // across
    slots = lax.all_to_all(keep.reshape(across, by_col, LANES).astype(BF16), "col", 0, 0)
    share = up(by_col, 16 * along) // along
    slots, hidden_after, act_before = lax.optimization_barrier((slots, hidden_after, act_before))
    (slots,) = call(
        shared_body,
        [((along, share, LANES), BF16)],
        [slots],
        [((along * share, LANES), F32)],
    )
    got = lax.all_to_all(slots, "tm", 0, 0)
    (result,) = call(
        part(result_body, size),
        [(features.shape, BF16)],
        [act_before, act_second, second, features],
        conv_scratch(size, 1, wide),
        mib=14,
        flops=work,
    )
    q, sums = call(
        part(back_first_body, size),
        [((FRAMES, size.cells, LANES), F32), stat],
        [hidden_grad, hidden_after, first, features, norm_first],
        conv_scratch(size, 1, wide),
        mib=14,
        flops=work,
    )
    got, result = lax.optimization_barrier((got, result))
    (slots,) = call(part(finished_body, factor), [((along, share, LANES), BF16)], [got])
    done = lax.all_to_all(slots, "tm", 0, 0).reshape(-1, LANES)[:by_col]
    parts = sum_parts(sums + row_swap(sums))
    parts = jnp.pad(parts, ((0, -parts.shape[0] % 16), (0, 0)))
    done = jnp.concatenate([done, parts], 0)
    mine = lax.all_to_all(jnp.broadcast_to(done[None], (across, *done.shape)), "col", 0, 0)
    first_grad, second_grad = placed(place, mine, row_swap(mine), by_col, rows)
    (feature_grad,) = call(
        part(feature_grad_body, size, peers),
        [(features.shape, BF16)],
        [features, out_grad, norm_first, q, mine[:, by_col:]],
    )
    return (result, feature_grad, first_grad.reshape(taps), second_grad.reshape(taps))


def solution(mesh):
    in_specs = (P("tm", "row", "col", None), P(), P(), P("tm", "row", "col", None))
    out_specs = (P("tm", "row", "col", None), P("tm", "row", "col", None), P(), P())
    return jax.shard_map(
        on_device, mesh=mesh, in_specs=in_specs, out_specs=out_specs, check_vma=False
    )
```

```python
import functools
import math

import jax
import jax.numpy as jnp
from jax import lax
from jax.experimental import pallas as pl
from jax.experimental.pallas import tpu as pltpu
from jax.sharding import PartitionSpec as P

GROUPS = 32
EPSILON = 1e-06
F32 = jnp.float32
BF16 = jnp.bfloat16
LANES = 128
FRAMES = 2
STATS = 8
PARTS = 3 * STATS


def up(count, step):
    return -(-count // step) * step


class Sizes:
    def __init__(self, high, wide):
        self.high, self.wide = high, wide
        self.cells = high * wide

    def stride(self, rim):
        return up(self.high + 2 * rim, 8)

    def main(self, rim):
        return FRAMES * (self.high + 2 * rim) * self.wide

    def rows(self, rim):
        return up(self.main(rim) + 2 * rim * FRAMES * self.stride(rim), 16)

    def tall(self):
        return self.high + 2

    def broad(self):
        return up(self.wide + 2, 8)


def call(body, outs, args, scratch=(), smem=0, far=0, sems=0, mib=8, flops=0, beside=False, out_far=0):
    specs = [pl.BlockSpec(memory_space=pltpu.SMEM)] * smem
    specs += [pl.BlockSpec(memory_space=pltpu.VMEM)] * (len(args) - smem - far)
    specs += [pl.BlockSpec(memory_space=pltpu.HBM)] * far
    near = len(args) - far
    args = [*args[:near], *(pltpu.with_memory_space_constraint(a, pltpu.HBM) for a in args[near:])]
    scratches = [pltpu.VMEM(shape, dtype) for shape, dtype in scratch]
    if sems:
        scratches.append(pltpu.SemaphoreType.DMA((sems,)))
    shapes = [jax.ShapeDtypeStruct(shape, dtype) for shape, dtype in outs]
    kept = len(outs) - out_far
    moved = sum(math.prod(a.shape) * a.dtype.itemsize for a in [*args, *shapes])
    moved = 0 if beside else moved
    return pl.pallas_call(
        body,
        out_shape=shapes[:kept] + [pltpu.HBM(o.shape, o.dtype) for o in shapes[kept:]],
        in_specs=specs,
        out_specs=[pl.BlockSpec(memory_space=pltpu.VMEM)] * kept
        + [pl.BlockSpec(memory_space=pltpu.HBM)] * out_far,
        scratch_shapes=scratches,
        cost_estimate=pl.CostEstimate(flops=flops, bytes_accessed=moved, transcendentals=0),
        compiler_params=pltpu.CompilerParams(vmem_limit_bytes=mib << 20),
    )(*args)


def logistic(values):
    return 0.5 * jnp.tanh(0.5 * values) + 0.5


def lane_totals(stat):
    lane = lax.broadcasted_iota(jnp.int32, stat.shape, 1)
    step = 1
    while step < LANES // GROUPS:
        ahead = pltpu.roll(stat, LANES - step, 1)
        behind = pltpu.roll(stat, step, 1)
        stat = stat + jnp.where((lane // step) % 2 == 0, ahead, behind)
        step *= 2
    return stat


def split3(stat):
    high = stat.astype(BF16).astype(F32)
    rest = stat - high
    middle = rest.astype(BF16).astype(F32)
    return jnp.concatenate([high, middle, rest - middle], 0)


def join3(parts):
    parts = parts.astype(F32)
    return parts[:STATS] + (parts[STATS : 2 * STATS] + parts[2 * STATS : PARTS])


def stat_block(first, second):
    rest = jnp.zeros((STATS - 2 * FRAMES, LANES), F32)
    return jnp.concatenate([*first, *second, rest], 0)


def measured(frames):
    means, squares = [], []
    for frame in frames:
        mean = jnp.sum(frame, 0, keepdims=True) / frame.shape[0]
        centred = frame - mean
        means.append(mean)
        squares.append(jnp.sum(centred * centred, 0, keepdims=True))
    return stat_block(means, squares)


def merged(one, two, cells):
    delta = one - two
    extra = (0.5 * cells) * delta * delta
    mean = 0.5 * (one[:FRAMES] + two[:FRAMES])
    square = one[FRAMES : 2 * FRAMES] + two[FRAMES : 2 * FRAMES] + extra[:FRAMES]
    return jnp.concatenate([mean, square, jnp.zeros((STATS - 2 * FRAMES, LANES), F32)], 0)


def concluded(blocks, cells):
    per_group = LANES // GROUPS
    mean = sum(blocks[1:], blocks[0])[:FRAMES]
    mean = lane_totals(mean) / (len(blocks) * per_group)
    total = jnp.zeros((FRAMES, LANES), F32)
    for block in blocks:
        off = block[:FRAMES] - mean
        total = total + block[FRAMES : 2 * FRAMES] + cells * off * off
    spread = lane_totals(total) / (cells * len(blocks) * per_group)
    rest = jnp.zeros((STATS - 2 * FRAMES, LANES), F32)
    return jnp.concatenate([mean, lax.rsqrt(spread + EPSILON), rest], 0)


def rim_rows(place, got):
    upper = place[0] == 0
    nothing = jnp.zeros_like(got)
    return jnp.where(upper, nothing, got), jnp.where(upper, got, nothing)


def in_frame(shape, place, across, size, rim):
    row = lax.broadcasted_iota(jnp.int32, shape, 0)
    col = lax.broadcasted_iota(jnp.int32, shape, 1)
    top = jnp.where(place[0] == 0, rim, 0)
    bottom = jnp.where(place[0] == 0, size.high + 2 * rim, size.high + rim)
    left = jnp.where(place[1] == 0, rim, 0)
    right = jnp.where(place[1] == across - 1, size.wide + rim, size.wide + 2 * rim)
    return (row >= top) & (row < bottom) & (col >= left) & (col < right)


def take_columns(size, arrays, flat):
    flat[...] = jnp.zeros_like(flat)
    at = 0
    for array, rim in arrays:
        for j in range(rim):
            for frame in range(FRAMES):
                for side, col in ((0, j), (1, size.wide - rim + j)):
                    rows = array[frame, :, col : col + 1].astype(F32)
                    rows = rows.reshape(size.high, LANES)
                    flat[side, at + rim : at + rim + size.high] = rows
                at += size.stride(rim)


def columns_body(size, hidden, flat):
    take_columns(size, ((hidden, 1),), flat)


def start_body(
    size, place, features_far, grad_far, pay, stats, flat, features, out_grad, sems
):
    high, wide = size.high, size.wide
    upper = place[0] == 0
    copies = [
        pltpu.make_async_copy(source.at[f], target.at[f], sems.at[FRAMES * k + f])
        for k, (source, target) in enumerate(((features_far, features), (grad_far, out_grad)))
        for f in range(FRAMES)
    ]
    for copy in copies:
        copy.start()
    for copy in copies[:FRAMES]:
        copy.wait()
    at = 0
    for frame in range(FRAMES):
        pay[at : at + wide] = jnp.where(upper, features[frame, high - 1], features[frame, 0])
        at += wide
    found = measured([features[f].astype(F32).reshape(size.cells, LANES) for f in range(FRAMES)])
    stats[...] = found
    for copy in copies[FRAMES:]:
        copy.wait()
    for frame in range(FRAMES):
        for row in range(2):
            edge = jnp.where(upper, out_grad[frame, high - 2 + row], out_grad[frame, row])
            pay[at : at + wide] = edge
            at += wide
    fill = jnp.zeros((pay.shape[0] - at - PARTS, LANES), F32)
    pay[at:] = jnp.concatenate([split3(found), fill], 0).astype(BF16)
    take_columns(size, ((features, 1), (out_grad, 2)), flat)


def slots_body(size, rims, across, place, flat, got, stats, slots, work):
    wide, high = size.wide, size.high
    upper = place[0] == 0
    work[...] = flat[...]
    at = base = 0
    for rim in rims:
        for j in range(rim):
            for frame in range(FRAMES):
                for row in range(rim):
                    start = base + (frame * rim + row) * wide
                    for side, col in ((0, j), (1, wide - rim + j)):
                        cell = start - start % 16 + 16 * ((start % 16 + col) // 16)
                        tile = got[cell : cell + 16].astype(F32)
                        edge = tile[start + col - cell : start + col - cell + 1]
                        nothing = jnp.zeros_like(edge)
                        top, bottom = at + row, at + rim + high + row
                        work[side, top : top + 1] = jnp.where(upper, nothing, edge)
                        work[side, bottom : bottom + 1] = jnp.where(upper, edge, nothing)
                at += size.stride(rim)
        base += FRAMES * rim * wide
    parts = split3(merged(stats[...], join3(got[base : base + PARTS]), size.cells))
    work[0, at : at + PARTS] = parts
    work[1, at : at + PARTS] = parts
    for peer in range(across):
        slots[peer] = jnp.where(peer > place[1], work[1], work[0]).astype(BF16)


def sides(place, across, got, first, count):
    left = got[jnp.maximum(place[1] - 1, 0), first : first + count].astype(F32)
    right = got[jnp.minimum(place[1] + 1, across - 1), first : first + count].astype(F32)
    nothing = jnp.zeros_like(left)
    left = jnp.where(place[1] > 0, left, nothing)
    right = jnp.where(place[1] < across - 1, right, nothing)
    return left, right


def padded_frame(size, own, top, bottom, left, right, frame):
    high, wide = size.high, size.wide
    frame[1 : high + 1, 1 : wide + 1] = own
    frame[0:1, 1 : wide + 1] = top[None]
    frame[high + 1 : high + 2, 1 : wide + 1] = bottom[None]
    tall = high + 2
    frame[:, 0:1] = left[:tall].reshape(tall, 1, LANES)
    frame[:, wide + 1 : wide + 2] = right[:tall].reshape(tall, 1, LANES)


def put_frame(size, frame, index, out):
    wide, tall, step = size.wide, size.tall(), size.stride(1)
    flat = frame[:, 1 : wide + 1].reshape(tall * wide, LANES)
    out[index * tall * wide : (index + 1) * tall * wide] = flat.astype(BF16)
    fill = jnp.zeros((step - tall, LANES), F32)
    left = frame[:, 0:1].reshape(tall, LANES)
    right = frame[:, wide + 1 : wide + 2].reshape(tall, LANES)
    return jnp.concatenate([left, fill], 0), jnp.concatenate([right, fill], 0)


def put_sides(out, first, blocks):
    fill = out.shape[0] - first - sum(b.shape[0] for b in blocks)
    if fill:
        blocks = [*blocks, jnp.zeros((fill, LANES), F32)]
    out[first:] = jnp.concatenate(blocks, 0).astype(BF16)


def act_first_body(
    size, across, place, features, out_grad, row_got, col_got, act, grad, norm, frame
):
    high, wide = size.high, size.wide
    at = FRAMES * size.stride(1) + 2 * FRAMES * size.stride(2)
    blocks = [join3(col_got[peer, at : at + PARTS]) for peer in range(across)]
    found = concluded(blocks, 2 * size.cells)
    norm[...] = found
    step = size.stride(1)
    left_all, right_all = sides(place, across, col_got, 0, FRAMES * step)
    ok = in_frame((size.tall(), size.broad(), LANES), place, across, size, 1)
    lefts, rights = [], []
    frame[...] = jnp.zeros_like(frame)
    for f in range(FRAMES):
        top, bottom = rim_rows(place, row_got[f * wide : (f + 1) * wide].astype(F32))
        padded_frame(
            size,
            features[f].astype(F32),
            top,
            bottom,
            left_all[f * step : (f + 1) * step],
            right_all[f * step : (f + 1) * step],
            frame,
        )
        normed = (frame[...] - found[f : f + 1][None]) * found[FRAMES + f : FRAMES + f + 1][None]
        frame[...] = jnp.where(ok, normed * logistic(normed), 0.0)
        left, right = put_frame(size, frame, f, act)
        lefts.append(left)
        rights.append(right)
    put_sides(act, size.main(1), lefts + rights)

    tall = high + 4
    for f in range(FRAMES):
        start = f * tall * wide
        for row in range(2):
            first = FRAMES * wide + (f * 2 + row) * wide
            top, bottom = rim_rows(place, row_got[first : first + wide])
            grad[start + row * wide : start + (row + 1) * wide] = top
            below = start + (high + 2 + row) * wide
            grad[below : below + wide] = bottom
        grad[start + 2 * wide : start + (high + 2) * wide] = out_grad[f].reshape(
            size.cells, LANES
        )
    left, right = sides(
        place, across, col_got, FRAMES * step, 2 * FRAMES * size.stride(2)
    )
    put_sides(grad, size.main(2), [left, right])


def spread_columns(size, rim, trim, wo, block, index, dst, at, frame):
    wide, high = size.wide, size.high
    tall, step = high + 2 * rim, size.stride(rim)
    main = block[index * tall * wide : (index + 1) * tall * wide].astype(F32)
    main = main.reshape(tall, wide, LANES)
    cut = rim - trim
    tall_out = tall - 2 * cut
    frame[:, trim : trim + wide] = main[cut : cut + tall_out]
    first = size.main(rim)
    edges = block[first:].astype(F32)
    for j in range(2 * rim):
        col = j - cut if j < rim else j - rim + trim + wide
        if j < cut or (j >= rim and j - rim >= trim):
            continue
        start = (j * FRAMES + index) * step
        edge = edges[start + cut : start + cut + tall_out]
        frame[:, col : col + 1] = edge.reshape(tall_out, 1, LANES)
    for c in range(3):
        dst[at, :, :, c * LANES : (c + 1) * LANES] = frame[:, c : c + wo].astype(BF16)


def spread_all(size, rim, trim, wo, near, far, dst, frame):
    filled = size.wide + 2 * trim
    if frame.shape[1] > filled:
        frame[:, filled:] = jnp.zeros((frame.shape[0], frame.shape[1] - filled, LANES), F32)
    for f in range(2 * FRAMES):
        block = near if f < FRAMES else far
        spread_columns(size, rim, trim, wo, block, f % FRAMES, dst, f, frame)


def convolved(x, kernel, turned):
    tall, wo = x.shape[1], x.shape[2]
    ho = tall - 2
    count = ho * wo
    span = 9 * LANES

    def cells(f):
        return jnp.concatenate(
            [x[f, b : b + ho].reshape(count, 3 * LANES) for b in range(3)], 1
        )

    def taps(a):
        if not turned:
            return kernel[a * span : (a + 1) * span]
        last = (3 - a) * 9 - 1
        return jnp.concatenate(
            [kernel[(last - k) * LANES : (last - k + 1) * LANES] for k in range(9)], 1
        )

    dims = (((1,), (1 if turned else 0,)), ((), ()))

    def dot(one, two):
        return lax.dot_general(one, two, dims, preferred_element_type=F32)

    def pair(one, two):
        return jnp.concatenate([one, two], 0 if turned else 1)

    both = dot(cells(1), pair(taps(1), taps(0))) + dot(cells(2), pair(taps(2), taps(1)))
    first = both[:, :LANES] + dot(cells(0), taps(0))
    second = both[:, LANES:] + dot(cells(3), taps(2))
    return first, second


def conv_scratch(size, trim, wo):
    tall = size.high + 2 * trim
    return [((2 * FRAMES, tall, wo, 3 * LANES), BF16), ((tall, up(wo + 2, 8), LANES), F32)]


def hidden_body(size, place, near, far, kernel, hidden, pay, stats, x, frame):
    high, wide = size.high, size.wide
    spread_all(size, 1, 1, wide, near, far, x, frame)
    sums = convolved(x, kernel, False)
    upper = place[0] == 0
    rounded = [s.astype(BF16) for s in sums]
    for f in range(FRAMES):
        hidden[f] = rounded[f].reshape(high, wide, LANES)
        edge = jnp.where(upper, rounded[f][size.cells - wide :], rounded[f][:wide])
        pay[f * wide : (f + 1) * wide] = edge
    found = measured([r.astype(F32) for r in rounded])
    stats[...] = found
    at = FRAMES * wide
    fill = jnp.zeros((pay.shape[0] - at - PARTS, LANES), F32)
    pay[at:] = jnp.concatenate([split3(found), fill], 0).astype(BF16)


def grad_act_body(size, near, far, kernel, out, x, frame):
    wo = x.shape[2]
    spread_all(size, 2, 2, wo, near, far, x, frame)
    sums = convolved(x, kernel, True)
    for f in range(FRAMES):
        out[f] = sums[f].reshape(size.tall(), wo, LANES)[:, : size.broad()]


def sums_second_body(size, across, hidden, col_got, grad_act, norm, slots):
    high, wide = size.high, size.wide
    at = FRAMES * size.stride(1)
    found = concluded(
        [join3(col_got[peer, at : at + PARTS]) for peer in range(across)], 2 * size.cells
    )
    norm[...] = found
    firsts, seconds = [], []
    for f in range(FRAMES):
        own = hidden[f].astype(F32)
        normed = (own - found[f : f + 1][None]) * found[FRAMES + f : FRAMES + f + 1][None]
        sigmoid = logistic(normed)
        grad = grad_act[f, 1 : high + 1, 1 : wide + 1]
        grad = grad * sigmoid * (1.0 + normed * (1.0 - sigmoid))
        grad, normed = grad.reshape(size.cells, LANES), normed.reshape(size.cells, LANES)
        firsts.append(jnp.sum(grad, 0, keepdims=True))
        seconds.append(jnp.sum(grad * normed, 0, keepdims=True))
    sums = stat_block(firsts, seconds)
    for peer in range(slots.shape[0]):
        slots[peer] = sums


def act_second_body(
    size, across, place, hidden, row_got, col_got, grad_act, norm, act, q_far, z_far, frame, q, z, sems
):
    wide = size.wide
    step = size.stride(1)
    left_all, right_all = sides(place, across, col_got, 0, FRAMES * step)
    ok = in_frame((size.tall(), size.broad(), LANES), place, across, size, 1)
    lefts, rights, copies = [], [], []
    frame[...] = jnp.zeros_like(frame)
    for f in range(FRAMES):
        top, bottom = rim_rows(place, row_got[f * wide : (f + 1) * wide].astype(F32))
        padded_frame(
            size,
            hidden[f].astype(F32),
            top,
            bottom,
            left_all[f * step : (f + 1) * step],
            right_all[f * step : (f + 1) * step],
            frame,
        )
        normed = (frame[...] - norm[f : f + 1][None]) * norm[FRAMES + f : FRAMES + f + 1][None]
        sigmoid = logistic(normed)
        frame[...] = jnp.where(ok, normed * sigmoid, 0.0)
        left, right = put_frame(size, frame, f, act)
        lefts.append(left)
        rights.append(right)
        z[f] = normed
        q[f] = grad_act[f] * sigmoid * (1.0 + normed * (1.0 - sigmoid))
        for k, (source, target) in enumerate(((q, q_far), (z, z_far))):
            copy = pltpu.make_async_copy(source.at[f], target.at[f], sems.at[2 * f + k])
            copy.start()
            copies.append(copy)
    put_sides(act, size.main(1), lefts + rights)
    for copy in copies:
        copy.wait()


def hidden_grad(size, across, place, q, z, got, norm, out, frame, arrive):
    peers = got.shape[0]
    total = got[0]
    for peer in range(1, peers):
        total = total + got[peer]
    means = lane_totals(total) / (size.cells * peers * (LANES // GROUPS))
    ok = in_frame((size.tall(), size.broad(), LANES), place, across, size, 1)
    lefts, rights = [], []
    for f in range(FRAMES):
        first, second = means[f : f + 1][None], means[FRAMES + f : FRAMES + f + 1][None]
        inv = norm[FRAMES + f : FRAMES + f + 1][None]
        arrive(f)
        frame[...] = jnp.where(ok, inv * (q[f] - first - z[f] * second), 0.0)
        left, right = put_frame(size, frame, f, out)
        lefts.append(left)
        rights.append(right)
    put_sides(out, size.main(1), lefts + rights)


def own_cells(size, block, f):
    start = (f * size.tall() + 1) * size.wide
    return block[start : start + size.cells]


def turned_cells(size, block, out):
    for f in range(FRAMES):
        cells = own_cells(size, block, f).astype(F32).T.astype(BF16)
        out[f * LANES : (f + 1) * LANES] = cells


def tap_sums(x, turned, b):
    ho, wo = x.shape[1] - 2, x.shape[2]

    def cells(f):
        return x[f, b : b + ho].reshape(ho * wo, 3 * LANES)

    def dot(one, two):
        return jnp.dot(one, two, preferred_element_type=F32)

    low = dot(turned[...], cells(1))
    high = dot(turned[...], cells(2))
    return (
        dot(turned[:LANES], cells(0)) + low[LANES:],
        low[:LANES] + high[LANES:],
        high[:LANES] + dot(turned[LANES:], cells(3)),
    )


def second_term_body(size, near, far, act, out_far, x, frame, turned, out, sems):
    spread_all(size, 2, 1, size.wide, near, far, x, frame)
    turned_cells(size, act, turned)
    span = 3 * LANES
    copies = []
    for b in range(3):
        for a, total in enumerate(tap_sums(x, turned, b)):
            for c in range(3):
                tap = ((2 - a) * 3 + 2 - b) * 3 + 2 - c
                out[tap * LANES : (tap + 1) * LANES] = total[:, c * LANES : (c + 1) * LANES]
            rows = pl.ds(((2 - a) * 3 + 2 - b) * span, span)
            copy = pltpu.make_async_copy(out.at[rows], out_far.at[rows], sems.at[3 * b + a])
            copy.start()
            copies.append(copy)
    for copy in copies:
        copy.wait()


def first_term_body(
    size,
    across,
    place,
    got,
    norm,
    q_far,
    z_far,
    near_far,
    far_far,
    second_far,
    grad,
    keep,
    give,
    x,
    frame,
    turned,
    both,
    near,
    far,
    second,
    q,
    z,
    sems,
):
    pairs = [(q_far.at[f], q.at[f]) for f in range(FRAMES)]
    pairs += [(z_far.at[f], z.at[f]) for f in range(FRAMES)]
    pairs += [(near_far, near), (far_far, far), (second_far, second)]
    copies = [
        pltpu.make_async_copy(source, target, sems.at[k])
        for k, (source, target) in enumerate(pairs)
    ]
    for k in (0, FRAMES, 1, FRAMES + 1, 2 * FRAMES, 2 * FRAMES + 1, 2 * FRAMES + 2):
        copies[k].start()

    def arrive(f):
        copies[f].wait()
        copies[FRAMES + f].wait()

    hidden_grad(size, across, place, q, z, got, norm, grad, frame, arrive)
    turned_cells(size, grad, turned)
    copies[2 * FRAMES].wait()
    copies[2 * FRAMES + 1].wait()
    spread_all(size, 1, 1, size.wide, near, far, x, frame)
    for b in range(3):
        for a, total in enumerate(tap_sums(x, turned, b)):
            first = (a * 3 + b) * 3 * LANES
            both[first : first + 3 * LANES] = total.T
    copies[2 * FRAMES + 2].wait()
    upper = place[0] == 0
    keep[...] = jnp.where(upper, both[...], second[...])
    give[...] = jnp.where(upper, second[...], both[...]).astype(BF16)


def result_body(size, near, far, kernel, features, out, x, frame):
    spread_all(size, 1, 1, size.wide, near, far, x, frame)
    sums = convolved(x, kernel, False)
    for f in range(FRAMES):
        total = features[f].astype(F32) + sums[f].reshape(size.high, size.wide, LANES)
        out[f] = total.astype(BF16)


def back_first_body(size, near, far, kernel, features, norm, q, sums, x, frame):
    spread_all(size, 1, 1, size.wide, near, far, x, frame)
    grads = convolved(x, kernel, True)
    firsts, seconds = [], []
    for f in range(FRAMES):
        values = features[f].astype(F32).reshape(size.cells, LANES)
        normed = (values - norm[f : f + 1]) * norm[FRAMES + f : FRAMES + f + 1]
        sigmoid = logistic(normed)
        grad = grads[f] * sigmoid * (1.0 + normed * (1.0 - sigmoid))
        q[f] = grad
        firsts.append(jnp.sum(grad, 0, keepdims=True))
        seconds.append(jnp.sum(grad * normed, 0, keepdims=True))
    sums[...] = stat_block(firsts, seconds)


def feature_grad_body(size, peers, features, out_grad, norm, q, got, out):
    total = join3(got[0])
    for peer in range(1, got.shape[0]):
        total = total + join3(got[peer])
    means = lane_totals(total) / (size.cells * peers * (LANES // GROUPS))
    for f in range(FRAMES):
        values = features[f].astype(F32).reshape(size.cells, LANES)
        inv = norm[FRAMES + f : FRAMES + f + 1]
        normed = (values - norm[f : f + 1]) * inv
        grad = inv * (q[f] - means[f : f + 1] - normed * means[FRAMES + f : FRAMES + f + 1])
        grad = out_grad[f].astype(F32) + grad.reshape(size.high, size.wide, LANES)
        out[f] = grad.astype(BF16)


def row_swap(values):
    return lax.ppermute(values, "row", [(0, 1), (1, 0)])


def later(values, by):
    peers = lax.axis_size("tm")
    pairs = [(i, i + by) for i in range(peers) if 0 <= i + by < peers]
    return lax.ppermute(values, "tm", pairs)


def sum_parts(stat):
    high = lax.reduce_precision(stat, 8, 7)
    rest = stat - high
    middle = lax.reduce_precision(rest, 8, 7)
    return jnp.concatenate([high, middle, rest - middle], 0).astype(BF16)


def total_of(got):
    total = got[0].astype(F32)
    for peer in range(1, got.shape[0]):
        total = total + got[peer].astype(F32)
    return total


def shared_body(got, out, flat):
    rows, share = got.shape[1], out.shape[1]
    if flat.shape[0] > rows:
        flat[rows:] = jnp.zeros((flat.shape[0] - rows, LANES), F32)
    flat[:rows] = total_of(got)
    for peer in range(out.shape[0]):
        out[peer] = flat[peer * share : (peer + 1) * share].astype(BF16)


def finished_body(factor, got, out):
    total = (total_of(got) * factor).astype(BF16)
    for peer in range(out.shape[0]):
        out[peer] = total


def placed_body(rows, place, mine, theirs, first, second, sems):
    def move(one, two):
        copies = []
        for peer in range(mine.shape[0]):
            for k, (source, target) in enumerate(((mine, one), (theirs, two))):
                copies.append(
                    pltpu.make_async_copy(
                        source.at[peer, pl.ds(0, rows)],
                        target.at[pl.ds(peer * rows, rows)],
                        sems.at[k, peer],
                    )
                )
        for copy in copies:
            copy.start()
        for copy in copies:
            copy.wait()

    @pl.when(place[0] == 0)
    def _():
        move(first, second)

    @pl.when(place[0] != 0)
    def _():
        move(second, first)


def placed(place, mine, theirs, rows, count):
    anywhere = pl.BlockSpec(memory_space=pl.ANY)
    return pl.pallas_call(
        functools.partial(placed_body, rows),
        out_shape=[jax.ShapeDtypeStruct((count, LANES), BF16)] * 2,
        in_specs=[pl.BlockSpec(memory_space=pltpu.SMEM), anywhere, anywhere],
        out_specs=[anywhere, anywhere],
        scratch_shapes=[pltpu.SemaphoreType.DMA((2, mine.shape[0]))],
        compiler_params=pltpu.CompilerParams(vmem_limit_bytes=1 << 20),
    )(place, mine, theirs)


def on_device(features, conv_first, conv_second, out_grad):
    frames, high, wide, chans = features.shape
    assert frames == FRAMES and chans == LANES and lax.axis_size("row") == 2
    size = Sizes(high, wide)
    across = lax.axis_size("col")
    peers = 2 * across
    factor = 1.0 / math.sqrt(size.cells * FRAMES * lax.axis_size("tm") * peers)
    place = jnp.stack([lax.axis_index("row"), lax.axis_index("col")]).astype(jnp.int32)
    taps = conv_first.shape
    first = conv_first.reshape(-1, LANES)
    second = conv_second.reshape(-1, LANES)
    work = 2 * first.size * size.cells * FRAMES
    part = functools.partial
    stat = ((STATS, LANES), F32)
    tall, broad = size.tall(), size.broad()
    frame = ((tall, broad, LANES), F32)

    edge = up(3 * FRAMES * wide + PARTS, 16)
    lines = up(FRAMES * size.stride(1) + 2 * FRAMES * size.stride(2) + PARTS, 16)
    flat = ((2, lines, LANES), F32)
    pay, stats, cols, features_near, grad_near = call(
        part(start_body, size),
        [((edge, LANES), BF16), stat, flat, (features.shape, BF16), (features.shape, BF16)],
        [place, features, out_grad],
        smem=1,
        far=2,
        sems=2 * FRAMES,
    )
    row_got = row_swap(pay)
    (slots,) = call(
        part(slots_body, size, (1, 2), across),
        [((across, lines, LANES), BF16)],
        [place, cols, row_got, stats],
        [flat],
        smem=1,
    )
    col_got = lax.all_to_all(slots, "col", 0, 0)
    block = ((size.rows(1), LANES), BF16)
    act_first, grad, norm_first = call(
        part(act_first_body, size, across),
        [block, ((size.rows(2), LANES), BF16), stat],
        [place, features_near, grad_near, row_got, col_got],
        [frame],
        smem=1,
    )
    act_before = later(act_first, 1)
    grad_after = later(grad, -1)

    edge = up(FRAMES * wide + PARTS, 16)
    hidden, pay, stats = call(
        part(hidden_body, size),
        [(features.shape, BF16), ((edge, LANES), BF16), stat],
        [place, act_before, act_first, first],
        conv_scratch(size, 1, wide),
        smem=1,
        mib=14,
        flops=work,
    )
    row_got = row_swap(pay)
    lines = up(FRAMES * size.stride(1) + PARTS, 16)
    flat = ((2, lines, LANES), F32)
    (cols,) = call(part(columns_body, size), [flat], [hidden])
    (slots,) = call(
        part(slots_body, size, (1,), across),
        [((across, lines, LANES), BF16)],
        [place, cols, row_got, stats],
        [flat],
        smem=1,
    )
    slots, grad_after = lax.optimization_barrier((slots, grad_after))
    col_got = lax.all_to_all(slots, "col", 0, 0)
    (grad_act,) = call(
        part(grad_act_body, size),
        [((FRAMES, tall, broad, LANES), F32)],
        [grad, grad_after, second],
        conv_scratch(size, 2, up(wide + 2, 16)),
        mib=16,
        flops=2 * work,
    )
    field = ((FRAMES, tall, broad, LANES), F32)
    norm_second, slots = call(
        part(sums_second_body, size, across),
        [stat, ((peers, STATS, LANES), F32)],
        [hidden, col_got, grad_act],
    )
    got = lax.all_to_all(slots, ("row", "col"), 0, 0)
    act_second, q, z = call(
        part(act_second_body, size, across),
        [block, field, field],
        [place, hidden, row_got, col_got, grad_act, norm_second],
        [frame, field, field],
        smem=1,
        sems=2 * FRAMES,
        beside=True,
        out_far=2,
    )
    turned = ((FRAMES * LANES, size.cells), BF16)
    (second_term,) = call(
        part(second_term_body, size),
        [(first.shape, F32)],
        [grad, grad_after, act_second],
        [*conv_scratch(size, 1, wide), turned, (first.shape, F32)],
        sems=9,
        mib=16,
        beside=True,
        out_far=1,
    )
    grad_second, keep, give = call(
        part(first_term_body, size, across),
        [block, (first.shape, F32), (first.shape, BF16)],
        [place, got, norm_second, q, z, act_before, act_first, second_term],
        [
            *conv_scratch(size, 1, wide),
            turned,
            (first.shape, F32),
            block,
            block,
            (first.shape, F32),
            field,
            field,
        ],
        smem=1,
        far=5,
        sems=2 * FRAMES + 3,
        mib=20,
        flops=work,
    )
    give, late_grad, late_act = lax.optimization_barrier((give, grad_second, act_second))
    act_second_before = later(late_act, 1)
    grad_second_after = later(late_grad, -1)

    along = lax.axis_size("tm")
    rows = first.shape[0]
    keep = keep + row_swap(give).astype(F32)
    by_col = rows // across
    slots = lax.all_to_all(keep.reshape(across, by_col, LANES).astype(BF16), "col", 0, 0)
    share = up(by_col, 16 * along) // along
    (slots,) = call(
        shared_body,
        [((along, share, LANES), BF16)],
        [slots],
        [((along * share, LANES), F32)],
    )
    got = lax.all_to_all(slots, "tm", 0, 0)
    (result,) = call(
        part(result_body, size),
        [(features.shape, BF16)],
        [act_second_before, act_second, second, features],
        conv_scratch(size, 1, wide),
        mib=14,
        flops=work,
    )
    q, sums = call(
        part(back_first_body, size),
        [((FRAMES, size.cells, LANES), F32), stat],
        [grad_second, grad_second_after, first, features, norm_first],
        conv_scratch(size, 1, wide),
        mib=14,
        flops=work,
    )
    got, result = lax.optimization_barrier((got, result))
    (slots,) = call(part(finished_body, factor), [((along, share, LANES), BF16)], [got])
    done = lax.all_to_all(slots, "tm", 0, 0).reshape(-1, LANES)[:by_col]
    parts = sum_parts(sums + row_swap(sums))
    parts = jnp.pad(parts, ((0, -parts.shape[0] % 16), (0, 0)))
    done = jnp.concatenate([done, parts], 0)
    mine = lax.all_to_all(jnp.broadcast_to(done[None], (across, *done.shape)), "col", 0, 0)
    first_grad, second_grad = placed(place, mine, row_swap(mine), by_col, rows)
    (feature_grad,) = call(
        part(feature_grad_body, size, peers),
        [(features.shape, BF16)],
        [features, out_grad, norm_first, q, mine[:, by_col:]],
    )
    return (result, feature_grad, first_grad.reshape(taps), second_grad.reshape(taps))


def solution(mesh):
    in_specs = (P("tm", "row", "col", None), P(), P(), P("tm", "row", "col", None))
    out_specs = (P("tm", "row", "col", None), P("tm", "row", "col", None), P(), P())
    return jax.shard_map(
        on_device, mesh=mesh, in_specs=in_specs, out_specs=out_specs, check_vma=False
    )
```

```python
import functools
import math

import jax
import jax.numpy as jnp
from jax import lax
from jax.experimental import pallas as pl
from jax.experimental.pallas import tpu as pltpu
from jax.sharding import PartitionSpec as P

GROUPS = 32
EPSILON = 1e-06
F32 = jnp.float32
BF16 = jnp.bfloat16
LANES = 128
FRAMES = 2
STATS = 8
PARTS = 3 * STATS


def up(count, step):
    return -(-count // step) * step


class Sizes:
    def __init__(self, high, wide):
        self.high, self.wide = high, wide
        self.cells = high * wide

    def stride(self, rim):
        return up(self.high + 2 * rim, 8)

    def main(self, rim):
        return FRAMES * (self.high + 2 * rim) * self.wide

    def rows(self, rim):
        return up(self.main(rim) + 2 * rim * FRAMES * self.stride(rim), 16)

    def tall(self):
        return self.high + 2

    def broad(self):
        return up(self.wide + 2, 8)


def call(body, outs, args, scratch=(), smem=0, far=0, sems=0, mib=8, flops=0, beside=False, out_far=0):
    specs = [pl.BlockSpec(memory_space=pltpu.SMEM)] * smem
    specs += [pl.BlockSpec(memory_space=pltpu.VMEM)] * (len(args) - smem - far)
    specs += [pl.BlockSpec(memory_space=pltpu.HBM)] * far
    near = len(args) - far
    args = [*args[:near], *(pltpu.with_memory_space_constraint(a, pltpu.HBM) for a in args[near:])]
    scratches = [pltpu.VMEM(shape, dtype) for shape, dtype in scratch]
    if sems:
        scratches.append(pltpu.SemaphoreType.DMA((sems,)))
    shapes = [jax.ShapeDtypeStruct(shape, dtype) for shape, dtype in outs]
    kept = len(outs) - out_far
    moved = sum(math.prod(a.shape) * a.dtype.itemsize for a in [*args, *shapes])
    moved = 0 if beside else moved
    return pl.pallas_call(
        body,
        out_shape=shapes[:kept] + [pltpu.HBM(o.shape, o.dtype) for o in shapes[kept:]],
        in_specs=specs,
        out_specs=[pl.BlockSpec(memory_space=pltpu.VMEM)] * kept
        + [pl.BlockSpec(memory_space=pltpu.HBM)] * out_far,
        scratch_shapes=scratches,
        cost_estimate=pl.CostEstimate(flops=flops, bytes_accessed=moved, transcendentals=0),
        compiler_params=pltpu.CompilerParams(vmem_limit_bytes=mib << 20),
    )(*args)


def logistic(values):
    return 0.5 * jnp.tanh(0.5 * values) + 0.5


def lane_totals(stat):
    lane = lax.broadcasted_iota(jnp.int32, stat.shape, 1)
    step = 1
    while step < LANES // GROUPS:
        ahead = pltpu.roll(stat, LANES - step, 1)
        behind = pltpu.roll(stat, step, 1)
        stat = stat + jnp.where((lane // step) % 2 == 0, ahead, behind)
        step *= 2
    return stat


def split3(stat):
    high = stat.astype(BF16).astype(F32)
    rest = stat - high
    middle = rest.astype(BF16).astype(F32)
    return jnp.concatenate([high, middle, rest - middle], 0)


def join3(parts):
    parts = parts.astype(F32)
    return parts[:STATS] + (parts[STATS : 2 * STATS] + parts[2 * STATS : PARTS])


def stat_block(first, second):
    rest = jnp.zeros((STATS - 2 * FRAMES, LANES), F32)
    return jnp.concatenate([*first, *second, rest], 0)


def measured(frames):
    means, squares = [], []
    for frame in frames:
        mean = jnp.sum(frame, 0, keepdims=True) / frame.shape[0]
        centred = frame - mean
        means.append(mean)
        squares.append(jnp.sum(centred * centred, 0, keepdims=True))
    return stat_block(means, squares)


def merged(one, two, cells):
    delta = one - two
    extra = (0.5 * cells) * delta * delta
    mean = 0.5 * (one[:FRAMES] + two[:FRAMES])
    square = one[FRAMES : 2 * FRAMES] + two[FRAMES : 2 * FRAMES] + extra[:FRAMES]
    return jnp.concatenate([mean, square, jnp.zeros((STATS - 2 * FRAMES, LANES), F32)], 0)


def concluded(blocks, cells):
    per_group = LANES // GROUPS
    mean = sum(blocks[1:], blocks[0])[:FRAMES]
    mean = lane_totals(mean) / (len(blocks) * per_group)
    total = jnp.zeros((FRAMES, LANES), F32)
    for block in blocks:
        off = block[:FRAMES] - mean
        total = total + block[FRAMES : 2 * FRAMES] + cells * off * off
    spread = lane_totals(total) / (cells * len(blocks) * per_group)
    rest = jnp.zeros((STATS - 2 * FRAMES, LANES), F32)
    return jnp.concatenate([mean, lax.rsqrt(spread + EPSILON), rest], 0)


def rim_rows(place, got):
    upper = place[0] == 0
    nothing = jnp.zeros_like(got)
    return jnp.where(upper, nothing, got), jnp.where(upper, got, nothing)


def in_frame(shape, place, across, size, rim):
    row = lax.broadcasted_iota(jnp.int32, shape, 0)
    col = lax.broadcasted_iota(jnp.int32, shape, 1)
    top = jnp.where(place[0] == 0, rim, 0)
    bottom = jnp.where(place[0] == 0, size.high + 2 * rim, size.high + rim)
    left = jnp.where(place[1] == 0, rim, 0)
    right = jnp.where(place[1] == across - 1, size.wide + rim, size.wide + 2 * rim)
    return (row >= top) & (row < bottom) & (col >= left) & (col < right)


def take_columns(size, arrays, flat):
    flat[...] = jnp.zeros_like(flat)
    at = 0
    for array, rim in arrays:
        for j in range(rim):
            for frame in range(FRAMES):
                for side, col in ((0, j), (1, size.wide - rim + j)):
                    rows = array[frame, :, col : col + 1].astype(F32)
                    rows = rows.reshape(size.high, LANES)
                    flat[side, at + rim : at + rim + size.high] = rows
                at += size.stride(rim)


def columns_body(size, hidden, flat):
    take_columns(size, ((hidden, 1),), flat)


def start_body(
    size, place, features_far, grad_far, pay, stats, flat, features, out_grad, sems
):
    high, wide = size.high, size.wide
    upper = place[0] == 0
    copies = [
        pltpu.make_async_copy(source.at[f], target.at[f], sems.at[FRAMES * k + f])
        for k, (source, target) in enumerate(((features_far, features), (grad_far, out_grad)))
        for f in range(FRAMES)
    ]
    for copy in copies:
        copy.start()
    for copy in copies[:FRAMES]:
        copy.wait()
    at = 0
    for frame in range(FRAMES):
        pay[at : at + wide] = jnp.where(upper, features[frame, high - 1], features[frame, 0])
        at += wide
    found = measured([features[f].astype(F32).reshape(size.cells, LANES) for f in range(FRAMES)])
    stats[...] = found
    for copy in copies[FRAMES:]:
        copy.wait()
    for frame in range(FRAMES):
        for row in range(2):
            edge = jnp.where(upper, out_grad[frame, high - 2 + row], out_grad[frame, row])
            pay[at : at + wide] = edge
            at += wide
    fill = jnp.zeros((pay.shape[0] - at - PARTS, LANES), F32)
    pay[at:] = jnp.concatenate([split3(found), fill], 0).astype(BF16)
    take_columns(size, ((features, 1), (out_grad, 2)), flat)


def slots_body(size, rims, across, place, flat, got, stats, slots, work):
    wide, high = size.wide, size.high
    upper = place[0] == 0
    work[...] = flat[...]
    at = base = 0
    for rim in rims:
        for j in range(rim):
            for frame in range(FRAMES):
                for row in range(rim):
                    start = base + (frame * rim + row) * wide
                    for side, col in ((0, j), (1, wide - rim + j)):
                        cell = start - start % 16 + 16 * ((start % 16 + col) // 16)
                        tile = got[cell : cell + 16].astype(F32)
                        edge = tile[start + col - cell : start + col - cell + 1]
                        nothing = jnp.zeros_like(edge)
                        top, bottom = at + row, at + rim + high + row
                        work[side, top : top + 1] = jnp.where(upper, nothing, edge)
                        work[side, bottom : bottom + 1] = jnp.where(upper, edge, nothing)
                at += size.stride(rim)
        base += FRAMES * rim * wide
    parts = split3(merged(stats[...], join3(got[base : base + PARTS]), size.cells))
    work[0, at : at + PARTS] = parts
    work[1, at : at + PARTS] = parts
    for peer in range(across):
        slots[peer] = jnp.where(peer > place[1], work[1], work[0]).astype(BF16)


def sides(place, across, got, first, count):
    left = got[jnp.maximum(place[1] - 1, 0), first : first + count].astype(F32)
    right = got[jnp.minimum(place[1] + 1, across - 1), first : first + count].astype(F32)
    nothing = jnp.zeros_like(left)
    left = jnp.where(place[1] > 0, left, nothing)
    right = jnp.where(place[1] < across - 1, right, nothing)
    return left, right


def padded_frame(size, own, top, bottom, left, right, frame):
    high, wide = size.high, size.wide
    frame[1 : high + 1, 1 : wide + 1] = own
    frame[0:1, 1 : wide + 1] = top[None]
    frame[high + 1 : high + 2, 1 : wide + 1] = bottom[None]
    tall = high + 2
    frame[:, 0:1] = left[:tall].reshape(tall, 1, LANES)
    frame[:, wide + 1 : wide + 2] = right[:tall].reshape(tall, 1, LANES)


def put_frame(size, frame, index, out):
    wide, tall, step = size.wide, size.tall(), size.stride(1)
    flat = frame[:, 1 : wide + 1].reshape(tall * wide, LANES)
    out[index * tall * wide : (index + 1) * tall * wide] = flat.astype(BF16)
    fill = jnp.zeros((step - tall, LANES), F32)
    left = frame[:, 0:1].reshape(tall, LANES)
    right = frame[:, wide + 1 : wide + 2].reshape(tall, LANES)
    return jnp.concatenate([left, fill], 0), jnp.concatenate([right, fill], 0)


def put_sides(out, first, blocks):
    fill = out.shape[0] - first - sum(b.shape[0] for b in blocks)
    if fill:
        blocks = [*blocks, jnp.zeros((fill, LANES), F32)]
    out[first:] = jnp.concatenate(blocks, 0).astype(BF16)


def act_first_body(
    size, across, place, features, out_grad, row_got, col_got, act, grad, norm, frame
):
    high, wide = size.high, size.wide
    at = FRAMES * size.stride(1) + 2 * FRAMES * size.stride(2)
    blocks = [join3(col_got[peer, at : at + PARTS]) for peer in range(across)]
    found = concluded(blocks, 2 * size.cells)
    norm[...] = found
    step = size.stride(1)
    left_all, right_all = sides(place, across, col_got, 0, FRAMES * step)
    ok = in_frame((size.tall(), size.broad(), LANES), place, across, size, 1)
    lefts, rights = [], []
    frame[...] = jnp.zeros_like(frame)
    for f in range(FRAMES):
        top, bottom = rim_rows(place, row_got[f * wide : (f + 1) * wide].astype(F32))
        padded_frame(
            size,
            features[f].astype(F32),
            top,
            bottom,
            left_all[f * step : (f + 1) * step],
            right_all[f * step : (f + 1) * step],
            frame,
        )
        normed = (frame[...] - found[f : f + 1][None]) * found[FRAMES + f : FRAMES + f + 1][None]
        frame[...] = jnp.where(ok, normed * logistic(normed), 0.0)
        left, right = put_frame(size, frame, f, act)
        lefts.append(left)
        rights.append(right)
    put_sides(act, size.main(1), lefts + rights)

    tall = high + 4
    for f in range(FRAMES):
        start = f * tall * wide
        for row in range(2):
            first = FRAMES * wide + (f * 2 + row) * wide
            top, bottom = rim_rows(place, row_got[first : first + wide])
            grad[start + row * wide : start + (row + 1) * wide] = top
            below = start + (high + 2 + row) * wide
            grad[below : below + wide] = bottom
        grad[start + 2 * wide : start + (high + 2) * wide] = out_grad[f].reshape(
            size.cells, LANES
        )
    left, right = sides(
        place, across, col_got, FRAMES * step, 2 * FRAMES * size.stride(2)
    )
    put_sides(grad, size.main(2), [left, right])


def spread_columns(size, rim, trim, wo, block, index, dst, at, frame):
    wide, high = size.wide, size.high
    tall, step = high + 2 * rim, size.stride(rim)
    main = block[index * tall * wide : (index + 1) * tall * wide].astype(F32)
    main = main.reshape(tall, wide, LANES)
    cut = rim - trim
    tall_out = tall - 2 * cut
    frame[:, trim : trim + wide] = main[cut : cut + tall_out]
    first = size.main(rim)
    edges = block[first:].astype(F32)
    for j in range(2 * rim):
        col = j - cut if j < rim else j - rim + trim + wide
        if j < cut or (j >= rim and j - rim >= trim):
            continue
        start = (j * FRAMES + index) * step
        edge = edges[start + cut : start + cut + tall_out]
        frame[:, col : col + 1] = edge.reshape(tall_out, 1, LANES)
    for c in range(3):
        dst[at, :, :, c * LANES : (c + 1) * LANES] = frame[:, c : c + wo].astype(BF16)


def spread_all(size, rim, trim, wo, near, far, dst, frame):
    filled = size.wide + 2 * trim
    if frame.shape[1] > filled:
        frame[:, filled:] = jnp.zeros((frame.shape[0], frame.shape[1] - filled, LANES), F32)
    for f in range(dst.shape[0]):
        block = near if f < FRAMES else far
        spread_columns(size, rim, trim, wo, block, f % FRAMES, dst, f, frame)


def tap_dot(x, kernel, turned):
    ho, wo = x.shape[1] - 2, x.shape[2]
    count = ho * wo
    span = 9 * LANES

    def cells(f):
        return jnp.concatenate(
            [x[f, b : b + ho].reshape(count, 3 * LANES) for b in range(3)], 1
        )

    def taps(a):
        if not turned:
            return kernel[a * span : (a + 1) * span]
        last = (3 - a) * 9 - 1
        return jnp.concatenate(
            [kernel[(last - k) * LANES : (last - k + 1) * LANES] for k in range(9)], 1
        )

    dims = (((1,), (1 if turned else 0,)), ((), ()))

    def dot(f, *times):
        weights = [taps(a) for a in times]
        if len(weights) > 1:
            weights = [jnp.concatenate(weights, 0 if turned else 1)]
        return lax.dot_general(cells(f), weights[0], dims, preferred_element_type=F32)

    return dot


def convolved(x, kernel, turned):
    dot = tap_dot(x, kernel, turned)
    both = dot(1, 1, 0) + dot(2, 2, 1)
    return both[:, :LANES] + dot(0, 0), both[:, LANES:] + dot(3, 2)


def conv_scratch(size, trim, wo, frames=2 * FRAMES):
    tall = size.high + 2 * trim
    return [((frames, tall, wo, 3 * LANES), BF16), ((tall, up(wo + 2, 8), LANES), F32)]


def hidden_own_body(size, own, kernel, sums, x_far, x, frame, sems):
    spread_all(size, 1, 1, size.wide, own, None, x, frame)
    copy = pltpu.make_async_copy(x, x_far, sems.at[0])
    copy.start()
    dot = tap_dot(x, kernel, False)
    both = dot(0, 2, 1)
    sums[0] = both[:, :LANES]
    sums[1] = both[:, LANES:] + dot(1, 2)
    copy.wait()


def hidden_body(
    size, place, before, sums, kernel, hidden, pay, stats, x_far, x, frame, sems
):
    high, wide = size.high, size.wide
    spread_all(size, 1, 1, wide, before, None, x, frame)
    copy = pltpu.make_async_copy(x, x_far, sems.at[0])
    copy.start()
    dot = tap_dot(x, kernel, False)
    both = dot(1, 1, 0)
    sums = (sums[0] + both[:, :LANES] + dot(0, 0), sums[1] + both[:, LANES:])
    upper = place[0] == 0
    rounded = [s.astype(BF16) for s in sums]
    for f in range(FRAMES):
        hidden[f] = rounded[f].reshape(high, wide, LANES)
        edge = jnp.where(upper, rounded[f][size.cells - wide :], rounded[f][:wide])
        pay[f * wide : (f + 1) * wide] = edge
    found = measured([r.astype(F32) for r in rounded])
    stats[...] = found
    at = FRAMES * wide
    fill = jnp.zeros((pay.shape[0] - at - PARTS, LANES), F32)
    pay[at:] = jnp.concatenate([split3(found), fill], 0).astype(BF16)
    copy.wait()


def grad_act_body(size, near, far, kernel, out, x, frame):
    wo = x.shape[2]
    spread_all(size, 2, 2, wo, near, far, x, frame)
    sums = convolved(x, kernel, True)
    for f in range(FRAMES):
        out[f] = sums[f].reshape(size.tall(), wo, LANES)[:, : size.broad()]


def sums_second_body(size, across, hidden, col_got, grad_act, norm, slots):
    high, wide = size.high, size.wide
    at = FRAMES * size.stride(1)
    found = concluded(
        [join3(col_got[peer, at : at + PARTS]) for peer in range(across)], 2 * size.cells
    )
    norm[...] = found
    firsts, seconds = [], []
    for f in range(FRAMES):
        own = hidden[f].astype(F32)
        normed = (own - found[f : f + 1][None]) * found[FRAMES + f : FRAMES + f + 1][None]
        sigmoid = logistic(normed)
        grad = grad_act[f, 1 : high + 1, 1 : wide + 1]
        grad = grad * sigmoid * (1.0 + normed * (1.0 - sigmoid))
        grad, normed = grad.reshape(size.cells, LANES), normed.reshape(size.cells, LANES)
        firsts.append(jnp.sum(grad, 0, keepdims=True))
        seconds.append(jnp.sum(grad * normed, 0, keepdims=True))
    sums = stat_block(firsts, seconds)
    for peer in range(slots.shape[0]):
        slots[peer] = sums


def act_second_body(
    size, across, place, hidden, row_got, col_got, grad_act, norm, act, q_far, z_far, frame, q, z, sems
):
    wide = size.wide
    step = size.stride(1)
    left_all, right_all = sides(place, across, col_got, 0, FRAMES * step)
    ok = in_frame((size.tall(), size.broad(), LANES), place, across, size, 1)
    lefts, rights, copies = [], [], []
    frame[...] = jnp.zeros_like(frame)
    for f in range(FRAMES):
        top, bottom = rim_rows(place, row_got[f * wide : (f + 1) * wide].astype(F32))
        padded_frame(
            size,
            hidden[f].astype(F32),
            top,
            bottom,
            left_all[f * step : (f + 1) * step],
            right_all[f * step : (f + 1) * step],
            frame,
        )
        normed = (frame[...] - norm[f : f + 1][None]) * norm[FRAMES + f : FRAMES + f + 1][None]
        sigmoid = logistic(normed)
        frame[...] = jnp.where(ok, normed * sigmoid, 0.0)
        left, right = put_frame(size, frame, f, act)
        lefts.append(left)
        rights.append(right)
        z[f] = normed
        q[f] = grad_act[f] * sigmoid * (1.0 + normed * (1.0 - sigmoid))
        for k, (source, target) in enumerate(((q, q_far), (z, z_far))):
            copy = pltpu.make_async_copy(source.at[f], target.at[f], sems.at[2 * f + k])
            copy.start()
            copies.append(copy)
    put_sides(act, size.main(1), lefts + rights)
    for copy in copies:
        copy.wait()


def hidden_grad(size, across, place, q, z, got, norm, out, frame, arrive):
    peers = got.shape[0]
    total = got[0]
    for peer in range(1, peers):
        total = total + got[peer]
    means = lane_totals(total) / (size.cells * peers * (LANES // GROUPS))
    ok = in_frame((size.tall(), size.broad(), LANES), place, across, size, 1)
    lefts, rights = [], []
    for f in range(FRAMES):
        first, second = means[f : f + 1][None], means[FRAMES + f : FRAMES + f + 1][None]
        inv = norm[FRAMES + f : FRAMES + f + 1][None]
        arrive(f)
        frame[...] = jnp.where(ok, inv * (q[f] - first - z[f] * second), 0.0)
        left, right = put_frame(size, frame, f, out)
        lefts.append(left)
        rights.append(right)
    put_sides(out, size.main(1), lefts + rights)


def own_cells(size, block, f):
    start = (f * size.tall() + 1) * size.wide
    return block[start : start + size.cells]


def turned_cells(size, block, out):
    for f in range(FRAMES):
        cells = own_cells(size, block, f).astype(F32).T.astype(BF16)
        out[f * LANES : (f + 1) * LANES] = cells


def tap_sums(x, turned, b):
    ho, wo = x.shape[1] - 2, x.shape[2]

    def cells(f):
        return x[f, b : b + ho].reshape(ho * wo, 3 * LANES)

    def dot(one, two):
        return jnp.dot(one, two, preferred_element_type=F32)

    low = dot(turned[...], cells(1))
    high = dot(turned[...], cells(2))
    return (
        dot(turned[:LANES], cells(0)) + low[LANES:],
        low[:LANES] + high[LANES:],
        high[:LANES] + dot(turned[LANES:], cells(3)),
    )


def second_term_body(size, near, far, act, out_far, x, frame, turned, out, sems):
    spread_all(size, 2, 1, size.wide, near, far, x, frame)
    turned_cells(size, act, turned)
    span = 3 * LANES
    copies = []
    for b in range(3):
        for a, total in enumerate(tap_sums(x, turned, b)):
            for c in range(3):
                tap = ((2 - a) * 3 + 2 - b) * 3 + 2 - c
                out[tap * LANES : (tap + 1) * LANES] = total[:, c * LANES : (c + 1) * LANES]
            rows = pl.ds(((2 - a) * 3 + 2 - b) * span, span)
            copy = pltpu.make_async_copy(out.at[rows], out_far.at[rows], sems.at[3 * b + a])
            copy.start()
            copies.append(copy)
    for copy in copies:
        copy.wait()


def first_term_body(
    size,
    across,
    place,
    got,
    norm,
    q_far,
    z_far,
    near_far,
    own_far,
    second_far,
    grad,
    keep,
    give,
    x,
    frame,
    turned,
    second,
    q,
    z,
    sems,
):
    pairs = [(q_far.at[f], q.at[f]) for f in range(FRAMES)]
    pairs += [(z_far.at[f], z.at[f]) for f in range(FRAMES)]
    pairs += [(near_far, x.at[pl.ds(0, FRAMES)]), (own_far, x.at[pl.ds(FRAMES, FRAMES)])]
    pairs += [(second_far, second)]
    copies = [
        pltpu.make_async_copy(source, target, sems.at[k])
        for k, (source, target) in enumerate(pairs)
    ]
    for k in (0, FRAMES, 1, FRAMES + 1, 2 * FRAMES, 2 * FRAMES + 1, 2 * FRAMES + 2):
        copies[k].start()

    def arrive(f):
        copies[f].wait()
        copies[FRAMES + f].wait()

    hidden_grad(size, across, place, q, z, got, norm, grad, frame, arrive)
    turned_cells(size, grad, turned)
    for copy in copies[2 * FRAMES :]:
        copy.wait()
    upper = place[0] == 0
    for b in range(3):
        for a, total in enumerate(tap_sums(x, turned, b)):
            rows = slice((a * 3 + b) * 3 * LANES, (a * 3 + b + 1) * 3 * LANES)
            one, two = total.T, second[rows]
            keep[rows] = jnp.where(upper, one, two)
            give[rows] = jnp.where(upper, two, one).astype(BF16)


def result_body(size, near, far, kernel, features, out, x, frame):
    spread_all(size, 1, 1, size.wide, near, far, x, frame)
    sums = convolved(x, kernel, False)
    for f in range(FRAMES):
        total = features[f].astype(F32) + sums[f].reshape(size.high, size.wide, LANES)
        out[f] = total.astype(BF16)


def back_first_body(size, near, far, kernel, features, norm, q, sums, x, frame):
    spread_all(size, 1, 1, size.wide, near, far, x, frame)
    grads = convolved(x, kernel, True)
    firsts, seconds = [], []
    for f in range(FRAMES):
        values = features[f].astype(F32).reshape(size.cells, LANES)
        normed = (values - norm[f : f + 1]) * norm[FRAMES + f : FRAMES + f + 1]
        sigmoid = logistic(normed)
        grad = grads[f] * sigmoid * (1.0 + normed * (1.0 - sigmoid))
        q[f] = grad
        firsts.append(jnp.sum(grad, 0, keepdims=True))
        seconds.append(jnp.sum(grad * normed, 0, keepdims=True))
    sums[...] = stat_block(firsts, seconds)


def feature_grad_body(size, peers, features, out_grad, norm, q, got, out):
    total = join3(got[0])
    for peer in range(1, got.shape[0]):
        total = total + join3(got[peer])
    means = lane_totals(total) / (size.cells * peers * (LANES // GROUPS))
    for f in range(FRAMES):
        values = features[f].astype(F32).reshape(size.cells, LANES)
        inv = norm[FRAMES + f : FRAMES + f + 1]
        normed = (values - norm[f : f + 1]) * inv
        grad = inv * (q[f] - means[f : f + 1] - normed * means[FRAMES + f : FRAMES + f + 1])
        grad = out_grad[f].astype(F32) + grad.reshape(size.high, size.wide, LANES)
        out[f] = grad.astype(BF16)


def row_swap(values):
    return lax.ppermute(values, "row", [(0, 1), (1, 0)])


def later(values, by):
    peers = lax.axis_size("tm")
    pairs = [(i, i + by) for i in range(peers) if 0 <= i + by < peers]
    return lax.ppermute(values, "tm", pairs)


def sum_parts(stat):
    high = lax.reduce_precision(stat, 8, 7)
    rest = stat - high
    middle = lax.reduce_precision(rest, 8, 7)
    return jnp.concatenate([high, middle, rest - middle], 0).astype(BF16)


def total_of(got):
    total = got[0].astype(F32)
    for peer in range(1, got.shape[0]):
        total = total + got[peer].astype(F32)
    return total


def joined_body(keep, got, out):
    share = out.shape[1]
    for peer in range(out.shape[0]):
        rows = slice(peer * share, (peer + 1) * share)
        out[peer] = (keep[rows] + got[rows].astype(F32)).astype(BF16)


def shared_body(got, out, flat):
    rows, share = got.shape[1], out.shape[1]
    if flat.shape[0] > rows:
        flat[rows:] = jnp.zeros((flat.shape[0] - rows, LANES), F32)
    flat[:rows] = total_of(got)
    for peer in range(out.shape[0]):
        out[peer] = flat[peer * share : (peer + 1) * share].astype(BF16)


def finished_body(factor, got, out):
    total = (total_of(got) * factor).astype(BF16)
    for peer in range(out.shape[0]):
        out[peer] = total


def placed_body(rows, swapped, *refs):
    place, block, first, second, sems = refs[0], refs[1], *refs[-3:]

    def move(target):
        copies = [
            pltpu.make_async_copy(
                block.at[peer, pl.ds(0, rows)], target.at[pl.ds(peer * rows, rows)], sems.at[peer]
            )
            for peer in range(block.shape[0])
        ]
        for copy in copies:
            copy.start()
        for copy in copies:
            copy.wait()

    @pl.when(place[0] == swapped)
    def _():
        move(first)

    @pl.when(place[0] != swapped)
    def _():
        move(second)


def placed(place, block, swapped, rows, so_far):
    anywhere = pl.BlockSpec(memory_space=pl.ANY)
    shape = (rows * block.shape[0], LANES)
    return pl.pallas_call(
        functools.partial(placed_body, rows, swapped),
        out_shape=[jax.ShapeDtypeStruct(shape, BF16)] * 2,
        in_specs=[pl.BlockSpec(memory_space=pltpu.SMEM)] + [anywhere] * (1 + len(so_far)),
        out_specs=[anywhere, anywhere],
        input_output_aliases={2 + k: k for k in range(len(so_far))},
        scratch_shapes=[pltpu.SemaphoreType.DMA((block.shape[0],))],
        compiler_params=pltpu.CompilerParams(vmem_limit_bytes=1 << 20),
    )(place, block, *so_far)


def on_device(features, conv_first, conv_second, out_grad):
    frames, high, wide, chans = features.shape
    assert frames == FRAMES and chans == LANES and lax.axis_size("row") == 2
    size = Sizes(high, wide)
    across = lax.axis_size("col")
    peers = 2 * across
    factor = 1.0 / math.sqrt(size.cells * FRAMES * lax.axis_size("tm") * peers)
    place = jnp.stack([lax.axis_index("row"), lax.axis_index("col")]).astype(jnp.int32)
    taps = conv_first.shape
    first = conv_first.reshape(-1, LANES)
    second = conv_second.reshape(-1, LANES)
    work = 2 * first.size * size.cells * FRAMES
    part = functools.partial
    stat = ((STATS, LANES), F32)
    tall, broad = size.tall(), size.broad()
    frame = ((tall, broad, LANES), F32)

    edge = up(3 * FRAMES * wide + PARTS, 16)
    lines = up(FRAMES * size.stride(1) + 2 * FRAMES * size.stride(2) + PARTS, 16)
    flat = ((2, lines, LANES), F32)
    pay, stats, cols, features_near, grad_near = call(
        part(start_body, size),
        [((edge, LANES), BF16), stat, flat, (features.shape, BF16), (features.shape, BF16)],
        [place, features, out_grad],
        smem=1,
        far=2,
        sems=2 * FRAMES,
    )
    row_got = row_swap(pay)
    (slots,) = call(
        part(slots_body, size, (1, 2), across),
        [((across, lines, LANES), BF16)],
        [place, cols, row_got, stats],
        [flat],
        smem=1,
    )
    col_got = lax.all_to_all(slots, "col", 0, 0)
    block = ((size.rows(1), LANES), BF16)
    act_first, grad, norm_first = call(
        part(act_first_body, size, across),
        [block, ((size.rows(2), LANES), BF16), stat],
        [place, features_near, grad_near, row_got, col_got],
        [frame],
        smem=1,
    )
    act_before = later(act_first, 1)
    grad_after = later(grad, -1)

    edge = up(FRAMES * wide + PARTS, 16)
    halves = ((FRAMES, tall, wide, 3 * LANES), BF16)
    sums, x_own = call(
        part(hidden_own_body, size),
        [((FRAMES, size.cells, LANES), F32), halves],
        [act_first, first],
        conv_scratch(size, 1, wide, FRAMES),
        sems=1,
        mib=12,
        flops=work // 2,
        out_far=1,
    )
    hidden, pay, stats, x_before = call(
        part(hidden_body, size),
        [(features.shape, BF16), ((edge, LANES), BF16), stat, halves],
        [place, act_before, sums, first],
        conv_scratch(size, 1, wide, FRAMES),
        smem=1,
        sems=1,
        mib=12,
        flops=work // 2,
        out_far=1,
    )
    row_got = row_swap(pay)
    lines = up(FRAMES * size.stride(1) + PARTS, 16)
    flat = ((2, lines, LANES), F32)
    (cols,) = call(part(columns_body, size), [flat], [hidden])
    (slots,) = call(
        part(slots_body, size, (1,), across),
        [((across, lines, LANES), BF16)],
        [place, cols, row_got, stats],
        [flat],
        smem=1,
    )
    slots, grad_after = lax.optimization_barrier((slots, grad_after))
    col_got = lax.all_to_all(slots, "col", 0, 0)
    (grad_act,) = call(
        part(grad_act_body, size),
        [((FRAMES, tall, broad, LANES), F32)],
        [grad, grad_after, second],
        conv_scratch(size, 2, up(wide + 2, 16)),
        mib=16,
        flops=2 * work,
    )
    field = ((FRAMES, tall, broad, LANES), F32)
    norm_second, slots = call(
        part(sums_second_body, size, across),
        [stat, ((peers, STATS, LANES), F32)],
        [hidden, col_got, grad_act],
    )
    got = lax.all_to_all(slots, ("row", "col"), 0, 0)
    act_second, q, z = call(
        part(act_second_body, size, across),
        [block, field, field],
        [place, hidden, row_got, col_got, grad_act, norm_second],
        [frame, field, field],
        smem=1,
        sems=2 * FRAMES,
        beside=True,
        out_far=2,
    )
    turned = ((FRAMES * LANES, size.cells), BF16)
    (second_term,) = call(
        part(second_term_body, size),
        [(first.shape, F32)],
        [grad, grad_after, act_second],
        [*conv_scratch(size, 1, wide), turned, (first.shape, F32)],
        sems=9,
        mib=16,
        beside=True,
        out_far=1,
    )
    grad_second, keep, give = call(
        part(first_term_body, size, across),
        [block, (first.shape, F32), (first.shape, BF16)],
        [place, got, norm_second, q, z, x_before, x_own, second_term],
        [*conv_scratch(size, 1, wide), turned, (first.shape, F32), field, field],
        smem=1,
        far=5,
        sems=2 * FRAMES + 3,
        mib=20,
        flops=work,
    )
    give, late_grad, late_act = lax.optimization_barrier((give, grad_second, act_second))
    act_second_before = later(late_act, 1)
    grad_second_after = later(late_grad, -1)

    along = lax.axis_size("tm")
    rows = first.shape[0]
    by_col = rows // across
    (slots,) = call(joined_body, [((across, by_col, LANES), BF16)], [keep, row_swap(give)])
    slots = lax.all_to_all(slots, "col", 0, 0)
    slots, grad_second_after = lax.optimization_barrier((slots, grad_second_after))
    share = up(by_col, 16 * along) // along
    (slots,) = call(
        shared_body,
        [((along, share, LANES), BF16)],
        [slots],
        [((along * share, LANES), F32)],
    )
    got = lax.all_to_all(slots, "tm", 0, 0)
    (result,) = call(
        part(result_body, size),
        [(features.shape, BF16)],
        [act_second_before, act_second, second, features],
        conv_scratch(size, 1, wide),
        mib=14,
        flops=work,
    )
    q, sums = call(
        part(back_first_body, size),
        [((FRAMES, size.cells, LANES), F32), stat],
        [grad_second, grad_second_after, first, features, norm_first],
        conv_scratch(size, 1, wide),
        mib=14,
        flops=work,
    )
    got, result = lax.optimization_barrier((got, result))
    (slots,) = call(part(finished_body, factor), [((along, share, LANES), BF16)], [got])
    done = lax.all_to_all(slots, "tm", 0, 0).reshape(-1, LANES)[:by_col]
    parts = sum_parts(sums + row_swap(sums))
    parts = jnp.pad(parts, ((0, -parts.shape[0] % 16), (0, 0)))
    done = jnp.concatenate([done, parts], 0)
    mine = lax.all_to_all(jnp.broadcast_to(done[None], (across, *done.shape)), "col", 0, 0)
    theirs = row_swap(mine)
    so_far = placed(place, mine, 0, by_col, [])
    first_grad, second_grad = placed(place, theirs, 1, by_col, so_far)
    (feature_grad,) = call(
        part(feature_grad_body, size, peers),
        [(features.shape, BF16)],
        [features, out_grad, norm_first, q, mine[:, by_col:]],
    )
    return (result, feature_grad, first_grad.reshape(taps), second_grad.reshape(taps))


def solution(mesh):
    in_specs = (P("tm", "row", "col", None), P(), P(), P("tm", "row", "col", None))
    out_specs = (P("tm", "row", "col", None), P("tm", "row", "col", None), P(), P())
    return jax.shard_map(
        on_device, mesh=mesh, in_specs=in_specs, out_specs=out_specs, check_vma=False
    )
```

```python
import functools
import math

import jax
import jax.numpy as jnp
from jax import lax
from jax.experimental import pallas as pl
from jax.experimental.pallas import tpu as pltpu
from jax.sharding import PartitionSpec as P

GROUPS = 32
EPSILON = 1e-06
F32 = jnp.float32
BF16 = jnp.bfloat16
LANES = 128
FRAMES = 2
STATS = 8
PARTS = 3 * STATS


def up(count, step):
    return -(-count // step) * step


class Sizes:
    def __init__(self, high, wide):
        self.high, self.wide = high, wide
        self.cells = high * wide

    def stride(self, rim):
        return up(self.high + 2 * rim, 8)

    def main(self, rim):
        return FRAMES * (self.high + 2 * rim) * self.wide

    def rows(self, rim):
        return up(self.main(rim) + 2 * rim * FRAMES * self.stride(rim), 16)

    def tall(self):
        return self.high + 2

    def broad(self):
        return up(self.wide + 2, 8)


def call(body, outs, args, scratch=(), smem=0, far=0, sems=0, mib=8, flops=0, beside=False, out_far=0):
    specs = [pl.BlockSpec(memory_space=pltpu.SMEM)] * smem
    specs += [pl.BlockSpec(memory_space=pltpu.VMEM)] * (len(args) - smem - far)
    specs += [pl.BlockSpec(memory_space=pltpu.HBM)] * far
    near = len(args) - far
    args = [*args[:near], *(pltpu.with_memory_space_constraint(a, pltpu.HBM) for a in args[near:])]
    scratches = [pltpu.VMEM(shape, dtype) for shape, dtype in scratch]
    if sems:
        scratches.append(pltpu.SemaphoreType.DMA((sems,)))
    shapes = [jax.ShapeDtypeStruct(shape, dtype) for shape, dtype in outs]
    kept = len(outs) - out_far
    moved = sum(math.prod(a.shape) * a.dtype.itemsize for a in [*args, *shapes])
    moved = 0 if beside else moved
    return pl.pallas_call(
        body,
        out_shape=shapes[:kept] + [pltpu.HBM(o.shape, o.dtype) for o in shapes[kept:]],
        in_specs=specs,
        out_specs=[pl.BlockSpec(memory_space=pltpu.VMEM)] * kept
        + [pl.BlockSpec(memory_space=pltpu.HBM)] * out_far,
        scratch_shapes=scratches,
        cost_estimate=pl.CostEstimate(flops=flops, bytes_accessed=moved, transcendentals=0),
        compiler_params=pltpu.CompilerParams(vmem_limit_bytes=mib << 20),
    )(*args)


def logistic(values):
    return 0.5 * jnp.tanh(0.5 * values) + 0.5


def lane_totals(stat):
    lane = lax.broadcasted_iota(jnp.int32, stat.shape, 1)
    step = 1
    while step < LANES // GROUPS:
        ahead = pltpu.roll(stat, LANES - step, 1)
        behind = pltpu.roll(stat, step, 1)
        stat = stat + jnp.where((lane // step) % 2 == 0, ahead, behind)
        step *= 2
    return stat


def split3(stat):
    high = stat.astype(BF16).astype(F32)
    rest = stat - high
    middle = rest.astype(BF16).astype(F32)
    return jnp.concatenate([high, middle, rest - middle], 0)


def join3(parts):
    parts = parts.astype(F32)
    return parts[:STATS] + (parts[STATS : 2 * STATS] + parts[2 * STATS : PARTS])


def stat_block(first, second):
    rest = jnp.zeros((STATS - 2 * FRAMES, LANES), F32)
    return jnp.concatenate([*first, *second, rest], 0)


def measured(frames):
    means, squares = [], []
    for frame in frames:
        mean = jnp.sum(frame, 0, keepdims=True) / frame.shape[0]
        centred = frame - mean
        means.append(mean)
        squares.append(jnp.sum(centred * centred, 0, keepdims=True))
    return stat_block(means, squares)


def merged(one, two, cells):
    delta = one - two
    extra = (0.5 * cells) * delta * delta
    mean = 0.5 * (one[:FRAMES] + two[:FRAMES])
    square = one[FRAMES : 2 * FRAMES] + two[FRAMES : 2 * FRAMES] + extra[:FRAMES]
    return jnp.concatenate([mean, square, jnp.zeros((STATS - 2 * FRAMES, LANES), F32)], 0)


def concluded(blocks, cells):
    per_group = LANES // GROUPS
    mean = sum(blocks[1:], blocks[0])[:FRAMES]
    mean = lane_totals(mean) / (len(blocks) * per_group)
    total = jnp.zeros((FRAMES, LANES), F32)
    for block in blocks:
        off = block[:FRAMES] - mean
        total = total + block[FRAMES : 2 * FRAMES] + cells * off * off
    spread = lane_totals(total) / (cells * len(blocks) * per_group)
    rest = jnp.zeros((STATS - 2 * FRAMES, LANES), F32)
    return jnp.concatenate([mean, lax.rsqrt(spread + EPSILON), rest], 0)


def rim_rows(place, got):
    upper = place[0] == 0
    nothing = jnp.zeros_like(got)
    return jnp.where(upper, nothing, got), jnp.where(upper, got, nothing)


def in_frame(shape, place, across, size, rim):
    row = lax.broadcasted_iota(jnp.int32, shape, 0)
    col = lax.broadcasted_iota(jnp.int32, shape, 1)
    top = jnp.where(place[0] == 0, rim, 0)
    bottom = jnp.where(place[0] == 0, size.high + 2 * rim, size.high + rim)
    left = jnp.where(place[1] == 0, rim, 0)
    right = jnp.where(place[1] == across - 1, size.wide + rim, size.wide + 2 * rim)
    return (row >= top) & (row < bottom) & (col >= left) & (col < right)


def take_columns(size, arrays, flat):
    flat[...] = jnp.zeros_like(flat)
    at = 0
    for array, rim in arrays:
        for j in range(rim):
            for frame in range(FRAMES):
                for side, col in ((0, j), (1, size.wide - rim + j)):
                    rows = array[frame, :, col : col + 1].astype(F32)
                    rows = rows.reshape(size.high, LANES)
                    flat[side, at + rim : at + rim + size.high] = rows
                at += size.stride(rim)


def start_body(
    size, place, features_far, grad_far, pay, stats, flat, features, out_grad, sems
):
    high, wide = size.high, size.wide
    upper = place[0] == 0
    copies = [
        pltpu.make_async_copy(source.at[f], target.at[f], sems.at[FRAMES * k + f])
        for k, (source, target) in enumerate(((features_far, features), (grad_far, out_grad)))
        for f in range(FRAMES)
    ]
    for copy in copies:
        copy.start()
    for copy in copies[:FRAMES]:
        copy.wait()
    at = 0
    for frame in range(FRAMES):
        pay[at : at + wide] = jnp.where(upper, features[frame, high - 1], features[frame, 0])
        at += wide
    found = measured([features[f].astype(F32).reshape(size.cells, LANES) for f in range(FRAMES)])
    stats[...] = found
    for copy in copies[FRAMES:]:
        copy.wait()
    for frame in range(FRAMES):
        for row in range(2):
            edge = jnp.where(upper, out_grad[frame, high - 2 + row], out_grad[frame, row])
            pay[at : at + wide] = edge
            at += wide
    fill = jnp.zeros((pay.shape[0] - at - PARTS, LANES), F32)
    pay[at:] = jnp.concatenate([split3(found), fill], 0).astype(BF16)
    take_columns(size, ((features, 1), (out_grad, 2)), flat)


def slots_body(size, rims, across, place, flat, got, stats, slots, work):
    wide, high = size.wide, size.high
    upper = place[0] == 0
    work[...] = flat[...]
    at = base = 0
    for rim in rims:
        for j in range(rim):
            for frame in range(FRAMES):
                for row in range(rim):
                    start = base + (frame * rim + row) * wide
                    for side, col in ((0, j), (1, wide - rim + j)):
                        cell = start - start % 16 + 16 * ((start % 16 + col) // 16)
                        tile = got[cell : cell + 16].astype(F32)
                        edge = tile[start + col - cell : start + col - cell + 1]
                        nothing = jnp.zeros_like(edge)
                        top, bottom = at + row, at + rim + high + row
                        work[side, top : top + 1] = jnp.where(upper, nothing, edge)
                        work[side, bottom : bottom + 1] = jnp.where(upper, edge, nothing)
                at += size.stride(rim)
        base += FRAMES * rim * wide
    parts = split3(merged(stats[...], join3(got[base : base + PARTS]), size.cells))
    work[0, at : at + PARTS] = parts
    work[1, at : at + PARTS] = parts
    for peer in range(across):
        slots[peer] = jnp.where(peer > place[1], work[1], work[0]).astype(BF16)


def sides(place, across, got, first, count):
    left = got[jnp.maximum(place[1] - 1, 0), first : first + count].astype(F32)
    right = got[jnp.minimum(place[1] + 1, across - 1), first : first + count].astype(F32)
    nothing = jnp.zeros_like(left)
    left = jnp.where(place[1] > 0, left, nothing)
    right = jnp.where(place[1] < across - 1, right, nothing)
    return left, right


def padded_frame(size, own, top, bottom, left, right, frame):
    high, wide = size.high, size.wide
    frame[1 : high + 1, 1 : wide + 1] = own
    frame[0:1, 1 : wide + 1] = top[None]
    frame[high + 1 : high + 2, 1 : wide + 1] = bottom[None]
    tall = high + 2
    frame[:, 0:1] = left[:tall].reshape(tall, 1, LANES)
    frame[:, wide + 1 : wide + 2] = right[:tall].reshape(tall, 1, LANES)


def put_frame(size, frame, index, out):
    wide, tall, step = size.wide, size.tall(), size.stride(1)
    flat = frame[:, 1 : wide + 1].reshape(tall * wide, LANES)
    out[index * tall * wide : (index + 1) * tall * wide] = flat.astype(BF16)
    fill = jnp.zeros((step - tall, LANES), F32)
    left = frame[:, 0:1].reshape(tall, LANES)
    right = frame[:, wide + 1 : wide + 2].reshape(tall, LANES)
    return jnp.concatenate([left, fill], 0), jnp.concatenate([right, fill], 0)


def put_sides(out, first, blocks):
    fill = out.shape[0] - first - sum(b.shape[0] for b in blocks)
    if fill:
        blocks = [*blocks, jnp.zeros((fill, LANES), F32)]
    out[first:] = jnp.concatenate(blocks, 0).astype(BF16)


def act_first_body(
    size, across, place, features, out_grad, row_got, col_got, act, grad, norm, frame
):
    high, wide = size.high, size.wide
    at = FRAMES * size.stride(1) + 2 * FRAMES * size.stride(2)
    blocks = [join3(col_got[peer, at : at + PARTS]) for peer in range(across)]
    found = concluded(blocks, 2 * size.cells)
    norm[...] = found
    step = size.stride(1)
    left_all, right_all = sides(place, across, col_got, 0, FRAMES * step)
    ok = in_frame((size.tall(), size.broad(), LANES), place, across, size, 1)
    lefts, rights = [], []
    frame[...] = jnp.zeros_like(frame)
    for f in range(FRAMES):
        top, bottom = rim_rows(place, row_got[f * wide : (f + 1) * wide].astype(F32))
        padded_frame(
            size,
            features[f].astype(F32),
            top,
            bottom,
            left_all[f * step : (f + 1) * step],
            right_all[f * step : (f + 1) * step],
            frame,
        )
        normed = (frame[...] - found[f : f + 1][None]) * found[FRAMES + f : FRAMES + f + 1][None]
        frame[...] = jnp.where(ok, normed * logistic(normed), 0.0)
        left, right = put_frame(size, frame, f, act)
        lefts.append(left)
        rights.append(right)
    put_sides(act, size.main(1), lefts + rights)

    tall = high + 4
    for f in range(FRAMES):
        start = f * tall * wide
        for row in range(2):
            first = FRAMES * wide + (f * 2 + row) * wide
            top, bottom = rim_rows(place, row_got[first : first + wide])
            grad[start + row * wide : start + (row + 1) * wide] = top
            below = start + (high + 2 + row) * wide
            grad[below : below + wide] = bottom
        grad[start + 2 * wide : start + (high + 2) * wide] = out_grad[f].reshape(
            size.cells, LANES
        )
    left, right = sides(
        place, across, col_got, FRAMES * step, 2 * FRAMES * size.stride(2)
    )
    put_sides(grad, size.main(2), [left, right])


def spread_columns(size, rim, trim, wo, block, index, dst, at, frame):
    wide, high = size.wide, size.high
    tall, step = high + 2 * rim, size.stride(rim)
    main = block[index * tall * wide : (index + 1) * tall * wide].astype(F32)
    main = main.reshape(tall, wide, LANES)
    cut = rim - trim
    tall_out = tall - 2 * cut
    frame[:, trim : trim + wide] = main[cut : cut + tall_out]
    first = size.main(rim)
    edges = block[first:].astype(F32)
    for j in range(2 * rim):
        col = j - cut if j < rim else j - rim + trim + wide
        if j < cut or (j >= rim and j - rim >= trim):
            continue
        start = (j * FRAMES + index) * step
        edge = edges[start + cut : start + cut + tall_out]
        frame[:, col : col + 1] = edge.reshape(tall_out, 1, LANES)
    for c in range(3):
        dst[at, :, :, c * LANES : (c + 1) * LANES] = frame[:, c : c + wo].astype(BF16)


def spread_all(size, rim, trim, wo, near, far, dst, frame):
    filled = size.wide + 2 * trim
    if frame.shape[1] > filled:
        frame[:, filled:] = jnp.zeros((frame.shape[0], frame.shape[1] - filled, LANES), F32)
    for f in range(dst.shape[0]):
        block = near if f < FRAMES else far
        spread_columns(size, rim, trim, wo, block, f % FRAMES, dst, f, frame)


def tap_dot(x, kernel, turned):
    ho, wo = x.shape[1] - 2, x.shape[2]
    count = ho * wo
    span = 9 * LANES

    def cells(f):
        return jnp.concatenate(
            [x[f, b : b + ho].reshape(count, 3 * LANES) for b in range(3)], 1
        )

    def taps(a):
        if not turned:
            return kernel[a * span : (a + 1) * span]
        last = (3 - a) * 9 - 1
        return jnp.concatenate(
            [kernel[(last - k) * LANES : (last - k + 1) * LANES] for k in range(9)], 1
        )

    dims = (((1,), (1 if turned else 0,)), ((), ()))

    def dot(f, *times):
        weights = [taps(a) for a in times]
        if len(weights) > 1:
            weights = [jnp.concatenate(weights, 0 if turned else 1)]
        return lax.dot_general(cells(f), weights[0], dims, preferred_element_type=F32)

    return dot


def convolved(x, kernel, turned):
    dot = tap_dot(x, kernel, turned)
    both = dot(1, 1, 0) + dot(2, 2, 1)
    return both[:, :LANES] + dot(0, 0), both[:, LANES:] + dot(3, 2)


def conv_scratch(size, trim, wo, frames=2 * FRAMES):
    tall = size.high + 2 * trim
    return [((frames, tall, wo, 3 * LANES), BF16), ((tall, up(wo + 2, 8), LANES), F32)]


def hidden_own_body(size, own, kernel, sums, x, frame):
    spread_all(size, 1, 1, size.wide, own, None, x, frame)
    dot = tap_dot(x, kernel, False)
    both = dot(0, 2, 1)
    sums[0] = both[:, :LANES]
    sums[1] = both[:, LANES:] + dot(1, 2)


def hidden_body(size, across, place, before, sums, kernel, hidden, slots, x, frame, flat):
    high, wide = size.high, size.wide
    spread_all(size, 1, 1, wide, before, None, x, frame)
    dot = tap_dot(x, kernel, False)
    both = dot(1, 1, 0)
    sums = (sums[0] + both[:, :LANES] + dot(0, 0), sums[1] + both[:, LANES:])
    rounded = [s.astype(BF16) for s in sums]
    for f in range(FRAMES):
        hidden[f] = rounded[f].reshape(high, wide, LANES)
    span = span_second(size)
    found = split3(measured([r.astype(F32) for r in rounded]))
    take_columns(size, ((hidden, 1),), flat)
    upper = place[0] == 0
    edges = [jnp.where(upper, r[size.cells - wide :], r[:wide]).astype(F32) for r in rounded]
    fill = jnp.zeros((span - FRAMES * wide, LANES), F32)
    edges = jnp.concatenate([*edges, fill] if fill.shape[0] else edges, 0)
    rest = jnp.zeros((slots.shape[1] - span - PARTS, LANES), F32)
    for peer in range(slots.shape[0]):
        col = peer % across
        side = jnp.where(col > place[1], flat[1], flat[0])
        content = jnp.where(col == place[1], edges, side)
        slots[peer] = jnp.concatenate([content, found, rest], 0).astype(BF16)


def grad_act_body(size, near, far, kernel, out, x, frame):
    wo = x.shape[2]
    spread_all(size, 2, 2, wo, near, far, x, frame)
    sums = convolved(x, kernel, True)
    for f in range(FRAMES):
        out[f] = sums[f].reshape(size.tall(), wo, LANES)[:, : size.broad()]


def crossed_sides(size, place, across, got):
    step, high = size.stride(1), size.high
    count = FRAMES * step
    upper = place[0] == 0
    row = lax.broadcasted_iota(jnp.int32, (count, LANES), 0)
    found = []
    for at, there in (
        (jnp.maximum(place[1] - 1, 0), place[1] > 0),
        (jnp.minimum(place[1] + 1, across - 1), place[1] < across - 1),
    ):
        block = got[place[0] * across + at, 0:count].astype(F32)
        cross = got[(1 - place[0]) * across + at, 0:count].astype(F32)
        for f in range(FRAMES):
            above = jnp.where(upper, 0.0, cross[f * step + high : f * step + high + 1])
            below = jnp.where(upper, cross[f * step + 1 : f * step + 2], 0.0)
            block = jnp.where(row == f * step, above, block)
            block = jnp.where(row == f * step + high + 1, below, block)
        found.append(jnp.where(there, block, 0.0))
    return found


def span_second(size):
    return up(max(FRAMES * size.wide, FRAMES * size.stride(1)), 16)


def sums_second_body(size, across, hidden, got, grad_act, norm, slots):
    high, wide = size.high, size.wide
    at = span_second(size)
    blocks = [join3(got[peer, at : at + PARTS]) for peer in range(got.shape[0])]
    found = concluded(blocks, size.cells)
    norm[...] = found
    firsts, seconds = [], []
    for f in range(FRAMES):
        own = hidden[f].astype(F32)
        normed = (own - found[f : f + 1][None]) * found[FRAMES + f : FRAMES + f + 1][None]
        sigmoid = logistic(normed)
        grad = grad_act[f, 1 : high + 1, 1 : wide + 1]
        grad = grad * sigmoid * (1.0 + normed * (1.0 - sigmoid))
        grad, normed = grad.reshape(size.cells, LANES), normed.reshape(size.cells, LANES)
        firsts.append(jnp.sum(grad, 0, keepdims=True))
        seconds.append(jnp.sum(grad * normed, 0, keepdims=True))
    sums = stat_block(firsts, seconds)
    for peer in range(slots.shape[0]):
        slots[peer] = sums


def act_second_body(
    size, across, place, hidden, got, grad_act, norm, act, q_far, z_far, frame, q, z, sems
):
    wide = size.wide
    step = size.stride(1)
    left_all, right_all = crossed_sides(size, place, across, got)
    ok = in_frame((size.tall(), size.broad(), LANES), place, across, size, 1)
    lefts, rights, copies = [], [], []
    frame[...] = jnp.zeros_like(frame)
    facing = (1 - place[0]) * across + place[1]
    for f in range(FRAMES):
        top, bottom = rim_rows(place, got[facing, f * wide : (f + 1) * wide].astype(F32))
        padded_frame(
            size,
            hidden[f].astype(F32),
            top,
            bottom,
            left_all[f * step : (f + 1) * step],
            right_all[f * step : (f + 1) * step],
            frame,
        )
        normed = (frame[...] - norm[f : f + 1][None]) * norm[FRAMES + f : FRAMES + f + 1][None]
        sigmoid = logistic(normed)
        frame[...] = jnp.where(ok, normed * sigmoid, 0.0)
        left, right = put_frame(size, frame, f, act)
        lefts.append(left)
        rights.append(right)
        z[f] = normed
        q[f] = grad_act[f] * sigmoid * (1.0 + normed * (1.0 - sigmoid))
        for k, (source, target) in enumerate(((q, q_far), (z, z_far))):
            copy = pltpu.make_async_copy(source.at[f], target.at[f], sems.at[2 * f + k])
            copy.start()
            copies.append(copy)
    put_sides(act, size.main(1), lefts + rights)
    for copy in copies:
        copy.wait()


def hidden_grad(size, across, place, q, z, got, norm, out, frame, arrive):
    peers = got.shape[0]
    total = got[0]
    for peer in range(1, peers):
        total = total + got[peer]
    means = lane_totals(total) / (size.cells * peers * (LANES // GROUPS))
    ok = in_frame((size.tall(), size.broad(), LANES), place, across, size, 1)
    lefts, rights = [], []
    for f in range(FRAMES):
        first, second = means[f : f + 1][None], means[FRAMES + f : FRAMES + f + 1][None]
        inv = norm[FRAMES + f : FRAMES + f + 1][None]
        arrive(f)
        frame[...] = jnp.where(ok, inv * (q[f] - first - z[f] * second), 0.0)
        left, right = put_frame(size, frame, f, out)
        lefts.append(left)
        rights.append(right)
    put_sides(out, size.main(1), lefts + rights)


def own_cells(size, block, f):
    start = (f * size.tall() + 1) * size.wide
    return block[start : start + size.cells]


def turned_cells(size, block, out):
    for f in range(FRAMES):
        cells = own_cells(size, block, f).astype(F32).T.astype(BF16)
        out[f * LANES : (f + 1) * LANES] = cells


def tap_sums(x, turned, b):
    ho, wo = x.shape[1] - 2, x.shape[2]

    def cells(f):
        return x[f, b : b + ho].reshape(ho * wo, 3 * LANES)

    def dot(one, two):
        return jnp.dot(one, two, preferred_element_type=F32)

    low = dot(turned[...], cells(1))
    high = dot(turned[...], cells(2))
    return (
        dot(turned[:LANES], cells(0)) + low[LANES:],
        low[:LANES] + high[LANES:],
        high[:LANES] + dot(turned[LANES:], cells(3)),
    )


def second_term_body(size, near, far, act, out_far, short_far, x, frame, turned, out, short, sems):
    spread_all(size, 2, 1, size.wide, near, far, x, frame)
    turned_cells(size, act, turned)
    span = 3 * LANES
    copies = []
    for b in range(3):
        for a, total in enumerate(tap_sums(x, turned, b)):
            for c in range(3):
                tap = ((2 - a) * 3 + 2 - b) * 3 + 2 - c
                rows = slice(tap * LANES, (tap + 1) * LANES)
                piece = total[:, c * LANES : (c + 1) * LANES]
                out[rows] = piece
                short[rows] = piece.astype(BF16)
            rows = pl.ds(((2 - a) * 3 + 2 - b) * span, span)
            for k, (source, target) in enumerate(((out, out_far), (short, short_far))):
                sem = sems.at[2 * (3 * b + a) + k]
                copy = pltpu.make_async_copy(source.at[rows], target.at[rows], sem)
                copy.start()
                copies.append(copy)
    for copy in copies:
        copy.wait()


def first_term_body(
    size,
    across,
    place,
    got,
    norm,
    q_far,
    z_far,
    near_far,
    own_far,
    short_far,
    out,
    give,
    grad_far,
    x,
    frame,
    turned,
    grad,
    near,
    own,
    short,
    q,
    z,
    sems,
):
    pairs = [(q_far.at[f], q.at[f]) for f in range(FRAMES)]
    pairs += [(z_far.at[f], z.at[f]) for f in range(FRAMES)]
    pairs += [(near_far, near), (own_far, own), (short_far, short)]
    copies = [
        pltpu.make_async_copy(source, target, sems.at[k])
        for k, (source, target) in enumerate(pairs)
    ]
    for k in (0, FRAMES, 1, FRAMES + 1, 2 * FRAMES, 2 * FRAMES + 1, 2 * FRAMES + 2):
        copies[k].start()

    def arrive(f):
        copies[f].wait()
        copies[FRAMES + f].wait()

    hidden_grad(size, across, place, q, z, got, norm, grad, frame, arrive)
    sent = pltpu.make_async_copy(grad, grad_far, sems.at[len(pairs)])
    sent.start()
    turned_cells(size, grad, turned)
    for copy in copies[2 * FRAMES :]:
        copy.wait()
    spread_all(size, 1, 1, size.wide, near, own, x, frame)
    upper = place[0] == 0
    for b in range(3):
        for a, total in enumerate(tap_sums(x, turned, b)):
            rows = slice((a * 3 + b) * 3 * LANES, (a * 3 + b + 1) * 3 * LANES)
            piece = total.T
            out[rows] = piece
            give[rows] = jnp.where(upper, short[rows], piece.astype(BF16))
    sent.wait()


def result_body(size, near, far, kernel, features, out, x, frame):
    spread_all(size, 1, 1, size.wide, near, far, x, frame)
    sums = convolved(x, kernel, False)
    for f in range(FRAMES):
        total = features[f].astype(F32) + sums[f].reshape(size.high, size.wide, LANES)
        out[f] = total.astype(BF16)


def back_first_body(size, near, far, kernel, features, norm, q, sums, x, frame):
    spread_all(size, 1, 1, size.wide, near, far, x, frame)
    grads = convolved(x, kernel, True)
    firsts, seconds = [], []
    for f in range(FRAMES):
        values = features[f].astype(F32).reshape(size.cells, LANES)
        normed = (values - norm[f : f + 1]) * norm[FRAMES + f : FRAMES + f + 1]
        sigmoid = logistic(normed)
        grad = grads[f] * sigmoid * (1.0 + normed * (1.0 - sigmoid))
        q[f] = grad
        firsts.append(jnp.sum(grad, 0, keepdims=True))
        seconds.append(jnp.sum(grad * normed, 0, keepdims=True))
    sums[...] = stat_block(firsts, seconds)


def feature_grad_body(size, peers, features, out_grad, norm, q, got, out):
    total = join3(got[0])
    for peer in range(1, got.shape[0]):
        total = total + join3(got[peer])
    means = lane_totals(total) / (size.cells * peers * (LANES // GROUPS))
    for f in range(FRAMES):
        values = features[f].astype(F32).reshape(size.cells, LANES)
        inv = norm[FRAMES + f : FRAMES + f + 1]
        normed = (values - norm[f : f + 1]) * inv
        grad = inv * (q[f] - means[f : f + 1] - normed * means[FRAMES + f : FRAMES + f + 1])
        grad = out_grad[f].astype(F32) + grad.reshape(size.high, size.wide, LANES)
        out[f] = grad.astype(BF16)


def row_swap(values):
    return lax.ppermute(values, "row", [(0, 1), (1, 0)])


def later(values, by):
    peers = lax.axis_size("tm")
    pairs = [(i, i + by) for i in range(peers) if 0 <= i + by < peers]
    return lax.ppermute(values, "tm", pairs)


def sum_parts(stat):
    high = lax.reduce_precision(stat, 8, 7)
    rest = stat - high
    middle = lax.reduce_precision(rest, 8, 7)
    return jnp.concatenate([high, middle, rest - middle], 0).astype(BF16)


def total_of(got):
    total = got[0].astype(F32)
    for peer in range(1, got.shape[0]):
        total = total + got[peer].astype(F32)
    return total


def joined_body(place, first, second, got, out):
    share = out.shape[1]
    upper = place[0] == 0
    for peer in range(out.shape[0]):
        rows = slice(peer * share, (peer + 1) * share)
        keep = jnp.where(upper, first[rows], second[rows])
        out[peer] = (keep + got[rows].astype(F32)).astype(BF16)


def shared_body(got, out, flat):
    rows, share = got.shape[1], out.shape[1]
    if flat.shape[0] > rows:
        flat[rows:] = jnp.zeros((flat.shape[0] - rows, LANES), F32)
    flat[:rows] = total_of(got)
    for peer in range(out.shape[0]):
        out[peer] = flat[peer * share : (peer + 1) * share].astype(BF16)


def finished_body(factor, got, out):
    total = (total_of(got) * factor).astype(BF16)
    for peer in range(out.shape[0]):
        out[peer] = total


def placed_body(rows, swapped, *refs):
    place, block, first, second, sems = refs[0], refs[1], *refs[-3:]

    def move(target):
        copies = [
            pltpu.make_async_copy(
                block.at[peer, pl.ds(0, rows)], target.at[pl.ds(peer * rows, rows)], sems.at[peer]
            )
            for peer in range(block.shape[0])
        ]
        for copy in copies:
            copy.start()
        for copy in copies:
            copy.wait()

    @pl.when(place[0] == swapped)
    def _():
        move(first)

    @pl.when(place[0] != swapped)
    def _():
        move(second)


def placed(place, block, swapped, rows, so_far):
    anywhere = pl.BlockSpec(memory_space=pl.ANY)
    shape = (rows * block.shape[0], LANES)
    return pl.pallas_call(
        functools.partial(placed_body, rows, swapped),
        out_shape=[jax.ShapeDtypeStruct(shape, BF16)] * 2,
        in_specs=[pl.BlockSpec(memory_space=pltpu.SMEM)] + [anywhere] * (1 + len(so_far)),
        out_specs=[anywhere, anywhere],
        input_output_aliases={2 + k: k for k in range(len(so_far))},
        scratch_shapes=[pltpu.SemaphoreType.DMA((block.shape[0],))],
        compiler_params=pltpu.CompilerParams(vmem_limit_bytes=1 << 20),
    )(place, block, *so_far)


def on_device(features, conv_first, conv_second, out_grad):
    frames, high, wide, chans = features.shape
    assert frames == FRAMES and chans == LANES and lax.axis_size("row") == 2
    size = Sizes(high, wide)
    across = lax.axis_size("col")
    peers = 2 * across
    factor = 1.0 / math.sqrt(size.cells * FRAMES * lax.axis_size("tm") * peers)
    place = jnp.stack([lax.axis_index("row"), lax.axis_index("col")]).astype(jnp.int32)
    taps = conv_first.shape
    first = conv_first.reshape(-1, LANES)
    second = conv_second.reshape(-1, LANES)
    work = 2 * first.size * size.cells * FRAMES
    part = functools.partial
    stat = ((STATS, LANES), F32)
    tall, broad = size.tall(), size.broad()
    frame = ((tall, broad, LANES), F32)

    edge = up(3 * FRAMES * wide + PARTS, 16)
    lines = up(FRAMES * size.stride(1) + 2 * FRAMES * size.stride(2) + PARTS, 16)
    flat = ((2, lines, LANES), F32)
    pay, stats, cols, features_near, grad_near = call(
        part(start_body, size),
        [((edge, LANES), BF16), stat, flat, (features.shape, BF16), (features.shape, BF16)],
        [place, features, out_grad],
        smem=1,
        far=2,
        sems=2 * FRAMES,
    )
    row_got = row_swap(pay)
    (slots,) = call(
        part(slots_body, size, (1, 2), across),
        [((across, lines, LANES), BF16)],
        [place, cols, row_got, stats],
        [flat],
        smem=1,
    )
    col_got = lax.all_to_all(slots, "col", 0, 0)
    block = ((size.rows(1), LANES), BF16)
    act_first, grad, norm_first = call(
        part(act_first_body, size, across),
        [block, ((size.rows(2), LANES), BF16), stat],
        [place, features_near, grad_near, row_got, col_got],
        [frame],
        smem=1,
    )
    grad_after = later(grad, -1)
    act_before = later(act_first, 1)

    edge = up(FRAMES * wide + PARTS, 16)
    (sums,) = call(
        part(hidden_own_body, size),
        [((FRAMES, size.cells, LANES), F32)],
        [act_first, first],
        conv_scratch(size, 1, wide, FRAMES),
        mib=12,
        flops=work // 2,
    )
    span = span_second(size)
    hidden, slots = call(
        part(hidden_body, size, across),
        [(features.shape, BF16), ((peers, up(span + PARTS, 16), LANES), BF16)],
        [place, act_before, sums, first],
        [*conv_scratch(size, 1, wide, FRAMES), ((2, span, LANES), F32)],
        smem=1,
        mib=12,
        flops=work // 2,
    )
    got = lax.all_to_all(slots, ("row", "col"), 0, 0)
    (grad_act,) = call(
        part(grad_act_body, size),
        [((FRAMES, tall, broad, LANES), F32)],
        [grad, grad_after, second],
        conv_scratch(size, 2, up(wide + 2, 16)),
        mib=16,
        flops=2 * work,
    )
    field = ((FRAMES, tall, broad, LANES), F32)
    norm_second, slots = call(
        part(sums_second_body, size, across),
        [stat, ((peers, STATS, LANES), F32)],
        [hidden, got, grad_act],
    )
    act_second, q, z = call(
        part(act_second_body, size, across),
        [block, field, field],
        [place, hidden, got, grad_act, norm_second],
        [frame, field, field],
        smem=1,
        sems=2 * FRAMES,
        beside=True,
        out_far=2,
    )
    got = lax.all_to_all(slots, ("row", "col"), 0, 0)
    turned = ((FRAMES * LANES, size.cells), BF16)
    second_term, second_short = call(
        part(second_term_body, size),
        [(first.shape, F32), (first.shape, BF16)],
        [grad, grad_after, act_second],
        [*conv_scratch(size, 1, wide), turned, (first.shape, F32), (first.shape, BF16)],
        sems=18,
        mib=16,
        beside=True,
        out_far=2,
    )
    first_term, give, grad_second = call(
        part(first_term_body, size, across),
        [(first.shape, F32), (first.shape, BF16), block],
        [place, got, norm_second, q, z, act_before, act_first, second_short],
        [*conv_scratch(size, 1, wide), turned, *[block] * 3, (first.shape, BF16), field, field],
        smem=1,
        far=5,
        sems=2 * FRAMES + 4,
        mib=20,
        flops=work,
        out_far=1,
    )
    give, late_grad, late_act = lax.optimization_barrier((give, grad_second, act_second))
    act_second_before = later(late_act, 1)
    grad_second_after = later(late_grad, -1)

    along = lax.axis_size("tm")
    rows = first.shape[0]
    by_col = rows // across
    (slots,) = call(
        joined_body,
        [((across, by_col, LANES), BF16)],
        [place, first_term, second_term, row_swap(give)],
        smem=1,
    )
    slots = lax.all_to_all(slots, "col", 0, 0)
    slots, grad_second_after = lax.optimization_barrier((slots, grad_second_after))
    share = up(by_col, 16 * along) // along
    (slots,) = call(
        shared_body,
        [((along, share, LANES), BF16)],
        [slots],
        [((along * share, LANES), F32)],
    )
    got = lax.all_to_all(slots, "tm", 0, 0)
    (result,) = call(
        part(result_body, size),
        [(features.shape, BF16)],
        [act_second_before, act_second, second, features],
        conv_scratch(size, 1, wide),
        mib=14,
        flops=work,
    )
    q, sums = call(
        part(back_first_body, size),
        [((FRAMES, size.cells, LANES), F32), stat],
        [grad_second, grad_second_after, first, features, norm_first],
        conv_scratch(size, 1, wide),
        mib=14,
        flops=work,
    )
    got, result = lax.optimization_barrier((got, result))
    (slots,) = call(part(finished_body, factor), [((along, share, LANES), BF16)], [got])
    done = lax.all_to_all(slots, "tm", 0, 0).reshape(-1, LANES)[:by_col]
    parts = sum_parts(sums + row_swap(sums))
    parts = jnp.pad(parts, ((0, -parts.shape[0] % 16), (0, 0)))
    done = jnp.concatenate([done, parts], 0)
    mine = lax.all_to_all(jnp.broadcast_to(done[None], (across, *done.shape)), "col", 0, 0)
    theirs = row_swap(mine)
    so_far = placed(place, mine, 0, by_col, [])
    first_grad, second_grad = placed(place, theirs, 1, by_col, so_far)
    (feature_grad,) = call(
        part(feature_grad_body, size, peers),
        [(features.shape, BF16)],
        [features, out_grad, norm_first, q, mine[:, by_col:]],
    )
    return (result, feature_grad, first_grad.reshape(taps), second_grad.reshape(taps))


def solution(mesh):
    in_specs = (P("tm", "row", "col", None), P(), P(), P("tm", "row", "col", None))
    out_specs = (P("tm", "row", "col", None), P("tm", "row", "col", None), P(), P())
    return jax.shard_map(
        on_device, mesh=mesh, in_specs=in_specs, out_specs=out_specs, check_vma=False
    )
```

```python
import functools
import math

import jax
import jax.numpy as jnp
from jax import lax
from jax.experimental import pallas as pl
from jax.experimental.pallas import tpu as pltpu
from jax.sharding import PartitionSpec as P

GROUPS = 32
EPSILON = 1e-06
F32 = jnp.float32
BF16 = jnp.bfloat16
LANES = 128
FRAMES = 2
STATS = 8
PARTS = 3 * STATS


def up(count, step):
    return -(-count // step) * step


class Sizes:
    def __init__(self, high, wide):
        self.high, self.wide = high, wide
        self.cells = high * wide

    def stride(self, rim):
        return up(self.high + 2 * rim, 8)

    def main(self, rim):
        return FRAMES * (self.high + 2 * rim) * self.wide

    def rows(self, rim):
        return up(self.main(rim) + 2 * rim * FRAMES * self.stride(rim), 16)

    def tall(self):
        return self.high + 2

    def broad(self):
        return up(self.wide + 2, 8)


def call(body, outs, args, scratch=(), smem=0, far=0, sems=0, mib=8, flops=0, beside=False, out_far=0):
    specs = [pl.BlockSpec(memory_space=pltpu.SMEM)] * smem
    specs += [pl.BlockSpec(memory_space=pltpu.VMEM)] * (len(args) - smem - far)
    specs += [pl.BlockSpec(memory_space=pltpu.HBM)] * far
    near = len(args) - far
    args = [*args[:near], *(pltpu.with_memory_space_constraint(a, pltpu.HBM) for a in args[near:])]
    scratches = [pltpu.VMEM(shape, dtype) for shape, dtype in scratch]
    if sems:
        scratches.append(pltpu.SemaphoreType.DMA((sems,)))
    shapes = [jax.ShapeDtypeStruct(shape, dtype) for shape, dtype in outs]
    kept = len(outs) - out_far
    moved = sum(math.prod(a.shape) * a.dtype.itemsize for a in [*args, *shapes])
    moved = 0 if beside else moved
    return pl.pallas_call(
        body,
        out_shape=shapes[:kept] + [pltpu.HBM(o.shape, o.dtype) for o in shapes[kept:]],
        in_specs=specs,
        out_specs=[pl.BlockSpec(memory_space=pltpu.VMEM)] * kept
        + [pl.BlockSpec(memory_space=pltpu.HBM)] * out_far,
        scratch_shapes=scratches,
        cost_estimate=pl.CostEstimate(flops=flops, bytes_accessed=moved, transcendentals=0),
        compiler_params=pltpu.CompilerParams(vmem_limit_bytes=mib << 20),
    )(*args)


def logistic(values):
    return 0.5 * jnp.tanh(0.5 * values) + 0.5


def lane_totals(stat):
    lane = lax.broadcasted_iota(jnp.int32, stat.shape, 1)
    step = 1
    while step < LANES // GROUPS:
        ahead = pltpu.roll(stat, LANES - step, 1)
        behind = pltpu.roll(stat, step, 1)
        stat = stat + jnp.where((lane // step) % 2 == 0, ahead, behind)
        step *= 2
    return stat


def split3(stat):
    high = stat.astype(BF16).astype(F32)
    rest = stat - high
    middle = rest.astype(BF16).astype(F32)
    return jnp.concatenate([high, middle, rest - middle], 0)


def join3(parts):
    parts = parts.astype(F32)
    return parts[:STATS] + (parts[STATS : 2 * STATS] + parts[2 * STATS : PARTS])


def stat_block(first, second):
    rest = jnp.zeros((STATS - 2 * FRAMES, LANES), F32)
    return jnp.concatenate([*first, *second, rest], 0)


def measured(frames):
    means, squares = [], []
    for frame in frames:
        mean = jnp.sum(frame, 0, keepdims=True) / frame.shape[0]
        centred = frame - mean
        means.append(mean)
        squares.append(jnp.sum(centred * centred, 0, keepdims=True))
    return stat_block(means, squares)


def merged(one, two, cells):
    delta = one - two
    extra = (0.5 * cells) * delta * delta
    mean = 0.5 * (one[:FRAMES] + two[:FRAMES])
    square = one[FRAMES : 2 * FRAMES] + two[FRAMES : 2 * FRAMES] + extra[:FRAMES]
    return jnp.concatenate([mean, square, jnp.zeros((STATS - 2 * FRAMES, LANES), F32)], 0)


def concluded(blocks, cells):
    per_group = LANES // GROUPS
    mean = sum(blocks[1:], blocks[0])[:FRAMES]
    mean = lane_totals(mean) / (len(blocks) * per_group)
    total = jnp.zeros((FRAMES, LANES), F32)
    for block in blocks:
        off = block[:FRAMES] - mean
        total = total + block[FRAMES : 2 * FRAMES] + cells * off * off
    spread = lane_totals(total) / (cells * len(blocks) * per_group)
    rest = jnp.zeros((STATS - 2 * FRAMES, LANES), F32)
    return jnp.concatenate([mean, lax.rsqrt(spread + EPSILON), rest], 0)


def rim_rows(place, got):
    upper = place[0] == 0
    nothing = jnp.zeros_like(got)
    return jnp.where(upper, nothing, got), jnp.where(upper, got, nothing)


def in_frame(shape, place, across, size, rim):
    row = lax.broadcasted_iota(jnp.int32, shape, 0)
    col = lax.broadcasted_iota(jnp.int32, shape, 1)
    top = jnp.where(place[0] == 0, rim, 0)
    bottom = jnp.where(place[0] == 0, size.high + 2 * rim, size.high + rim)
    left = jnp.where(place[1] == 0, rim, 0)
    right = jnp.where(place[1] == across - 1, size.wide + rim, size.wide + 2 * rim)
    return (row >= top) & (row < bottom) & (col >= left) & (col < right)


def take_columns(size, arrays, flat):
    flat[...] = jnp.zeros_like(flat)
    at = 0
    for array, rim in arrays:
        for j in range(rim):
            for frame in range(FRAMES):
                for side, col in ((0, j), (1, size.wide - rim + j)):
                    rows = array[frame, :, col : col + 1].astype(F32)
                    rows = rows.reshape(size.high, LANES)
                    flat[side, at + rim : at + rim + size.high] = rows
                at += size.stride(rim)


def start_body(
    size, place, features_far, grad_far, pay, stats, flat, features, out_grad, sems
):
    high, wide = size.high, size.wide
    upper = place[0] == 0
    copies = [
        pltpu.make_async_copy(source.at[f], target.at[f], sems.at[FRAMES * k + f])
        for k, (source, target) in enumerate(((features_far, features), (grad_far, out_grad)))
        for f in range(FRAMES)
    ]
    for copy in copies:
        copy.start()
    for copy in copies[:FRAMES]:
        copy.wait()
    at = 0
    for frame in range(FRAMES):
        pay[at : at + wide] = jnp.where(upper, features[frame, high - 1], features[frame, 0])
        at += wide
    found = measured([features[f].astype(F32).reshape(size.cells, LANES) for f in range(FRAMES)])
    stats[...] = found
    for copy in copies[FRAMES:]:
        copy.wait()
    for frame in range(FRAMES):
        for row in range(2):
            edge = jnp.where(upper, out_grad[frame, high - 2 + row], out_grad[frame, row])
            pay[at : at + wide] = edge
            at += wide
    fill = jnp.zeros((pay.shape[0] - at - PARTS, LANES), F32)
    pay[at:] = jnp.concatenate([split3(found), fill], 0).astype(BF16)
    take_columns(size, ((features, 1), (out_grad, 2)), flat)


def slots_body(size, rims, across, place, flat, got, stats, slots, work):
    wide, high = size.wide, size.high
    upper = place[0] == 0
    work[...] = flat[...]
    at = base = 0
    for rim in rims:
        for j in range(rim):
            for frame in range(FRAMES):
                for row in range(rim):
                    start = base + (frame * rim + row) * wide
                    for side, col in ((0, j), (1, wide - rim + j)):
                        cell = start - start % 16 + 16 * ((start % 16 + col) // 16)
                        tile = got[cell : cell + 16].astype(F32)
                        edge = tile[start + col - cell : start + col - cell + 1]
                        nothing = jnp.zeros_like(edge)
                        top, bottom = at + row, at + rim + high + row
                        work[side, top : top + 1] = jnp.where(upper, nothing, edge)
                        work[side, bottom : bottom + 1] = jnp.where(upper, edge, nothing)
                at += size.stride(rim)
        base += FRAMES * rim * wide
    parts = split3(merged(stats[...], join3(got[base : base + PARTS]), size.cells))
    work[0, at : at + PARTS] = parts
    work[1, at : at + PARTS] = parts
    for peer in range(across):
        slots[peer] = jnp.where(peer > place[1], work[1], work[0]).astype(BF16)


def sides(place, across, got, first, count):
    left = got[jnp.maximum(place[1] - 1, 0), first : first + count].astype(F32)
    right = got[jnp.minimum(place[1] + 1, across - 1), first : first + count].astype(F32)
    nothing = jnp.zeros_like(left)
    left = jnp.where(place[1] > 0, left, nothing)
    right = jnp.where(place[1] < across - 1, right, nothing)
    return left, right


def padded_frame(size, own, top, bottom, left, right, frame):
    high, wide = size.high, size.wide
    frame[1 : high + 1, 1 : wide + 1] = own
    frame[0:1, 1 : wide + 1] = top[None]
    frame[high + 1 : high + 2, 1 : wide + 1] = bottom[None]
    tall = high + 2
    frame[:, 0:1] = left[:tall].reshape(tall, 1, LANES)
    frame[:, wide + 1 : wide + 2] = right[:tall].reshape(tall, 1, LANES)


def put_frame(size, frame, index, out):
    wide, tall, step = size.wide, size.tall(), size.stride(1)
    flat = frame[:, 1 : wide + 1].reshape(tall * wide, LANES)
    out[index * tall * wide : (index + 1) * tall * wide] = flat.astype(BF16)
    fill = jnp.zeros((step - tall, LANES), F32)
    left = frame[:, 0:1].reshape(tall, LANES)
    right = frame[:, wide + 1 : wide + 2].reshape(tall, LANES)
    return jnp.concatenate([left, fill], 0), jnp.concatenate([right, fill], 0)


def put_sides(out, first, blocks):
    fill = out.shape[0] - first - sum(b.shape[0] for b in blocks)
    if fill:
        blocks = [*blocks, jnp.zeros((fill, LANES), F32)]
    out[first:] = jnp.concatenate(blocks, 0).astype(BF16)


def act_first_body(
    size, across, place, features, out_grad, row_got, col_got, act, grad, norm, frame
):
    high, wide = size.high, size.wide
    at = FRAMES * size.stride(1) + 2 * FRAMES * size.stride(2)
    blocks = [join3(col_got[peer, at : at + PARTS]) for peer in range(across)]
    found = concluded(blocks, 2 * size.cells)
    norm[...] = found
    step = size.stride(1)
    left_all, right_all = sides(place, across, col_got, 0, FRAMES * step)
    ok = in_frame((size.tall(), size.broad(), LANES), place, across, size, 1)
    lefts, rights = [], []
    frame[...] = jnp.zeros_like(frame)
    for f in range(FRAMES):
        top, bottom = rim_rows(place, row_got[f * wide : (f + 1) * wide].astype(F32))
        padded_frame(
            size,
            features[f].astype(F32),
            top,
            bottom,
            left_all[f * step : (f + 1) * step],
            right_all[f * step : (f + 1) * step],
            frame,
        )
        normed = (frame[...] - found[f : f + 1][None]) * found[FRAMES + f : FRAMES + f + 1][None]
        frame[...] = jnp.where(ok, normed * logistic(normed), 0.0)
        left, right = put_frame(size, frame, f, act)
        lefts.append(left)
        rights.append(right)
    put_sides(act, size.main(1), lefts + rights)

    tall = high + 4
    for f in range(FRAMES):
        start = f * tall * wide
        for row in range(2):
            first = FRAMES * wide + (f * 2 + row) * wide
            top, bottom = rim_rows(place, row_got[first : first + wide])
            grad[start + row * wide : start + (row + 1) * wide] = top
            below = start + (high + 2 + row) * wide
            grad[below : below + wide] = bottom
        grad[start + 2 * wide : start + (high + 2) * wide] = out_grad[f].reshape(
            size.cells, LANES
        )
    left, right = sides(
        place, across, col_got, FRAMES * step, 2 * FRAMES * size.stride(2)
    )
    put_sides(grad, size.main(2), [left, right])


def spread_columns(size, rim, trim, wo, block, index, dst, at, frame):
    wide, high = size.wide, size.high
    tall, step = high + 2 * rim, size.stride(rim)
    main = block[index * tall * wide : (index + 1) * tall * wide].astype(F32)
    main = main.reshape(tall, wide, LANES)
    cut = rim - trim
    tall_out = tall - 2 * cut
    frame[:, trim : trim + wide] = main[cut : cut + tall_out]
    first = size.main(rim)
    edges = block[first:].astype(F32)
    for j in range(2 * rim):
        col = j - cut if j < rim else j - rim + trim + wide
        if j < cut or (j >= rim and j - rim >= trim):
            continue
        start = (j * FRAMES + index) * step
        edge = edges[start + cut : start + cut + tall_out]
        frame[:, col : col + 1] = edge.reshape(tall_out, 1, LANES)
    for c in range(3):
        dst[at, :, :, c * LANES : (c + 1) * LANES] = frame[:, c : c + wo].astype(BF16)


def spread_all(size, rim, trim, wo, near, far, dst, frame):
    filled = size.wide + 2 * trim
    if frame.shape[1] > filled:
        frame[:, filled:] = jnp.zeros((frame.shape[0], frame.shape[1] - filled, LANES), F32)
    for f in range(dst.shape[0]):
        block = near if f < FRAMES else far
        spread_columns(size, rim, trim, wo, block, f % FRAMES, dst, f, frame)


def tap_dot(x, kernel, turned):
    ho, wo = x.shape[1] - 2, x.shape[2]
    count = ho * wo
    span = 9 * LANES

    def cells(f):
        return jnp.concatenate(
            [x[f, b : b + ho].reshape(count, 3 * LANES) for b in range(3)], 1
        )

    def taps(a):
        if not turned:
            return kernel[a * span : (a + 1) * span]
        last = (3 - a) * 9 - 1
        return jnp.concatenate(
            [kernel[(last - k) * LANES : (last - k + 1) * LANES] for k in range(9)], 1
        )

    dims = (((1,), (1 if turned else 0,)), ((), ()))

    def dot(f, *times):
        weights = [taps(a) for a in times]
        if len(weights) > 1:
            weights = [jnp.concatenate(weights, 0 if turned else 1)]
        return lax.dot_general(cells(f), weights[0], dims, preferred_element_type=F32)

    return dot


def convolved(x, kernel, turned):
    dot = tap_dot(x, kernel, turned)
    both = dot(1, 1, 0) + dot(2, 2, 1)
    return both[:, :LANES] + dot(0, 0), both[:, LANES:] + dot(3, 2)


def conv_scratch(size, trim, wo, frames=2 * FRAMES):
    tall = size.high + 2 * trim
    return [((frames, tall, wo, 3 * LANES), BF16), ((tall, up(wo + 2, 8), LANES), F32)]


def hidden_own_body(size, own, kernel, sums, x, frame):
    spread_all(size, 1, 1, size.wide, own, None, x, frame)
    dot = tap_dot(x, kernel, False)
    both = dot(0, 2, 1)
    sums[0] = both[:, :LANES]
    sums[1] = both[:, LANES:] + dot(1, 2)


def hidden_body(size, across, place, before, sums, kernel, hidden, slots, x, frame, flat):
    high, wide = size.high, size.wide
    spread_all(size, 1, 1, wide, before, None, x, frame)
    dot = tap_dot(x, kernel, False)
    both = dot(1, 1, 0)
    sums = (sums[0] + both[:, :LANES] + dot(0, 0), sums[1] + both[:, LANES:])
    rounded = [s.astype(BF16) for s in sums]
    for f in range(FRAMES):
        hidden[f] = rounded[f].reshape(high, wide, LANES)
    span = span_second(size)
    found = split3(measured([r.astype(F32) for r in rounded]))
    take_columns(size, ((hidden, 1),), flat)
    upper = place[0] == 0
    edges = [jnp.where(upper, r[size.cells - wide :], r[:wide]).astype(F32) for r in rounded]
    fill = jnp.zeros((span - FRAMES * wide, LANES), F32)
    edges = jnp.concatenate([*edges, fill] if fill.shape[0] else edges, 0)
    rest = jnp.zeros((slots.shape[1] - span - PARTS, LANES), F32)
    for peer in range(slots.shape[0]):
        col = peer % across
        side = jnp.where(col > place[1], flat[1], flat[0])
        content = jnp.where(col == place[1], edges, side)
        slots[peer] = jnp.concatenate([content, found, rest], 0).astype(BF16)


def grad_act_body(size, near, far, kernel_far, out, x, frame, kernel, sems):
    wo = x.shape[2]
    copy = pltpu.make_async_copy(kernel_far, kernel, sems.at[0])
    copy.start()
    spread_all(size, 2, 2, wo, near, far, x, frame)
    copy.wait()
    sums = convolved(x, kernel, True)
    for f in range(FRAMES):
        out[f] = sums[f].reshape(size.tall(), wo, LANES)[:, : size.broad()]


def crossed_sides(size, place, across, got):
    step, high = size.stride(1), size.high
    count = FRAMES * step
    upper = place[0] == 0
    row = lax.broadcasted_iota(jnp.int32, (count, LANES), 0)
    found = []
    for at, there in (
        (jnp.maximum(place[1] - 1, 0), place[1] > 0),
        (jnp.minimum(place[1] + 1, across - 1), place[1] < across - 1),
    ):
        block = got[place[0] * across + at, 0:count].astype(F32)
        cross = got[(1 - place[0]) * across + at, 0:count].astype(F32)
        for f in range(FRAMES):
            above = jnp.where(upper, 0.0, cross[f * step + high : f * step + high + 1])
            below = jnp.where(upper, cross[f * step + 1 : f * step + 2], 0.0)
            block = jnp.where(row == f * step, above, block)
            block = jnp.where(row == f * step + high + 1, below, block)
        found.append(jnp.where(there, block, 0.0))
    return found


def span_second(size):
    return up(max(FRAMES * size.wide, FRAMES * size.stride(1)), 16)


def sums_second_body(size, across, hidden, got, grad_act, norm, slots):
    high, wide = size.high, size.wide
    at = span_second(size)
    blocks = [join3(got[peer, at : at + PARTS]) for peer in range(got.shape[0])]
    found = concluded(blocks, size.cells)
    norm[...] = found
    firsts, seconds = [], []
    for f in range(FRAMES):
        own = hidden[f].astype(F32)
        normed = (own - found[f : f + 1][None]) * found[FRAMES + f : FRAMES + f + 1][None]
        sigmoid = logistic(normed)
        grad = grad_act[f, 1 : high + 1, 1 : wide + 1]
        grad = grad * sigmoid * (1.0 + normed * (1.0 - sigmoid))
        grad, normed = grad.reshape(size.cells, LANES), normed.reshape(size.cells, LANES)
        firsts.append(jnp.sum(grad, 0, keepdims=True))
        seconds.append(jnp.sum(grad * normed, 0, keepdims=True))
    sums = stat_block(firsts, seconds)
    for peer in range(slots.shape[0]):
        slots[peer] = sums


def act_second_body(
    size, across, place, hidden, got, grad_act, norm, act, q_far, z_far, frame, q, z, sems
):
    wide = size.wide
    step = size.stride(1)
    left_all, right_all = crossed_sides(size, place, across, got)
    ok = in_frame((size.tall(), size.broad(), LANES), place, across, size, 1)
    lefts, rights, copies = [], [], []
    frame[...] = jnp.zeros_like(frame)
    facing = (1 - place[0]) * across + place[1]
    for f in range(FRAMES):
        top, bottom = rim_rows(place, got[facing, f * wide : (f + 1) * wide].astype(F32))
        padded_frame(
            size,
            hidden[f].astype(F32),
            top,
            bottom,
            left_all[f * step : (f + 1) * step],
            right_all[f * step : (f + 1) * step],
            frame,
        )
        normed = (frame[...] - norm[f : f + 1][None]) * norm[FRAMES + f : FRAMES + f + 1][None]
        sigmoid = logistic(normed)
        frame[...] = jnp.where(ok, normed * sigmoid, 0.0)
        left, right = put_frame(size, frame, f, act)
        lefts.append(left)
        rights.append(right)
        z[f] = normed
        q[f] = grad_act[f] * sigmoid * (1.0 + normed * (1.0 - sigmoid))
        for k, (source, target) in enumerate(((q, q_far), (z, z_far))):
            copy = pltpu.make_async_copy(source.at[f], target.at[f], sems.at[2 * f + k])
            copy.start()
            copies.append(copy)
    put_sides(act, size.main(1), lefts + rights)
    for copy in copies:
        copy.wait()


def hidden_grad(size, across, place, q, z, got, norm, out, frame, arrive):
    peers = got.shape[0]
    total = got[0]
    for peer in range(1, peers):
        total = total + got[peer]
    means = lane_totals(total) / (size.cells * peers * (LANES // GROUPS))
    ok = in_frame((size.tall(), size.broad(), LANES), place, across, size, 1)
    lefts, rights = [], []
    for f in range(FRAMES):
        first, second = means[f : f + 1][None], means[FRAMES + f : FRAMES + f + 1][None]
        inv = norm[FRAMES + f : FRAMES + f + 1][None]
        arrive(f)
        frame[...] = jnp.where(ok, inv * (q[f] - first - z[f] * second), 0.0)
        left, right = put_frame(size, frame, f, out)
        lefts.append(left)
        rights.append(right)
    put_sides(out, size.main(1), lefts + rights)


def own_cells(size, block, f):
    start = (f * size.tall() + 1) * size.wide
    return block[start : start + size.cells]


def turned_cells(size, block, out):
    for f in range(FRAMES):
        cells = own_cells(size, block, f).astype(F32).T.astype(BF16)
        out[f * LANES : (f + 1) * LANES] = cells


def tap_sums(x, turned, b):
    ho, wo = x.shape[1] - 2, x.shape[2]

    def cells(f):
        return x[f, b : b + ho].reshape(ho * wo, 3 * LANES)

    def dot(one, two):
        return jnp.dot(one, two, preferred_element_type=F32)

    low = dot(turned[...], cells(1))
    high = dot(turned[...], cells(2))
    return (
        dot(turned[:LANES], cells(0)) + low[LANES:],
        low[:LANES] + high[LANES:],
        high[:LANES] + dot(turned[LANES:], cells(3)),
    )


def second_term_body(size, near, far, act, out_far, short_far, x, frame, turned, out, short, sems):
    spread_all(size, 2, 1, size.wide, near, far, x, frame)
    turned_cells(size, act, turned)
    span = 3 * LANES
    copies = []
    for b in range(3):
        for a, total in enumerate(tap_sums(x, turned, b)):
            for c in range(3):
                tap = ((2 - a) * 3 + 2 - b) * 3 + 2 - c
                rows = slice(tap * LANES, (tap + 1) * LANES)
                piece = total[:, c * LANES : (c + 1) * LANES]
                out[rows] = piece
                short[rows] = piece.astype(BF16)
            rows = pl.ds(((2 - a) * 3 + 2 - b) * span, span)
            for k, (source, target) in enumerate(((out, out_far), (short, short_far))):
                sem = sems.at[2 * (3 * b + a) + k]
                copy = pltpu.make_async_copy(source.at[rows], target.at[rows], sem)
                copy.start()
                copies.append(copy)
    for copy in copies:
        copy.wait()


def first_term_body(
    size,
    across,
    place,
    got,
    norm,
    q_far,
    z_far,
    near_far,
    own_far,
    short_far,
    out,
    give,
    grad_far,
    x,
    frame,
    turned,
    grad,
    near,
    own,
    q,
    z,
    sems,
):
    pairs = [(q_far.at[f], q.at[f]) for f in range(FRAMES)]
    pairs += [(z_far.at[f], z.at[f]) for f in range(FRAMES)]
    pairs += [(near_far, near), (own_far, own)]
    copies = [
        pltpu.make_async_copy(source, target, sems.at[k])
        for k, (source, target) in enumerate(pairs)
    ]
    for k in (0, FRAMES, 1, FRAMES + 1, 2 * FRAMES, 2 * FRAMES + 1):
        copies[k].start()
    upper = place[0] == 0
    given = pltpu.make_async_copy(short_far, give, sems.at[len(pairs) + 1])

    @pl.when(upper)
    def _():
        given.start()

    def arrive(f):
        copies[f].wait()
        copies[FRAMES + f].wait()

    hidden_grad(size, across, place, q, z, got, norm, grad, frame, arrive)
    sent = pltpu.make_async_copy(grad, grad_far, sems.at[len(pairs)])
    sent.start()
    turned_cells(size, grad, turned)
    for copy in copies[2 * FRAMES :]:
        copy.wait()
    spread_all(size, 1, 1, size.wide, near, own, x, frame)
    for b in range(3):
        for a, total in enumerate(tap_sums(x, turned, b)):
            rows = slice((a * 3 + b) * 3 * LANES, (a * 3 + b + 1) * 3 * LANES)
            out[rows] = total.T

    @pl.when(jnp.logical_not(upper))
    def _():
        give[...] = out[...].astype(BF16)

    @pl.when(upper)
    def _():
        given.wait()

    sent.wait()


def result_body(size, near, far, kernel, features, out, x, frame):
    spread_all(size, 1, 1, size.wide, near, far, x, frame)
    sums = convolved(x, kernel, False)
    for f in range(FRAMES):
        total = features[f].astype(F32) + sums[f].reshape(size.high, size.wide, LANES)
        out[f] = total.astype(BF16)


def back_first_body(size, near, far, kernel, features, norm, q, sums, x, frame):
    spread_all(size, 1, 1, size.wide, near, far, x, frame)
    grads = convolved(x, kernel, True)
    firsts, seconds = [], []
    for f in range(FRAMES):
        values = features[f].astype(F32).reshape(size.cells, LANES)
        normed = (values - norm[f : f + 1]) * norm[FRAMES + f : FRAMES + f + 1]
        sigmoid = logistic(normed)
        grad = grads[f] * sigmoid * (1.0 + normed * (1.0 - sigmoid))
        q[f] = grad
        firsts.append(jnp.sum(grad, 0, keepdims=True))
        seconds.append(jnp.sum(grad * normed, 0, keepdims=True))
    sums[...] = stat_block(firsts, seconds)


def feature_grad_body(size, peers, features, out_grad, norm, q, got, out):
    total = join3(got[0])
    for peer in range(1, got.shape[0]):
        total = total + join3(got[peer])
    means = lane_totals(total) / (size.cells * peers * (LANES // GROUPS))
    for f in range(FRAMES):
        values = features[f].astype(F32).reshape(size.cells, LANES)
        inv = norm[FRAMES + f : FRAMES + f + 1]
        normed = (values - norm[f : f + 1]) * inv
        grad = inv * (q[f] - means[f : f + 1] - normed * means[FRAMES + f : FRAMES + f + 1])
        grad = out_grad[f].astype(F32) + grad.reshape(size.high, size.wide, LANES)
        out[f] = grad.astype(BF16)


def row_swap(values):
    return lax.ppermute(values, "row", [(0, 1), (1, 0)])


def later(values, by):
    peers = lax.axis_size("tm")
    pairs = [(i, i + by) for i in range(peers) if 0 <= i + by < peers]
    return lax.ppermute(values, "tm", pairs)


def sum_parts(stat):
    high = lax.reduce_precision(stat, 8, 7)
    rest = stat - high
    middle = lax.reduce_precision(rest, 8, 7)
    return jnp.concatenate([high, middle, rest - middle], 0).astype(BF16)


def total_of(got):
    total = got[0].astype(F32)
    for peer in range(1, got.shape[0]):
        total = total + got[peer].astype(F32)
    return total


def joined_body(place, first, second, got, out):
    share = out.shape[1]

    def add(keep):
        for peer in range(out.shape[0]):
            rows = slice(peer * share, (peer + 1) * share)
            out[peer] = (keep[rows] + got[rows].astype(F32)).astype(BF16)

    @pl.when(place[0] == 0)
    def _():
        add(first)

    @pl.when(place[0] != 0)
    def _():
        add(second)


def shared_body(got, out, flat):
    rows, share = got.shape[1], out.shape[1]
    if flat.shape[0] > rows:
        flat[rows:] = jnp.zeros((flat.shape[0] - rows, LANES), F32)
    flat[:rows] = total_of(got)
    for peer in range(out.shape[0]):
        out[peer] = flat[peer * share : (peer + 1) * share].astype(BF16)


def finished_body(factor, got, out):
    total = (total_of(got) * factor).astype(BF16)
    for peer in range(out.shape[0]):
        out[peer] = total


def placed_body(rows, swapped, *refs):
    place, block, first, second, sems = refs[0], refs[1], *refs[-3:]

    def move(target):
        copies = [
            pltpu.make_async_copy(
                block.at[peer, pl.ds(0, rows)], target.at[pl.ds(peer * rows, rows)], sems.at[peer]
            )
            for peer in range(block.shape[0])
        ]
        for copy in copies:
            copy.start()
        for copy in copies:
            copy.wait()

    @pl.when(place[0] == swapped)
    def _():
        move(first)

    @pl.when(place[0] != swapped)
    def _():
        move(second)


def placed(place, block, swapped, rows, so_far):
    anywhere = pl.BlockSpec(memory_space=pl.ANY)
    shape = (rows * block.shape[0], LANES)
    return pl.pallas_call(
        functools.partial(placed_body, rows, swapped),
        out_shape=[jax.ShapeDtypeStruct(shape, BF16)] * 2,
        in_specs=[pl.BlockSpec(memory_space=pltpu.SMEM)] + [anywhere] * (1 + len(so_far)),
        out_specs=[anywhere, anywhere],
        input_output_aliases={2 + k: k for k in range(len(so_far))},
        scratch_shapes=[pltpu.SemaphoreType.DMA((block.shape[0],))],
        compiler_params=pltpu.CompilerParams(vmem_limit_bytes=1 << 20),
    )(place, block, *so_far)


def on_device(features, conv_first, conv_second, out_grad):
    frames, high, wide, chans = features.shape
    assert frames == FRAMES and chans == LANES and lax.axis_size("row") == 2
    size = Sizes(high, wide)
    across = lax.axis_size("col")
    peers = 2 * across
    factor = 1.0 / math.sqrt(size.cells * FRAMES * lax.axis_size("tm") * peers)
    place = jnp.stack([lax.axis_index("row"), lax.axis_index("col")]).astype(jnp.int32)
    taps = conv_first.shape
    first = conv_first.reshape(-1, LANES)
    second = conv_second.reshape(-1, LANES)
    work = 2 * first.size * size.cells * FRAMES
    part = functools.partial
    stat = ((STATS, LANES), F32)
    tall, broad = size.tall(), size.broad()
    frame = ((tall, broad, LANES), F32)

    edge = up(3 * FRAMES * wide + PARTS, 16)
    lines = up(FRAMES * size.stride(1) + 2 * FRAMES * size.stride(2) + PARTS, 16)
    flat = ((2, lines, LANES), F32)
    pay, stats, cols, features_near, grad_near = call(
        part(start_body, size),
        [((edge, LANES), BF16), stat, flat, (features.shape, BF16), (features.shape, BF16)],
        [place, features, out_grad],
        smem=1,
        far=2,
        sems=2 * FRAMES,
    )
    row_got = row_swap(pay)
    (slots,) = call(
        part(slots_body, size, (1, 2), across),
        [((across, lines, LANES), BF16)],
        [place, cols, row_got, stats],
        [flat],
        smem=1,
    )
    col_got = lax.all_to_all(slots, "col", 0, 0)
    block = ((size.rows(1), LANES), BF16)
    act_first, grad, norm_first = call(
        part(act_first_body, size, across),
        [block, ((size.rows(2), LANES), BF16), stat],
        [place, features_near, grad_near, row_got, col_got],
        [frame],
        smem=1,
    )
    grad_after = later(grad, -1)
    act_before = later(act_first, 1)

    edge = up(FRAMES * wide + PARTS, 16)
    (sums,) = call(
        part(hidden_own_body, size),
        [((FRAMES, size.cells, LANES), F32)],
        [act_first, first],
        conv_scratch(size, 1, wide, FRAMES),
        mib=12,
        flops=work // 2,
    )
    span = span_second(size)
    hidden, slots = call(
        part(hidden_body, size, across),
        [(features.shape, BF16), ((peers, up(span + PARTS, 16), LANES), BF16)],
        [place, act_before, sums, first],
        [*conv_scratch(size, 1, wide, FRAMES), ((2, span, LANES), F32)],
        smem=1,
        mib=12,
        flops=work // 2,
    )
    got = lax.all_to_all(slots, ("row", "col"), 0, 0)
    (grad_act,) = call(
        part(grad_act_body, size),
        [((FRAMES, tall, broad, LANES), F32)],
        [grad, grad_after, second],
        [*conv_scratch(size, 2, up(wide + 2, 16)), (second.shape, BF16)],
        far=1,
        sems=1,
        mib=18,
        flops=2 * work,
    )
    field = ((FRAMES, tall, broad, LANES), F32)
    norm_second, slots = call(
        part(sums_second_body, size, across),
        [stat, ((peers, STATS, LANES), F32)],
        [hidden, got, grad_act],
    )
    act_second, q, z = call(
        part(act_second_body, size, across),
        [block, field, field],
        [place, hidden, got, grad_act, norm_second],
        [frame, field, field],
        smem=1,
        sems=2 * FRAMES,
        beside=True,
        out_far=2,
    )
    got = lax.all_to_all(slots, ("row", "col"), 0, 0)
    turned = ((FRAMES * LANES, size.cells), BF16)
    second_term, second_short = call(
        part(second_term_body, size),
        [(first.shape, F32), (first.shape, BF16)],
        [grad, grad_after, act_second],
        [*conv_scratch(size, 1, wide), turned, (first.shape, F32), (first.shape, BF16)],
        sems=18,
        mib=16,
        beside=True,
        out_far=2,
    )
    first_term, give, grad_second = call(
        part(first_term_body, size, across),
        [(first.shape, F32), (first.shape, BF16), block],
        [place, got, norm_second, q, z, act_before, act_first, second_short],
        [*conv_scratch(size, 1, wide), turned, *[block] * 3, field, field],
        smem=1,
        far=5,
        sems=2 * FRAMES + 4,
        mib=20,
        flops=work,
        out_far=1,
    )
    give, late_grad, late_act = lax.optimization_barrier((give, grad_second, act_second))
    act_second_before = later(late_act, 1)
    grad_second_after = later(late_grad, -1)

    along = lax.axis_size("tm")
    rows = first.shape[0]
    by_col = rows // across
    (slots,) = call(
        joined_body,
        [((across, by_col, LANES), BF16)],
        [place, first_term, second_term, row_swap(give)],
        smem=1,
    )
    slots = lax.all_to_all(slots, "col", 0, 0)
    slots, grad_second_after = lax.optimization_barrier((slots, grad_second_after))
    share = up(by_col, 16 * along) // along
    (slots,) = call(
        shared_body,
        [((along, share, LANES), BF16)],
        [slots],
        [((along * share, LANES), F32)],
    )
    got = lax.all_to_all(slots, "tm", 0, 0)
    (result,) = call(
        part(result_body, size),
        [(features.shape, BF16)],
        [act_second_before, act_second, second, features],
        conv_scratch(size, 1, wide),
        mib=14,
        flops=work,
    )
    q, sums = call(
        part(back_first_body, size),
        [((FRAMES, size.cells, LANES), F32), stat],
        [grad_second, grad_second_after, first, features, norm_first],
        conv_scratch(size, 1, wide),
        mib=14,
        flops=work,
    )
    got, result = lax.optimization_barrier((got, result))
    (slots,) = call(part(finished_body, factor), [((along, share, LANES), BF16)], [got])
    done = lax.all_to_all(slots, "tm", 0, 0).reshape(-1, LANES)[:by_col]
    parts = sum_parts(sums + row_swap(sums))
    parts = jnp.pad(parts, ((0, -parts.shape[0] % 16), (0, 0)))
    done = jnp.concatenate([done, parts], 0)
    mine = lax.all_to_all(jnp.broadcast_to(done[None], (across, *done.shape)), "col", 0, 0)
    theirs = row_swap(mine)
    so_far = placed(place, mine, 0, by_col, [])
    first_grad, second_grad = placed(place, theirs, 1, by_col, so_far)
    (feature_grad,) = call(
        part(feature_grad_body, size, peers),
        [(features.shape, BF16)],
        [features, out_grad, norm_first, q, mine[:, by_col:]],
    )
    return (result, feature_grad, first_grad.reshape(taps), second_grad.reshape(taps))


def solution(mesh):
    in_specs = (P("tm", "row", "col", None), P(), P(), P("tm", "row", "col", None))
    out_specs = (P("tm", "row", "col", None), P("tm", "row", "col", None), P(), P())
    return jax.shard_map(
        on_device, mesh=mesh, in_specs=in_specs, out_specs=out_specs, check_vma=False
    )
```

```python
import functools
import math

import jax
import jax.numpy as jnp
from jax import lax
from jax.experimental import pallas as pl
from jax.experimental.pallas import tpu as pltpu
from jax.sharding import PartitionSpec as P

GROUPS = 32
EPSILON = 1e-06
F32 = jnp.float32
BF16 = jnp.bfloat16
LANES = 128
FRAMES = 2
STATS = 8
PARTS = 3 * STATS


def up(count, step):
    return -(-count // step) * step


class Sizes:
    def __init__(self, high, wide):
        self.high, self.wide = high, wide
        self.cells = high * wide

    def stride(self, rim):
        return up(self.high + 2 * rim, 8)

    def main(self, rim):
        return FRAMES * (self.high + 2 * rim) * self.wide

    def rows(self, rim):
        return up(self.main(rim) + 2 * rim * FRAMES * self.stride(rim), 16)

    def tall(self):
        return self.high + 2

    def broad(self):
        return up(self.wide + 2, 8)


def call(body, outs, args, scratch=(), smem=0, far=0, sems=0, mib=8, flops=0, beside=False, out_far=0):
    specs = [pl.BlockSpec(memory_space=pltpu.SMEM)] * smem
    specs += [pl.BlockSpec(memory_space=pltpu.VMEM)] * (len(args) - smem - far)
    specs += [pl.BlockSpec(memory_space=pltpu.HBM)] * far
    near = len(args) - far
    args = [*args[:near], *(pltpu.with_memory_space_constraint(a, pltpu.HBM) for a in args[near:])]
    scratches = [pltpu.VMEM(shape, dtype) for shape, dtype in scratch]
    if sems:
        scratches.append(pltpu.SemaphoreType.DMA((sems,)))
    shapes = [jax.ShapeDtypeStruct(shape, dtype) for shape, dtype in outs]
    kept = len(outs) - out_far
    moved = sum(math.prod(a.shape) * a.dtype.itemsize for a in [*args, *shapes])
    moved = 0 if beside else moved
    return pl.pallas_call(
        body,
        out_shape=shapes[:kept] + [pltpu.HBM(o.shape, o.dtype) for o in shapes[kept:]],
        in_specs=specs,
        out_specs=[pl.BlockSpec(memory_space=pltpu.VMEM)] * kept
        + [pl.BlockSpec(memory_space=pltpu.HBM)] * out_far,
        scratch_shapes=scratches,
        cost_estimate=pl.CostEstimate(flops=flops, bytes_accessed=moved, transcendentals=0),
        compiler_params=pltpu.CompilerParams(vmem_limit_bytes=mib << 20),
    )(*args)


def logistic(values):
    return 0.5 * jnp.tanh(0.5 * values) + 0.5


def lane_totals(stat):
    lane = lax.broadcasted_iota(jnp.int32, stat.shape, 1)
    step = 1
    while step < LANES // GROUPS:
        ahead = pltpu.roll(stat, LANES - step, 1)
        behind = pltpu.roll(stat, step, 1)
        stat = stat + jnp.where((lane // step) % 2 == 0, ahead, behind)
        step *= 2
    return stat


def split3(stat):
    high = stat.astype(BF16).astype(F32)
    rest = stat - high
    middle = rest.astype(BF16).astype(F32)
    return jnp.concatenate([high, middle, rest - middle], 0)


def join3(parts):
    parts = parts.astype(F32)
    return parts[:STATS] + (parts[STATS : 2 * STATS] + parts[2 * STATS : PARTS])


def stat_block(first, second):
    rest = jnp.zeros((STATS - 2 * FRAMES, LANES), F32)
    return jnp.concatenate([*first, *second, rest], 0)


def measured(frames):
    means, squares = [], []
    for frame in frames:
        mean = jnp.sum(frame, 0, keepdims=True) / frame.shape[0]
        centred = frame - mean
        means.append(mean)
        squares.append(jnp.sum(centred * centred, 0, keepdims=True))
    return stat_block(means, squares)


def merged(one, two, cells):
    delta = one - two
    extra = (0.5 * cells) * delta * delta
    mean = 0.5 * (one[:FRAMES] + two[:FRAMES])
    square = one[FRAMES : 2 * FRAMES] + two[FRAMES : 2 * FRAMES] + extra[:FRAMES]
    return jnp.concatenate([mean, square, jnp.zeros((STATS - 2 * FRAMES, LANES), F32)], 0)


def concluded(blocks, cells):
    per_group = LANES // GROUPS
    mean = sum(blocks[1:], blocks[0])[:FRAMES]
    mean = lane_totals(mean) / (len(blocks) * per_group)
    total = jnp.zeros((FRAMES, LANES), F32)
    for block in blocks:
        off = block[:FRAMES] - mean
        total = total + block[FRAMES : 2 * FRAMES] + cells * off * off
    spread = lane_totals(total) / (cells * len(blocks) * per_group)
    rest = jnp.zeros((STATS - 2 * FRAMES, LANES), F32)
    return jnp.concatenate([mean, lax.rsqrt(spread + EPSILON), rest], 0)


def rim_rows(place, got):
    upper = place[0] == 0
    nothing = jnp.zeros_like(got)
    return jnp.where(upper, nothing, got), jnp.where(upper, got, nothing)


def in_frame(shape, place, across, size, rim):
    row = lax.broadcasted_iota(jnp.int32, shape, 0)
    col = lax.broadcasted_iota(jnp.int32, shape, 1)
    top = jnp.where(place[0] == 0, rim, 0)
    bottom = jnp.where(place[0] == 0, size.high + 2 * rim, size.high + rim)
    left = jnp.where(place[1] == 0, rim, 0)
    right = jnp.where(place[1] == across - 1, size.wide + rim, size.wide + 2 * rim)
    return (row >= top) & (row < bottom) & (col >= left) & (col < right)


def take_columns(size, arrays, flat):
    flat[...] = jnp.zeros_like(flat)
    at = 0
    for array, rim in arrays:
        for j in range(rim):
            for frame in range(FRAMES):
                for side, col in ((0, j), (1, size.wide - rim + j)):
                    rows = array[frame, :, col : col + 1].astype(F32)
                    rows = rows.reshape(size.high, LANES)
                    flat[side, at + rim : at + rim + size.high] = rows
                at += size.stride(rim)


def start_body(
    size, place, features_far, grad_far, pay, stats, flat, features, out_grad, sems
):
    high, wide = size.high, size.wide
    upper = place[0] == 0
    copies = [
        pltpu.make_async_copy(source.at[f], target.at[f], sems.at[FRAMES * k + f])
        for k, (source, target) in enumerate(((features_far, features), (grad_far, out_grad)))
        for f in range(FRAMES)
    ]
    for copy in copies:
        copy.start()
    for copy in copies[:FRAMES]:
        copy.wait()
    at = 0
    for frame in range(FRAMES):
        pay[at : at + wide] = jnp.where(upper, features[frame, high - 1], features[frame, 0])
        at += wide
    found = measured([features[f].astype(F32).reshape(size.cells, LANES) for f in range(FRAMES)])
    stats[...] = found
    for copy in copies[FRAMES:]:
        copy.wait()
    for frame in range(FRAMES):
        for row in range(2):
            edge = jnp.where(upper, out_grad[frame, high - 2 + row], out_grad[frame, row])
            pay[at : at + wide] = edge
            at += wide
    fill = jnp.zeros((pay.shape[0] - at - PARTS, LANES), F32)
    pay[at:] = jnp.concatenate([split3(found), fill], 0).astype(BF16)
    take_columns(size, ((features, 1), (out_grad, 2)), flat)


def slots_body(size, rims, across, place, flat, got, stats, slots, work):
    wide, high = size.wide, size.high
    upper = place[0] == 0
    work[...] = flat[...]
    at = base = 0
    for rim in rims:
        for j in range(rim):
            for frame in range(FRAMES):
                for row in range(rim):
                    start = base + (frame * rim + row) * wide
                    for side, col in ((0, j), (1, wide - rim + j)):
                        cell = start - start % 16 + 16 * ((start % 16 + col) // 16)
                        tile = got[cell : cell + 16].astype(F32)
                        edge = tile[start + col - cell : start + col - cell + 1]
                        nothing = jnp.zeros_like(edge)
                        top, bottom = at + row, at + rim + high + row
                        work[side, top : top + 1] = jnp.where(upper, nothing, edge)
                        work[side, bottom : bottom + 1] = jnp.where(upper, edge, nothing)
                at += size.stride(rim)
        base += FRAMES * rim * wide
    parts = split3(merged(stats[...], join3(got[base : base + PARTS]), size.cells))
    work[0, at : at + PARTS] = parts
    work[1, at : at + PARTS] = parts
    for peer in range(across):
        slots[peer] = jnp.where(peer > place[1], work[1], work[0]).astype(BF16)


def sides(place, across, got, first, count):
    left = got[jnp.maximum(place[1] - 1, 0), first : first + count].astype(F32)
    right = got[jnp.minimum(place[1] + 1, across - 1), first : first + count].astype(F32)
    nothing = jnp.zeros_like(left)
    left = jnp.where(place[1] > 0, left, nothing)
    right = jnp.where(place[1] < across - 1, right, nothing)
    return left, right


def padded_frame(size, own, top, bottom, left, right, frame):
    high, wide = size.high, size.wide
    frame[1 : high + 1, 1 : wide + 1] = own
    frame[0:1, 1 : wide + 1] = top[None]
    frame[high + 1 : high + 2, 1 : wide + 1] = bottom[None]
    tall = high + 2
    frame[:, 0:1] = left[:tall].reshape(tall, 1, LANES)
    frame[:, wide + 1 : wide + 2] = right[:tall].reshape(tall, 1, LANES)


def put_frame(size, frame, index, out):
    wide, tall, step = size.wide, size.tall(), size.stride(1)
    flat = frame[:, 1 : wide + 1].reshape(tall * wide, LANES)
    out[index * tall * wide : (index + 1) * tall * wide] = flat.astype(BF16)
    fill = jnp.zeros((step - tall, LANES), F32)
    left = frame[:, 0:1].reshape(tall, LANES)
    right = frame[:, wide + 1 : wide + 2].reshape(tall, LANES)
    return jnp.concatenate([left, fill], 0), jnp.concatenate([right, fill], 0)


def put_sides(out, first, blocks):
    fill = out.shape[0] - first - sum(b.shape[0] for b in blocks)
    if fill:
        blocks = [*blocks, jnp.zeros((fill, LANES), F32)]
    out[first:] = jnp.concatenate(blocks, 0).astype(BF16)


def act_first_body(
    size, across, place, features, out_grad, row_got, col_got, act, grad, norm, frame
):
    high, wide = size.high, size.wide
    at = FRAMES * size.stride(1) + 2 * FRAMES * size.stride(2)
    blocks = [join3(col_got[peer, at : at + PARTS]) for peer in range(across)]
    found = concluded(blocks, 2 * size.cells)
    norm[...] = found
    step = size.stride(1)
    left_all, right_all = sides(place, across, col_got, 0, FRAMES * step)
    ok = in_frame((size.tall(), size.broad(), LANES), place, across, size, 1)
    lefts, rights = [], []
    frame[...] = jnp.zeros_like(frame)
    for f in range(FRAMES):
        top, bottom = rim_rows(place, row_got[f * wide : (f + 1) * wide].astype(F32))
        padded_frame(
            size,
            features[f].astype(F32),
            top,
            bottom,
            left_all[f * step : (f + 1) * step],
            right_all[f * step : (f + 1) * step],
            frame,
        )
        normed = (frame[...] - found[f : f + 1][None]) * found[FRAMES + f : FRAMES + f + 1][None]
        frame[...] = jnp.where(ok, normed * logistic(normed), 0.0)
        left, right = put_frame(size, frame, f, act)
        lefts.append(left)
        rights.append(right)
    put_sides(act, size.main(1), lefts + rights)

    tall = high + 4
    for f in range(FRAMES):
        start = f * tall * wide
        for row in range(2):
            first = FRAMES * wide + (f * 2 + row) * wide
            top, bottom = rim_rows(place, row_got[first : first + wide])
            grad[start + row * wide : start + (row + 1) * wide] = top
            below = start + (high + 2 + row) * wide
            grad[below : below + wide] = bottom
        grad[start + 2 * wide : start + (high + 2) * wide] = out_grad[f].reshape(
            size.cells, LANES
        )
    left, right = sides(
        place, across, col_got, FRAMES * step, 2 * FRAMES * size.stride(2)
    )
    put_sides(grad, size.main(2), [left, right])


def spread_columns(size, rim, trim, wo, block, index, dst, at, frame):
    wide, high = size.wide, size.high
    tall, step = high + 2 * rim, size.stride(rim)
    main = block[index * tall * wide : (index + 1) * tall * wide].astype(F32)
    main = main.reshape(tall, wide, LANES)
    cut = rim - trim
    tall_out = tall - 2 * cut
    frame[:, trim : trim + wide] = main[cut : cut + tall_out]
    first = size.main(rim)
    edges = block[first:].astype(F32)
    for j in range(2 * rim):
        col = j - cut if j < rim else j - rim + trim + wide
        if j < cut or (j >= rim and j - rim >= trim):
            continue
        start = (j * FRAMES + index) * step
        edge = edges[start + cut : start + cut + tall_out]
        frame[:, col : col + 1] = edge.reshape(tall_out, 1, LANES)
    for c in range(3):
        dst[at, :, :, c * LANES : (c + 1) * LANES] = frame[:, c : c + wo].astype(BF16)


def spread_all(size, rim, trim, wo, near, far, dst, frame):
    filled = size.wide + 2 * trim
    if frame.shape[1] > filled:
        frame[:, filled:] = jnp.zeros((frame.shape[0], frame.shape[1] - filled, LANES), F32)
    for f in range(dst.shape[0]):
        block = near if f < FRAMES else far
        spread_columns(size, rim, trim, wo, block, f % FRAMES, dst, f, frame)


def tap_dot(x, kernel, turned):
    ho, wo = x.shape[1] - 2, x.shape[2]
    count = ho * wo
    span = 9 * LANES

    def cells(f):
        return jnp.concatenate(
            [x[f, b : b + ho].reshape(count, 3 * LANES) for b in range(3)], 1
        )

    def taps(a):
        if not turned:
            return kernel[a * span : (a + 1) * span]
        last = (3 - a) * 9 - 1
        return jnp.concatenate(
            [kernel[(last - k) * LANES : (last - k + 1) * LANES] for k in range(9)], 1
        )

    dims = (((1,), (1 if turned else 0,)), ((), ()))

    def dot(f, *times):
        weights = [taps(a) for a in times]
        if len(weights) > 1:
            weights = [jnp.concatenate(weights, 0 if turned else 1)]
        return lax.dot_general(cells(f), weights[0], dims, preferred_element_type=F32)

    return dot


def convolved(x, kernel, turned):
    dot = tap_dot(x, kernel, turned)
    both = dot(1, 1, 0) + dot(2, 2, 1)
    return both[:, :LANES] + dot(0, 0), both[:, LANES:] + dot(3, 2)


def conv_scratch(size, trim, wo, frames=2 * FRAMES):
    tall = size.high + 2 * trim
    return [((frames, tall, wo, 3 * LANES), BF16), ((tall, up(wo + 2, 8), LANES), F32)]


def hidden_own_body(size, own, kernel, sums, x, frame):
    spread_all(size, 1, 1, size.wide, own, None, x, frame)
    dot = tap_dot(x, kernel, False)
    both = dot(0, 2, 1)
    sums[0] = both[:, :LANES]
    sums[1] = both[:, LANES:] + dot(1, 2)


def hidden_body(size, across, place, before, sums, kernel, hidden, slots, x, frame, flat):
    high, wide = size.high, size.wide
    spread_all(size, 1, 1, wide, before, None, x, frame)
    dot = tap_dot(x, kernel, False)
    both = dot(1, 1, 0)
    sums = (sums[0] + both[:, :LANES] + dot(0, 0), sums[1] + both[:, LANES:])
    rounded = [s.astype(BF16) for s in sums]
    for f in range(FRAMES):
        hidden[f] = rounded[f].reshape(high, wide, LANES)
    span = span_second(size)
    found = split3(measured([r.astype(F32) for r in rounded]))
    take_columns(size, ((hidden, 1),), flat)
    upper = place[0] == 0
    edges = [jnp.where(upper, r[size.cells - wide :], r[:wide]).astype(F32) for r in rounded]
    fill = jnp.zeros((span - FRAMES * wide, LANES), F32)
    edges = jnp.concatenate([*edges, fill] if fill.shape[0] else edges, 0)
    rest = jnp.zeros((slots.shape[1] - span - PARTS, LANES), F32)
    for peer in range(slots.shape[0]):
        col = peer % across
        side = jnp.where(col > place[1], flat[1], flat[0])
        content = jnp.where(col == place[1], edges, side)
        slots[peer] = jnp.concatenate([content, found, rest], 0).astype(BF16)


def grad_act_body(size, near, far, kernel_far, out, x, frame, kernel, sems):
    wo = x.shape[2]
    copy = pltpu.make_async_copy(kernel_far, kernel, sems.at[0])
    copy.start()
    spread_all(size, 2, 2, wo, near, far, x, frame)
    copy.wait()
    sums = convolved(x, kernel, True)
    for f in range(FRAMES):
        out[f] = sums[f].reshape(size.tall(), wo, LANES)[:, : size.broad()]


def crossed_sides(size, place, across, got):
    step, high = size.stride(1), size.high
    count = FRAMES * step
    upper = place[0] == 0
    row = lax.broadcasted_iota(jnp.int32, (count, LANES), 0)
    found = []
    for at, there in (
        (jnp.maximum(place[1] - 1, 0), place[1] > 0),
        (jnp.minimum(place[1] + 1, across - 1), place[1] < across - 1),
    ):
        block = got[place[0] * across + at, 0:count].astype(F32)
        cross = got[(1 - place[0]) * across + at, 0:count].astype(F32)
        for f in range(FRAMES):
            above = jnp.where(upper, 0.0, cross[f * step + high : f * step + high + 1])
            below = jnp.where(upper, cross[f * step + 1 : f * step + 2], 0.0)
            block = jnp.where(row == f * step, above, block)
            block = jnp.where(row == f * step + high + 1, below, block)
        found.append(jnp.where(there, block, 0.0))
    return found


def span_second(size):
    return up(max(FRAMES * size.wide, FRAMES * size.stride(1)), 16)


def sums_second_body(size, across, hidden, got, grad_act, norm, slots):
    high, wide = size.high, size.wide
    at = span_second(size)
    blocks = [join3(got[peer, at : at + PARTS]) for peer in range(got.shape[0])]
    found = concluded(blocks, size.cells)
    norm[...] = found
    firsts, seconds = [], []
    for f in range(FRAMES):
        own = hidden[f].astype(F32)
        normed = (own - found[f : f + 1][None]) * found[FRAMES + f : FRAMES + f + 1][None]
        sigmoid = logistic(normed)
        grad = grad_act[f, 1 : high + 1, 1 : wide + 1]
        grad = grad * sigmoid * (1.0 + normed * (1.0 - sigmoid))
        grad, normed = grad.reshape(size.cells, LANES), normed.reshape(size.cells, LANES)
        firsts.append(jnp.sum(grad, 0, keepdims=True))
        seconds.append(jnp.sum(grad * normed, 0, keepdims=True))
    sums = stat_block(firsts, seconds)
    for peer in range(slots.shape[0]):
        slots[peer] = sums


def act_second_body(
    size, across, place, hidden, got, grad_act, norm, act, q_far, z_far, frame, q, z, sems
):
    wide = size.wide
    step = size.stride(1)
    left_all, right_all = crossed_sides(size, place, across, got)
    ok = in_frame((size.tall(), size.broad(), LANES), place, across, size, 1)
    lefts, rights, copies = [], [], []
    frame[...] = jnp.zeros_like(frame)
    facing = (1 - place[0]) * across + place[1]
    for f in range(FRAMES):
        top, bottom = rim_rows(place, got[facing, f * wide : (f + 1) * wide].astype(F32))
        padded_frame(
            size,
            hidden[f].astype(F32),
            top,
            bottom,
            left_all[f * step : (f + 1) * step],
            right_all[f * step : (f + 1) * step],
            frame,
        )
        normed = (frame[...] - norm[f : f + 1][None]) * norm[FRAMES + f : FRAMES + f + 1][None]
        sigmoid = logistic(normed)
        frame[...] = jnp.where(ok, normed * sigmoid, 0.0)
        left, right = put_frame(size, frame, f, act)
        lefts.append(left)
        rights.append(right)
        z[f] = normed
        q[f] = grad_act[f] * sigmoid * (1.0 + normed * (1.0 - sigmoid))
        for k, (source, target) in enumerate(((q, q_far), (z, z_far))):
            copy = pltpu.make_async_copy(source.at[f], target.at[f], sems.at[2 * f + k])
            copy.start()
            copies.append(copy)
    put_sides(act, size.main(1), lefts + rights)
    for copy in copies:
        copy.wait()


def hidden_grad(size, across, place, q, z, got, norm, out, frame, arrive):
    peers = got.shape[0]
    total = got[0]
    for peer in range(1, peers):
        total = total + got[peer]
    means = lane_totals(total) / (size.cells * peers * (LANES // GROUPS))
    ok = in_frame((size.tall(), size.broad(), LANES), place, across, size, 1)
    lefts, rights = [], []
    for f in range(FRAMES):
        first, second = means[f : f + 1][None], means[FRAMES + f : FRAMES + f + 1][None]
        inv = norm[FRAMES + f : FRAMES + f + 1][None]
        arrive(f)
        frame[...] = jnp.where(ok, inv * (q[f] - first - z[f] * second), 0.0)
        left, right = put_frame(size, frame, f, out)
        lefts.append(left)
        rights.append(right)
    put_sides(out, size.main(1), lefts + rights)


def own_cells(size, block, f):
    start = (f * size.tall() + 1) * size.wide
    return block[start : start + size.cells]


def turned_cells(size, block, out):
    for f in range(FRAMES):
        cells = own_cells(size, block, f).astype(F32).T.astype(BF16)
        out[f * LANES : (f + 1) * LANES] = cells


def tap_sums(x, turned, b):
    ho, wo = x.shape[1] - 2, x.shape[2]

    def cells(f):
        return x[f, b : b + ho].reshape(ho * wo, 3 * LANES)

    def dot(one, two):
        return jnp.dot(one, two, preferred_element_type=F32)

    low = dot(turned[...], cells(1))
    high = dot(turned[...], cells(2))
    return (
        dot(turned[:LANES], cells(0)) + low[LANES:],
        low[:LANES] + high[LANES:],
        high[:LANES] + dot(turned[LANES:], cells(3)),
    )


def second_term_body(size, near, far, act, out_far, short_far, x, frame, turned, out, short, sems):
    spread_all(size, 2, 1, size.wide, near, far, x, frame)
    turned_cells(size, act, turned)
    span = 3 * LANES
    copies = []
    for b in range(3):
        for a, total in enumerate(tap_sums(x, turned, b)):
            for c in range(3):
                tap = ((2 - a) * 3 + 2 - b) * 3 + 2 - c
                rows = slice(tap * LANES, (tap + 1) * LANES)
                piece = total[:, c * LANES : (c + 1) * LANES]
                out[rows] = piece
                short[rows] = piece.astype(BF16)
            rows = pl.ds(((2 - a) * 3 + 2 - b) * span, span)
            for k, (source, target) in enumerate(((out, out_far), (short, short_far))):
                sem = sems.at[2 * (3 * b + a) + k]
                copy = pltpu.make_async_copy(source.at[rows], target.at[rows], sem)
                copy.start()
                copies.append(copy)
    for copy in copies:
        copy.wait()


def first_term_body(
    size,
    across,
    place,
    got,
    norm,
    q_far,
    z_far,
    near_far,
    own_far,
    short_far,
    second_far,
    keep,
    give,
    grad_far,
    x,
    frame,
    turned,
    grad,
    near,
    own,
    q,
    z,
    sems,
):
    pairs = [(q_far.at[f], q.at[f]) for f in range(FRAMES)]
    pairs += [(z_far.at[f], z.at[f]) for f in range(FRAMES)]
    pairs += [(near_far, near), (own_far, own)]
    copies = [
        pltpu.make_async_copy(source, target, sems.at[k])
        for k, (source, target) in enumerate(pairs)
    ]
    for k in (0, FRAMES, 1, FRAMES + 1, 2 * FRAMES, 2 * FRAMES + 1):
        copies[k].start()
    upper = place[0] == 0
    given = pltpu.make_async_copy(short_far, give, sems.at[len(pairs) + 1])
    kept = pltpu.make_async_copy(second_far, keep, sems.at[len(pairs) + 2])

    @pl.when(upper)
    def _():
        given.start()

    @pl.when(jnp.logical_not(upper))
    def _():
        kept.start()

    def arrive(f):
        copies[f].wait()
        copies[FRAMES + f].wait()

    hidden_grad(size, across, place, q, z, got, norm, grad, frame, arrive)
    sent = pltpu.make_async_copy(grad, grad_far, sems.at[len(pairs)])
    sent.start()
    turned_cells(size, grad, turned)
    for copy in copies[2 * FRAMES :]:
        copy.wait()
    spread_all(size, 1, 1, size.wide, near, own, x, frame)

    def put(rows, piece):
        @pl.when(upper)
        def _():
            keep[rows] = piece

        @pl.when(jnp.logical_not(upper))
        def _():
            give[rows] = piece.astype(BF16)

    for b in range(3):
        for a, total in enumerate(tap_sums(x, turned, b)):
            rows = slice((a * 3 + b) * 3 * LANES, (a * 3 + b + 1) * 3 * LANES)
            put(rows, total.T)

    @pl.when(upper)
    def _():
        given.wait()

    @pl.when(jnp.logical_not(upper))
    def _():
        kept.wait()

    sent.wait()


def result_body(size, near, far, kernel, features, out, x, frame):
    spread_all(size, 1, 1, size.wide, near, far, x, frame)
    sums = convolved(x, kernel, False)
    for f in range(FRAMES):
        total = features[f].astype(F32) + sums[f].reshape(size.high, size.wide, LANES)
        out[f] = total.astype(BF16)


def back_first_body(size, near, far, kernel, features, norm, q, sums, x, frame):
    spread_all(size, 1, 1, size.wide, near, far, x, frame)
    grads = convolved(x, kernel, True)
    firsts, seconds = [], []
    for f in range(FRAMES):
        values = features[f].astype(F32).reshape(size.cells, LANES)
        normed = (values - norm[f : f + 1]) * norm[FRAMES + f : FRAMES + f + 1]
        sigmoid = logistic(normed)
        grad = grads[f] * sigmoid * (1.0 + normed * (1.0 - sigmoid))
        q[f] = grad
        firsts.append(jnp.sum(grad, 0, keepdims=True))
        seconds.append(jnp.sum(grad * normed, 0, keepdims=True))
    sums[...] = stat_block(firsts, seconds)


def feature_grad_body(size, peers, features, out_grad, norm, q, got, out):
    total = join3(got[0])
    for peer in range(1, got.shape[0]):
        total = total + join3(got[peer])
    means = lane_totals(total) / (size.cells * peers * (LANES // GROUPS))
    for f in range(FRAMES):
        values = features[f].astype(F32).reshape(size.cells, LANES)
        inv = norm[FRAMES + f : FRAMES + f + 1]
        normed = (values - norm[f : f + 1]) * inv
        grad = inv * (q[f] - means[f : f + 1] - normed * means[FRAMES + f : FRAMES + f + 1])
        grad = out_grad[f].astype(F32) + grad.reshape(size.high, size.wide, LANES)
        out[f] = grad.astype(BF16)


def row_swap(values):
    return lax.ppermute(values, "row", [(0, 1), (1, 0)])


def later(values, by):
    peers = lax.axis_size("tm")
    pairs = [(i, i + by) for i in range(peers) if 0 <= i + by < peers]
    return lax.ppermute(values, "tm", pairs)


def sum_parts(stat):
    high = lax.reduce_precision(stat, 8, 7)
    rest = stat - high
    middle = lax.reduce_precision(rest, 8, 7)
    return jnp.concatenate([high, middle, rest - middle], 0).astype(BF16)


def total_of(got):
    total = got[0].astype(F32)
    for peer in range(1, got.shape[0]):
        total = total + got[peer].astype(F32)
    return total


def joined_body(keep, got, out):
    share = out.shape[1]
    for peer in range(out.shape[0]):
        rows = slice(peer * share, (peer + 1) * share)
        out[peer] = (keep[rows] + got[rows].astype(F32)).astype(BF16)


def shared_body(got, out, flat):
    rows, share = got.shape[1], out.shape[1]
    if flat.shape[0] > rows:
        flat[rows:] = jnp.zeros((flat.shape[0] - rows, LANES), F32)
    flat[:rows] = total_of(got)
    for peer in range(out.shape[0]):
        out[peer] = flat[peer * share : (peer + 1) * share].astype(BF16)


def finished_body(factor, got, out):
    total = (total_of(got) * factor).astype(BF16)
    for peer in range(out.shape[0]):
        out[peer] = total


def placed_body(rows, swapped, *refs):
    place, block, first, second, sems = refs[0], refs[1], *refs[-3:]

    def move(target):
        copies = [
            pltpu.make_async_copy(
                block.at[peer, pl.ds(0, rows)], target.at[pl.ds(peer * rows, rows)], sems.at[peer]
            )
            for peer in range(block.shape[0])
        ]
        for copy in copies:
            copy.start()
        for copy in copies:
            copy.wait()

    @pl.when(place[0] == swapped)
    def _():
        move(first)

    @pl.when(place[0] != swapped)
    def _():
        move(second)


def placed(place, block, swapped, rows, so_far):
    anywhere = pl.BlockSpec(memory_space=pl.ANY)
    shape = (rows * block.shape[0], LANES)
    return pl.pallas_call(
        functools.partial(placed_body, rows, swapped),
        out_shape=[jax.ShapeDtypeStruct(shape, BF16)] * 2,
        in_specs=[pl.BlockSpec(memory_space=pltpu.SMEM)] + [anywhere] * (1 + len(so_far)),
        out_specs=[anywhere, anywhere],
        input_output_aliases={2 + k: k for k in range(len(so_far))},
        scratch_shapes=[pltpu.SemaphoreType.DMA((block.shape[0],))],
        compiler_params=pltpu.CompilerParams(vmem_limit_bytes=1 << 20),
    )(place, block, *so_far)


def on_device(features, conv_first, conv_second, out_grad):
    frames, high, wide, chans = features.shape
    assert frames == FRAMES and chans == LANES and lax.axis_size("row") == 2
    size = Sizes(high, wide)
    across = lax.axis_size("col")
    peers = 2 * across
    factor = 1.0 / math.sqrt(size.cells * FRAMES * lax.axis_size("tm") * peers)
    place = jnp.stack([lax.axis_index("row"), lax.axis_index("col")]).astype(jnp.int32)
    taps = conv_first.shape
    first = conv_first.reshape(-1, LANES)
    second = conv_second.reshape(-1, LANES)
    work = 2 * first.size * size.cells * FRAMES
    part = functools.partial
    stat = ((STATS, LANES), F32)
    tall, broad = size.tall(), size.broad()
    frame = ((tall, broad, LANES), F32)

    edge = up(3 * FRAMES * wide + PARTS, 16)
    lines = up(FRAMES * size.stride(1) + 2 * FRAMES * size.stride(2) + PARTS, 16)
    flat = ((2, lines, LANES), F32)
    pay, stats, cols, features_near, grad_near = call(
        part(start_body, size),
        [((edge, LANES), BF16), stat, flat, (features.shape, BF16), (features.shape, BF16)],
        [place, features, out_grad],
        smem=1,
        far=2,
        sems=2 * FRAMES,
    )
    row_got = row_swap(pay)
    (slots,) = call(
        part(slots_body, size, (1, 2), across),
        [((across, lines, LANES), BF16)],
        [place, cols, row_got, stats],
        [flat],
        smem=1,
    )
    col_got = lax.all_to_all(slots, "col", 0, 0)
    block = ((size.rows(1), LANES), BF16)
    act_first, grad, norm_first = call(
        part(act_first_body, size, across),
        [block, ((size.rows(2), LANES), BF16), stat],
        [place, features_near, grad_near, row_got, col_got],
        [frame],
        smem=1,
    )
    grad_after = later(grad, -1)
    act_before = later(act_first, 1)

    edge = up(FRAMES * wide + PARTS, 16)
    (sums,) = call(
        part(hidden_own_body, size),
        [((FRAMES, size.cells, LANES), F32)],
        [act_first, first],
        conv_scratch(size, 1, wide, FRAMES),
        mib=12,
        flops=work // 2,
    )
    span = span_second(size)
    hidden, slots = call(
        part(hidden_body, size, across),
        [(features.shape, BF16), ((peers, up(span + PARTS, 16), LANES), BF16)],
        [place, act_before, sums, first],
        [*conv_scratch(size, 1, wide, FRAMES), ((2, span, LANES), F32)],
        smem=1,
        mib=12,
        flops=2 * work,
    )
    got = lax.all_to_all(slots, ("row", "col"), 0, 0)
    (grad_act,) = call(
        part(grad_act_body, size),
        [((FRAMES, tall, broad, LANES), F32)],
        [grad, grad_after, second],
        [*conv_scratch(size, 2, up(wide + 2, 16)), (second.shape, BF16)],
        far=1,
        sems=1,
        mib=18,
        flops=2 * work,
    )
    field = ((FRAMES, tall, broad, LANES), F32)
    norm_second, slots = call(
        part(sums_second_body, size, across),
        [stat, ((peers, STATS, LANES), F32)],
        [hidden, got, grad_act],
    )
    act_second, q, z = call(
        part(act_second_body, size, across),
        [block, field, field],
        [place, hidden, got, grad_act, norm_second],
        [frame, field, field],
        smem=1,
        sems=2 * FRAMES,
        beside=True,
        out_far=2,
    )
    got = lax.all_to_all(slots, ("row", "col"), 0, 0)
    turned = ((FRAMES * LANES, size.cells), BF16)
    second_term, second_short = call(
        part(second_term_body, size),
        [(first.shape, F32), (first.shape, BF16)],
        [grad, grad_after, act_second],
        [*conv_scratch(size, 1, wide), turned, (first.shape, F32), (first.shape, BF16)],
        sems=18,
        mib=16,
        beside=True,
        out_far=2,
    )
    keep, give, grad_second = call(
        part(first_term_body, size, across),
        [(first.shape, F32), (first.shape, BF16), block],
        [place, got, norm_second, q, z, act_before, act_first, second_short, second_term],
        [*conv_scratch(size, 1, wide), turned, *[block] * 3, field, field],
        smem=1,
        far=6,
        sems=2 * FRAMES + 5,
        mib=20,
        flops=work,
        out_far=1,
    )
    give, late_grad, late_act = lax.optimization_barrier((give, grad_second, act_second))
    act_second_before = later(late_act, 1)
    grad_second_after = later(late_grad, -1)

    along = lax.axis_size("tm")
    rows = first.shape[0]
    by_col = rows // across
    (slots,) = call(joined_body, [((across, by_col, LANES), BF16)], [keep, row_swap(give)])
    slots = lax.all_to_all(slots, "col", 0, 0)
    slots, grad_second_after = lax.optimization_barrier((slots, grad_second_after))
    share = up(by_col, 16 * along) // along
    (slots,) = call(
        shared_body,
        [((along, share, LANES), BF16)],
        [slots],
        [((along * share, LANES), F32)],
    )
    got = lax.all_to_all(slots, "tm", 0, 0)
    (result,) = call(
        part(result_body, size),
        [(features.shape, BF16)],
        [act_second_before, act_second, second, features],
        conv_scratch(size, 1, wide),
        mib=14,
        flops=work,
    )
    q, sums = call(
        part(back_first_body, size),
        [((FRAMES, size.cells, LANES), F32), stat],
        [grad_second, grad_second_after, first, features, norm_first],
        conv_scratch(size, 1, wide),
        mib=14,
        flops=work,
    )
    got, result = lax.optimization_barrier((got, result))
    (slots,) = call(part(finished_body, factor), [((along, share, LANES), BF16)], [got])
    done = lax.all_to_all(slots, "tm", 0, 0).reshape(-1, LANES)[:by_col]
    parts = sum_parts(sums + row_swap(sums))
    parts = jnp.pad(parts, ((0, -parts.shape[0] % 16), (0, 0)))
    done = jnp.concatenate([done, parts], 0)
    mine = lax.all_to_all(jnp.broadcast_to(done[None], (across, *done.shape)), "col", 0, 0)
    theirs = row_swap(mine)
    so_far = placed(place, mine, 0, by_col, [])
    first_grad, second_grad = placed(place, theirs, 1, by_col, so_far)
    (feature_grad,) = call(
        part(feature_grad_body, size, peers),
        [(features.shape, BF16)],
        [features, out_grad, norm_first, q, mine[:, by_col:]],
    )
    return (result, feature_grad, first_grad.reshape(taps), second_grad.reshape(taps))


def solution(mesh):
    in_specs = (P("tm", "row", "col", None), P(), P(), P("tm", "row", "col", None))
    out_specs = (P("tm", "row", "col", None), P("tm", "row", "col", None), P(), P())
    return jax.shard_map(
        on_device, mesh=mesh, in_specs=in_specs, out_specs=out_specs, check_vma=False
    )
```

```python
import functools
import math

import jax
import jax.numpy as jnp
from jax import lax
from jax.experimental import pallas as pl
from jax.experimental.pallas import tpu as pltpu
from jax.sharding import PartitionSpec as P

GROUPS = 32
EPSILON = 1e-06
F32 = jnp.float32
BF16 = jnp.bfloat16
LANES = 128
FRAMES = 2
STATS = 8
PARTS = 3 * STATS


def up(count, step):
    return -(-count // step) * step


class Sizes:
    def __init__(self, high, wide):
        self.high, self.wide = high, wide
        self.cells = high * wide

    def stride(self, rim):
        return up(self.high + 2 * rim, 8)

    def main(self, rim):
        return FRAMES * (self.high + 2 * rim) * self.wide

    def rows(self, rim):
        return up(self.main(rim) + 2 * rim * FRAMES * self.stride(rim), 16)

    def tall(self):
        return self.high + 2

    def broad(self):
        return up(self.wide + 2, 8)


def call(body, outs, args, scratch=(), smem=0, far=0, sems=0, mib=8, flops=0, beside=False, out_far=0):
    specs = [pl.BlockSpec(memory_space=pltpu.SMEM)] * smem
    specs += [pl.BlockSpec(memory_space=pltpu.VMEM)] * (len(args) - smem - far)
    specs += [pl.BlockSpec(memory_space=pltpu.HBM)] * far
    near = len(args) - far
    args = [*args[:near], *(pltpu.with_memory_space_constraint(a, pltpu.HBM) for a in args[near:])]
    scratches = [pltpu.VMEM(shape, dtype) for shape, dtype in scratch]
    if sems:
        scratches.append(pltpu.SemaphoreType.DMA((sems,)))
    shapes = [jax.ShapeDtypeStruct(shape, dtype) for shape, dtype in outs]
    kept = len(outs) - out_far
    moved = sum(math.prod(a.shape) * a.dtype.itemsize for a in [*args, *shapes])
    moved = 0 if beside else moved
    return pl.pallas_call(
        body,
        out_shape=shapes[:kept] + [pltpu.HBM(o.shape, o.dtype) for o in shapes[kept:]],
        in_specs=specs,
        out_specs=[pl.BlockSpec(memory_space=pltpu.VMEM)] * kept
        + [pl.BlockSpec(memory_space=pltpu.HBM)] * out_far,
        scratch_shapes=scratches,
        cost_estimate=pl.CostEstimate(flops=flops, bytes_accessed=moved, transcendentals=0),
        compiler_params=pltpu.CompilerParams(vmem_limit_bytes=mib << 20),
    )(*args)


def logistic(values):
    return 0.5 * jnp.tanh(0.5 * values) + 0.5


def lane_totals(stat):
    lane = lax.broadcasted_iota(jnp.int32, stat.shape, 1)
    step = 1
    while step < LANES // GROUPS:
        ahead = pltpu.roll(stat, LANES - step, 1)
        behind = pltpu.roll(stat, step, 1)
        stat = stat + jnp.where((lane // step) % 2 == 0, ahead, behind)
        step *= 2
    return stat


def split3(stat):
    high = stat.astype(BF16).astype(F32)
    rest = stat - high
    middle = rest.astype(BF16).astype(F32)
    return jnp.concatenate([high, middle, rest - middle], 0)


def join3(parts):
    parts = parts.astype(F32)
    return parts[:STATS] + (parts[STATS : 2 * STATS] + parts[2 * STATS : PARTS])


def stat_block(first, second):
    rest = jnp.zeros((STATS - 2 * FRAMES, LANES), F32)
    return jnp.concatenate([*first, *second, rest], 0)


def measured(frames):
    means, squares = [], []
    for frame in frames:
        mean = jnp.sum(frame, 0, keepdims=True) / frame.shape[0]
        centred = frame - mean
        means.append(mean)
        squares.append(jnp.sum(centred * centred, 0, keepdims=True))
    return stat_block(means, squares)


def merged(one, two, cells):
    delta = one - two
    extra = (0.5 * cells) * delta * delta
    mean = 0.5 * (one[:FRAMES] + two[:FRAMES])
    square = one[FRAMES : 2 * FRAMES] + two[FRAMES : 2 * FRAMES] + extra[:FRAMES]
    return jnp.concatenate([mean, square, jnp.zeros((STATS - 2 * FRAMES, LANES), F32)], 0)


def concluded(blocks, cells):
    per_group = LANES // GROUPS
    mean = sum(blocks[1:], blocks[0])[:FRAMES]
    mean = lane_totals(mean) / (len(blocks) * per_group)
    total = jnp.zeros((FRAMES, LANES), F32)
    for block in blocks:
        off = block[:FRAMES] - mean
        total = total + block[FRAMES : 2 * FRAMES] + cells * off * off
    spread = lane_totals(total) / (cells * len(blocks) * per_group)
    rest = jnp.zeros((STATS - 2 * FRAMES, LANES), F32)
    return jnp.concatenate([mean, lax.rsqrt(spread + EPSILON), rest], 0)


def rim_rows(place, got):
    upper = place[0] == 0
    nothing = jnp.zeros_like(got)
    return jnp.where(upper, nothing, got), jnp.where(upper, got, nothing)


def in_frame(shape, place, across, size, rim):
    row = lax.broadcasted_iota(jnp.int32, shape, 0)
    col = lax.broadcasted_iota(jnp.int32, shape, 1)
    top = jnp.where(place[0] == 0, rim, 0)
    bottom = jnp.where(place[0] == 0, size.high + 2 * rim, size.high + rim)
    left = jnp.where(place[1] == 0, rim, 0)
    right = jnp.where(place[1] == across - 1, size.wide + rim, size.wide + 2 * rim)
    return (row >= top) & (row < bottom) & (col >= left) & (col < right)


def take_columns(size, arrays, flat):
    flat[...] = jnp.zeros_like(flat)
    at = 0
    for array, rim in arrays:
        for j in range(rim):
            for frame in range(FRAMES):
                for side, col in ((0, j), (1, size.wide - rim + j)):
                    rows = array[frame, :, col : col + 1].astype(F32)
                    rows = rows.reshape(size.high, LANES)
                    flat[side, at + rim : at + rim + size.high] = rows
                at += size.stride(rim)


def start_body(
    size, place, features_far, grad_far, pay, stats, flat, features, out_grad, sems
):
    high, wide = size.high, size.wide
    upper = place[0] == 0
    copies = [
        pltpu.make_async_copy(source.at[f], target.at[f], sems.at[FRAMES * k + f])
        for k, (source, target) in enumerate(((features_far, features), (grad_far, out_grad)))
        for f in range(FRAMES)
    ]
    for copy in copies:
        copy.start()
    for copy in copies[:FRAMES]:
        copy.wait()
    at = 0
    for frame in range(FRAMES):
        pay[at : at + wide] = jnp.where(upper, features[frame, high - 1], features[frame, 0])
        at += wide
    found = measured([features[f].astype(F32).reshape(size.cells, LANES) for f in range(FRAMES)])
    stats[...] = found
    for copy in copies[FRAMES:]:
        copy.wait()
    for frame in range(FRAMES):
        for row in range(2):
            edge = jnp.where(upper, out_grad[frame, high - 2 + row], out_grad[frame, row])
            pay[at : at + wide] = edge
            at += wide
    fill = jnp.zeros((pay.shape[0] - at - PARTS, LANES), F32)
    pay[at:] = jnp.concatenate([split3(found), fill], 0).astype(BF16)
    take_columns(size, ((features, 1), (out_grad, 2)), flat)


def slots_body(size, rims, across, place, flat, got, stats, slots, work):
    wide, high = size.wide, size.high
    upper = place[0] == 0
    work[...] = flat[...]
    at = base = 0
    for rim in rims:
        for j in range(rim):
            for frame in range(FRAMES):
                for row in range(rim):
                    start = base + (frame * rim + row) * wide
                    for side, col in ((0, j), (1, wide - rim + j)):
                        cell = start - start % 16 + 16 * ((start % 16 + col) // 16)
                        tile = got[cell : cell + 16].astype(F32)
                        edge = tile[start + col - cell : start + col - cell + 1]
                        nothing = jnp.zeros_like(edge)
                        top, bottom = at + row, at + rim + high + row
                        work[side, top : top + 1] = jnp.where(upper, nothing, edge)
                        work[side, bottom : bottom + 1] = jnp.where(upper, edge, nothing)
                at += size.stride(rim)
        base += FRAMES * rim * wide
    parts = split3(merged(stats[...], join3(got[base : base + PARTS]), size.cells))
    work[0, at : at + PARTS] = parts
    work[1, at : at + PARTS] = parts
    for peer in range(across):
        slots[peer] = jnp.where(peer > place[1], work[1], work[0]).astype(BF16)


def sides(place, across, got, first, count):
    left = got[jnp.maximum(place[1] - 1, 0), first : first + count].astype(F32)
    right = got[jnp.minimum(place[1] + 1, across - 1), first : first + count].astype(F32)
    nothing = jnp.zeros_like(left)
    left = jnp.where(place[1] > 0, left, nothing)
    right = jnp.where(place[1] < across - 1, right, nothing)
    return left, right


def padded_frame(size, own, top, bottom, left, right, frame):
    high, wide = size.high, size.wide
    frame[1 : high + 1, 1 : wide + 1] = own
    frame[0:1, 1 : wide + 1] = top[None]
    frame[high + 1 : high + 2, 1 : wide + 1] = bottom[None]
    tall = high + 2
    frame[:, 0:1] = left[:tall].reshape(tall, 1, LANES)
    frame[:, wide + 1 : wide + 2] = right[:tall].reshape(tall, 1, LANES)


def put_frame(size, frame, index, out):
    wide, tall, step = size.wide, size.tall(), size.stride(1)
    flat = frame[:, 1 : wide + 1].reshape(tall * wide, LANES)
    out[index * tall * wide : (index + 1) * tall * wide] = flat.astype(BF16)
    fill = jnp.zeros((step - tall, LANES), F32)
    left = frame[:, 0:1].reshape(tall, LANES)
    right = frame[:, wide + 1 : wide + 2].reshape(tall, LANES)
    return jnp.concatenate([left, fill], 0), jnp.concatenate([right, fill], 0)


def put_sides(out, first, blocks):
    fill = out.shape[0] - first - sum(b.shape[0] for b in blocks)
    if fill:
        blocks = [*blocks, jnp.zeros((fill, LANES), F32)]
    out[first:] = jnp.concatenate(blocks, 0).astype(BF16)


def act_first_body(
    size, across, place, features, out_grad, row_got, col_got, act, grad, norm, frame
):
    high, wide = size.high, size.wide
    at = FRAMES * size.stride(1) + 2 * FRAMES * size.stride(2)
    blocks = [join3(col_got[peer, at : at + PARTS]) for peer in range(across)]
    found = concluded(blocks, 2 * size.cells)
    norm[...] = found
    step = size.stride(1)
    left_all, right_all = sides(place, across, col_got, 0, FRAMES * step)
    ok = in_frame((size.tall(), size.broad(), LANES), place, across, size, 1)
    lefts, rights = [], []
    frame[...] = jnp.zeros_like(frame)
    for f in range(FRAMES):
        top, bottom = rim_rows(place, row_got[f * wide : (f + 1) * wide].astype(F32))
        padded_frame(
            size,
            features[f].astype(F32),
            top,
            bottom,
            left_all[f * step : (f + 1) * step],
            right_all[f * step : (f + 1) * step],
            frame,
        )
        normed = (frame[...] - found[f : f + 1][None]) * found[FRAMES + f : FRAMES + f + 1][None]
        frame[...] = jnp.where(ok, normed * logistic(normed), 0.0)
        left, right = put_frame(size, frame, f, act)
        lefts.append(left)
        rights.append(right)
    put_sides(act, size.main(1), lefts + rights)

    tall = high + 4
    for f in range(FRAMES):
        start = f * tall * wide
        for row in range(2):
            first = FRAMES * wide + (f * 2 + row) * wide
            top, bottom = rim_rows(place, row_got[first : first + wide])
            grad[start + row * wide : start + (row + 1) * wide] = top
            below = start + (high + 2 + row) * wide
            grad[below : below + wide] = bottom
        grad[start + 2 * wide : start + (high + 2) * wide] = out_grad[f].reshape(
            size.cells, LANES
        )
    left, right = sides(
        place, across, col_got, FRAMES * step, 2 * FRAMES * size.stride(2)
    )
    put_sides(grad, size.main(2), [left, right])


def spread_columns(size, rim, trim, wo, block, index, dst, at, frame):
    wide, high = size.wide, size.high
    tall, step = high + 2 * rim, size.stride(rim)
    main = block[index * tall * wide : (index + 1) * tall * wide].astype(F32)
    main = main.reshape(tall, wide, LANES)
    cut = rim - trim
    tall_out = tall - 2 * cut
    frame[:, trim : trim + wide] = main[cut : cut + tall_out]
    first = size.main(rim)
    edges = block[first:].astype(F32)
    for j in range(2 * rim):
        col = j - cut if j < rim else j - rim + trim + wide
        if j < cut or (j >= rim and j - rim >= trim):
            continue
        start = (j * FRAMES + index) * step
        edge = edges[start + cut : start + cut + tall_out]
        frame[:, col : col + 1] = edge.reshape(tall_out, 1, LANES)
    for c in range(3):
        dst[at, :, :, c * LANES : (c + 1) * LANES] = frame[:, c : c + wo].astype(BF16)


def spread_all(size, rim, trim, wo, near, far, dst, frame):
    filled = size.wide + 2 * trim
    if frame.shape[1] > filled:
        frame[:, filled:] = jnp.zeros((frame.shape[0], frame.shape[1] - filled, LANES), F32)
    for f in range(dst.shape[0]):
        block = near if f < FRAMES else far
        spread_columns(size, rim, trim, wo, block, f % FRAMES, dst, f, frame)


def tap_dot(x, kernel, turned):
    ho, wo = x.shape[1] - 2, x.shape[2]
    count = ho * wo
    span = 9 * LANES

    def cells(f):
        return jnp.concatenate(
            [x[f, b : b + ho].reshape(count, 3 * LANES) for b in range(3)], 1
        )

    def taps(a):
        if not turned:
            return kernel[a * span : (a + 1) * span]
        last = (3 - a) * 9 - 1
        return jnp.concatenate(
            [kernel[(last - k) * LANES : (last - k + 1) * LANES] for k in range(9)], 1
        )

    dims = (((1,), (1 if turned else 0,)), ((), ()))

    def dot(f, *times):
        weights = [taps(a) for a in times]
        if len(weights) > 1:
            weights = [jnp.concatenate(weights, 0 if turned else 1)]
        return lax.dot_general(cells(f), weights[0], dims, preferred_element_type=F32)

    return dot


def convolved(x, kernel, turned):
    dot = tap_dot(x, kernel, turned)
    both = dot(1, 1, 0) + dot(2, 2, 1)
    return both[:, :LANES] + dot(0, 0), both[:, LANES:] + dot(3, 2)


def conv_scratch(size, trim, wo, frames=2 * FRAMES):
    tall = size.high + 2 * trim
    return [((frames, tall, wo, 3 * LANES), BF16), ((tall, up(wo + 2, 8), LANES), F32)]


def hidden_own_body(size, own, kernel, sums, x, frame):
    spread_all(size, 1, 1, size.wide, own, None, x, frame)
    dot = tap_dot(x, kernel, False)
    both = dot(0, 2, 1)
    sums[0] = both[:, :LANES]
    sums[1] = both[:, LANES:] + dot(1, 2)


def hidden_body(size, across, place, before, sums, kernel, hidden, slots, x, frame, flat):
    high, wide = size.high, size.wide
    spread_all(size, 1, 1, wide, before, None, x, frame)
    dot = tap_dot(x, kernel, False)
    both = dot(1, 1, 0)
    sums = (sums[0] + both[:, :LANES] + dot(0, 0), sums[1] + both[:, LANES:])
    rounded = [s.astype(BF16) for s in sums]
    for f in range(FRAMES):
        hidden[f] = rounded[f].reshape(high, wide, LANES)
    span = span_second(size)
    found = split3(measured([r.astype(F32) for r in rounded]))
    take_columns(size, ((hidden, 1),), flat)
    upper = place[0] == 0
    edges = [jnp.where(upper, r[size.cells - wide :], r[:wide]).astype(F32) for r in rounded]
    fill = jnp.zeros((span - FRAMES * wide, LANES), F32)
    edges = jnp.concatenate([*edges, fill] if fill.shape[0] else edges, 0)
    rest = jnp.zeros((slots.shape[1] - span - PARTS, LANES), F32)
    for peer in range(slots.shape[0]):
        col = peer % across
        side = jnp.where(col > place[1], flat[1], flat[0])
        content = jnp.where(col == place[1], edges, side)
        slots[peer] = jnp.concatenate([content, found, rest], 0).astype(BF16)


def grad_act_body(size, near, far, kernel_far, out, x, frame, kernel, sems):
    wo = x.shape[2]
    copy = pltpu.make_async_copy(kernel_far, kernel, sems.at[0])
    copy.start()
    spread_all(size, 2, 2, wo, near, far, x, frame)
    copy.wait()
    sums = convolved(x, kernel, True)
    for f in range(FRAMES):
        out[f] = sums[f].reshape(size.tall(), wo, LANES)[:, : size.broad()]


def crossed_sides(size, place, across, got):
    step, high = size.stride(1), size.high
    count = FRAMES * step
    upper = place[0] == 0
    row = lax.broadcasted_iota(jnp.int32, (count, LANES), 0)
    found = []
    for at, there in (
        (jnp.maximum(place[1] - 1, 0), place[1] > 0),
        (jnp.minimum(place[1] + 1, across - 1), place[1] < across - 1),
    ):
        block = got[place[0] * across + at, 0:count].astype(F32)
        cross = got[(1 - place[0]) * across + at, 0:count].astype(F32)
        for f in range(FRAMES):
            above = jnp.where(upper, 0.0, cross[f * step + high : f * step + high + 1])
            below = jnp.where(upper, cross[f * step + 1 : f * step + 2], 0.0)
            block = jnp.where(row == f * step, above, block)
            block = jnp.where(row == f * step + high + 1, below, block)
        found.append(jnp.where(there, block, 0.0))
    return found


def span_second(size):
    return up(max(FRAMES * size.wide, FRAMES * size.stride(1)), 16)


def sums_second_body(size, across, hidden, got, grad_act, norm, slots):
    high, wide = size.high, size.wide
    at = span_second(size)
    blocks = [join3(got[peer, at : at + PARTS]) for peer in range(got.shape[0])]
    found = concluded(blocks, size.cells)
    norm[...] = found
    firsts, seconds = [], []
    for f in range(FRAMES):
        own = hidden[f].astype(F32)
        normed = (own - found[f : f + 1][None]) * found[FRAMES + f : FRAMES + f + 1][None]
        sigmoid = logistic(normed)
        grad = grad_act[f, 1 : high + 1, 1 : wide + 1]
        grad = grad * sigmoid * (1.0 + normed * (1.0 - sigmoid))
        grad, normed = grad.reshape(size.cells, LANES), normed.reshape(size.cells, LANES)
        firsts.append(jnp.sum(grad, 0, keepdims=True))
        seconds.append(jnp.sum(grad * normed, 0, keepdims=True))
    sums = stat_block(firsts, seconds)
    for peer in range(slots.shape[0]):
        slots[peer] = sums


def act_second_body(
    size, across, place, hidden, got, grad_act, norm, act, q_far, z_far, frame, q, z, sems
):
    wide = size.wide
    step = size.stride(1)
    left_all, right_all = crossed_sides(size, place, across, got)
    ok = in_frame((size.tall(), size.broad(), LANES), place, across, size, 1)
    lefts, rights, copies = [], [], []
    frame[...] = jnp.zeros_like(frame)
    facing = (1 - place[0]) * across + place[1]
    for f in range(FRAMES):
        top, bottom = rim_rows(place, got[facing, f * wide : (f + 1) * wide].astype(F32))
        padded_frame(
            size,
            hidden[f].astype(F32),
            top,
            bottom,
            left_all[f * step : (f + 1) * step],
            right_all[f * step : (f + 1) * step],
            frame,
        )
        normed = (frame[...] - norm[f : f + 1][None]) * norm[FRAMES + f : FRAMES + f + 1][None]
        sigmoid = logistic(normed)
        frame[...] = jnp.where(ok, normed * sigmoid, 0.0)
        left, right = put_frame(size, frame, f, act)
        lefts.append(left)
        rights.append(right)
        z[f] = normed
        q[f] = grad_act[f] * sigmoid * (1.0 + normed * (1.0 - sigmoid))
        for k, (source, target) in enumerate(((q, q_far), (z, z_far))):
            copy = pltpu.make_async_copy(source.at[f], target.at[f], sems.at[2 * f + k])
            copy.start()
            copies.append(copy)
    put_sides(act, size.main(1), lefts + rights)
    for copy in copies:
        copy.wait()


def hidden_grad(size, across, place, q, z, got, norm, out, frame, arrive):
    peers = got.shape[0]
    total = got[0]
    for peer in range(1, peers):
        total = total + got[peer]
    means = lane_totals(total) / (size.cells * peers * (LANES // GROUPS))
    ok = in_frame((size.tall(), size.broad(), LANES), place, across, size, 1)
    lefts, rights = [], []
    for f in range(FRAMES):
        first, second = means[f : f + 1][None], means[FRAMES + f : FRAMES + f + 1][None]
        inv = norm[FRAMES + f : FRAMES + f + 1][None]
        arrive(f)
        frame[...] = jnp.where(ok, inv * (q[f] - first - z[f] * second), 0.0)
        left, right = put_frame(size, frame, f, out)
        lefts.append(left)
        rights.append(right)
    put_sides(out, size.main(1), lefts + rights)


def own_cells(size, block, f):
    start = (f * size.tall() + 1) * size.wide
    return block[start : start + size.cells]


def turned_cells(size, block, out):
    for f in range(FRAMES):
        cells = own_cells(size, block, f).astype(F32).T.astype(BF16)
        out[f * LANES : (f + 1) * LANES] = cells


def tap_sums(x, turned, b):
    ho, wo = x.shape[1] - 2, x.shape[2]

    def cells(f):
        return x[f, b : b + ho].reshape(ho * wo, 3 * LANES)

    def dot(one, two):
        return jnp.dot(one, two, preferred_element_type=F32)

    low = dot(turned[...], cells(1))
    high = dot(turned[...], cells(2))
    return (
        dot(turned[:LANES], cells(0)) + low[LANES:],
        low[:LANES] + high[LANES:],
        high[:LANES] + dot(turned[LANES:], cells(3)),
    )


def second_term_body(size, near, far, act, out_far, short_far, x, frame, turned, out, short, sems):
    spread_all(size, 2, 1, size.wide, near, far, x, frame)
    turned_cells(size, act, turned)
    span = 3 * LANES
    copies = []
    for b in range(3):
        for a, total in enumerate(tap_sums(x, turned, b)):
            for c in range(3):
                tap = ((2 - a) * 3 + 2 - b) * 3 + 2 - c
                rows = slice(tap * LANES, (tap + 1) * LANES)
                piece = total[:, c * LANES : (c + 1) * LANES]
                out[rows] = piece
                short[rows] = piece.astype(BF16)
            rows = pl.ds(((2 - a) * 3 + 2 - b) * span, span)
            for k, (source, target) in enumerate(((out, out_far), (short, short_far))):
                sem = sems.at[2 * (3 * b + a) + k]
                copy = pltpu.make_async_copy(source.at[rows], target.at[rows], sem)
                copy.start()
                copies.append(copy)
    for copy in copies:
        copy.wait()


def first_term_body(
    size,
    across,
    place,
    got,
    norm,
    q_far,
    z_far,
    near_far,
    own_far,
    short_far,
    second_far,
    out,
    give,
    second,
    grad_far,
    x,
    frame,
    turned,
    grad,
    near,
    own,
    q,
    z,
    sems,
):
    pairs = [(q_far.at[f], q.at[f]) for f in range(FRAMES)]
    pairs += [(z_far.at[f], z.at[f]) for f in range(FRAMES)]
    pairs += [(near_far, near), (own_far, own)]
    copies = [
        pltpu.make_async_copy(source, target, sems.at[k])
        for k, (source, target) in enumerate(pairs)
    ]
    for k in (0, FRAMES, 1, FRAMES + 1, 2 * FRAMES, 2 * FRAMES + 1):
        copies[k].start()
    upper = place[0] == 0
    given = pltpu.make_async_copy(short_far, give, sems.at[len(pairs) + 1])
    fetched = pltpu.make_async_copy(second_far, second, sems.at[len(pairs) + 2])

    @pl.when(upper)
    def _():
        given.start()

    fetched.start()

    def arrive(f):
        copies[f].wait()
        copies[FRAMES + f].wait()

    hidden_grad(size, across, place, q, z, got, norm, grad, frame, arrive)
    sent = pltpu.make_async_copy(grad, grad_far, sems.at[len(pairs)])
    sent.start()
    turned_cells(size, grad, turned)
    for copy in copies[2 * FRAMES :]:
        copy.wait()
    spread_all(size, 1, 1, size.wide, near, own, x, frame)

    for b in range(3):
        for a, total in enumerate(tap_sums(x, turned, b)):
            rows = slice((a * 3 + b) * 3 * LANES, (a * 3 + b + 1) * 3 * LANES)
            out[rows] = total.T

    @pl.when(jnp.logical_not(upper))
    def _():
        give[...] = out[...].astype(BF16)

    @pl.when(upper)
    def _():
        given.wait()

    fetched.wait()
    sent.wait()


def result_body(size, near, far, kernel, features, out, x, frame):
    spread_all(size, 1, 1, size.wide, near, far, x, frame)
    sums = convolved(x, kernel, False)
    for f in range(FRAMES):
        total = features[f].astype(F32) + sums[f].reshape(size.high, size.wide, LANES)
        out[f] = total.astype(BF16)


def back_first_body(size, near, far, kernel, features, norm, q, sums, x, frame):
    spread_all(size, 1, 1, size.wide, near, far, x, frame)
    grads = convolved(x, kernel, True)
    firsts, seconds = [], []
    for f in range(FRAMES):
        values = features[f].astype(F32).reshape(size.cells, LANES)
        normed = (values - norm[f : f + 1]) * norm[FRAMES + f : FRAMES + f + 1]
        sigmoid = logistic(normed)
        grad = grads[f] * sigmoid * (1.0 + normed * (1.0 - sigmoid))
        q[f] = grad
        firsts.append(jnp.sum(grad, 0, keepdims=True))
        seconds.append(jnp.sum(grad * normed, 0, keepdims=True))
    sums[...] = stat_block(firsts, seconds)


def feature_grad_body(size, peers, features, out_grad, norm, q, got, out):
    total = join3(got[0])
    for peer in range(1, got.shape[0]):
        total = total + join3(got[peer])
    means = lane_totals(total) / (size.cells * peers * (LANES // GROUPS))
    for f in range(FRAMES):
        values = features[f].astype(F32).reshape(size.cells, LANES)
        inv = norm[FRAMES + f : FRAMES + f + 1]
        normed = (values - norm[f : f + 1]) * inv
        grad = inv * (q[f] - means[f : f + 1] - normed * means[FRAMES + f : FRAMES + f + 1])
        grad = out_grad[f].astype(F32) + grad.reshape(size.high, size.wide, LANES)
        out[f] = grad.astype(BF16)


def row_swap(values):
    return lax.ppermute(values, "row", [(0, 1), (1, 0)])


def later(values, by):
    peers = lax.axis_size("tm")
    pairs = [(i, i + by) for i in range(peers) if 0 <= i + by < peers]
    return lax.ppermute(values, "tm", pairs)


def sum_parts(stat):
    high = lax.reduce_precision(stat, 8, 7)
    rest = stat - high
    middle = lax.reduce_precision(rest, 8, 7)
    return jnp.concatenate([high, middle, rest - middle], 0).astype(BF16)


def total_of(got):
    total = got[0].astype(F32)
    for peer in range(1, got.shape[0]):
        total = total + got[peer].astype(F32)
    return total


def joined_body(place, first, second, got, out):
    share = out.shape[1]

    def add(keep):
        for peer in range(out.shape[0]):
            rows = slice(peer * share, (peer + 1) * share)
            out[peer] = (keep[rows] + got[rows].astype(F32)).astype(BF16)

    @pl.when(place[0] == 0)
    def _():
        add(first)

    @pl.when(place[0] != 0)
    def _():
        add(second)


def shared_body(got, out, flat):
    rows, share = got.shape[1], out.shape[1]
    if flat.shape[0] > rows:
        flat[rows:] = jnp.zeros((flat.shape[0] - rows, LANES), F32)
    flat[:rows] = total_of(got)
    for peer in range(out.shape[0]):
        out[peer] = flat[peer * share : (peer + 1) * share].astype(BF16)


def finished_body(factor, got, out):
    total = (total_of(got) * factor).astype(BF16)
    for peer in range(out.shape[0]):
        out[peer] = total


def placed_body(rows, swapped, *refs):
    place, block, first, second, sems = refs[0], refs[1], *refs[-3:]

    def move(target):
        copies = [
            pltpu.make_async_copy(
                block.at[peer, pl.ds(0, rows)], target.at[pl.ds(peer * rows, rows)], sems.at[peer]
            )
            for peer in range(block.shape[0])
        ]
        for copy in copies:
            copy.start()
        for copy in copies:
            copy.wait()

    @pl.when(place[0] == swapped)
    def _():
        move(first)

    @pl.when(place[0] != swapped)
    def _():
        move(second)


def placed(place, block, swapped, rows, so_far):
    anywhere = pl.BlockSpec(memory_space=pl.ANY)
    shape = (rows * block.shape[0], LANES)
    return pl.pallas_call(
        functools.partial(placed_body, rows, swapped),
        out_shape=[jax.ShapeDtypeStruct(shape, BF16)] * 2,
        in_specs=[pl.BlockSpec(memory_space=pltpu.SMEM)] + [anywhere] * (1 + len(so_far)),
        out_specs=[anywhere, anywhere],
        input_output_aliases={2 + k: k for k in range(len(so_far))},
        scratch_shapes=[pltpu.SemaphoreType.DMA((block.shape[0],))],
        compiler_params=pltpu.CompilerParams(vmem_limit_bytes=1 << 20),
    )(place, block, *so_far)


def on_device(features, conv_first, conv_second, out_grad):
    frames, high, wide, chans = features.shape
    assert frames == FRAMES and chans == LANES and lax.axis_size("row") == 2
    size = Sizes(high, wide)
    across = lax.axis_size("col")
    peers = 2 * across
    factor = 1.0 / math.sqrt(size.cells * FRAMES * lax.axis_size("tm") * peers)
    place = jnp.stack([lax.axis_index("row"), lax.axis_index("col")]).astype(jnp.int32)
    taps = conv_first.shape
    first = conv_first.reshape(-1, LANES)
    second = conv_second.reshape(-1, LANES)
    work = 2 * first.size * size.cells * FRAMES
    part = functools.partial
    stat = ((STATS, LANES), F32)
    tall, broad = size.tall(), size.broad()
    frame = ((tall, broad, LANES), F32)

    edge = up(3 * FRAMES * wide + PARTS, 16)
    lines = up(FRAMES * size.stride(1) + 2 * FRAMES * size.stride(2) + PARTS, 16)
    flat = ((2, lines, LANES), F32)
    pay, stats, cols, features_near, grad_near = call(
        part(start_body, size),
        [((edge, LANES), BF16), stat, flat, (features.shape, BF16), (features.shape, BF16)],
        [place, features, out_grad],
        smem=1,
        far=2,
        sems=2 * FRAMES,
    )
    row_got = row_swap(pay)
    (slots,) = call(
        part(slots_body, size, (1, 2), across),
        [((across, lines, LANES), BF16)],
        [place, cols, row_got, stats],
        [flat],
        smem=1,
    )
    col_got = lax.all_to_all(slots, "col", 0, 0)
    block = ((size.rows(1), LANES), BF16)
    act_first, grad, norm_first = call(
        part(act_first_body, size, across),
        [block, ((size.rows(2), LANES), BF16), stat],
        [place, features_near, grad_near, row_got, col_got],
        [frame],
        smem=1,
    )
    grad_after = later(grad, -1)
    act_before = later(act_first, 1)

    edge = up(FRAMES * wide + PARTS, 16)
    (sums,) = call(
        part(hidden_own_body, size),
        [((FRAMES, size.cells, LANES), F32)],
        [act_first, first],
        conv_scratch(size, 1, wide, FRAMES),
        mib=12,
        flops=work // 2,
    )
    span = span_second(size)
    hidden, slots = call(
        part(hidden_body, size, across),
        [(features.shape, BF16), ((peers, up(span + PARTS, 16), LANES), BF16)],
        [place, act_before, sums, first],
        [*conv_scratch(size, 1, wide, FRAMES), ((2, span, LANES), F32)],
        smem=1,
        mib=12,
        flops=2 * work,
    )
    got = lax.all_to_all(slots, ("row", "col"), 0, 0)
    (grad_act,) = call(
        part(grad_act_body, size),
        [((FRAMES, tall, broad, LANES), F32)],
        [grad, grad_after, second],
        [*conv_scratch(size, 2, up(wide + 2, 16)), (second.shape, BF16)],
        far=1,
        sems=1,
        mib=18,
        flops=2 * work,
    )
    field = ((FRAMES, tall, broad, LANES), F32)
    norm_second, slots = call(
        part(sums_second_body, size, across),
        [stat, ((peers, STATS, LANES), F32)],
        [hidden, got, grad_act],
    )
    act_second, q, z = call(
        part(act_second_body, size, across),
        [block, field, field],
        [place, hidden, got, grad_act, norm_second],
        [frame, field, field],
        smem=1,
        sems=2 * FRAMES,
        beside=True,
        out_far=2,
    )
    got = lax.all_to_all(slots, ("row", "col"), 0, 0)
    turned = ((FRAMES * LANES, size.cells), BF16)
    second_term, second_short = call(
        part(second_term_body, size),
        [(first.shape, F32), (first.shape, BF16)],
        [grad, grad_after, act_second],
        [*conv_scratch(size, 1, wide), turned, (first.shape, F32), (first.shape, BF16)],
        sems=18,
        mib=16,
        beside=True,
        out_far=2,
    )
    first_term, give, second_near, grad_second = call(
        part(first_term_body, size, across),
        [(first.shape, F32), (first.shape, BF16), (first.shape, F32), block],
        [place, got, norm_second, q, z, act_before, act_first, second_short, second_term],
        [*conv_scratch(size, 1, wide), turned, *[block] * 3, field, field],
        smem=1,
        far=6,
        sems=2 * FRAMES + 5,
        mib=20,
        flops=work,
        out_far=1,
    )
    give, late_grad, late_act = lax.optimization_barrier((give, grad_second, act_second))
    act_second_before = later(late_act, 1)
    grad_second_after = later(late_grad, -1)

    along = lax.axis_size("tm")
    rows = first.shape[0]
    by_col = rows // across
    (slots,) = call(
        joined_body,
        [((across, by_col, LANES), BF16)],
        [place, first_term, second_near, row_swap(give)],
        smem=1,
    )
    slots = lax.all_to_all(slots, "col", 0, 0)
    slots, grad_second_after = lax.optimization_barrier((slots, grad_second_after))
    share = up(by_col, 16 * along) // along
    (slots,) = call(
        shared_body,
        [((along, share, LANES), BF16)],
        [slots],
        [((along * share, LANES), F32)],
    )
    got = lax.all_to_all(slots, "tm", 0, 0)
    (result,) = call(
        part(result_body, size),
        [(features.shape, BF16)],
        [act_second_before, act_second, second, features],
        conv_scratch(size, 1, wide),
        mib=14,
        flops=work,
    )
    q, sums = call(
        part(back_first_body, size),
        [((FRAMES, size.cells, LANES), F32), stat],
        [grad_second, grad_second_after, first, features, norm_first],
        conv_scratch(size, 1, wide),
        mib=14,
        flops=work,
    )
    got, result = lax.optimization_barrier((got, result))
    (slots,) = call(part(finished_body, factor), [((along, share, LANES), BF16)], [got])
    done = lax.all_to_all(slots, "tm", 0, 0).reshape(-1, LANES)[:by_col]
    parts = sum_parts(sums + row_swap(sums))
    parts = jnp.pad(parts, ((0, -parts.shape[0] % 16), (0, 0)))
    done = jnp.concatenate([done, parts], 0)
    mine = lax.all_to_all(jnp.broadcast_to(done[None], (across, *done.shape)), "col", 0, 0)
    theirs = row_swap(mine)
    so_far = placed(place, mine, 0, by_col, [])
    first_grad, second_grad = placed(place, theirs, 1, by_col, so_far)
    (feature_grad,) = call(
        part(feature_grad_body, size, peers),
        [(features.shape, BF16)],
        [features, out_grad, norm_first, q, mine[:, by_col:]],
    )
    return (result, feature_grad, first_grad.reshape(taps), second_grad.reshape(taps))


def solution(mesh):
    in_specs = (P("tm", "row", "col", None), P(), P(), P("tm", "row", "col", None))
    out_specs = (P("tm", "row", "col", None), P("tm", "row", "col", None), P(), P())
    return jax.shard_map(
        on_device, mesh=mesh, in_specs=in_specs, out_specs=out_specs, check_vma=False
    )
```

```python
import functools
import math

import jax
import jax.numpy as jnp
from jax import lax
from jax.experimental import pallas as pl
from jax.experimental.pallas import tpu as pltpu
from jax.sharding import PartitionSpec as P

GROUPS = 32
EPSILON = 1e-06
F32 = jnp.float32
BF16 = jnp.bfloat16
LANES = 128
FRAMES = 2
STATS = 8
PARTS = 3 * STATS


def up(count, step):
    return -(-count // step) * step


class Sizes:
    def __init__(self, high, wide):
        self.high, self.wide = high, wide
        self.cells = high * wide

    def stride(self, rim):
        return up(self.high + 2 * rim, 8)

    def main(self, rim):
        return FRAMES * (self.high + 2 * rim) * self.wide

    def rows(self, rim):
        return up(self.main(rim) + 2 * rim * FRAMES * self.stride(rim), 16)

    def tall(self):
        return self.high + 2

    def broad(self):
        return up(self.wide + 2, 8)


def call(body, outs, args, scratch=(), smem=0, far=0, sems=0, mib=8, flops=0, beside=False, out_far=0):
    specs = [pl.BlockSpec(memory_space=pltpu.SMEM)] * smem
    specs += [pl.BlockSpec(memory_space=pltpu.VMEM)] * (len(args) - smem - far)
    specs += [pl.BlockSpec(memory_space=pltpu.HBM)] * far
    near = len(args) - far
    args = [*args[:near], *(pltpu.with_memory_space_constraint(a, pltpu.HBM) for a in args[near:])]
    scratches = [pltpu.VMEM(shape, dtype) for shape, dtype in scratch]
    if sems:
        scratches.append(pltpu.SemaphoreType.DMA((sems,)))
    shapes = [jax.ShapeDtypeStruct(shape, dtype) for shape, dtype in outs]
    kept = len(outs) - out_far
    moved = sum(math.prod(a.shape) * a.dtype.itemsize for a in [*args, *shapes])
    moved = 0 if beside else moved
    return pl.pallas_call(
        body,
        out_shape=shapes[:kept] + [pltpu.HBM(o.shape, o.dtype) for o in shapes[kept:]],
        in_specs=specs,
        out_specs=[pl.BlockSpec(memory_space=pltpu.VMEM)] * kept
        + [pl.BlockSpec(memory_space=pltpu.HBM)] * out_far,
        scratch_shapes=scratches,
        cost_estimate=pl.CostEstimate(flops=flops, bytes_accessed=moved, transcendentals=0),
        compiler_params=pltpu.CompilerParams(vmem_limit_bytes=mib << 20),
    )(*args)


def logistic(values):
    return 0.5 * jnp.tanh(0.5 * values) + 0.5


def lane_totals(stat):
    lane = lax.broadcasted_iota(jnp.int32, stat.shape, 1)
    step = 1
    while step < LANES // GROUPS:
        ahead = pltpu.roll(stat, LANES - step, 1)
        behind = pltpu.roll(stat, step, 1)
        stat = stat + jnp.where((lane // step) % 2 == 0, ahead, behind)
        step *= 2
    return stat


def split3(stat):
    high = stat.astype(BF16).astype(F32)
    rest = stat - high
    middle = rest.astype(BF16).astype(F32)
    return jnp.concatenate([high, middle, rest - middle], 0)


def join3(parts):
    parts = parts.astype(F32)
    return parts[:STATS] + (parts[STATS : 2 * STATS] + parts[2 * STATS : PARTS])


def stat_block(first, second):
    rest = jnp.zeros((STATS - 2 * FRAMES, LANES), F32)
    return jnp.concatenate([*first, *second, rest], 0)


def measured(frames):
    means, squares = [], []
    for frame in frames:
        mean = jnp.sum(frame, 0, keepdims=True) / frame.shape[0]
        centred = frame - mean
        means.append(mean)
        squares.append(jnp.sum(centred * centred, 0, keepdims=True))
    return stat_block(means, squares)


def merged(one, two, cells):
    delta = one - two
    extra = (0.5 * cells) * delta * delta
    mean = 0.5 * (one[:FRAMES] + two[:FRAMES])
    square = one[FRAMES : 2 * FRAMES] + two[FRAMES : 2 * FRAMES] + extra[:FRAMES]
    return jnp.concatenate([mean, square, jnp.zeros((STATS - 2 * FRAMES, LANES), F32)], 0)


def concluded(blocks, cells):
    per_group = LANES // GROUPS
    mean = sum(blocks[1:], blocks[0])[:FRAMES]
    mean = lane_totals(mean) / (len(blocks) * per_group)
    total = jnp.zeros((FRAMES, LANES), F32)
    for block in blocks:
        off = block[:FRAMES] - mean
        total = total + block[FRAMES : 2 * FRAMES] + cells * off * off
    spread = lane_totals(total) / (cells * len(blocks) * per_group)
    rest = jnp.zeros((STATS - 2 * FRAMES, LANES), F32)
    return jnp.concatenate([mean, lax.rsqrt(spread + EPSILON), rest], 0)


def rim_rows(place, got):
    upper = place[0] == 0
    nothing = jnp.zeros_like(got)
    return jnp.where(upper, nothing, got), jnp.where(upper, got, nothing)


def in_frame(shape, place, across, size, rim):
    row = lax.broadcasted_iota(jnp.int32, shape, 0)
    col = lax.broadcasted_iota(jnp.int32, shape, 1)
    top = jnp.where(place[0] == 0, rim, 0)
    bottom = jnp.where(place[0] == 0, size.high + 2 * rim, size.high + rim)
    left = jnp.where(place[1] == 0, rim, 0)
    right = jnp.where(place[1] == across - 1, size.wide + rim, size.wide + 2 * rim)
    return (row >= top) & (row < bottom) & (col >= left) & (col < right)


def take_columns(size, arrays, flat):
    flat[...] = jnp.zeros_like(flat)
    at = 0
    for array, rim in arrays:
        for j in range(rim):
            for frame in range(FRAMES):
                for side, col in ((0, j), (1, size.wide - rim + j)):
                    rows = array[frame, :, col : col + 1].astype(F32)
                    rows = rows.reshape(size.high, LANES)
                    flat[side, at + rim : at + rim + size.high] = rows
                at += size.stride(rim)


def start_body(
    size, place, features_far, grad_far, pay, stats, flat, features, out_grad, sems
):
    high, wide = size.high, size.wide
    upper = place[0] == 0
    copies = [
        pltpu.make_async_copy(source.at[f], target.at[f], sems.at[FRAMES * k + f])
        for k, (source, target) in enumerate(((features_far, features), (grad_far, out_grad)))
        for f in range(FRAMES)
    ]
    for copy in copies:
        copy.start()
    for copy in copies[:FRAMES]:
        copy.wait()
    at = 0
    for frame in range(FRAMES):
        pay[at : at + wide] = jnp.where(upper, features[frame, high - 1], features[frame, 0])
        at += wide
    found = measured([features[f].astype(F32).reshape(size.cells, LANES) for f in range(FRAMES)])
    stats[...] = found
    for copy in copies[FRAMES:]:
        copy.wait()
    for frame in range(FRAMES):
        for row in range(2):
            edge = jnp.where(upper, out_grad[frame, high - 2 + row], out_grad[frame, row])
            pay[at : at + wide] = edge
            at += wide
    fill = jnp.zeros((pay.shape[0] - at - PARTS, LANES), F32)
    pay[at:] = jnp.concatenate([split3(found), fill], 0).astype(BF16)
    take_columns(size, ((features, 1), (out_grad, 2)), flat)


def slots_body(size, rims, across, place, flat, got, stats, slots, work):
    wide, high = size.wide, size.high
    upper = place[0] == 0
    work[...] = flat[...]
    at = base = 0
    for rim in rims:
        for j in range(rim):
            for frame in range(FRAMES):
                for row in range(rim):
                    start = base + (frame * rim + row) * wide
                    for side, col in ((0, j), (1, wide - rim + j)):
                        cell = start - start % 16 + 16 * ((start % 16 + col) // 16)
                        tile = got[cell : cell + 16].astype(F32)
                        edge = tile[start + col - cell : start + col - cell + 1]
                        nothing = jnp.zeros_like(edge)
                        top, bottom = at + row, at + rim + high + row
                        work[side, top : top + 1] = jnp.where(upper, nothing, edge)
                        work[side, bottom : bottom + 1] = jnp.where(upper, edge, nothing)
                at += size.stride(rim)
        base += FRAMES * rim * wide
    parts = split3(merged(stats[...], join3(got[base : base + PARTS]), size.cells))
    work[0, at : at + PARTS] = parts
    work[1, at : at + PARTS] = parts
    for peer in range(across):
        slots[peer] = jnp.where(peer > place[1], work[1], work[0]).astype(BF16)


def sides(place, across, got, first, count):
    left = got[jnp.maximum(place[1] - 1, 0), first : first + count].astype(F32)
    right = got[jnp.minimum(place[1] + 1, across - 1), first : first + count].astype(F32)
    nothing = jnp.zeros_like(left)
    left = jnp.where(place[1] > 0, left, nothing)
    right = jnp.where(place[1] < across - 1, right, nothing)
    return left, right


def padded_frame(size, own, top, bottom, left, right, frame):
    high, wide = size.high, size.wide
    frame[1 : high + 1, 1 : wide + 1] = own
    frame[0:1, 1 : wide + 1] = top[None]
    frame[high + 1 : high + 2, 1 : wide + 1] = bottom[None]
    tall = high + 2
    frame[:, 0:1] = left[:tall].reshape(tall, 1, LANES)
    frame[:, wide + 1 : wide + 2] = right[:tall].reshape(tall, 1, LANES)


def put_frame(size, frame, index, out):
    wide, tall, step = size.wide, size.tall(), size.stride(1)
    flat = frame[:, 1 : wide + 1].reshape(tall * wide, LANES)
    out[index * tall * wide : (index + 1) * tall * wide] = flat.astype(BF16)
    fill = jnp.zeros((step - tall, LANES), F32)
    left = frame[:, 0:1].reshape(tall, LANES)
    right = frame[:, wide + 1 : wide + 2].reshape(tall, LANES)
    return jnp.concatenate([left, fill], 0), jnp.concatenate([right, fill], 0)


def put_sides(out, first, blocks):
    fill = out.shape[0] - first - sum(b.shape[0] for b in blocks)
    if fill:
        blocks = [*blocks, jnp.zeros((fill, LANES), F32)]
    out[first:] = jnp.concatenate(blocks, 0).astype(BF16)


def act_first_body(
    size, across, place, features, out_grad, row_got, col_got, act, grad, norm, frame
):
    high, wide = size.high, size.wide
    at = FRAMES * size.stride(1) + 2 * FRAMES * size.stride(2)
    blocks = [join3(col_got[peer, at : at + PARTS]) for peer in range(across)]
    found = concluded(blocks, 2 * size.cells)
    norm[...] = found
    step = size.stride(1)
    left_all, right_all = sides(place, across, col_got, 0, FRAMES * step)
    ok = in_frame((size.tall(), size.broad(), LANES), place, across, size, 1)
    lefts, rights = [], []
    frame[...] = jnp.zeros_like(frame)
    for f in range(FRAMES):
        top, bottom = rim_rows(place, row_got[f * wide : (f + 1) * wide].astype(F32))
        padded_frame(
            size,
            features[f].astype(F32),
            top,
            bottom,
            left_all[f * step : (f + 1) * step],
            right_all[f * step : (f + 1) * step],
            frame,
        )
        normed = (frame[...] - found[f : f + 1][None]) * found[FRAMES + f : FRAMES + f + 1][None]
        frame[...] = jnp.where(ok, normed * logistic(normed), 0.0)
        left, right = put_frame(size, frame, f, act)
        lefts.append(left)
        rights.append(right)
    put_sides(act, size.main(1), lefts + rights)

    tall = high + 4
    for f in range(FRAMES):
        start = f * tall * wide
        for row in range(2):
            first = FRAMES * wide + (f * 2 + row) * wide
            top, bottom = rim_rows(place, row_got[first : first + wide])
            grad[start + row * wide : start + (row + 1) * wide] = top
            below = start + (high + 2 + row) * wide
            grad[below : below + wide] = bottom
        grad[start + 2 * wide : start + (high + 2) * wide] = out_grad[f].reshape(
            size.cells, LANES
        )
    left, right = sides(
        place, across, col_got, FRAMES * step, 2 * FRAMES * size.stride(2)
    )
    put_sides(grad, size.main(2), [left, right])


def spread_columns(size, rim, trim, wo, block, index, dst, at, frame):
    wide, high = size.wide, size.high
    tall, step = high + 2 * rim, size.stride(rim)
    main = block[index * tall * wide : (index + 1) * tall * wide].astype(F32)
    main = main.reshape(tall, wide, LANES)
    cut = rim - trim
    tall_out = tall - 2 * cut
    frame[:, trim : trim + wide] = main[cut : cut + tall_out]
    first = size.main(rim)
    edges = block[first:].astype(F32)
    for j in range(2 * rim):
        col = j - cut if j < rim else j - rim + trim + wide
        if j < cut or (j >= rim and j - rim >= trim):
            continue
        start = (j * FRAMES + index) * step
        edge = edges[start + cut : start + cut + tall_out]
        frame[:, col : col + 1] = edge.reshape(tall_out, 1, LANES)
    for c in range(3):
        dst[at, :, :, c * LANES : (c + 1) * LANES] = frame[:, c : c + wo].astype(BF16)


def spread_all(size, rim, trim, wo, near, far, dst, frame):
    filled = size.wide + 2 * trim
    if frame.shape[1] > filled:
        frame[:, filled:] = jnp.zeros((frame.shape[0], frame.shape[1] - filled, LANES), F32)
    for f in range(dst.shape[0]):
        block = near if f < FRAMES else far
        spread_columns(size, rim, trim, wo, block, f % FRAMES, dst, f, frame)


def tap_dot(x, kernel, turned):
    ho, wo = x.shape[1] - 2, x.shape[2]
    count = ho * wo
    span = 9 * LANES

    def cells(f):
        return jnp.concatenate(
            [x[f, b : b + ho].reshape(count, 3 * LANES) for b in range(3)], 1
        )

    def taps(a):
        if not turned:
            return kernel[a * span : (a + 1) * span]
        last = (3 - a) * 9 - 1
        return jnp.concatenate(
            [kernel[(last - k) * LANES : (last - k + 1) * LANES] for k in range(9)], 1
        )

    dims = (((1,), (1 if turned else 0,)), ((), ()))

    def dot(f, *times):
        weights = [taps(a) for a in times]
        if len(weights) > 1:
            weights = [jnp.concatenate(weights, 0 if turned else 1)]
        return lax.dot_general(cells(f), weights[0], dims, preferred_element_type=F32)

    return dot


def convolved(x, kernel, turned):
    dot = tap_dot(x, kernel, turned)
    both = dot(1, 1, 0) + dot(2, 2, 1)
    return both[:, :LANES] + dot(0, 0), both[:, LANES:] + dot(3, 2)


def conv_scratch(size, trim, wo, frames=2 * FRAMES):
    tall = size.high + 2 * trim
    return [((frames, tall, wo, 3 * LANES), BF16), ((tall, up(wo + 2, 8), LANES), F32)]


def hidden_own_body(size, own, kernel, sums, x, frame):
    spread_all(size, 1, 1, size.wide, own, None, x, frame)
    dot = tap_dot(x, kernel, False)
    both = dot(0, 2, 1)
    sums[0] = both[:, :LANES]
    sums[1] = both[:, LANES:] + dot(1, 2)


def hidden_body(size, across, place, before, sums, kernel, hidden, slots, x, frame, flat):
    high, wide = size.high, size.wide
    spread_all(size, 1, 1, wide, before, None, x, frame)
    dot = tap_dot(x, kernel, False)
    both = dot(1, 1, 0)
    sums = (sums[0] + both[:, :LANES] + dot(0, 0), sums[1] + both[:, LANES:])
    rounded = [s.astype(BF16) for s in sums]
    for f in range(FRAMES):
        hidden[f] = rounded[f].reshape(high, wide, LANES)
    span = span_second(size)
    found = split3(measured([r.astype(F32) for r in rounded]))
    take_columns(size, ((hidden, 1),), flat)
    upper = place[0] == 0
    edges = [jnp.where(upper, r[size.cells - wide :], r[:wide]).astype(F32) for r in rounded]
    fill = jnp.zeros((span - FRAMES * wide, LANES), F32)
    edges = jnp.concatenate([*edges, fill] if fill.shape[0] else edges, 0)
    rest = jnp.zeros((slots.shape[1] - span - PARTS, LANES), F32)
    for peer in range(slots.shape[0]):
        col = peer % across
        side = jnp.where(col > place[1], flat[1], flat[0])
        content = jnp.where(col == place[1], edges, side)
        slots[peer] = jnp.concatenate([content, found, rest], 0).astype(BF16)


def grad_act_body(size, near, far, kernel_far, out, x, frame, kernel, sems):
    wo = x.shape[2]
    copy = pltpu.make_async_copy(kernel_far, kernel, sems.at[0])
    copy.start()
    spread_all(size, 2, 2, wo, near, far, x, frame)
    copy.wait()
    sums = convolved(x, kernel, True)
    for f in range(FRAMES):
        out[f] = sums[f].reshape(size.tall(), wo, LANES)[:, : size.broad()]


def crossed_sides(size, place, across, got):
    step, high = size.stride(1), size.high
    count = FRAMES * step
    upper = place[0] == 0
    row = lax.broadcasted_iota(jnp.int32, (count, LANES), 0)
    found = []
    for at, there in (
        (jnp.maximum(place[1] - 1, 0), place[1] > 0),
        (jnp.minimum(place[1] + 1, across - 1), place[1] < across - 1),
    ):
        block = got[place[0] * across + at, 0:count].astype(F32)
        cross = got[(1 - place[0]) * across + at, 0:count].astype(F32)
        for f in range(FRAMES):
            above = jnp.where(upper, 0.0, cross[f * step + high : f * step + high + 1])
            below = jnp.where(upper, cross[f * step + 1 : f * step + 2], 0.0)
            block = jnp.where(row == f * step, above, block)
            block = jnp.where(row == f * step + high + 1, below, block)
        found.append(jnp.where(there, block, 0.0))
    return found


def span_second(size):
    return up(max(FRAMES * size.wide, FRAMES * size.stride(1)), 16)


def sums_second_body(size, across, hidden, got, grad_act, norm, slots):
    high, wide = size.high, size.wide
    at = span_second(size)
    blocks = [join3(got[peer, at : at + PARTS]) for peer in range(got.shape[0])]
    found = concluded(blocks, size.cells)
    norm[...] = found
    firsts, seconds = [], []
    for f in range(FRAMES):
        own = hidden[f].astype(F32)
        normed = (own - found[f : f + 1][None]) * found[FRAMES + f : FRAMES + f + 1][None]
        sigmoid = logistic(normed)
        grad = grad_act[f, 1 : high + 1, 1 : wide + 1]
        grad = grad * sigmoid * (1.0 + normed * (1.0 - sigmoid))
        grad, normed = grad.reshape(size.cells, LANES), normed.reshape(size.cells, LANES)
        firsts.append(jnp.sum(grad, 0, keepdims=True))
        seconds.append(jnp.sum(grad * normed, 0, keepdims=True))
    sums = stat_block(firsts, seconds)
    for peer in range(slots.shape[0]):
        slots[peer] = sums


def act_second_body(
    size, across, place, hidden, got, grad_act, norm, act, q_far, z_far, frame, q, z, sems
):
    wide = size.wide
    step = size.stride(1)
    left_all, right_all = crossed_sides(size, place, across, got)
    ok = in_frame((size.tall(), size.broad(), LANES), place, across, size, 1)
    lefts, rights, copies = [], [], []
    frame[...] = jnp.zeros_like(frame)
    facing = (1 - place[0]) * across + place[1]
    for f in range(FRAMES):
        top, bottom = rim_rows(place, got[facing, f * wide : (f + 1) * wide].astype(F32))
        padded_frame(
            size,
            hidden[f].astype(F32),
            top,
            bottom,
            left_all[f * step : (f + 1) * step],
            right_all[f * step : (f + 1) * step],
            frame,
        )
        normed = (frame[...] - norm[f : f + 1][None]) * norm[FRAMES + f : FRAMES + f + 1][None]
        sigmoid = logistic(normed)
        frame[...] = jnp.where(ok, normed * sigmoid, 0.0)
        left, right = put_frame(size, frame, f, act)
        lefts.append(left)
        rights.append(right)
        z[f] = normed
        q[f] = grad_act[f] * sigmoid * (1.0 + normed * (1.0 - sigmoid))
        for k, (source, target) in enumerate(((q, q_far), (z, z_far))):
            copy = pltpu.make_async_copy(source.at[f], target.at[f], sems.at[2 * f + k])
            copy.start()
            copies.append(copy)
    put_sides(act, size.main(1), lefts + rights)
    for copy in copies:
        copy.wait()


def hidden_grad(size, across, place, q, z, got, norm, out, frame, arrive):
    peers = got.shape[0]
    total = got[0]
    for peer in range(1, peers):
        total = total + got[peer]
    means = lane_totals(total) / (size.cells * peers * (LANES // GROUPS))
    ok = in_frame((size.tall(), size.broad(), LANES), place, across, size, 1)
    lefts, rights = [], []
    for f in range(FRAMES):
        first, second = means[f : f + 1][None], means[FRAMES + f : FRAMES + f + 1][None]
        inv = norm[FRAMES + f : FRAMES + f + 1][None]
        arrive(f)
        frame[...] = jnp.where(ok, inv * (q[f] - first - z[f] * second), 0.0)
        left, right = put_frame(size, frame, f, out)
        lefts.append(left)
        rights.append(right)
    put_sides(out, size.main(1), lefts + rights)


def own_cells(size, block, f):
    start = (f * size.tall() + 1) * size.wide
    return block[start : start + size.cells]


def turned_cells(size, block, out):
    for f in range(FRAMES):
        cells = own_cells(size, block, f).astype(F32).T.astype(BF16)
        out[f * LANES : (f + 1) * LANES] = cells


def tap_sums(x, turned, b):
    ho, wo = x.shape[1] - 2, x.shape[2]

    def cells(f):
        return x[f, b : b + ho].reshape(ho * wo, 3 * LANES)

    def dot(one, two):
        return jnp.dot(one, two, preferred_element_type=F32)

    low = dot(turned[...], cells(1))
    high = dot(turned[...], cells(2))
    return (
        dot(turned[:LANES], cells(0)) + low[LANES:],
        low[:LANES] + high[LANES:],
        high[:LANES] + dot(turned[LANES:], cells(3)),
    )


def second_term_body(size, near, far, act, out_far, x, frame, turned, out, sems):
    spread_all(size, 2, 1, size.wide, near, far, x, frame)
    turned_cells(size, act, turned)
    span = 3 * LANES
    copies = []
    for b in range(3):
        for a, total in enumerate(tap_sums(x, turned, b)):
            for c in range(3):
                tap = ((2 - a) * 3 + 2 - b) * 3 + 2 - c
                rows = slice(tap * LANES, (tap + 1) * LANES)
                out[rows] = total[:, c * LANES : (c + 1) * LANES]
            rows = pl.ds(((2 - a) * 3 + 2 - b) * span, span)
            copy = pltpu.make_async_copy(out.at[rows], out_far.at[rows], sems.at[3 * b + a])
            copy.start()
            copies.append(copy)
    for copy in copies:
        copy.wait()


def first_term_body(
    size,
    across,
    place,
    got,
    norm,
    q_far,
    z_far,
    near_far,
    own_far,
    second_far,
    both,
    give,
    grad_far,
    x,
    frame,
    turned,
    grad,
    near,
    own,
    q,
    z,
    sems,
):
    pairs = [(q_far.at[f], q.at[f]) for f in range(FRAMES)]
    pairs += [(z_far.at[f], z.at[f]) for f in range(FRAMES)]
    pairs += [(near_far, near), (own_far, own)]
    copies = [
        pltpu.make_async_copy(source, target, sems.at[k])
        for k, (source, target) in enumerate(pairs)
    ]
    for k in (0, FRAMES, 1, FRAMES + 1, 2 * FRAMES, 2 * FRAMES + 1):
        copies[k].start()
    upper = place[0] == 0
    fetched = pltpu.make_async_copy(second_far, both.at[1], sems.at[len(pairs) + 1])
    fetched.start()

    def arrive(f):
        copies[f].wait()
        copies[FRAMES + f].wait()

    hidden_grad(size, across, place, q, z, got, norm, grad, frame, arrive)
    sent = pltpu.make_async_copy(grad, grad_far, sems.at[len(pairs)])
    sent.start()
    turned_cells(size, grad, turned)
    for copy in copies[2 * FRAMES :]:
        copy.wait()
    spread_all(size, 1, 1, size.wide, near, own, x, frame)
    fetched.wait()

    @pl.when(upper)
    def _():
        give[...] = both[1].astype(BF16)

    for b in range(3):
        for a, total in enumerate(tap_sums(x, turned, b)):
            rows = slice((a * 3 + b) * 3 * LANES, (a * 3 + b + 1) * 3 * LANES)
            both[0, rows] = total.T

    @pl.when(jnp.logical_not(upper))
    def _():
        give[...] = both[0].astype(BF16)

    sent.wait()


def result_body(size, near, far, kernel, features, out, x, frame):
    spread_all(size, 1, 1, size.wide, near, far, x, frame)
    sums = convolved(x, kernel, False)
    for f in range(FRAMES):
        total = features[f].astype(F32) + sums[f].reshape(size.high, size.wide, LANES)
        out[f] = total.astype(BF16)


def back_first_body(size, near, far, kernel, features, norm, q, sums, x, frame):
    spread_all(size, 1, 1, size.wide, near, far, x, frame)
    grads = convolved(x, kernel, True)
    firsts, seconds = [], []
    for f in range(FRAMES):
        values = features[f].astype(F32).reshape(size.cells, LANES)
        normed = (values - norm[f : f + 1]) * norm[FRAMES + f : FRAMES + f + 1]
        sigmoid = logistic(normed)
        grad = grads[f] * sigmoid * (1.0 + normed * (1.0 - sigmoid))
        q[f] = grad
        firsts.append(jnp.sum(grad, 0, keepdims=True))
        seconds.append(jnp.sum(grad * normed, 0, keepdims=True))
    sums[...] = stat_block(firsts, seconds)


def feature_grad_body(size, peers, features, out_grad, norm, q, got, out):
    total = join3(got[0])
    for peer in range(1, got.shape[0]):
        total = total + join3(got[peer])
    means = lane_totals(total) / (size.cells * peers * (LANES // GROUPS))
    for f in range(FRAMES):
        values = features[f].astype(F32).reshape(size.cells, LANES)
        inv = norm[FRAMES + f : FRAMES + f + 1]
        normed = (values - norm[f : f + 1]) * inv
        grad = inv * (q[f] - means[f : f + 1] - normed * means[FRAMES + f : FRAMES + f + 1])
        grad = out_grad[f].astype(F32) + grad.reshape(size.high, size.wide, LANES)
        out[f] = grad.astype(BF16)


def row_swap(values):
    return lax.ppermute(values, "row", [(0, 1), (1, 0)])


def later(values, by):
    peers = lax.axis_size("tm")
    pairs = [(i, i + by) for i in range(peers) if 0 <= i + by < peers]
    return lax.ppermute(values, "tm", pairs)


def sum_parts(stat):
    high = lax.reduce_precision(stat, 8, 7)
    rest = stat - high
    middle = lax.reduce_precision(rest, 8, 7)
    return jnp.concatenate([high, middle, rest - middle], 0).astype(BF16)


def total_of(got):
    total = got[0].astype(F32)
    for peer in range(1, got.shape[0]):
        total = total + got[peer].astype(F32)
    return total


def joined_body(place, both, got, out):
    share = out.shape[1]
    for peer in range(out.shape[0]):
        rows = slice(peer * share, (peer + 1) * share)
        out[peer] = (both[place[0], rows] + got[rows].astype(F32)).astype(BF16)


def shared_body(got, out, flat):
    rows, share = got.shape[1], out.shape[1]
    if flat.shape[0] > rows:
        flat[rows:] = jnp.zeros((flat.shape[0] - rows, LANES), F32)
    flat[:rows] = total_of(got)
    for peer in range(out.shape[0]):
        out[peer] = flat[peer * share : (peer + 1) * share].astype(BF16)


def finished_body(factor, got, out):
    total = (total_of(got) * factor).astype(BF16)
    for peer in range(out.shape[0]):
        out[peer] = total


def placed_body(rows, swapped, *refs):
    place, block, first, second, sems = refs[0], refs[1], *refs[-3:]

    def move(target):
        copies = [
            pltpu.make_async_copy(
                block.at[peer, pl.ds(0, rows)], target.at[pl.ds(peer * rows, rows)], sems.at[peer]
            )
            for peer in range(block.shape[0])
        ]
        for copy in copies:
            copy.start()
        for copy in copies:
            copy.wait()

    @pl.when(place[0] == swapped)
    def _():
        move(first)

    @pl.when(place[0] != swapped)
    def _():
        move(second)


def placed(place, block, swapped, rows, so_far):
    anywhere = pl.BlockSpec(memory_space=pl.ANY)
    shape = (rows * block.shape[0], LANES)
    return pl.pallas_call(
        functools.partial(placed_body, rows, swapped),
        out_shape=[jax.ShapeDtypeStruct(shape, BF16)] * 2,
        in_specs=[pl.BlockSpec(memory_space=pltpu.SMEM)] + [anywhere] * (1 + len(so_far)),
        out_specs=[anywhere, anywhere],
        input_output_aliases={2 + k: k for k in range(len(so_far))},
        scratch_shapes=[pltpu.SemaphoreType.DMA((block.shape[0],))],
        compiler_params=pltpu.CompilerParams(vmem_limit_bytes=1 << 20),
    )(place, block, *so_far)


def on_device(features, conv_first, conv_second, out_grad):
    frames, high, wide, chans = features.shape
    assert frames == FRAMES and chans == LANES and lax.axis_size("row") == 2
    size = Sizes(high, wide)
    across = lax.axis_size("col")
    peers = 2 * across
    factor = 1.0 / math.sqrt(size.cells * FRAMES * lax.axis_size("tm") * peers)
    place = jnp.stack([lax.axis_index("row"), lax.axis_index("col")]).astype(jnp.int32)
    taps = conv_first.shape
    first = conv_first.reshape(-1, LANES)
    second = conv_second.reshape(-1, LANES)
    work = 2 * first.size * size.cells * FRAMES
    part = functools.partial
    stat = ((STATS, LANES), F32)
    tall, broad = size.tall(), size.broad()
    frame = ((tall, broad, LANES), F32)

    edge = up(3 * FRAMES * wide + PARTS, 16)
    lines = up(FRAMES * size.stride(1) + 2 * FRAMES * size.stride(2) + PARTS, 16)
    flat = ((2, lines, LANES), F32)
    pay, stats, cols, features_near, grad_near = call(
        part(start_body, size),
        [((edge, LANES), BF16), stat, flat, (features.shape, BF16), (features.shape, BF16)],
        [place, features, out_grad],
        smem=1,
        far=2,
        sems=2 * FRAMES,
    )
    row_got = row_swap(pay)
    (slots,) = call(
        part(slots_body, size, (1, 2), across),
        [((across, lines, LANES), BF16)],
        [place, cols, row_got, stats],
        [flat],
        smem=1,
    )
    col_got = lax.all_to_all(slots, "col", 0, 0)
    block = ((size.rows(1), LANES), BF16)
    act_first, grad, norm_first = call(
        part(act_first_body, size, across),
        [block, ((size.rows(2), LANES), BF16), stat],
        [place, features_near, grad_near, row_got, col_got],
        [frame],
        smem=1,
    )
    grad_after = later(grad, -1)
    act_before = later(act_first, 1)

    edge = up(FRAMES * wide + PARTS, 16)
    (sums,) = call(
        part(hidden_own_body, size),
        [((FRAMES, size.cells, LANES), F32)],
        [act_first, first],
        conv_scratch(size, 1, wide, FRAMES),
        mib=12,
        flops=work // 2,
    )
    span = span_second(size)
    hidden, slots = call(
        part(hidden_body, size, across),
        [(features.shape, BF16), ((peers, up(span + PARTS, 16), LANES), BF16)],
        [place, act_before, sums, first],
        [*conv_scratch(size, 1, wide, FRAMES), ((2, span, LANES), F32)],
        smem=1,
        mib=12,
        flops=2 * work,
    )
    got = lax.all_to_all(slots, ("row", "col"), 0, 0)
    (grad_act,) = call(
        part(grad_act_body, size),
        [((FRAMES, tall, broad, LANES), F32)],
        [grad, grad_after, second],
        [*conv_scratch(size, 2, up(wide + 2, 16)), (second.shape, BF16)],
        far=1,
        sems=1,
        mib=18,
        flops=2 * work,
    )
    field = ((FRAMES, tall, broad, LANES), F32)
    norm_second, slots = call(
        part(sums_second_body, size, across),
        [stat, ((peers, STATS, LANES), F32)],
        [hidden, got, grad_act],
    )
    act_second, q, z = call(
        part(act_second_body, size, across),
        [block, field, field],
        [place, hidden, got, grad_act, norm_second],
        [frame, field, field],
        smem=1,
        sems=2 * FRAMES,
        beside=True,
        out_far=2,
    )
    got = lax.all_to_all(slots, ("row", "col"), 0, 0)
    turned = ((FRAMES * LANES, size.cells), BF16)
    (second_term,) = call(
        part(second_term_body, size),
        [(first.shape, F32)],
        [grad, grad_after, act_second],
        [*conv_scratch(size, 1, wide), turned, (first.shape, F32)],
        sems=9,
        mib=16,
        beside=True,
        out_far=1,
    )
    both, give, grad_second = call(
        part(first_term_body, size, across),
        [((2, *first.shape), F32), (first.shape, BF16), block],
        [place, got, norm_second, q, z, act_before, act_first, second_term],
        [*conv_scratch(size, 1, wide), turned, *[block] * 3, field, field],
        smem=1,
        far=5,
        sems=2 * FRAMES + 4,
        mib=20,
        flops=work,
        out_far=1,
    )
    give, late_grad, late_act = lax.optimization_barrier((give, grad_second, act_second))
    act_second_before = later(late_act, 1)
    grad_second_after = later(late_grad, -1)

    along = lax.axis_size("tm")
    rows = first.shape[0]
    by_col = rows // across
    (slots,) = call(
        joined_body,
        [((across, by_col, LANES), BF16)],
        [place, both, row_swap(give)],
        smem=1,
    )
    slots = lax.all_to_all(slots, "col", 0, 0)
    slots, grad_second_after = lax.optimization_barrier((slots, grad_second_after))
    share = up(by_col, 16 * along) // along
    (slots,) = call(
        shared_body,
        [((along, share, LANES), BF16)],
        [slots],
        [((along * share, LANES), F32)],
    )
    got = lax.all_to_all(slots, "tm", 0, 0)
    (result,) = call(
        part(result_body, size),
        [(features.shape, BF16)],
        [act_second_before, act_second, second, features],
        conv_scratch(size, 1, wide),
        mib=14,
        flops=work,
    )
    q, sums = call(
        part(back_first_body, size),
        [((FRAMES, size.cells, LANES), F32), stat],
        [grad_second, grad_second_after, first, features, norm_first],
        conv_scratch(size, 1, wide),
        mib=14,
        flops=work,
    )
    got, result = lax.optimization_barrier((got, result))
    (slots,) = call(part(finished_body, factor), [((along, share, LANES), BF16)], [got])
    done = lax.all_to_all(slots, "tm", 0, 0).reshape(-1, LANES)[:by_col]
    parts = sum_parts(sums + row_swap(sums))
    parts = jnp.pad(parts, ((0, -parts.shape[0] % 16), (0, 0)))
    done = jnp.concatenate([done, parts], 0)
    mine = lax.all_to_all(jnp.broadcast_to(done[None], (across, *done.shape)), "col", 0, 0)
    theirs = row_swap(mine)
    so_far = placed(place, mine, 0, by_col, [])
    first_grad, second_grad = placed(place, theirs, 1, by_col, so_far)
    (feature_grad,) = call(
        part(feature_grad_body, size, peers),
        [(features.shape, BF16)],
        [features, out_grad, norm_first, q, mine[:, by_col:]],
    )
    return (result, feature_grad, first_grad.reshape(taps), second_grad.reshape(taps))


def solution(mesh):
    in_specs = (P("tm", "row", "col", None), P(), P(), P("tm", "row", "col", None))
    out_specs = (P("tm", "row", "col", None), P("tm", "row", "col", None), P(), P())
    return jax.shard_map(
        on_device, mesh=mesh, in_specs=in_specs, out_specs=out_specs, check_vma=False
    )
```

```python
import functools
import math

import jax
import jax.numpy as jnp
from jax import lax
from jax.experimental import pallas as pl
from jax.experimental.pallas import tpu as pltpu
from jax.sharding import PartitionSpec as P

GROUPS = 32
EPSILON = 1e-06
F32 = jnp.float32
BF16 = jnp.bfloat16
LANES = 128
FRAMES = 2
STATS = 8
PARTS = 3 * STATS


def up(count, step):
    return -(-count // step) * step


class Sizes:
    def __init__(self, high, wide):
        self.high, self.wide = high, wide
        self.cells = high * wide

    def stride(self, rim):
        return up(self.high + 2 * rim, 8)

    def main(self, rim):
        return FRAMES * (self.high + 2 * rim) * self.wide

    def rows(self, rim):
        return up(self.main(rim) + 2 * rim * FRAMES * self.stride(rim), 16)

    def tall(self):
        return self.high + 2

    def broad(self):
        return up(self.wide + 2, 8)


def here():
    return lax.axis_index("row"), lax.axis_index("col")


def call(body, outs, args, scratch=(), placed=False, far=0, sems=0, mib=8, flops=0, beside=False, out_far=0):
    inner = body
    if placed:
        body = lambda *refs: inner(here(), *refs)
    specs = [pl.BlockSpec(memory_space=pltpu.VMEM)] * (len(args) - far)
    specs += [pl.BlockSpec(memory_space=pltpu.HBM)] * far
    near = len(args) - far
    args = [*args[:near], *(pltpu.with_memory_space_constraint(a, pltpu.HBM) for a in args[near:])]
    scratches = [pltpu.VMEM(shape, dtype) for shape, dtype in scratch]
    if sems:
        scratches.append(pltpu.SemaphoreType.DMA((sems,)))
    shapes = [jax.ShapeDtypeStruct(shape, dtype) for shape, dtype in outs]
    kept = len(outs) - out_far
    moved = sum(math.prod(a.shape) * a.dtype.itemsize for a in [*args, *shapes])
    moved = 0 if beside else moved
    return pl.pallas_call(
        body,
        out_shape=shapes[:kept] + [pltpu.HBM(o.shape, o.dtype) for o in shapes[kept:]],
        in_specs=specs,
        out_specs=[pl.BlockSpec(memory_space=pltpu.VMEM)] * kept
        + [pl.BlockSpec(memory_space=pltpu.HBM)] * out_far,
        scratch_shapes=scratches,
        cost_estimate=pl.CostEstimate(flops=flops, bytes_accessed=moved, transcendentals=0),
        compiler_params=pltpu.CompilerParams(vmem_limit_bytes=mib << 20),
    )(*args)


def logistic(values):
    return 0.5 * jnp.tanh(0.5 * values) + 0.5


def lane_totals(stat):
    lane = lax.broadcasted_iota(jnp.int32, stat.shape, 1)
    step = 1
    while step < LANES // GROUPS:
        ahead = pltpu.roll(stat, LANES - step, 1)
        behind = pltpu.roll(stat, step, 1)
        stat = stat + jnp.where((lane // step) % 2 == 0, ahead, behind)
        step *= 2
    return stat


def split3(stat):
    high = stat.astype(BF16).astype(F32)
    rest = stat - high
    middle = rest.astype(BF16).astype(F32)
    return jnp.concatenate([high, middle, rest - middle], 0)


def join3(parts):
    parts = parts.astype(F32)
    return parts[:STATS] + (parts[STATS : 2 * STATS] + parts[2 * STATS : PARTS])


def stat_block(first, second):
    rest = jnp.zeros((STATS - 2 * FRAMES, LANES), F32)
    return jnp.concatenate([*first, *second, rest], 0)


def measured(frames):
    means, squares = [], []
    for frame in frames:
        mean = jnp.sum(frame, 0, keepdims=True) / frame.shape[0]
        centred = frame - mean
        means.append(mean)
        squares.append(jnp.sum(centred * centred, 0, keepdims=True))
    return stat_block(means, squares)


def merged(one, two, cells):
    delta = one - two
    extra = (0.5 * cells) * delta * delta
    mean = 0.5 * (one[:FRAMES] + two[:FRAMES])
    square = one[FRAMES : 2 * FRAMES] + two[FRAMES : 2 * FRAMES] + extra[:FRAMES]
    return jnp.concatenate([mean, square, jnp.zeros((STATS - 2 * FRAMES, LANES), F32)], 0)


def concluded(blocks, cells):
    per_group = LANES // GROUPS
    mean = sum(blocks[1:], blocks[0])[:FRAMES]
    mean = lane_totals(mean) / (len(blocks) * per_group)
    total = jnp.zeros((FRAMES, LANES), F32)
    for block in blocks:
        off = block[:FRAMES] - mean
        total = total + block[FRAMES : 2 * FRAMES] + cells * off * off
    spread = lane_totals(total) / (cells * len(blocks) * per_group)
    rest = jnp.zeros((STATS - 2 * FRAMES, LANES), F32)
    return jnp.concatenate([mean, lax.rsqrt(spread + EPSILON), rest], 0)


def rim_rows(place, got):
    upper = place[0] == 0
    nothing = jnp.zeros_like(got)
    return jnp.where(upper, nothing, got), jnp.where(upper, got, nothing)


def in_frame(shape, place, across, size, rim):
    row = lax.broadcasted_iota(jnp.int32, shape, 0)
    col = lax.broadcasted_iota(jnp.int32, shape, 1)
    top = jnp.where(place[0] == 0, rim, 0)
    bottom = jnp.where(place[0] == 0, size.high + 2 * rim, size.high + rim)
    left = jnp.where(place[1] == 0, rim, 0)
    right = jnp.where(place[1] == across - 1, size.wide + rim, size.wide + 2 * rim)
    return (row >= top) & (row < bottom) & (col >= left) & (col < right)


def take_columns(size, arrays, flat):
    flat[...] = jnp.zeros_like(flat)
    at = 0
    for array, rim in arrays:
        for j in range(rim):
            for frame in range(FRAMES):
                for side, col in ((0, j), (1, size.wide - rim + j)):
                    rows = array[frame, :, col : col + 1].astype(F32)
                    rows = rows.reshape(size.high, LANES)
                    flat[side, at + rim : at + rim + size.high] = rows
                at += size.stride(rim)


def start_body(
    size, place, features_far, grad_far, pay, stats, flat, features, out_grad, sems
):
    high, wide = size.high, size.wide
    upper = place[0] == 0
    copies = [
        pltpu.make_async_copy(source.at[f], target.at[f], sems.at[FRAMES * k + f])
        for k, (source, target) in enumerate(((features_far, features), (grad_far, out_grad)))
        for f in range(FRAMES)
    ]
    for copy in copies:
        copy.start()
    for copy in copies[:FRAMES]:
        copy.wait()
    at = 0
    for frame in range(FRAMES):
        pay[at : at + wide] = jnp.where(upper, features[frame, high - 1], features[frame, 0])
        at += wide
    found = measured([features[f].astype(F32).reshape(size.cells, LANES) for f in range(FRAMES)])
    stats[...] = found
    for copy in copies[FRAMES:]:
        copy.wait()
    for frame in range(FRAMES):
        for row in range(2):
            edge = jnp.where(upper, out_grad[frame, high - 2 + row], out_grad[frame, row])
            pay[at : at + wide] = edge
            at += wide
    fill = jnp.zeros((pay.shape[0] - at - PARTS, LANES), F32)
    pay[at:] = jnp.concatenate([split3(found), fill], 0).astype(BF16)
    take_columns(size, ((features, 1), (out_grad, 2)), flat)


def slots_body(size, rims, across, place, flat, got, stats, slots, work):
    wide, high = size.wide, size.high
    upper = place[0] == 0
    work[...] = flat[...]
    at = base = 0
    for rim in rims:
        for j in range(rim):
            for frame in range(FRAMES):
                for row in range(rim):
                    start = base + (frame * rim + row) * wide
                    for side, col in ((0, j), (1, wide - rim + j)):
                        cell = start - start % 16 + 16 * ((start % 16 + col) // 16)
                        tile = got[cell : cell + 16].astype(F32)
                        edge = tile[start + col - cell : start + col - cell + 1]
                        nothing = jnp.zeros_like(edge)
                        top, bottom = at + row, at + rim + high + row
                        work[side, top : top + 1] = jnp.where(upper, nothing, edge)
                        work[side, bottom : bottom + 1] = jnp.where(upper, edge, nothing)
                at += size.stride(rim)
        base += FRAMES * rim * wide
    parts = split3(merged(stats[...], join3(got[base : base + PARTS]), size.cells))
    work[0, at : at + PARTS] = parts
    work[1, at : at + PARTS] = parts
    for peer in range(across):
        slots[peer] = jnp.where(peer > place[1], work[1], work[0]).astype(BF16)


def sides(place, across, got, first, count):
    left = got[jnp.maximum(place[1] - 1, 0), first : first + count].astype(F32)
    right = got[jnp.minimum(place[1] + 1, across - 1), first : first + count].astype(F32)
    nothing = jnp.zeros_like(left)
    left = jnp.where(place[1] > 0, left, nothing)
    right = jnp.where(place[1] < across - 1, right, nothing)
    return left, right


def padded_frame(size, own, top, bottom, left, right, frame):
    high, wide = size.high, size.wide
    frame[1 : high + 1, 1 : wide + 1] = own
    frame[0:1, 1 : wide + 1] = top[None]
    frame[high + 1 : high + 2, 1 : wide + 1] = bottom[None]
    tall = high + 2
    frame[:, 0:1] = left[:tall].reshape(tall, 1, LANES)
    frame[:, wide + 1 : wide + 2] = right[:tall].reshape(tall, 1, LANES)


def put_frame(size, frame, index, out):
    wide, tall, step = size.wide, size.tall(), size.stride(1)
    flat = frame[:, 1 : wide + 1].reshape(tall * wide, LANES)
    out[index * tall * wide : (index + 1) * tall * wide] = flat.astype(BF16)
    fill = jnp.zeros((step - tall, LANES), F32)
    left = frame[:, 0:1].reshape(tall, LANES)
    right = frame[:, wide + 1 : wide + 2].reshape(tall, LANES)
    return jnp.concatenate([left, fill], 0), jnp.concatenate([right, fill], 0)


def put_sides(out, first, blocks):
    fill = out.shape[0] - first - sum(b.shape[0] for b in blocks)
    if fill:
        blocks = [*blocks, jnp.zeros((fill, LANES), F32)]
    out[first:] = jnp.concatenate(blocks, 0).astype(BF16)


def act_first_body(
    size, across, place, features, out_grad, row_got, col_got, act, grad, norm, frame
):
    high, wide = size.high, size.wide
    at = FRAMES * size.stride(1) + 2 * FRAMES * size.stride(2)
    blocks = [join3(col_got[peer, at : at + PARTS]) for peer in range(across)]
    found = concluded(blocks, 2 * size.cells)
    norm[...] = found
    step = size.stride(1)
    left_all, right_all = sides(place, across, col_got, 0, FRAMES * step)
    ok = in_frame((size.tall(), size.broad(), LANES), place, across, size, 1)
    lefts, rights = [], []
    frame[...] = jnp.zeros_like(frame)
    for f in range(FRAMES):
        top, bottom = rim_rows(place, row_got[f * wide : (f + 1) * wide].astype(F32))
        padded_frame(
            size,
            features[f].astype(F32),
            top,
            bottom,
            left_all[f * step : (f + 1) * step],
            right_all[f * step : (f + 1) * step],
            frame,
        )
        normed = (frame[...] - found[f : f + 1][None]) * found[FRAMES + f : FRAMES + f + 1][None]
        frame[...] = jnp.where(ok, normed * logistic(normed), 0.0)
        left, right = put_frame(size, frame, f, act)
        lefts.append(left)
        rights.append(right)
    put_sides(act, size.main(1), lefts + rights)

    tall = high + 4
    for f in range(FRAMES):
        start = f * tall * wide
        for row in range(2):
            first = FRAMES * wide + (f * 2 + row) * wide
            top, bottom = rim_rows(place, row_got[first : first + wide])
            grad[start + row * wide : start + (row + 1) * wide] = top
            below = start + (high + 2 + row) * wide
            grad[below : below + wide] = bottom
        grad[start + 2 * wide : start + (high + 2) * wide] = out_grad[f].reshape(
            size.cells, LANES
        )
    left, right = sides(
        place, across, col_got, FRAMES * step, 2 * FRAMES * size.stride(2)
    )
    put_sides(grad, size.main(2), [left, right])


def spread_columns(size, rim, trim, wo, block, index, dst, at, frame):
    wide, high = size.wide, size.high
    tall, step = high + 2 * rim, size.stride(rim)
    main = block[index * tall * wide : (index + 1) * tall * wide].astype(F32)
    main = main.reshape(tall, wide, LANES)
    cut = rim - trim
    tall_out = tall - 2 * cut
    frame[:, trim : trim + wide] = main[cut : cut + tall_out]
    first = size.main(rim)
    edges = block[first:].astype(F32)
    for j in range(2 * rim):
        col = j - cut if j < rim else j - rim + trim + wide
        if j < cut or (j >= rim and j - rim >= trim):
            continue
        start = (j * FRAMES + index) * step
        edge = edges[start + cut : start + cut + tall_out]
        frame[:, col : col + 1] = edge.reshape(tall_out, 1, LANES)
    for c in range(3):
        dst[at, :, :, c * LANES : (c + 1) * LANES] = frame[:, c : c + wo].astype(BF16)


def spread_all(size, rim, trim, wo, near, far, dst, frame):
    filled = size.wide + 2 * trim
    if frame.shape[1] > filled:
        frame[:, filled:] = jnp.zeros((frame.shape[0], frame.shape[1] - filled, LANES), F32)
    for f in range(dst.shape[0]):
        block = near if f < FRAMES else far
        spread_columns(size, rim, trim, wo, block, f % FRAMES, dst, f, frame)


def tap_dot(x, kernel, turned):
    ho, wo = x.shape[1] - 2, x.shape[2]
    count = ho * wo
    span = 9 * LANES

    def cells(f):
        return jnp.concatenate(
            [x[f, b : b + ho].reshape(count, 3 * LANES) for b in range(3)], 1
        )

    def taps(a):
        if not turned:
            return kernel[a * span : (a + 1) * span]
        last = (3 - a) * 9 - 1
        return jnp.concatenate(
            [kernel[(last - k) * LANES : (last - k + 1) * LANES] for k in range(9)], 1
        )

    dims = (((1,), (1 if turned else 0,)), ((), ()))

    def dot(f, *times):
        weights = [taps(a) for a in times]
        if len(weights) > 1:
            weights = [jnp.concatenate(weights, 0 if turned else 1)]
        return lax.dot_general(cells(f), weights[0], dims, preferred_element_type=F32)

    return dot


def convolved(x, kernel, turned):
    dot = tap_dot(x, kernel, turned)
    both = dot(1, 1, 0) + dot(2, 2, 1)
    return both[:, :LANES] + dot(0, 0), both[:, LANES:] + dot(3, 2)


def conv_scratch(size, trim, wo, frames=2 * FRAMES):
    tall = size.high + 2 * trim
    return [((frames, tall, wo, 3 * LANES), BF16), ((tall, up(wo + 2, 8), LANES), F32)]


def hidden_own_body(size, own, kernel, sums, x, frame):
    spread_all(size, 1, 1, size.wide, own, None, x, frame)
    dot = tap_dot(x, kernel, False)
    both = dot(0, 2, 1)
    sums[0] = both[:, :LANES]
    sums[1] = both[:, LANES:] + dot(1, 2)


def hidden_body(size, across, place, before, sums, kernel, hidden, slots, x, frame, flat):
    high, wide = size.high, size.wide
    spread_all(size, 1, 1, wide, before, None, x, frame)
    dot = tap_dot(x, kernel, False)
    both = dot(1, 1, 0)
    sums = (sums[0] + both[:, :LANES] + dot(0, 0), sums[1] + both[:, LANES:])
    rounded = [s.astype(BF16) for s in sums]
    for f in range(FRAMES):
        hidden[f] = rounded[f].reshape(high, wide, LANES)
    span = span_second(size)
    found = split3(measured([r.astype(F32) for r in rounded]))
    take_columns(size, ((hidden, 1),), flat)
    upper = place[0] == 0
    edges = [jnp.where(upper, r[size.cells - wide :], r[:wide]).astype(F32) for r in rounded]
    fill = jnp.zeros((span - FRAMES * wide, LANES), F32)
    edges = jnp.concatenate([*edges, fill] if fill.shape[0] else edges, 0)
    rest = jnp.zeros((slots.shape[1] - span - PARTS, LANES), F32)
    for peer in range(slots.shape[0]):
        col = peer % across
        side = jnp.where(col > place[1], flat[1], flat[0])
        content = jnp.where(col == place[1], edges, side)
        slots[peer] = jnp.concatenate([content, found, rest], 0).astype(BF16)


def grad_act_body(size, near, far, kernel_far, out, x, frame, kernel, sems):
    wo = x.shape[2]
    copy = pltpu.make_async_copy(kernel_far, kernel, sems.at[0])
    copy.start()
    spread_all(size, 2, 2, wo, near, far, x, frame)
    copy.wait()
    sums = convolved(x, kernel, True)
    for f in range(FRAMES):
        out[f] = sums[f].reshape(size.tall(), wo, LANES)[:, : size.broad()]


def crossed_sides(size, place, across, got):
    step, high = size.stride(1), size.high
    count = FRAMES * step
    upper = place[0] == 0
    row = lax.broadcasted_iota(jnp.int32, (count, LANES), 0)
    found = []
    for at, there in (
        (jnp.maximum(place[1] - 1, 0), place[1] > 0),
        (jnp.minimum(place[1] + 1, across - 1), place[1] < across - 1),
    ):
        block = got[place[0] * across + at, 0:count].astype(F32)
        cross = got[(1 - place[0]) * across + at, 0:count].astype(F32)
        for f in range(FRAMES):
            above = jnp.where(upper, 0.0, cross[f * step + high : f * step + high + 1])
            below = jnp.where(upper, cross[f * step + 1 : f * step + 2], 0.0)
            block = jnp.where(row == f * step, above, block)
            block = jnp.where(row == f * step + high + 1, below, block)
        found.append(jnp.where(there, block, 0.0))
    return found


def span_second(size):
    return up(max(FRAMES * size.wide, FRAMES * size.stride(1)), 16)


def sums_second_body(size, across, hidden, got, grad_act, norm, slots):
    high, wide = size.high, size.wide
    at = span_second(size)
    blocks = [join3(got[peer, at : at + PARTS]) for peer in range(got.shape[0])]
    found = concluded(blocks, size.cells)
    norm[...] = found
    firsts, seconds = [], []
    for f in range(FRAMES):
        own = hidden[f].astype(F32)
        normed = (own - found[f : f + 1][None]) * found[FRAMES + f : FRAMES + f + 1][None]
        sigmoid = logistic(normed)
        grad = grad_act[f, 1 : high + 1, 1 : wide + 1]
        grad = grad * sigmoid * (1.0 + normed * (1.0 - sigmoid))
        grad, normed = grad.reshape(size.cells, LANES), normed.reshape(size.cells, LANES)
        firsts.append(jnp.sum(grad, 0, keepdims=True))
        seconds.append(jnp.sum(grad * normed, 0, keepdims=True))
    sums = stat_block(firsts, seconds)
    for peer in range(slots.shape[0]):
        slots[peer] = sums


def act_second_body(
    size, across, place, hidden, got, grad_act, norm, act, q_far, z_far, frame, q, z, sems
):
    wide = size.wide
    step = size.stride(1)
    left_all, right_all = crossed_sides(size, place, across, got)
    ok = in_frame((size.tall(), size.broad(), LANES), place, across, size, 1)
    lefts, rights, copies = [], [], []
    frame[...] = jnp.zeros_like(frame)
    facing = (1 - place[0]) * across + place[1]
    for f in range(FRAMES):
        top, bottom = rim_rows(place, got[facing, f * wide : (f + 1) * wide].astype(F32))
        padded_frame(
            size,
            hidden[f].astype(F32),
            top,
            bottom,
            left_all[f * step : (f + 1) * step],
            right_all[f * step : (f + 1) * step],
            frame,
        )
        normed = (frame[...] - norm[f : f + 1][None]) * norm[FRAMES + f : FRAMES + f + 1][None]
        sigmoid = logistic(normed)
        frame[...] = jnp.where(ok, normed * sigmoid, 0.0)
        left, right = put_frame(size, frame, f, act)
        lefts.append(left)
        rights.append(right)
        z[f] = normed
        q[f] = grad_act[f] * sigmoid * (1.0 + normed * (1.0 - sigmoid))
        for k, (source, target) in enumerate(((q, q_far), (z, z_far))):
            copy = pltpu.make_async_copy(source.at[f], target.at[f], sems.at[2 * f + k])
            copy.start()
            copies.append(copy)
    put_sides(act, size.main(1), lefts + rights)
    for copy in copies:
        copy.wait()


def hidden_grad(size, across, place, q, z, got, norm, out, frame, arrive):
    peers = got.shape[0]
    total = got[0]
    for peer in range(1, peers):
        total = total + got[peer]
    means = lane_totals(total) / (size.cells * peers * (LANES // GROUPS))
    ok = in_frame((size.tall(), size.broad(), LANES), place, across, size, 1)
    lefts, rights = [], []
    for f in range(FRAMES):
        first, second = means[f : f + 1][None], means[FRAMES + f : FRAMES + f + 1][None]
        inv = norm[FRAMES + f : FRAMES + f + 1][None]
        arrive(f)
        frame[...] = jnp.where(ok, inv * (q[f] - first - z[f] * second), 0.0)
        left, right = put_frame(size, frame, f, out)
        lefts.append(left)
        rights.append(right)
    put_sides(out, size.main(1), lefts + rights)


def own_cells(size, block, f):
    start = (f * size.tall() + 1) * size.wide
    return block[start : start + size.cells]


def turned_cells(size, block, out):
    for f in range(FRAMES):
        cells = own_cells(size, block, f).astype(F32).T.astype(BF16)
        out[f * LANES : (f + 1) * LANES] = cells


def tap_sums(x, turned, b):
    ho, wo = x.shape[1] - 2, x.shape[2]

    def cells(f):
        return x[f, b : b + ho].reshape(ho * wo, 3 * LANES)

    def dot(one, two):
        return jnp.dot(one, two, preferred_element_type=F32)

    low = dot(turned[...], cells(1))
    high = dot(turned[...], cells(2))
    return (
        dot(turned[:LANES], cells(0)) + low[LANES:],
        low[:LANES] + high[LANES:],
        high[:LANES] + dot(turned[LANES:], cells(3)),
    )


def second_term_body(size, near, far, act, out_far, x, frame, turned, out, sems):
    spread_all(size, 2, 1, size.wide, near, far, x, frame)
    turned_cells(size, act, turned)
    span = 3 * LANES
    copies = []
    for b in range(3):
        for a, total in enumerate(tap_sums(x, turned, b)):
            for c in range(3):
                tap = ((2 - a) * 3 + 2 - b) * 3 + 2 - c
                rows = slice(tap * LANES, (tap + 1) * LANES)
                out[rows] = total[:, c * LANES : (c + 1) * LANES]
            rows = pl.ds(((2 - a) * 3 + 2 - b) * span, span)
            copy = pltpu.make_async_copy(out.at[rows], out_far.at[rows], sems.at[3 * b + a])
            copy.start()
            copies.append(copy)
    for copy in copies:
        copy.wait()


def first_term_body(
    size,
    across,
    place,
    got,
    norm,
    q_far,
    z_far,
    near_far,
    own_far,
    second_far,
    both,
    give,
    grad_far,
    x,
    frame,
    turned,
    grad,
    near,
    own,
    q,
    z,
    sems,
):
    pairs = [(q_far.at[f], q.at[f]) for f in range(FRAMES)]
    pairs += [(z_far.at[f], z.at[f]) for f in range(FRAMES)]
    pairs += [(near_far, near), (own_far, own)]
    copies = [
        pltpu.make_async_copy(source, target, sems.at[k])
        for k, (source, target) in enumerate(pairs)
    ]
    for k in (0, FRAMES, 1, FRAMES + 1, 2 * FRAMES, 2 * FRAMES + 1):
        copies[k].start()
    upper = place[0] == 0
    fetched = pltpu.make_async_copy(second_far, both.at[1], sems.at[len(pairs) + 1])
    fetched.start()

    def arrive(f):
        copies[f].wait()
        copies[FRAMES + f].wait()

    hidden_grad(size, across, place, q, z, got, norm, grad, frame, arrive)
    sent = pltpu.make_async_copy(grad, grad_far, sems.at[len(pairs)])
    sent.start()
    turned_cells(size, grad, turned)
    for copy in copies[2 * FRAMES :]:
        copy.wait()
    spread_all(size, 1, 1, size.wide, near, own, x, frame)
    fetched.wait()

    @pl.when(upper)
    def _():
        give[...] = both[1].astype(BF16)

    for b in range(3):
        for a, total in enumerate(tap_sums(x, turned, b)):
            rows = slice((a * 3 + b) * 3 * LANES, (a * 3 + b + 1) * 3 * LANES)
            both[0, rows] = total.T

    @pl.when(jnp.logical_not(upper))
    def _():
        give[...] = both[0].astype(BF16)

    sent.wait()


def result_body(size, near, far, kernel, features, out, x, frame):
    spread_all(size, 1, 1, size.wide, near, far, x, frame)
    sums = convolved(x, kernel, False)
    for f in range(FRAMES):
        total = features[f].astype(F32) + sums[f].reshape(size.high, size.wide, LANES)
        out[f] = total.astype(BF16)


def back_first_body(size, near, far, kernel, features, norm, q, sums, x, frame):
    spread_all(size, 1, 1, size.wide, near, far, x, frame)
    grads = convolved(x, kernel, True)
    firsts, seconds = [], []
    for f in range(FRAMES):
        values = features[f].astype(F32).reshape(size.cells, LANES)
        normed = (values - norm[f : f + 1]) * norm[FRAMES + f : FRAMES + f + 1]
        sigmoid = logistic(normed)
        grad = grads[f] * sigmoid * (1.0 + normed * (1.0 - sigmoid))
        q[f] = grad
        firsts.append(jnp.sum(grad, 0, keepdims=True))
        seconds.append(jnp.sum(grad * normed, 0, keepdims=True))
    sums[...] = stat_block(firsts, seconds)


def feature_grad_body(size, peers, features, out_grad, norm, q, got, out):
    total = join3(got[0])
    for peer in range(1, got.shape[0]):
        total = total + join3(got[peer])
    means = lane_totals(total) / (size.cells * peers * (LANES // GROUPS))
    for f in range(FRAMES):
        values = features[f].astype(F32).reshape(size.cells, LANES)
        inv = norm[FRAMES + f : FRAMES + f + 1]
        normed = (values - norm[f : f + 1]) * inv
        grad = inv * (q[f] - means[f : f + 1] - normed * means[FRAMES + f : FRAMES + f + 1])
        grad = out_grad[f].astype(F32) + grad.reshape(size.high, size.wide, LANES)
        out[f] = grad.astype(BF16)


def row_swap(values):
    return lax.ppermute(values, "row", [(0, 1), (1, 0)])


def later(values, by):
    peers = lax.axis_size("tm")
    pairs = [(i, i + by) for i in range(peers) if 0 <= i + by < peers]
    return lax.ppermute(values, "tm", pairs)


def sum_parts(stat):
    high = lax.reduce_precision(stat, 8, 7)
    rest = stat - high
    middle = lax.reduce_precision(rest, 8, 7)
    return jnp.concatenate([high, middle, rest - middle], 0).astype(BF16)


def total_of(got):
    total = got[0].astype(F32)
    for peer in range(1, got.shape[0]):
        total = total + got[peer].astype(F32)
    return total


def joined_body(place, both, got, out):
    share = out.shape[1]
    for peer in range(out.shape[0]):
        rows = slice(peer * share, (peer + 1) * share)
        out[peer] = (both[place[0], rows] + got[rows].astype(F32)).astype(BF16)


def shared_body(got, out, flat):
    rows, share = got.shape[1], out.shape[1]
    if flat.shape[0] > rows:
        flat[rows:] = jnp.zeros((flat.shape[0] - rows, LANES), F32)
    flat[:rows] = total_of(got)
    for peer in range(out.shape[0]):
        out[peer] = flat[peer * share : (peer + 1) * share].astype(BF16)


def finished_body(factor, got, out):
    total = (total_of(got) * factor).astype(BF16)
    for peer in range(out.shape[0]):
        out[peer] = total


def placed_body(rows, swapped, *refs):
    block, first, second, sems = refs[0], *refs[-3:]
    place = here()

    def move(target):
        copies = [
            pltpu.make_async_copy(
                block.at[peer, pl.ds(0, rows)], target.at[pl.ds(peer * rows, rows)], sems.at[peer]
            )
            for peer in range(block.shape[0])
        ]
        for copy in copies:
            copy.start()
        for copy in copies:
            copy.wait()

    @pl.when(place[0] == swapped)
    def _():
        move(first)

    @pl.when(place[0] != swapped)
    def _():
        move(second)


def deliver(block, swapped, rows, so_far):
    anywhere = pl.BlockSpec(memory_space=pl.ANY)
    shape = (rows * block.shape[0], LANES)
    return pl.pallas_call(
        functools.partial(placed_body, rows, swapped),
        out_shape=[jax.ShapeDtypeStruct(shape, BF16)] * 2,
        in_specs=[anywhere] * (1 + len(so_far)),
        out_specs=[anywhere, anywhere],
        input_output_aliases={1 + k: k for k in range(len(so_far))},
        scratch_shapes=[pltpu.SemaphoreType.DMA((block.shape[0],))],
        compiler_params=pltpu.CompilerParams(vmem_limit_bytes=1 << 20),
    )(block, *so_far)


def on_device(features, conv_first, conv_second, out_grad):
    frames, high, wide, chans = features.shape
    assert frames == FRAMES and chans == LANES and lax.axis_size("row") == 2
    size = Sizes(high, wide)
    across = lax.axis_size("col")
    peers = 2 * across
    factor = 1.0 / math.sqrt(size.cells * FRAMES * lax.axis_size("tm") * peers)
    taps = conv_first.shape
    first = conv_first.reshape(-1, LANES)
    second = conv_second.reshape(-1, LANES)
    work = 2 * first.size * size.cells * FRAMES
    part = functools.partial
    stat = ((STATS, LANES), F32)
    tall, broad = size.tall(), size.broad()
    frame = ((tall, broad, LANES), F32)

    edge = up(3 * FRAMES * wide + PARTS, 16)
    lines = up(FRAMES * size.stride(1) + 2 * FRAMES * size.stride(2) + PARTS, 16)
    flat = ((2, lines, LANES), F32)
    pay, stats, cols, features_near, grad_near = call(
        part(start_body, size),
        [((edge, LANES), BF16), stat, flat, (features.shape, BF16), (features.shape, BF16)],
        [features, out_grad],
        placed=True,
        far=2,
        sems=2 * FRAMES,
    )
    row_got = row_swap(pay)
    (slots,) = call(
        part(slots_body, size, (1, 2), across),
        [((across, lines, LANES), BF16)],
        [cols, row_got, stats],
        [flat],
        placed=True,
    )
    col_got = lax.all_to_all(slots, "col", 0, 0)
    block = ((size.rows(1), LANES), BF16)
    act_first, grad, norm_first = call(
        part(act_first_body, size, across),
        [block, ((size.rows(2), LANES), BF16), stat],
        [features_near, grad_near, row_got, col_got],
        [frame],
        placed=True,
    )
    grad_after = later(grad, -1)
    act_before = later(act_first, 1)

    edge = up(FRAMES * wide + PARTS, 16)
    (sums,) = call(
        part(hidden_own_body, size),
        [((FRAMES, size.cells, LANES), F32)],
        [act_first, first],
        conv_scratch(size, 1, wide, FRAMES),
        mib=12,
        flops=work // 2,
    )
    span = span_second(size)
    hidden, slots = call(
        part(hidden_body, size, across),
        [(features.shape, BF16), ((peers, up(span + PARTS, 16), LANES), BF16)],
        [act_before, sums, first],
        [*conv_scratch(size, 1, wide, FRAMES), ((2, span, LANES), F32)],
        placed=True,
        mib=12,
        flops=2 * work,
    )
    got = lax.all_to_all(slots, ("row", "col"), 0, 0)
    (grad_act,) = call(
        part(grad_act_body, size),
        [((FRAMES, tall, broad, LANES), F32)],
        [grad, grad_after, second],
        [*conv_scratch(size, 2, up(wide + 2, 16)), (second.shape, BF16)],
        far=1,
        sems=1,
        mib=18,
        flops=2 * work,
    )
    field = ((FRAMES, tall, broad, LANES), F32)
    norm_second, slots = call(
        part(sums_second_body, size, across),
        [stat, ((peers, STATS, LANES), F32)],
        [hidden, got, grad_act],
    )
    act_second, q, z = call(
        part(act_second_body, size, across),
        [block, field, field],
        [hidden, got, grad_act, norm_second],
        [frame, field, field],
        placed=True,
        sems=2 * FRAMES,
        beside=True,
        out_far=2,
    )
    got = lax.all_to_all(slots, ("row", "col"), 0, 0)
    turned = ((FRAMES * LANES, size.cells), BF16)
    (second_term,) = call(
        part(second_term_body, size),
        [(first.shape, F32)],
        [grad, grad_after, act_second],
        [*conv_scratch(size, 1, wide), turned, (first.shape, F32)],
        sems=9,
        mib=16,
        beside=True,
        out_far=1,
    )
    both, give, grad_second = call(
        part(first_term_body, size, across),
        [((2, *first.shape), F32), (first.shape, BF16), block],
        [got, norm_second, q, z, act_before, act_first, second_term],
        [*conv_scratch(size, 1, wide), turned, *[block] * 3, field, field],
        placed=True,
        far=5,
        sems=2 * FRAMES + 4,
        mib=20,
        flops=work,
        out_far=1,
    )
    give, late_grad, late_act = lax.optimization_barrier((give, grad_second, act_second))
    act_second_before = later(late_act, 1)
    grad_second_after = later(late_grad, -1)

    along = lax.axis_size("tm")
    rows = first.shape[0]
    by_col = rows // across
    (slots,) = call(
        joined_body,
        [((across, by_col, LANES), BF16)],
        [both, row_swap(give)],
        placed=True,
    )
    slots = lax.all_to_all(slots, "col", 0, 0)
    slots, grad_second_after = lax.optimization_barrier((slots, grad_second_after))
    share = up(by_col, 16 * along) // along
    (slots,) = call(
        shared_body,
        [((along, share, LANES), BF16)],
        [slots],
        [((along * share, LANES), F32)],
    )
    got = lax.all_to_all(slots, "tm", 0, 0)
    (result,) = call(
        part(result_body, size),
        [(features.shape, BF16)],
        [act_second_before, act_second, second, features],
        conv_scratch(size, 1, wide),
        mib=14,
        flops=work,
    )
    q, sums = call(
        part(back_first_body, size),
        [((FRAMES, size.cells, LANES), F32), stat],
        [grad_second, grad_second_after, first, features, norm_first],
        conv_scratch(size, 1, wide),
        mib=14,
        flops=work,
    )
    got, result = lax.optimization_barrier((got, result))
    (slots,) = call(part(finished_body, factor), [((along, share, LANES), BF16)], [got])
    done = lax.all_to_all(slots, "tm", 0, 0).reshape(-1, LANES)[:by_col]
    parts = sum_parts(sums + row_swap(sums))
    parts = jnp.pad(parts, ((0, -parts.shape[0] % 16), (0, 0)))
    done = jnp.concatenate([done, parts], 0)
    mine = lax.all_to_all(jnp.broadcast_to(done[None], (across, *done.shape)), "col", 0, 0)
    theirs = row_swap(mine)
    so_far = deliver(mine, 0, by_col, [])
    first_grad, second_grad = deliver(theirs, 1, by_col, so_far)
    (feature_grad,) = call(
        part(feature_grad_body, size, peers),
        [(features.shape, BF16)],
        [features, out_grad, norm_first, q, mine[:, by_col:]],
    )
    return (result, feature_grad, first_grad.reshape(taps), second_grad.reshape(taps))


def solution(mesh):
    in_specs = (P("tm", "row", "col", None), P(), P(), P("tm", "row", "col", None))
    out_specs = (P("tm", "row", "col", None), P("tm", "row", "col", None), P(), P())
    return jax.shard_map(
        on_device, mesh=mesh, in_specs=in_specs, out_specs=out_specs, check_vma=False
    )
```

```python
import functools
import math

import jax
import jax.numpy as jnp
from jax import lax
from jax.experimental import pallas as pl
from jax.experimental.pallas import tpu as pltpu
from jax.sharding import PartitionSpec as P

GROUPS = 32
EPSILON = 1e-06
F32 = jnp.float32
BF16 = jnp.bfloat16
LANES = 128
FRAMES = 2
STATS = 8
PARTS = 3 * STATS


def up(count, step):
    return -(-count // step) * step


class Sizes:
    def __init__(self, high, wide):
        self.high, self.wide = high, wide
        self.cells = high * wide

    def stride(self, rim):
        return up(self.high + 2 * rim, 8)

    def main(self, rim):
        return FRAMES * (self.high + 2 * rim) * self.wide

    def rows(self, rim):
        return up(self.main(rim) + 2 * rim * FRAMES * self.stride(rim), 16)

    def tall(self):
        return self.high + 2

    def broad(self):
        return up(self.wide + 2, 8)


def here():
    return lax.axis_index("row"), lax.axis_index("col")


def call(body, outs, args, scratch=(), placed=False, far=0, sems=0, mib=8, flops=0, beside=False, out_far=0):
    inner = body
    if placed:
        body = lambda *refs: inner(here(), *refs)
    specs = [pl.BlockSpec(memory_space=pltpu.VMEM)] * (len(args) - far)
    specs += [pl.BlockSpec(memory_space=pltpu.HBM)] * far
    near = len(args) - far
    args = [*args[:near], *(pltpu.with_memory_space_constraint(a, pltpu.HBM) for a in args[near:])]
    scratches = [pltpu.VMEM(shape, dtype) for shape, dtype in scratch]
    if sems:
        scratches.append(pltpu.SemaphoreType.DMA((sems,)))
    shapes = [jax.ShapeDtypeStruct(shape, dtype) for shape, dtype in outs]
    kept = len(outs) - out_far
    moved = sum(math.prod(a.shape) * a.dtype.itemsize for a in [*args, *shapes])
    moved = 0 if beside else moved
    return pl.pallas_call(
        body,
        out_shape=shapes[:kept] + [pltpu.HBM(o.shape, o.dtype) for o in shapes[kept:]],
        in_specs=specs,
        out_specs=[pl.BlockSpec(memory_space=pltpu.VMEM)] * kept
        + [pl.BlockSpec(memory_space=pltpu.HBM)] * out_far,
        scratch_shapes=scratches,
        cost_estimate=pl.CostEstimate(flops=flops, bytes_accessed=moved, transcendentals=0),
        compiler_params=pltpu.CompilerParams(vmem_limit_bytes=mib << 20),
    )(*args)


def logistic(values):
    return 0.5 * jnp.tanh(0.5 * values) + 0.5


def lane_totals(stat):
    lane = lax.broadcasted_iota(jnp.int32, stat.shape, 1)
    step = 1
    while step < LANES // GROUPS:
        ahead = pltpu.roll(stat, LANES - step, 1)
        behind = pltpu.roll(stat, step, 1)
        stat = stat + jnp.where((lane // step) % 2 == 0, ahead, behind)
        step *= 2
    return stat


def split3(stat):
    high = stat.astype(BF16).astype(F32)
    rest = stat - high
    middle = rest.astype(BF16).astype(F32)
    return jnp.concatenate([high, middle, rest - middle], 0)


def join3(parts):
    parts = parts.astype(F32)
    return parts[:STATS] + (parts[STATS : 2 * STATS] + parts[2 * STATS : PARTS])


def stat_block(first, second):
    rest = jnp.zeros((STATS - 2 * FRAMES, LANES), F32)
    return jnp.concatenate([*first, *second, rest], 0)


def measured(frames):
    means, squares = [], []
    for frame in frames:
        mean = jnp.sum(frame, 0, keepdims=True) / frame.shape[0]
        centred = frame - mean
        means.append(mean)
        squares.append(jnp.sum(centred * centred, 0, keepdims=True))
    return stat_block(means, squares)


def merged(one, two, cells):
    delta = one - two
    extra = (0.5 * cells) * delta * delta
    mean = 0.5 * (one[:FRAMES] + two[:FRAMES])
    square = one[FRAMES : 2 * FRAMES] + two[FRAMES : 2 * FRAMES] + extra[:FRAMES]
    return jnp.concatenate([mean, square, jnp.zeros((STATS - 2 * FRAMES, LANES), F32)], 0)


def concluded(blocks, cells):
    per_group = LANES // GROUPS
    mean = sum(blocks[1:], blocks[0])[:FRAMES]
    mean = lane_totals(mean) / (len(blocks) * per_group)
    total = jnp.zeros((FRAMES, LANES), F32)
    for block in blocks:
        off = block[:FRAMES] - mean
        total = total + block[FRAMES : 2 * FRAMES] + cells * off * off
    spread = lane_totals(total) / (cells * len(blocks) * per_group)
    rest = jnp.zeros((STATS - 2 * FRAMES, LANES), F32)
    return jnp.concatenate([mean, lax.rsqrt(spread + EPSILON), rest], 0)


def rim_rows(place, got):
    upper = place[0] == 0
    nothing = jnp.zeros_like(got)
    return jnp.where(upper, nothing, got), jnp.where(upper, got, nothing)


def in_frame(shape, place, across, size, rim):
    row = lax.broadcasted_iota(jnp.int32, shape, 0)
    col = lax.broadcasted_iota(jnp.int32, shape, 1)
    top = jnp.where(place[0] == 0, rim, 0)
    bottom = jnp.where(place[0] == 0, size.high + 2 * rim, size.high + rim)
    left = jnp.where(place[1] == 0, rim, 0)
    right = jnp.where(place[1] == across - 1, size.wide + rim, size.wide + 2 * rim)
    return (row >= top) & (row < bottom) & (col >= left) & (col < right)


def take_columns(size, arrays, flat):
    flat[...] = jnp.zeros_like(flat)
    at = 0
    for array, rim in arrays:
        for j in range(rim):
            for frame in range(FRAMES):
                for side, col in ((0, j), (1, size.wide - rim + j)):
                    rows = array[frame, :, col : col + 1].astype(F32)
                    rows = rows.reshape(size.high, LANES)
                    flat[side, at + rim : at + rim + size.high] = rows
                at += size.stride(rim)


def start_body(
    size, place, features_far, grad_far, pay, stats, flat, features, out_grad, sems
):
    high, wide = size.high, size.wide
    upper = place[0] == 0
    copies = [
        pltpu.make_async_copy(source.at[f], target.at[f], sems.at[FRAMES * k + f])
        for k, (source, target) in enumerate(((features_far, features), (grad_far, out_grad)))
        for f in range(FRAMES)
    ]
    for copy in copies:
        copy.start()
    for copy in copies[:FRAMES]:
        copy.wait()
    at = 0
    for frame in range(FRAMES):
        pay[at : at + wide] = jnp.where(upper, features[frame, high - 1], features[frame, 0])
        at += wide
    found = measured([features[f].astype(F32).reshape(size.cells, LANES) for f in range(FRAMES)])
    stats[...] = found
    for copy in copies[FRAMES:]:
        copy.wait()
    for frame in range(FRAMES):
        for row in range(2):
            edge = jnp.where(upper, out_grad[frame, high - 2 + row], out_grad[frame, row])
            pay[at : at + wide] = edge
            at += wide
    fill = jnp.zeros((pay.shape[0] - at - PARTS, LANES), F32)
    pay[at:] = jnp.concatenate([split3(found), fill], 0).astype(BF16)
    take_columns(size, ((features, 1), (out_grad, 2)), flat)


def slots_body(size, rims, across, place, flat, got, stats, slots, work):
    wide, high = size.wide, size.high
    upper = place[0] == 0
    work[...] = flat[...]
    at = base = 0
    for rim in rims:
        for j in range(rim):
            for frame in range(FRAMES):
                for row in range(rim):
                    start = base + (frame * rim + row) * wide
                    for side, col in ((0, j), (1, wide - rim + j)):
                        cell = start - start % 16 + 16 * ((start % 16 + col) // 16)
                        tile = got[cell : cell + 16].astype(F32)
                        edge = tile[start + col - cell : start + col - cell + 1]
                        nothing = jnp.zeros_like(edge)
                        top, bottom = at + row, at + rim + high + row
                        work[side, top : top + 1] = jnp.where(upper, nothing, edge)
                        work[side, bottom : bottom + 1] = jnp.where(upper, edge, nothing)
                at += size.stride(rim)
        base += FRAMES * rim * wide
    parts = split3(merged(stats[...], join3(got[base : base + PARTS]), size.cells))
    work[0, at : at + PARTS] = parts
    work[1, at : at + PARTS] = parts
    for peer in range(across):
        slots[peer] = jnp.where(peer > place[1], work[1], work[0]).astype(BF16)


def sides(place, across, got, first, count):
    left = got[jnp.maximum(place[1] - 1, 0), first : first + count].astype(F32)
    right = got[jnp.minimum(place[1] + 1, across - 1), first : first + count].astype(F32)
    nothing = jnp.zeros_like(left)
    left = jnp.where(place[1] > 0, left, nothing)
    right = jnp.where(place[1] < across - 1, right, nothing)
    return left, right


def padded_frame(size, own, top, bottom, left, right, frame):
    high, wide = size.high, size.wide
    frame[1 : high + 1, 1 : wide + 1] = own
    frame[0:1, 1 : wide + 1] = top[None]
    frame[high + 1 : high + 2, 1 : wide + 1] = bottom[None]
    tall = high + 2
    frame[:, 0:1] = left[:tall].reshape(tall, 1, LANES)
    frame[:, wide + 1 : wide + 2] = right[:tall].reshape(tall, 1, LANES)


def put_frame(size, frame, index, out):
    wide, tall, step = size.wide, size.tall(), size.stride(1)
    flat = frame[:, 1 : wide + 1].reshape(tall * wide, LANES)
    out[index * tall * wide : (index + 1) * tall * wide] = flat.astype(BF16)
    fill = jnp.zeros((step - tall, LANES), F32)
    left = frame[:, 0:1].reshape(tall, LANES)
    right = frame[:, wide + 1 : wide + 2].reshape(tall, LANES)
    return jnp.concatenate([left, fill], 0), jnp.concatenate([right, fill], 0)


def put_sides(out, first, blocks):
    fill = out.shape[0] - first - sum(b.shape[0] for b in blocks)
    if fill:
        blocks = [*blocks, jnp.zeros((fill, LANES), F32)]
    out[first:] = jnp.concatenate(blocks, 0).astype(BF16)


def act_first_body(
    size, across, place, features, out_grad, row_got, col_got, act, grad, norm, frame
):
    high, wide = size.high, size.wide
    at = FRAMES * size.stride(1) + 2 * FRAMES * size.stride(2)
    blocks = [join3(col_got[peer, at : at + PARTS]) for peer in range(across)]
    found = concluded(blocks, 2 * size.cells)
    norm[...] = found
    step = size.stride(1)
    left_all, right_all = sides(place, across, col_got, 0, FRAMES * step)
    ok = in_frame((size.tall(), size.broad(), LANES), place, across, size, 1)
    lefts, rights = [], []
    frame[...] = jnp.zeros_like(frame)
    for f in range(FRAMES):
        top, bottom = rim_rows(place, row_got[f * wide : (f + 1) * wide].astype(F32))
        padded_frame(
            size,
            features[f].astype(F32),
            top,
            bottom,
            left_all[f * step : (f + 1) * step],
            right_all[f * step : (f + 1) * step],
            frame,
        )
        normed = (frame[...] - found[f : f + 1][None]) * found[FRAMES + f : FRAMES + f + 1][None]
        frame[...] = jnp.where(ok, normed * logistic(normed), 0.0)
        left, right = put_frame(size, frame, f, act)
        lefts.append(left)
        rights.append(right)
    put_sides(act, size.main(1), lefts + rights)

    tall = high + 4
    for f in range(FRAMES):
        start = f * tall * wide
        for row in range(2):
            first = FRAMES * wide + (f * 2 + row) * wide
            top, bottom = rim_rows(place, row_got[first : first + wide])
            grad[start + row * wide : start + (row + 1) * wide] = top
            below = start + (high + 2 + row) * wide
            grad[below : below + wide] = bottom
        grad[start + 2 * wide : start + (high + 2) * wide] = out_grad[f].reshape(
            size.cells, LANES
        )
    left, right = sides(
        place, across, col_got, FRAMES * step, 2 * FRAMES * size.stride(2)
    )
    put_sides(grad, size.main(2), [left, right])


def spread_columns(size, rim, trim, wo, block, index, dst, at, frame):
    wide, high = size.wide, size.high
    tall, step = high + 2 * rim, size.stride(rim)
    main = block[index * tall * wide : (index + 1) * tall * wide].astype(F32)
    main = main.reshape(tall, wide, LANES)
    cut = rim - trim
    tall_out = tall - 2 * cut
    frame[:, trim : trim + wide] = main[cut : cut + tall_out]
    first = size.main(rim)
    edges = block[first:].astype(F32)
    for j in range(2 * rim):
        col = j - cut if j < rim else j - rim + trim + wide
        if j < cut or (j >= rim and j - rim >= trim):
            continue
        start = (j * FRAMES + index) * step
        edge = edges[start + cut : start + cut + tall_out]
        frame[:, col : col + 1] = edge.reshape(tall_out, 1, LANES)
    for c in range(3):
        dst[at, :, :, c * LANES : (c + 1) * LANES] = frame[:, c : c + wo].astype(BF16)


def spread_all(size, rim, trim, wo, near, far, dst, frame):
    filled = size.wide + 2 * trim
    if frame.shape[1] > filled:
        frame[:, filled:] = jnp.zeros((frame.shape[0], frame.shape[1] - filled, LANES), F32)
    for f in range(dst.shape[0]):
        block = near if f < FRAMES else far
        spread_columns(size, rim, trim, wo, block, f % FRAMES, dst, f, frame)


def tap_dot(x, kernel, turned):
    ho, wo = x.shape[1] - 2, x.shape[2]
    count = ho * wo
    span = 9 * LANES

    def cells(f):
        return jnp.concatenate(
            [x[f, b : b + ho].reshape(count, 3 * LANES) for b in range(3)], 1
        )

    def taps(a):
        if not turned:
            return kernel[a * span : (a + 1) * span]
        last = (3 - a) * 9 - 1
        return jnp.concatenate(
            [kernel[(last - k) * LANES : (last - k + 1) * LANES] for k in range(9)], 1
        )

    dims = (((1,), (1 if turned else 0,)), ((), ()))

    def dot(f, *times):
        weights = [taps(a) for a in times]
        if len(weights) > 1:
            weights = [jnp.concatenate(weights, 0 if turned else 1)]
        return lax.dot_general(cells(f), weights[0], dims, preferred_element_type=F32)

    return dot


def convolved(x, kernel, turned):
    dot = tap_dot(x, kernel, turned)
    both = dot(1, 1, 0) + dot(2, 2, 1)
    return both[:, :LANES] + dot(0, 0), both[:, LANES:] + dot(3, 2)


def conv_scratch(size, trim, wo, frames=2 * FRAMES):
    tall = size.high + 2 * trim
    return [((frames, tall, wo, 3 * LANES), BF16), ((tall, up(wo + 2, 8), LANES), F32)]


def hidden_own_body(size, own, kernel, sums, x, frame):
    spread_all(size, 1, 1, size.wide, own, None, x, frame)
    dot = tap_dot(x, kernel, False)
    both = dot(0, 2, 1)
    sums[0] = both[:, :LANES]
    sums[1] = both[:, LANES:] + dot(1, 2)


def hidden_body(size, across, place, before, sums, kernel, hidden, slots, x, frame, flat):
    high, wide = size.high, size.wide
    spread_all(size, 1, 1, wide, before, None, x, frame)
    dot = tap_dot(x, kernel, False)
    both = dot(1, 1, 0)
    sums = (sums[0] + both[:, :LANES] + dot(0, 0), sums[1] + both[:, LANES:])
    rounded = [s.astype(BF16) for s in sums]
    for f in range(FRAMES):
        hidden[f] = rounded[f].reshape(high, wide, LANES)
    span = span_second(size)
    found = split3(measured([r.astype(F32) for r in rounded]))
    take_columns(size, ((hidden, 1),), flat)
    upper = place[0] == 0
    edges = [jnp.where(upper, r[size.cells - wide :], r[:wide]).astype(F32) for r in rounded]
    fill = jnp.zeros((span - FRAMES * wide, LANES), F32)
    edges = jnp.concatenate([*edges, fill] if fill.shape[0] else edges, 0)
    rest = jnp.zeros((slots.shape[1] - span - PARTS, LANES), F32)
    for peer in range(slots.shape[0]):
        col = peer % across
        side = jnp.where(col > place[1], flat[1], flat[0])
        content = jnp.where(col == place[1], edges, side)
        slots[peer] = jnp.concatenate([content, found, rest], 0).astype(BF16)


def grad_act_body(size, near, far, kernel_far, out, x, frame, kernel, sems):
    wo = x.shape[2]
    copy = pltpu.make_async_copy(kernel_far, kernel, sems.at[0])
    copy.start()
    spread_all(size, 2, 2, wo, near, far, x, frame)
    copy.wait()
    sums = convolved(x, kernel, True)
    for f in range(FRAMES):
        out[f] = sums[f].reshape(size.tall(), wo, LANES)[:, : size.broad()]


def crossed_sides(size, place, across, got):
    step, high = size.stride(1), size.high
    count = FRAMES * step
    upper = place[0] == 0
    row = lax.broadcasted_iota(jnp.int32, (count, LANES), 0)
    found = []
    for at, there in (
        (jnp.maximum(place[1] - 1, 0), place[1] > 0),
        (jnp.minimum(place[1] + 1, across - 1), place[1] < across - 1),
    ):
        block = got[place[0] * across + at, 0:count].astype(F32)
        cross = got[(1 - place[0]) * across + at, 0:count].astype(F32)
        for f in range(FRAMES):
            above = jnp.where(upper, 0.0, cross[f * step + high : f * step + high + 1])
            below = jnp.where(upper, cross[f * step + 1 : f * step + 2], 0.0)
            block = jnp.where(row == f * step, above, block)
            block = jnp.where(row == f * step + high + 1, below, block)
        found.append(jnp.where(there, block, 0.0))
    return found


def span_second(size):
    return up(max(FRAMES * size.wide, FRAMES * size.stride(1)), 16)


def sums_second_body(
    size, across, got, hidden_far, grad_far, norm, slots, hidden, grad_act, sems
):
    high, wide = size.high, size.wide
    pairs = ((hidden_far, hidden), (grad_far, grad_act))
    copies = [
        pltpu.make_async_copy(source.at[f], target.at[f], sems.at[2 * f + k])
        for f in range(FRAMES)
        for k, (source, target) in enumerate(pairs)
    ]
    for copy in copies:
        copy.start()
    at = span_second(size)
    blocks = [join3(got[peer, at : at + PARTS]) for peer in range(got.shape[0])]
    found = concluded(blocks, size.cells)
    norm[...] = found
    firsts, seconds = [], []
    for f in range(FRAMES):
        copies[2 * f].wait()
        copies[2 * f + 1].wait()
        own = hidden[f].astype(F32)
        normed = (own - found[f : f + 1][None]) * found[FRAMES + f : FRAMES + f + 1][None]
        sigmoid = logistic(normed)
        grad = grad_act[f, 1 : high + 1, 1 : wide + 1]
        grad = grad * sigmoid * (1.0 + normed * (1.0 - sigmoid))
        grad, normed = grad.reshape(size.cells, LANES), normed.reshape(size.cells, LANES)
        firsts.append(jnp.sum(grad, 0, keepdims=True))
        seconds.append(jnp.sum(grad * normed, 0, keepdims=True))
    sums = stat_block(firsts, seconds)
    for peer in range(slots.shape[0]):
        slots[peer] = sums


def act_second_body(
    size, across, place, hidden, got, grad_act, norm, act, q_far, z_far, frame, q, z, sems
):
    wide = size.wide
    step = size.stride(1)
    left_all, right_all = crossed_sides(size, place, across, got)
    ok = in_frame((size.tall(), size.broad(), LANES), place, across, size, 1)
    lefts, rights, copies = [], [], []
    frame[...] = jnp.zeros_like(frame)
    facing = (1 - place[0]) * across + place[1]
    for f in range(FRAMES):
        top, bottom = rim_rows(place, got[facing, f * wide : (f + 1) * wide].astype(F32))
        padded_frame(
            size,
            hidden[f].astype(F32),
            top,
            bottom,
            left_all[f * step : (f + 1) * step],
            right_all[f * step : (f + 1) * step],
            frame,
        )
        normed = (frame[...] - norm[f : f + 1][None]) * norm[FRAMES + f : FRAMES + f + 1][None]
        sigmoid = logistic(normed)
        frame[...] = jnp.where(ok, normed * sigmoid, 0.0)
        left, right = put_frame(size, frame, f, act)
        lefts.append(left)
        rights.append(right)
        z[f] = normed
        q[f] = grad_act[f] * sigmoid * (1.0 + normed * (1.0 - sigmoid))
        for k, (source, target) in enumerate(((q, q_far), (z, z_far))):
            copy = pltpu.make_async_copy(source.at[f], target.at[f], sems.at[2 * f + k])
            copy.start()
            copies.append(copy)
    put_sides(act, size.main(1), lefts + rights)
    for copy in copies:
        copy.wait()


def hidden_grad(size, across, place, q, z, got, norm, out, frame, arrive):
    peers = got.shape[0]
    total = got[0]
    for peer in range(1, peers):
        total = total + got[peer]
    means = lane_totals(total) / (size.cells * peers * (LANES // GROUPS))
    ok = in_frame((size.tall(), size.broad(), LANES), place, across, size, 1)
    lefts, rights = [], []
    for f in range(FRAMES):
        first, second = means[f : f + 1][None], means[FRAMES + f : FRAMES + f + 1][None]
        inv = norm[FRAMES + f : FRAMES + f + 1][None]
        arrive(f)
        frame[...] = jnp.where(ok, inv * (q[f] - first - z[f] * second), 0.0)
        left, right = put_frame(size, frame, f, out)
        lefts.append(left)
        rights.append(right)
    put_sides(out, size.main(1), lefts + rights)


def own_cells(size, block, f):
    start = (f * size.tall() + 1) * size.wide
    return block[start : start + size.cells]


def turned_cells(size, block, out):
    for f in range(FRAMES):
        cells = own_cells(size, block, f).astype(F32).T.astype(BF16)
        out[f * LANES : (f + 1) * LANES] = cells


def tap_sums(x, turned, b):
    ho, wo = x.shape[1] - 2, x.shape[2]

    def cells(f):
        return x[f, b : b + ho].reshape(ho * wo, 3 * LANES)

    def dot(one, two):
        return jnp.dot(one, two, preferred_element_type=F32)

    low = dot(turned[...], cells(1))
    high = dot(turned[...], cells(2))
    return (
        dot(turned[:LANES], cells(0)) + low[LANES:],
        low[:LANES] + high[LANES:],
        high[:LANES] + dot(turned[LANES:], cells(3)),
    )


def second_term_body(size, near, far, act, out_far, x, frame, turned, out, sems):
    spread_all(size, 2, 1, size.wide, near, far, x, frame)
    turned_cells(size, act, turned)
    span = 3 * LANES
    copies = []
    for b in range(3):
        for a, total in enumerate(tap_sums(x, turned, b)):
            for c in range(3):
                tap = ((2 - a) * 3 + 2 - b) * 3 + 2 - c
                rows = slice(tap * LANES, (tap + 1) * LANES)
                out[rows] = total[:, c * LANES : (c + 1) * LANES]
            rows = pl.ds(((2 - a) * 3 + 2 - b) * span, span)
            copy = pltpu.make_async_copy(out.at[rows], out_far.at[rows], sems.at[3 * b + a])
            copy.start()
            copies.append(copy)
    for copy in copies:
        copy.wait()


def first_term_body(
    size,
    across,
    place,
    got,
    norm,
    q_far,
    z_far,
    near_far,
    own_far,
    second_far,
    both,
    give,
    grad_far,
    x,
    frame,
    turned,
    grad,
    near,
    own,
    q,
    z,
    sems,
):
    pairs = [(q_far.at[f], q.at[f]) for f in range(FRAMES)]
    pairs += [(z_far.at[f], z.at[f]) for f in range(FRAMES)]
    pairs += [(near_far, near), (own_far, own)]
    copies = [
        pltpu.make_async_copy(source, target, sems.at[k])
        for k, (source, target) in enumerate(pairs)
    ]
    for k in (0, FRAMES, 1, FRAMES + 1, 2 * FRAMES, 2 * FRAMES + 1):
        copies[k].start()
    upper = place[0] == 0
    fetched = pltpu.make_async_copy(second_far, both.at[1], sems.at[len(pairs) + 1])
    fetched.start()

    def arrive(f):
        copies[f].wait()
        copies[FRAMES + f].wait()

    hidden_grad(size, across, place, q, z, got, norm, grad, frame, arrive)
    sent = pltpu.make_async_copy(grad, grad_far, sems.at[len(pairs)])
    sent.start()
    turned_cells(size, grad, turned)
    for copy in copies[2 * FRAMES :]:
        copy.wait()
    spread_all(size, 1, 1, size.wide, near, own, x, frame)
    fetched.wait()

    @pl.when(upper)
    def _():
        give[...] = both[1].astype(BF16)

    for b in range(3):
        for a, total in enumerate(tap_sums(x, turned, b)):
            rows = slice((a * 3 + b) * 3 * LANES, (a * 3 + b + 1) * 3 * LANES)
            both[0, rows] = total.T

    @pl.when(jnp.logical_not(upper))
    def _():
        give[...] = both[0].astype(BF16)

    sent.wait()


def result_body(size, near, far, kernel, features, out, x, frame):
    spread_all(size, 1, 1, size.wide, near, far, x, frame)
    sums = convolved(x, kernel, False)
    for f in range(FRAMES):
        total = features[f].astype(F32) + sums[f].reshape(size.high, size.wide, LANES)
        out[f] = total.astype(BF16)


def back_first_body(
    size, near, kernel, features, norm, after, q, sums, x, frame, far, sems
):
    copy = pltpu.make_async_copy(after, far, sems.at[0])
    copy.start()
    copy.wait()
    spread_all(size, 1, 1, size.wide, near, far, x, frame)
    grads = convolved(x, kernel, True)
    firsts, seconds = [], []
    for f in range(FRAMES):
        values = features[f].astype(F32).reshape(size.cells, LANES)
        normed = (values - norm[f : f + 1]) * norm[FRAMES + f : FRAMES + f + 1]
        sigmoid = logistic(normed)
        grad = grads[f] * sigmoid * (1.0 + normed * (1.0 - sigmoid))
        q[f] = grad
        firsts.append(jnp.sum(grad, 0, keepdims=True))
        seconds.append(jnp.sum(grad * normed, 0, keepdims=True))
    sums[...] = stat_block(firsts, seconds)


def feature_grad_body(size, peers, features, out_grad, norm, q, got, out):
    total = join3(got[0])
    for peer in range(1, got.shape[0]):
        total = total + join3(got[peer])
    means = lane_totals(total) / (size.cells * peers * (LANES // GROUPS))
    for f in range(FRAMES):
        values = features[f].astype(F32).reshape(size.cells, LANES)
        inv = norm[FRAMES + f : FRAMES + f + 1]
        normed = (values - norm[f : f + 1]) * inv
        grad = inv * (q[f] - means[f : f + 1] - normed * means[FRAMES + f : FRAMES + f + 1])
        grad = out_grad[f].astype(F32) + grad.reshape(size.high, size.wide, LANES)
        out[f] = grad.astype(BF16)


def row_swap(values):
    return lax.ppermute(values, "row", [(0, 1), (1, 0)])


def later(values, by):
    peers = lax.axis_size("tm")
    pairs = [(i, i + by) for i in range(peers) if 0 <= i + by < peers]
    return lax.ppermute(values, "tm", pairs)


def sum_parts(stat):
    high = lax.reduce_precision(stat, 8, 7)
    rest = stat - high
    middle = lax.reduce_precision(rest, 8, 7)
    return jnp.concatenate([high, middle, rest - middle], 0).astype(BF16)


def total_of(got):
    total = got[0].astype(F32)
    for peer in range(1, got.shape[0]):
        total = total + got[peer].astype(F32)
    return total


def joined_body(place, both, got, out):
    share = out.shape[1]
    for peer in range(out.shape[0]):
        rows = slice(peer * share, (peer + 1) * share)
        out[peer] = (both[place[0], rows] + got[rows].astype(F32)).astype(BF16)


def shared_body(got, out, flat):
    rows, share = got.shape[1], out.shape[1]
    if flat.shape[0] > rows:
        flat[rows:] = jnp.zeros((flat.shape[0] - rows, LANES), F32)
    flat[:rows] = total_of(got)
    for peer in range(out.shape[0]):
        out[peer] = flat[peer * share : (peer + 1) * share].astype(BF16)


def finished_body(factor, got, out):
    total = (total_of(got) * factor).astype(BF16)
    for peer in range(out.shape[0]):
        out[peer] = total


def placed_body(rows, swapped, *refs):
    block, first, second, sems = refs[0], *refs[-3:]
    place = here()

    def move(target):
        copies = [
            pltpu.make_async_copy(
                block.at[peer, pl.ds(0, rows)], target.at[pl.ds(peer * rows, rows)], sems.at[peer]
            )
            for peer in range(block.shape[0])
        ]
        for copy in copies:
            copy.start()
        for copy in copies:
            copy.wait()

    @pl.when(place[0] == swapped)
    def _():
        move(first)

    @pl.when(place[0] != swapped)
    def _():
        move(second)


def deliver(block, swapped, rows, so_far):
    anywhere = pl.BlockSpec(memory_space=pl.ANY)
    shape = (rows * block.shape[0], LANES)
    return pl.pallas_call(
        functools.partial(placed_body, rows, swapped),
        out_shape=[jax.ShapeDtypeStruct(shape, BF16)] * 2,
        in_specs=[anywhere] * (1 + len(so_far)),
        out_specs=[anywhere, anywhere],
        input_output_aliases={1 + k: k for k in range(len(so_far))},
        scratch_shapes=[pltpu.SemaphoreType.DMA((block.shape[0],))],
        compiler_params=pltpu.CompilerParams(vmem_limit_bytes=1 << 20),
    )(block, *so_far)


def on_device(features, conv_first, conv_second, out_grad):
    frames, high, wide, chans = features.shape
    assert frames == FRAMES and chans == LANES and lax.axis_size("row") == 2
    size = Sizes(high, wide)
    across = lax.axis_size("col")
    peers = 2 * across
    factor = 1.0 / math.sqrt(size.cells * FRAMES * lax.axis_size("tm") * peers)
    taps = conv_first.shape
    first = conv_first.reshape(-1, LANES)
    second = conv_second.reshape(-1, LANES)
    work = 2 * first.size * size.cells * FRAMES
    part = functools.partial
    stat = ((STATS, LANES), F32)
    tall, broad = size.tall(), size.broad()
    frame = ((tall, broad, LANES), F32)

    edge = up(3 * FRAMES * wide + PARTS, 16)
    lines = up(FRAMES * size.stride(1) + 2 * FRAMES * size.stride(2) + PARTS, 16)
    flat = ((2, lines, LANES), F32)
    pay, stats, cols, features_near, grad_near = call(
        part(start_body, size),
        [((edge, LANES), BF16), stat, flat, (features.shape, BF16), (features.shape, BF16)],
        [features, out_grad],
        placed=True,
        far=2,
        sems=2 * FRAMES,
    )
    row_got = row_swap(pay)
    (slots,) = call(
        part(slots_body, size, (1, 2), across),
        [((across, lines, LANES), BF16)],
        [cols, row_got, stats],
        [flat],
        placed=True,
    )
    col_got = lax.all_to_all(slots, "col", 0, 0)
    block = ((size.rows(1), LANES), BF16)
    act_first, grad, norm_first = call(
        part(act_first_body, size, across),
        [block, ((size.rows(2), LANES), BF16), stat],
        [features_near, grad_near, row_got, col_got],
        [frame],
        placed=True,
    )
    grad_after = later(grad, -1)
    act_before = later(act_first, 1)

    edge = up(FRAMES * wide + PARTS, 16)
    (sums,) = call(
        part(hidden_own_body, size),
        [((FRAMES, size.cells, LANES), F32)],
        [act_first, first],
        conv_scratch(size, 1, wide, FRAMES),
        mib=12,
        flops=work // 2,
    )
    span = span_second(size)
    hidden, slots = call(
        part(hidden_body, size, across),
        [(features.shape, BF16), ((peers, up(span + PARTS, 16), LANES), BF16)],
        [act_before, sums, first],
        [*conv_scratch(size, 1, wide, FRAMES), ((2, span, LANES), F32)],
        placed=True,
        mib=12,
        flops=2 * work,
    )
    got = lax.all_to_all(slots, ("row", "col"), 0, 0)
    (grad_act,) = call(
        part(grad_act_body, size),
        [((FRAMES, tall, broad, LANES), F32)],
        [grad, grad_after, second],
        [*conv_scratch(size, 2, up(wide + 2, 16)), (second.shape, BF16)],
        far=1,
        sems=1,
        mib=18,
        flops=2 * work,
    )
    field = ((FRAMES, tall, broad, LANES), F32)
    norm_second, slots = call(
        part(sums_second_body, size, across),
        [stat, ((peers, STATS, LANES), F32)],
        [got, hidden, grad_act],
        [(features.shape, BF16), field],
        far=2,
        sems=2 * FRAMES,
    )
    act_second, q, z = call(
        part(act_second_body, size, across),
        [block, field, field],
        [hidden, got, grad_act, norm_second],
        [frame, field, field],
        placed=True,
        sems=2 * FRAMES,
        beside=True,
        out_far=2,
    )
    got = lax.all_to_all(slots, ("row", "col"), 0, 0)
    turned = ((FRAMES * LANES, size.cells), BF16)
    (second_term,) = call(
        part(second_term_body, size),
        [(first.shape, F32)],
        [grad, grad_after, act_second],
        [*conv_scratch(size, 1, wide), turned, (first.shape, F32)],
        sems=9,
        mib=16,
        beside=True,
        out_far=1,
    )
    both, give, grad_second = call(
        part(first_term_body, size, across),
        [((2, *first.shape), F32), (first.shape, BF16), block],
        [got, norm_second, q, z, act_before, act_first, second_term],
        [*conv_scratch(size, 1, wide), turned, *[block] * 3, field, field],
        placed=True,
        far=5,
        sems=2 * FRAMES + 4,
        mib=20,
        flops=work,
        out_far=1,
    )
    give, late_grad, late_act = lax.optimization_barrier((give, grad_second, act_second))
    act_second_before = later(late_act, 1)
    grad_second_after = later(late_grad, -1)

    along = lax.axis_size("tm")
    rows = first.shape[0]
    by_col = rows // across
    (slots,) = call(
        joined_body,
        [((across, by_col, LANES), BF16)],
        [both, row_swap(give)],
        placed=True,
    )
    slots = lax.all_to_all(slots, "col", 0, 0)
    slots, grad_second_after = lax.optimization_barrier((slots, grad_second_after))
    share = up(by_col, 16 * along) // along
    (slots,) = call(
        shared_body,
        [((along, share, LANES), BF16)],
        [slots],
        [((along * share, LANES), F32)],
    )
    got = lax.all_to_all(slots, "tm", 0, 0)
    (result,) = call(
        part(result_body, size),
        [(features.shape, BF16)],
        [act_second_before, act_second, second, features],
        conv_scratch(size, 1, wide),
        mib=14,
        flops=work,
    )
    q, sums = call(
        part(back_first_body, size),
        [((FRAMES, size.cells, LANES), F32), stat],
        [grad_second, first, features, norm_first, grad_second_after],
        [*conv_scratch(size, 1, wide), block],
        far=1,
        sems=1,
        mib=14,
        flops=work,
    )
    got, result = lax.optimization_barrier((got, result))
    (slots,) = call(part(finished_body, factor), [((along, share, LANES), BF16)], [got])
    done = lax.all_to_all(slots, "tm", 0, 0).reshape(-1, LANES)[:by_col]
    parts = sum_parts(sums + row_swap(sums))
    parts = jnp.pad(parts, ((0, -parts.shape[0] % 16), (0, 0)))
    done = jnp.concatenate([done, parts], 0)
    mine = lax.all_to_all(jnp.broadcast_to(done[None], (across, *done.shape)), "col", 0, 0)
    theirs = row_swap(mine)
    so_far = deliver(mine, 0, by_col, [])
    first_grad, second_grad = deliver(theirs, 1, by_col, so_far)
    (feature_grad,) = call(
        part(feature_grad_body, size, peers),
        [(features.shape, BF16)],
        [features, out_grad, norm_first, q, mine[:, by_col:]],
    )
    return (result, feature_grad, first_grad.reshape(taps), second_grad.reshape(taps))


def solution(mesh):
    in_specs = (P("tm", "row", "col", None), P(), P(), P("tm", "row", "col", None))
    out_specs = (P("tm", "row", "col", None), P("tm", "row", "col", None), P(), P())
    return jax.shard_map(
        on_device, mesh=mesh, in_specs=in_specs, out_specs=out_specs, check_vma=False
    )
```

```python
import functools
import math

import jax
import jax.numpy as jnp
from jax import lax
from jax.experimental import pallas as pl
from jax.experimental.pallas import tpu as pltpu
from jax.sharding import PartitionSpec as P

GROUPS = 32
EPSILON = 1e-06
F32 = jnp.float32
BF16 = jnp.bfloat16
LANES = 128
FRAMES = 2
STATS = 8
PARTS = 3 * STATS


def up(count, step):
    return -(-count // step) * step


class Sizes:
    def __init__(self, high, wide):
        self.high, self.wide = high, wide
        self.cells = high * wide

    def stride(self, rim):
        return up(self.high + 2 * rim, 8)

    def main(self, rim):
        return FRAMES * (self.high + 2 * rim) * self.wide

    def rows(self, rim):
        return up(self.main(rim) + 2 * rim * FRAMES * self.stride(rim), 16)

    def tall(self):
        return self.high + 2

    def broad(self):
        return up(self.wide + 2, 8)


def here():
    return lax.axis_index("row"), lax.axis_index("col")


def call(body, outs, args, scratch=(), placed=False, far=0, sems=0, mib=8, flops=0, beside=False, out_far=0):
    inner = body
    if placed:
        body = lambda *refs: inner(here(), *refs)
    specs = [pl.BlockSpec(memory_space=pltpu.VMEM)] * (len(args) - far)
    specs += [pl.BlockSpec(memory_space=pltpu.HBM)] * far
    near = len(args) - far
    args = [*args[:near], *(pltpu.with_memory_space_constraint(a, pltpu.HBM) for a in args[near:])]
    scratches = [pltpu.VMEM(shape, dtype) for shape, dtype in scratch]
    if sems:
        scratches.append(pltpu.SemaphoreType.DMA((sems,)))
    shapes = [jax.ShapeDtypeStruct(shape, dtype) for shape, dtype in outs]
    kept = len(outs) - out_far
    moved = sum(math.prod(a.shape) * a.dtype.itemsize for a in [*args, *shapes])
    moved = 0 if beside else moved
    return pl.pallas_call(
        body,
        out_shape=shapes[:kept] + [pltpu.HBM(o.shape, o.dtype) for o in shapes[kept:]],
        in_specs=specs,
        out_specs=[pl.BlockSpec(memory_space=pltpu.VMEM)] * kept
        + [pl.BlockSpec(memory_space=pltpu.HBM)] * out_far,
        scratch_shapes=scratches,
        cost_estimate=pl.CostEstimate(flops=flops, bytes_accessed=moved, transcendentals=0),
        compiler_params=pltpu.CompilerParams(vmem_limit_bytes=mib << 20),
    )(*args)


def logistic(values):
    return 0.5 * jnp.tanh(0.5 * values) + 0.5


def lane_totals(stat):
    lane = lax.broadcasted_iota(jnp.int32, stat.shape, 1)
    step = 1
    while step < LANES // GROUPS:
        ahead = pltpu.roll(stat, LANES - step, 1)
        behind = pltpu.roll(stat, step, 1)
        stat = stat + jnp.where((lane // step) % 2 == 0, ahead, behind)
        step *= 2
    return stat


def split3(stat):
    high = stat.astype(BF16).astype(F32)
    rest = stat - high
    middle = rest.astype(BF16).astype(F32)
    return jnp.concatenate([high, middle, rest - middle], 0)


def join3(parts):
    parts = parts.astype(F32)
    return parts[:STATS] + (parts[STATS : 2 * STATS] + parts[2 * STATS : PARTS])


def stat_block(first, second):
    rest = jnp.zeros((STATS - 2 * FRAMES, LANES), F32)
    return jnp.concatenate([*first, *second, rest], 0)


def measured(frames):
    means, squares = [], []
    for frame in frames:
        mean = jnp.sum(frame, 0, keepdims=True) / frame.shape[0]
        centred = frame - mean
        means.append(mean)
        squares.append(jnp.sum(centred * centred, 0, keepdims=True))
    return stat_block(means, squares)


def merged(one, two, cells):
    delta = one - two
    extra = (0.5 * cells) * delta * delta
    mean = 0.5 * (one[:FRAMES] + two[:FRAMES])
    square = one[FRAMES : 2 * FRAMES] + two[FRAMES : 2 * FRAMES] + extra[:FRAMES]
    return jnp.concatenate([mean, square, jnp.zeros((STATS - 2 * FRAMES, LANES), F32)], 0)


def concluded(blocks, cells):
    per_group = LANES // GROUPS
    mean = sum(blocks[1:], blocks[0])[:FRAMES]
    mean = lane_totals(mean) / (len(blocks) * per_group)
    total = jnp.zeros((FRAMES, LANES), F32)
    for block in blocks:
        off = block[:FRAMES] - mean
        total = total + block[FRAMES : 2 * FRAMES] + cells * off * off
    spread = lane_totals(total) / (cells * len(blocks) * per_group)
    rest = jnp.zeros((STATS - 2 * FRAMES, LANES), F32)
    return jnp.concatenate([mean, lax.rsqrt(spread + EPSILON), rest], 0)


def rim_rows(place, got):
    upper = place[0] == 0
    nothing = jnp.zeros_like(got)
    return jnp.where(upper, nothing, got), jnp.where(upper, got, nothing)


def in_frame(shape, place, across, size, rim):
    row = lax.broadcasted_iota(jnp.int32, shape, 0)
    col = lax.broadcasted_iota(jnp.int32, shape, 1)
    top = jnp.where(place[0] == 0, rim, 0)
    bottom = jnp.where(place[0] == 0, size.high + 2 * rim, size.high + rim)
    left = jnp.where(place[1] == 0, rim, 0)
    right = jnp.where(place[1] == across - 1, size.wide + rim, size.wide + 2 * rim)
    return (row >= top) & (row < bottom) & (col >= left) & (col < right)


def take_columns(size, arrays, flat):
    flat[...] = jnp.zeros_like(flat)
    at = 0
    for array, rim in arrays:
        for j in range(rim):
            for frame in range(FRAMES):
                for side, col in ((0, j), (1, size.wide - rim + j)):
                    rows = array[frame, :, col : col + 1].astype(F32)
                    rows = rows.reshape(size.high, LANES)
                    flat[side, at + rim : at + rim + size.high] = rows
                at += size.stride(rim)


def start_body(
    size, place, features_far, grad_far, pay, stats, flat, features, out_grad, sems
):
    high, wide = size.high, size.wide
    upper = place[0] == 0
    copies = [
        pltpu.make_async_copy(source.at[f], target.at[f], sems.at[FRAMES * k + f])
        for k, (source, target) in enumerate(((features_far, features), (grad_far, out_grad)))
        for f in range(FRAMES)
    ]
    for copy in copies:
        copy.start()
    for copy in copies[:FRAMES]:
        copy.wait()
    at = 0
    for frame in range(FRAMES):
        pay[at : at + wide] = jnp.where(upper, features[frame, high - 1], features[frame, 0])
        at += wide
    found = measured([features[f].astype(F32).reshape(size.cells, LANES) for f in range(FRAMES)])
    stats[...] = found
    for copy in copies[FRAMES:]:
        copy.wait()
    for frame in range(FRAMES):
        for row in range(2):
            edge = jnp.where(upper, out_grad[frame, high - 2 + row], out_grad[frame, row])
            pay[at : at + wide] = edge
            at += wide
    fill = jnp.zeros((pay.shape[0] - at - PARTS, LANES), F32)
    pay[at:] = jnp.concatenate([split3(found), fill], 0).astype(BF16)
    take_columns(size, ((features, 1), (out_grad, 2)), flat)


def slots_body(size, rims, across, place, flat, got, stats, slots, work):
    wide, high = size.wide, size.high
    upper = place[0] == 0
    work[...] = flat[...]
    at = base = 0
    for rim in rims:
        for j in range(rim):
            for frame in range(FRAMES):
                for row in range(rim):
                    start = base + (frame * rim + row) * wide
                    for side, col in ((0, j), (1, wide - rim + j)):
                        cell = start - start % 16 + 16 * ((start % 16 + col) // 16)
                        tile = got[cell : cell + 16].astype(F32)
                        edge = tile[start + col - cell : start + col - cell + 1]
                        nothing = jnp.zeros_like(edge)
                        top, bottom = at + row, at + rim + high + row
                        work[side, top : top + 1] = jnp.where(upper, nothing, edge)
                        work[side, bottom : bottom + 1] = jnp.where(upper, edge, nothing)
                at += size.stride(rim)
        base += FRAMES * rim * wide
    parts = split3(merged(stats[...], join3(got[base : base + PARTS]), size.cells))
    work[0, at : at + PARTS] = parts
    work[1, at : at + PARTS] = parts
    for peer in range(across):
        slots[peer] = jnp.where(peer > place[1], work[1], work[0]).astype(BF16)


def sides(place, across, got, first, count):
    left = got[jnp.maximum(place[1] - 1, 0), first : first + count].astype(F32)
    right = got[jnp.minimum(place[1] + 1, across - 1), first : first + count].astype(F32)
    nothing = jnp.zeros_like(left)
    left = jnp.where(place[1] > 0, left, nothing)
    right = jnp.where(place[1] < across - 1, right, nothing)
    return left, right


def padded_frame(size, own, top, bottom, left, right, frame):
    high, wide = size.high, size.wide
    frame[1 : high + 1, 1 : wide + 1] = own
    frame[0:1, 1 : wide + 1] = top[None]
    frame[high + 1 : high + 2, 1 : wide + 1] = bottom[None]
    tall = high + 2
    frame[:, 0:1] = left[:tall].reshape(tall, 1, LANES)
    frame[:, wide + 1 : wide + 2] = right[:tall].reshape(tall, 1, LANES)


def put_frame(size, frame, index, out):
    wide, tall, step = size.wide, size.tall(), size.stride(1)
    flat = frame[:, 1 : wide + 1].reshape(tall * wide, LANES)
    out[index * tall * wide : (index + 1) * tall * wide] = flat.astype(BF16)
    fill = jnp.zeros((step - tall, LANES), F32)
    left = frame[:, 0:1].reshape(tall, LANES)
    right = frame[:, wide + 1 : wide + 2].reshape(tall, LANES)
    return jnp.concatenate([left, fill], 0), jnp.concatenate([right, fill], 0)


def put_sides(out, first, blocks):
    fill = out.shape[0] - first - sum(b.shape[0] for b in blocks)
    if fill:
        blocks = [*blocks, jnp.zeros((fill, LANES), F32)]
    out[first:] = jnp.concatenate(blocks, 0).astype(BF16)


def act_first_body(
    size, across, place, features, out_grad, row_got, col_got, act, grad, norm, frame
):
    high, wide = size.high, size.wide
    at = FRAMES * size.stride(1) + 2 * FRAMES * size.stride(2)
    blocks = [join3(col_got[peer, at : at + PARTS]) for peer in range(across)]
    found = concluded(blocks, 2 * size.cells)
    norm[...] = found
    step = size.stride(1)
    left_all, right_all = sides(place, across, col_got, 0, FRAMES * step)
    ok = in_frame((size.tall(), size.broad(), LANES), place, across, size, 1)
    lefts, rights = [], []
    frame[...] = jnp.zeros_like(frame)
    for f in range(FRAMES):
        top, bottom = rim_rows(place, row_got[f * wide : (f + 1) * wide].astype(F32))
        padded_frame(
            size,
            features[f].astype(F32),
            top,
            bottom,
            left_all[f * step : (f + 1) * step],
            right_all[f * step : (f + 1) * step],
            frame,
        )
        normed = (frame[...] - found[f : f + 1][None]) * found[FRAMES + f : FRAMES + f + 1][None]
        frame[...] = jnp.where(ok, normed * logistic(normed), 0.0)
        left, right = put_frame(size, frame, f, act)
        lefts.append(left)
        rights.append(right)
    put_sides(act, size.main(1), lefts + rights)

    tall = high + 4
    for f in range(FRAMES):
        start = f * tall * wide
        for row in range(2):
            first = FRAMES * wide + (f * 2 + row) * wide
            top, bottom = rim_rows(place, row_got[first : first + wide])
            grad[start + row * wide : start + (row + 1) * wide] = top
            below = start + (high + 2 + row) * wide
            grad[below : below + wide] = bottom
        grad[start + 2 * wide : start + (high + 2) * wide] = out_grad[f].reshape(
            size.cells, LANES
        )
    left, right = sides(
        place, across, col_got, FRAMES * step, 2 * FRAMES * size.stride(2)
    )
    put_sides(grad, size.main(2), [left, right])


def spread_columns(size, rim, trim, wo, block, index, dst, at, frame):
    wide, high = size.wide, size.high
    tall, step = high + 2 * rim, size.stride(rim)
    main = block[index * tall * wide : (index + 1) * tall * wide].astype(F32)
    main = main.reshape(tall, wide, LANES)
    cut = rim - trim
    tall_out = tall - 2 * cut
    frame[:, trim : trim + wide] = main[cut : cut + tall_out]
    first = size.main(rim)
    edges = block[first:].astype(F32)
    for j in range(2 * rim):
        col = j - cut if j < rim else j - rim + trim + wide
        if j < cut or (j >= rim and j - rim >= trim):
            continue
        start = (j * FRAMES + index) * step
        edge = edges[start + cut : start + cut + tall_out]
        frame[:, col : col + 1] = edge.reshape(tall_out, 1, LANES)
    for c in range(3):
        dst[at, :, :, c * LANES : (c + 1) * LANES] = frame[:, c : c + wo].astype(BF16)


def spread_all(size, rim, trim, wo, near, far, dst, frame):
    filled = size.wide + 2 * trim
    if frame.shape[1] > filled:
        frame[:, filled:] = jnp.zeros((frame.shape[0], frame.shape[1] - filled, LANES), F32)
    for f in range(dst.shape[0]):
        block = near if f < FRAMES else far
        spread_columns(size, rim, trim, wo, block, f % FRAMES, dst, f, frame)


def tap_dot(x, kernel, turned):
    ho, wo = x.shape[1] - 2, x.shape[2]
    count = ho * wo
    span = 9 * LANES

    def cells(f):
        return jnp.concatenate(
            [x[f, b : b + ho].reshape(count, 3 * LANES) for b in range(3)], 1
        )

    def taps(a):
        if not turned:
            return kernel[a * span : (a + 1) * span]
        last = (3 - a) * 9 - 1
        return jnp.concatenate(
            [kernel[(last - k) * LANES : (last - k + 1) * LANES] for k in range(9)], 1
        )

    dims = (((1,), (1 if turned else 0,)), ((), ()))

    def dot(f, *times):
        weights = [taps(a) for a in times]
        if len(weights) > 1:
            weights = [jnp.concatenate(weights, 0 if turned else 1)]
        return lax.dot_general(cells(f), weights[0], dims, preferred_element_type=F32)

    return dot


def convolved(x, kernel, turned):
    dot = tap_dot(x, kernel, turned)
    both = dot(1, 1, 0) + dot(2, 2, 1)
    return both[:, :LANES] + dot(0, 0), both[:, LANES:] + dot(3, 2)


def conv_scratch(size, trim, wo, frames=2 * FRAMES):
    tall = size.high + 2 * trim
    return [((frames, tall, wo, 3 * LANES), BF16), ((tall, up(wo + 2, 8), LANES), F32)]


def hidden_own_body(size, own, kernel, sums, x, frame):
    spread_all(size, 1, 1, size.wide, own, None, x, frame)
    dot = tap_dot(x, kernel, False)
    both = dot(0, 2, 1)
    sums[0] = both[:, :LANES]
    sums[1] = both[:, LANES:] + dot(1, 2)


def hidden_body(size, across, place, before, sums, kernel, hidden, slots, x, frame, flat):
    high, wide = size.high, size.wide
    spread_all(size, 1, 1, wide, before, None, x, frame)
    dot = tap_dot(x, kernel, False)
    both = dot(1, 1, 0)
    sums = (sums[0] + both[:, :LANES] + dot(0, 0), sums[1] + both[:, LANES:])
    rounded = [s.astype(BF16) for s in sums]
    for f in range(FRAMES):
        hidden[f] = rounded[f].reshape(high, wide, LANES)
    span = span_second(size)
    found = split3(measured([r.astype(F32) for r in rounded]))
    take_columns(size, ((hidden, 1),), flat)
    upper = place[0] == 0
    edges = [jnp.where(upper, r[size.cells - wide :], r[:wide]).astype(F32) for r in rounded]
    fill = jnp.zeros((span - FRAMES * wide, LANES), F32)
    edges = jnp.concatenate([*edges, fill] if fill.shape[0] else edges, 0)
    rest = jnp.zeros((slots.shape[1] - span - PARTS, LANES), F32)
    for peer in range(slots.shape[0]):
        col = peer % across
        side = jnp.where(col > place[1], flat[1], flat[0])
        content = jnp.where(col == place[1], edges, side)
        slots[peer] = jnp.concatenate([content, found, rest], 0).astype(BF16)


def grad_act_body(size, near, far, kernel_far, out, x, frame, kernel, sems):
    wo = x.shape[2]
    copy = pltpu.make_async_copy(kernel_far, kernel, sems.at[0])
    copy.start()
    spread_all(size, 2, 2, wo, near, far, x, frame)
    copy.wait()
    sums = convolved(x, kernel, True)
    for f in range(FRAMES):
        out[f] = sums[f].reshape(size.tall(), wo, LANES)[:, : size.broad()]


def crossed_sides(size, place, across, got):
    step, high = size.stride(1), size.high
    count = FRAMES * step
    upper = place[0] == 0
    row = lax.broadcasted_iota(jnp.int32, (count, LANES), 0)
    found = []
    for at, there in (
        (jnp.maximum(place[1] - 1, 0), place[1] > 0),
        (jnp.minimum(place[1] + 1, across - 1), place[1] < across - 1),
    ):
        block = got[place[0] * across + at, 0:count].astype(F32)
        cross = got[(1 - place[0]) * across + at, 0:count].astype(F32)
        for f in range(FRAMES):
            above = jnp.where(upper, 0.0, cross[f * step + high : f * step + high + 1])
            below = jnp.where(upper, cross[f * step + 1 : f * step + 2], 0.0)
            block = jnp.where(row == f * step, above, block)
            block = jnp.where(row == f * step + high + 1, below, block)
        found.append(jnp.where(there, block, 0.0))
    return found


def span_second(size):
    return up(max(FRAMES * size.wide, FRAMES * size.stride(1)), 16)


def sums_second_body(size, across, hidden, got, grad_act, norm, slots):
    high, wide = size.high, size.wide
    at = span_second(size)
    blocks = [join3(got[peer, at : at + PARTS]) for peer in range(got.shape[0])]
    found = concluded(blocks, size.cells)
    norm[...] = found
    firsts, seconds = [], []
    for f in range(FRAMES):
        own = hidden[f].astype(F32)
        normed = (own - found[f : f + 1][None]) * found[FRAMES + f : FRAMES + f + 1][None]
        sigmoid = logistic(normed)
        grad = grad_act[f, 1 : high + 1, 1 : wide + 1]
        grad = grad * sigmoid * (1.0 + normed * (1.0 - sigmoid))
        grad, normed = grad.reshape(size.cells, LANES), normed.reshape(size.cells, LANES)
        firsts.append(jnp.sum(grad, 0, keepdims=True))
        seconds.append(jnp.sum(grad * normed, 0, keepdims=True))
    sums = stat_block(firsts, seconds)
    for peer in range(slots.shape[0]):
        slots[peer] = sums


def act_second_body(
    size, across, place, hidden, got, grad_act, norm, act, q_far, z_far, frame, q, z, sems
):
    wide = size.wide
    step = size.stride(1)
    left_all, right_all = crossed_sides(size, place, across, got)
    ok = in_frame((size.tall(), size.broad(), LANES), place, across, size, 1)
    lefts, rights, copies = [], [], []
    frame[...] = jnp.zeros_like(frame)
    facing = (1 - place[0]) * across + place[1]
    for f in range(FRAMES):
        top, bottom = rim_rows(place, got[facing, f * wide : (f + 1) * wide].astype(F32))
        padded_frame(
            size,
            hidden[f].astype(F32),
            top,
            bottom,
            left_all[f * step : (f + 1) * step],
            right_all[f * step : (f + 1) * step],
            frame,
        )
        normed = (frame[...] - norm[f : f + 1][None]) * norm[FRAMES + f : FRAMES + f + 1][None]
        sigmoid = logistic(normed)
        frame[...] = jnp.where(ok, normed * sigmoid, 0.0)
        left, right = put_frame(size, frame, f, act)
        lefts.append(left)
        rights.append(right)
        z[f] = normed
        q[f] = grad_act[f] * sigmoid * (1.0 + normed * (1.0 - sigmoid))
        for k, (source, target) in enumerate(((q, q_far), (z, z_far))):
            copy = pltpu.make_async_copy(source.at[f], target.at[f], sems.at[2 * f + k])
            copy.start()
            copies.append(copy)
    put_sides(act, size.main(1), lefts + rights)
    for copy in copies:
        copy.wait()


def hidden_grad(size, across, place, q, z, got, norm, out, frame, arrive):
    peers = got.shape[0]
    total = got[0]
    for peer in range(1, peers):
        total = total + got[peer]
    means = lane_totals(total) / (size.cells * peers * (LANES // GROUPS))
    ok = in_frame((size.tall(), size.broad(), LANES), place, across, size, 1)
    lefts, rights = [], []
    for f in range(FRAMES):
        first, second = means[f : f + 1][None], means[FRAMES + f : FRAMES + f + 1][None]
        inv = norm[FRAMES + f : FRAMES + f + 1][None]
        arrive(f)
        frame[...] = jnp.where(ok, inv * (q[f] - first - z[f] * second), 0.0)
        left, right = put_frame(size, frame, f, out)
        lefts.append(left)
        rights.append(right)
    put_sides(out, size.main(1), lefts + rights)


def own_cells(size, block, f):
    start = (f * size.tall() + 1) * size.wide
    return block[start : start + size.cells]


def turned_cells(size, block, out):
    for f in range(FRAMES):
        cells = own_cells(size, block, f).astype(F32).T.astype(BF16)
        out[f * LANES : (f + 1) * LANES] = cells


def tap_sums(x, turned, b):
    ho, wo = x.shape[1] - 2, x.shape[2]

    def cells(f):
        return x[f, b : b + ho].reshape(ho * wo, 3 * LANES)

    def dot(one, two):
        return jnp.dot(one, two, preferred_element_type=F32)

    low = dot(turned[...], cells(1))
    high = dot(turned[...], cells(2))
    return (
        dot(turned[:LANES], cells(0)) + low[LANES:],
        low[:LANES] + high[LANES:],
        high[:LANES] + dot(turned[LANES:], cells(3)),
    )


def second_term_body(size, near, far, act, out_far, x, frame, turned, out, sems):
    spread_all(size, 2, 1, size.wide, near, far, x, frame)
    turned_cells(size, act, turned)
    span = 3 * LANES
    copies = []
    for b in range(3):
        for a, total in enumerate(tap_sums(x, turned, b)):
            for c in range(3):
                tap = ((2 - a) * 3 + 2 - b) * 3 + 2 - c
                rows = slice(tap * LANES, (tap + 1) * LANES)
                out[rows] = total[:, c * LANES : (c + 1) * LANES]
            rows = pl.ds(((2 - a) * 3 + 2 - b) * span, span)
            copy = pltpu.make_async_copy(out.at[rows], out_far.at[rows], sems.at[3 * b + a])
            copy.start()
            copies.append(copy)
    for copy in copies:
        copy.wait()


def first_term_body(
    size,
    across,
    place,
    got,
    norm,
    q_far,
    z_far,
    near_far,
    own_far,
    second_far,
    both,
    give,
    grad_far,
    x,
    frame,
    turned,
    grad,
    near,
    own,
    q,
    z,
    sems,
):
    pairs = [(q_far.at[f], q.at[f]) for f in range(FRAMES)]
    pairs += [(z_far.at[f], z.at[f]) for f in range(FRAMES)]
    pairs += [(near_far, near), (own_far, own)]
    copies = [
        pltpu.make_async_copy(source, target, sems.at[k])
        for k, (source, target) in enumerate(pairs)
    ]
    for k in (0, FRAMES, 1, FRAMES + 1, 2 * FRAMES, 2 * FRAMES + 1):
        copies[k].start()
    upper = place[0] == 0
    fetched = pltpu.make_async_copy(second_far, both.at[1], sems.at[len(pairs) + 1])
    fetched.start()

    def arrive(f):
        copies[f].wait()
        copies[FRAMES + f].wait()

    hidden_grad(size, across, place, q, z, got, norm, grad, frame, arrive)
    sent = pltpu.make_async_copy(grad, grad_far, sems.at[len(pairs)])
    sent.start()
    turned_cells(size, grad, turned)
    for copy in copies[2 * FRAMES :]:
        copy.wait()
    spread_all(size, 1, 1, size.wide, near, own, x, frame)
    fetched.wait()

    @pl.when(upper)
    def _():
        give[...] = both[1].astype(BF16)

    for b in range(3):
        for a, total in enumerate(tap_sums(x, turned, b)):
            rows = slice((a * 3 + b) * 3 * LANES, (a * 3 + b + 1) * 3 * LANES)
            both[0, rows] = total.T

    @pl.when(jnp.logical_not(upper))
    def _():
        give[...] = both[0].astype(BF16)

    sent.wait()


def result_body(size, near, far, kernel, features, out, x, frame):
    spread_all(size, 1, 1, size.wide, near, far, x, frame)
    sums = convolved(x, kernel, False)
    for f in range(FRAMES):
        total = features[f].astype(F32) + sums[f].reshape(size.high, size.wide, LANES)
        out[f] = total.astype(BF16)


def back_first_body(
    size, near, kernel, features, norm, after, q, sums, x, frame, far, sems
):
    copy = pltpu.make_async_copy(after, far, sems.at[0])
    copy.start()
    copy.wait()
    spread_all(size, 1, 1, size.wide, near, far, x, frame)
    grads = convolved(x, kernel, True)
    firsts, seconds = [], []
    for f in range(FRAMES):
        values = features[f].astype(F32).reshape(size.cells, LANES)
        normed = (values - norm[f : f + 1]) * norm[FRAMES + f : FRAMES + f + 1]
        sigmoid = logistic(normed)
        grad = grads[f] * sigmoid * (1.0 + normed * (1.0 - sigmoid))
        q[f] = grad
        firsts.append(jnp.sum(grad, 0, keepdims=True))
        seconds.append(jnp.sum(grad * normed, 0, keepdims=True))
    sums[...] = stat_block(firsts, seconds)


def feature_grad_body(size, peers, features, out_grad, norm, q, got, out):
    total = join3(got[0])
    for peer in range(1, got.shape[0]):
        total = total + join3(got[peer])
    means = lane_totals(total) / (size.cells * peers * (LANES // GROUPS))
    for f in range(FRAMES):
        values = features[f].astype(F32).reshape(size.cells, LANES)
        inv = norm[FRAMES + f : FRAMES + f + 1]
        normed = (values - norm[f : f + 1]) * inv
        grad = inv * (q[f] - means[f : f + 1] - normed * means[FRAMES + f : FRAMES + f + 1])
        grad = out_grad[f].astype(F32) + grad.reshape(size.high, size.wide, LANES)
        out[f] = grad.astype(BF16)


def row_swap(values):
    return lax.ppermute(values, "row", [(0, 1), (1, 0)])


def later(values, by):
    peers = lax.axis_size("tm")
    pairs = [(i, i + by) for i in range(peers) if 0 <= i + by < peers]
    return lax.ppermute(values, "tm", pairs)


def sum_parts(stat):
    high = lax.reduce_precision(stat, 8, 7)
    rest = stat - high
    middle = lax.reduce_precision(rest, 8, 7)
    return jnp.concatenate([high, middle, rest - middle], 0).astype(BF16)


def total_of(got):
    total = got[0].astype(F32)
    for peer in range(1, got.shape[0]):
        total = total + got[peer].astype(F32)
    return total


def joined_body(place, both, got, out):
    share = out.shape[1]
    for peer in range(out.shape[0]):
        rows = slice(peer * share, (peer + 1) * share)
        out[peer] = (both[place[0], rows] + got[rows].astype(F32)).astype(BF16)


def shared_body(got, out, flat):
    rows, share = got.shape[1], out.shape[1]
    if flat.shape[0] > rows:
        flat[rows:] = jnp.zeros((flat.shape[0] - rows, LANES), F32)
    flat[:rows] = total_of(got)
    for peer in range(out.shape[0]):
        out[peer] = flat[peer * share : (peer + 1) * share].astype(BF16)


def finished_body(factor, got, out):
    total = (total_of(got) * factor).astype(BF16)
    for peer in range(out.shape[0]):
        out[peer] = total


def placed_body(rows, swapped, *refs):
    block, first, second, sems = refs[0], *refs[-3:]
    place = here()

    def move(target):
        copies = [
            pltpu.make_async_copy(
                block.at[peer, pl.ds(0, rows)], target.at[pl.ds(peer * rows, rows)], sems.at[peer]
            )
            for peer in range(block.shape[0])
        ]
        for copy in copies:
            copy.start()
        for copy in copies:
            copy.wait()

    @pl.when(place[0] == swapped)
    def _():
        move(first)

    @pl.when(place[0] != swapped)
    def _():
        move(second)


def deliver(block, swapped, rows, so_far):
    anywhere = pl.BlockSpec(memory_space=pl.ANY)
    shape = (rows * block.shape[0], LANES)
    return pl.pallas_call(
        functools.partial(placed_body, rows, swapped),
        out_shape=[jax.ShapeDtypeStruct(shape, BF16)] * 2,
        in_specs=[anywhere] * (1 + len(so_far)),
        out_specs=[anywhere, anywhere],
        input_output_aliases={1 + k: k for k in range(len(so_far))},
        scratch_shapes=[pltpu.SemaphoreType.DMA((block.shape[0],))],
        compiler_params=pltpu.CompilerParams(vmem_limit_bytes=1 << 20),
    )(block, *so_far)


def on_device(features, conv_first, conv_second, out_grad):
    frames, high, wide, chans = features.shape
    assert frames == FRAMES and chans == LANES and lax.axis_size("row") == 2
    size = Sizes(high, wide)
    across = lax.axis_size("col")
    peers = 2 * across
    factor = 1.0 / math.sqrt(size.cells * FRAMES * lax.axis_size("tm") * peers)
    taps = conv_first.shape
    first = conv_first.reshape(-1, LANES)
    second = conv_second.reshape(-1, LANES)
    work = 2 * first.size * size.cells * FRAMES
    part = functools.partial
    stat = ((STATS, LANES), F32)
    tall, broad = size.tall(), size.broad()
    frame = ((tall, broad, LANES), F32)

    edge = up(3 * FRAMES * wide + PARTS, 16)
    lines = up(FRAMES * size.stride(1) + 2 * FRAMES * size.stride(2) + PARTS, 16)
    flat = ((2, lines, LANES), F32)
    pay, stats, cols, features_near, grad_near = call(
        part(start_body, size),
        [((edge, LANES), BF16), stat, flat, (features.shape, BF16), (features.shape, BF16)],
        [features, out_grad],
        placed=True,
        far=2,
        sems=2 * FRAMES,
    )
    row_got = row_swap(pay)
    (slots,) = call(
        part(slots_body, size, (1, 2), across),
        [((across, lines, LANES), BF16)],
        [cols, row_got, stats],
        [flat],
        placed=True,
    )
    col_got = lax.all_to_all(slots, "col", 0, 0)
    block = ((size.rows(1), LANES), BF16)
    act_first, grad, norm_first = call(
        part(act_first_body, size, across),
        [block, ((size.rows(2), LANES), BF16), stat],
        [features_near, grad_near, row_got, col_got],
        [frame],
        placed=True,
    )
    grad_after = later(grad, -1)
    act_before = later(act_first, 1)

    edge = up(FRAMES * wide + PARTS, 16)
    (sums,) = call(
        part(hidden_own_body, size),
        [((FRAMES, size.cells, LANES), F32)],
        [act_first, first],
        conv_scratch(size, 1, wide, FRAMES),
        mib=12,
        flops=work // 2,
    )
    span = span_second(size)
    hidden, slots = call(
        part(hidden_body, size, across),
        [(features.shape, BF16), ((peers, up(span + PARTS, 16), LANES), BF16)],
        [act_before, sums, first],
        [*conv_scratch(size, 1, wide, FRAMES), ((2, span, LANES), F32)],
        placed=True,
        mib=12,
        flops=2 * work,
    )
    got = lax.all_to_all(slots, ("row", "col"), 0, 0)
    (grad_act,) = call(
        part(grad_act_body, size),
        [((FRAMES, tall, broad, LANES), F32)],
        [grad, grad_after, second],
        [*conv_scratch(size, 2, up(wide + 2, 16)), (second.shape, BF16)],
        far=1,
        sems=1,
        mib=18,
        flops=2 * work,
    )
    field = ((FRAMES, tall, broad, LANES), F32)
    norm_second, slots = call(
        part(sums_second_body, size, across),
        [stat, ((peers, STATS, LANES), F32)],
        [hidden, got, grad_act],
    )
    act_second, q, z = call(
        part(act_second_body, size, across),
        [block, field, field],
        [hidden, got, grad_act, norm_second],
        [frame, field, field],
        placed=True,
        sems=2 * FRAMES,
        beside=True,
        out_far=2,
    )
    got = lax.all_to_all(slots, ("row", "col"), 0, 0)
    turned = ((FRAMES * LANES, size.cells), BF16)
    (second_term,) = call(
        part(second_term_body, size),
        [(first.shape, F32)],
        [grad, grad_after, act_second],
        [*conv_scratch(size, 1, wide), turned, (first.shape, F32)],
        sems=9,
        mib=16,
        beside=True,
        out_far=1,
    )
    both, give, grad_second = call(
        part(first_term_body, size, across),
        [((2, *first.shape), F32), (first.shape, BF16), block],
        [got, norm_second, q, z, act_before, act_first, second_term],
        [*conv_scratch(size, 1, wide), turned, *[block] * 3, field, field],
        placed=True,
        far=5,
        sems=2 * FRAMES + 4,
        mib=20,
        flops=work,
        out_far=1,
    )
    give, late_grad, late_act = lax.optimization_barrier((give, grad_second, act_second))
    act_second_before = later(late_act, 1)
    grad_second_after = later(late_grad, -1)

    along = lax.axis_size("tm")
    rows = first.shape[0]
    by_col = rows // across
    (slots,) = call(
        joined_body,
        [((across, by_col, LANES), BF16)],
        [both, row_swap(give)],
        placed=True,
    )
    slots = lax.all_to_all(slots, "col", 0, 0)
    slots, grad_second_after = lax.optimization_barrier((slots, grad_second_after))
    share = up(by_col, 16 * along) // along
    (slots,) = call(
        shared_body,
        [((along, share, LANES), BF16)],
        [slots],
        [((along * share, LANES), F32)],
    )
    got = lax.all_to_all(slots, "tm", 0, 0)
    (result,) = call(
        part(result_body, size),
        [(features.shape, BF16)],
        [act_second_before, act_second, second, features],
        conv_scratch(size, 1, wide),
        mib=14,
        flops=work,
    )
    q, sums = call(
        part(back_first_body, size),
        [((FRAMES, size.cells, LANES), F32), stat],
        [grad_second, first, features, norm_first, grad_second_after],
        [*conv_scratch(size, 1, wide), block],
        far=1,
        sems=1,
        mib=14,
        flops=work,
    )
    got, result = lax.optimization_barrier((got, result))
    (slots,) = call(part(finished_body, factor), [((along, share, LANES), BF16)], [got])
    done = lax.all_to_all(slots, "tm", 0, 0).reshape(-1, LANES)[:by_col]
    parts = sum_parts(sums + row_swap(sums))
    parts = jnp.pad(parts, ((0, -parts.shape[0] % 16), (0, 0)))
    done = jnp.concatenate([done, parts], 0)
    mine = lax.all_to_all(jnp.broadcast_to(done[None], (across, *done.shape)), "col", 0, 0)
    theirs = row_swap(mine)
    so_far = deliver(mine, 0, by_col, [])
    first_grad, second_grad = deliver(theirs, 1, by_col, so_far)
    (feature_grad,) = call(
        part(feature_grad_body, size, peers),
        [(features.shape, BF16)],
        [features, out_grad, norm_first, q, mine[:, by_col:]],
    )
    return (result, feature_grad, first_grad.reshape(taps), second_grad.reshape(taps))


def solution(mesh):
    in_specs = (P("tm", "row", "col", None), P(), P(), P("tm", "row", "col", None))
    out_specs = (P("tm", "row", "col", None), P("tm", "row", "col", None), P(), P())
    return jax.shard_map(
        on_device, mesh=mesh, in_specs=in_specs, out_specs=out_specs, check_vma=False
    )
```

```python
import functools
import math

import jax
import jax.numpy as jnp
from jax import lax
from jax.experimental import pallas as pl
from jax.experimental.pallas import tpu as pltpu
from jax.sharding import PartitionSpec as P

GROUPS = 32
EPSILON = 1e-06
F32 = jnp.float32
BF16 = jnp.bfloat16
LANES = 128
FRAMES = 2
STATS = 8
PARTS = 3 * STATS


def up(count, step):
    return -(-count // step) * step


class Sizes:
    def __init__(self, high, wide):
        self.high, self.wide = high, wide
        self.cells = high * wide

    def stride(self, rim):
        return up(self.high + 2 * rim, 8)

    def main(self, rim):
        return FRAMES * (self.high + 2 * rim) * self.wide

    def rows(self, rim):
        return up(self.main(rim) + 2 * rim * FRAMES * self.stride(rim), 16)

    def tall(self):
        return self.high + 2

    def broad(self):
        return up(self.wide + 2, 8)


def here():
    return lax.axis_index("row"), lax.axis_index("col")


def call(body, outs, args, scratch=(), placed=False, far=0, sems=0, mib=8, flops=0, beside=False, out_far=0):
    inner = body
    if placed:
        body = lambda *refs: inner(here(), *refs)
    specs = [pl.BlockSpec(memory_space=pltpu.VMEM)] * (len(args) - far)
    specs += [pl.BlockSpec(memory_space=pltpu.HBM)] * far
    near = len(args) - far
    args = [*args[:near], *(pltpu.with_memory_space_constraint(a, pltpu.HBM) for a in args[near:])]
    scratches = [pltpu.VMEM(shape, dtype) for shape, dtype in scratch]
    if sems:
        scratches.append(pltpu.SemaphoreType.DMA((sems,)))
    shapes = [jax.ShapeDtypeStruct(shape, dtype) for shape, dtype in outs]
    kept = len(outs) - out_far
    moved = sum(math.prod(a.shape) * a.dtype.itemsize for a in [*args, *shapes])
    moved = 0 if beside else moved
    return pl.pallas_call(
        body,
        out_shape=shapes[:kept] + [pltpu.HBM(o.shape, o.dtype) for o in shapes[kept:]],
        in_specs=specs,
        out_specs=[pl.BlockSpec(memory_space=pltpu.VMEM)] * kept
        + [pl.BlockSpec(memory_space=pltpu.HBM)] * out_far,
        scratch_shapes=scratches,
        cost_estimate=pl.CostEstimate(flops=flops, bytes_accessed=moved, transcendentals=0),
        compiler_params=pltpu.CompilerParams(vmem_limit_bytes=mib << 20),
    )(*args)


def logistic(values):
    return 0.5 * jnp.tanh(0.5 * values) + 0.5


def lane_totals(stat):
    lane = lax.broadcasted_iota(jnp.int32, stat.shape, 1)
    step = 1
    while step < LANES // GROUPS:
        ahead = pltpu.roll(stat, LANES - step, 1)
        behind = pltpu.roll(stat, step, 1)
        stat = stat + jnp.where((lane // step) % 2 == 0, ahead, behind)
        step *= 2
    return stat


def split3(stat):
    high = stat.astype(BF16).astype(F32)
    rest = stat - high
    middle = rest.astype(BF16).astype(F32)
    return jnp.concatenate([high, middle, rest - middle], 0)


def join3(parts):
    parts = parts.astype(F32)
    return parts[:STATS] + (parts[STATS : 2 * STATS] + parts[2 * STATS : PARTS])


def stat_block(first, second):
    rest = jnp.zeros((STATS - 2 * FRAMES, LANES), F32)
    return jnp.concatenate([*first, *second, rest], 0)


def measured(frames):
    means, squares = [], []
    for frame in frames:
        mean = jnp.sum(frame, 0, keepdims=True) / frame.shape[0]
        centred = frame - mean
        means.append(mean)
        squares.append(jnp.sum(centred * centred, 0, keepdims=True))
    return stat_block(means, squares)


def merged(one, two, cells):
    delta = one - two
    extra = (0.5 * cells) * delta * delta
    mean = 0.5 * (one[:FRAMES] + two[:FRAMES])
    square = one[FRAMES : 2 * FRAMES] + two[FRAMES : 2 * FRAMES] + extra[:FRAMES]
    return jnp.concatenate([mean, square, jnp.zeros((STATS - 2 * FRAMES, LANES), F32)], 0)


def concluded(blocks, cells):
    per_group = LANES // GROUPS
    mean = sum(blocks[1:], blocks[0])[:FRAMES]
    mean = lane_totals(mean) / (len(blocks) * per_group)
    total = jnp.zeros((FRAMES, LANES), F32)
    for block in blocks:
        off = block[:FRAMES] - mean
        total = total + block[FRAMES : 2 * FRAMES] + cells * off * off
    spread = lane_totals(total) / (cells * len(blocks) * per_group)
    rest = jnp.zeros((STATS - 2 * FRAMES, LANES), F32)
    return jnp.concatenate([mean, lax.rsqrt(spread + EPSILON), rest], 0)


def rim_rows(place, got):
    upper = place[0] == 0
    nothing = jnp.zeros_like(got)
    return jnp.where(upper, nothing, got), jnp.where(upper, got, nothing)


def in_frame(shape, place, across, size, rim):
    row = lax.broadcasted_iota(jnp.int32, shape, 0)
    col = lax.broadcasted_iota(jnp.int32, shape, 1)
    top = jnp.where(place[0] == 0, rim, 0)
    bottom = jnp.where(place[0] == 0, size.high + 2 * rim, size.high + rim)
    left = jnp.where(place[1] == 0, rim, 0)
    right = jnp.where(place[1] == across - 1, size.wide + rim, size.wide + 2 * rim)
    return (row >= top) & (row < bottom) & (col >= left) & (col < right)


def take_columns(size, arrays, flat):
    flat[...] = jnp.zeros_like(flat)
    at = 0
    for array, rim in arrays:
        for j in range(rim):
            for frame in range(FRAMES):
                for side, col in ((0, j), (1, size.wide - rim + j)):
                    rows = array[frame, :, col : col + 1].astype(F32)
                    rows = rows.reshape(size.high, LANES)
                    flat[side, at + rim : at + rim + size.high] = rows
                at += size.stride(rim)


def start_body(
    size, place, features_far, grad_far, pay, stats, flat, features, out_grad, sems
):
    high, wide = size.high, size.wide
    upper = place[0] == 0
    copies = [
        pltpu.make_async_copy(source.at[f], target.at[f], sems.at[FRAMES * k + f])
        for k, (source, target) in enumerate(((features_far, features), (grad_far, out_grad)))
        for f in range(FRAMES)
    ]
    for copy in copies:
        copy.start()
    for copy in copies[:FRAMES]:
        copy.wait()
    at = 0
    for frame in range(FRAMES):
        pay[at : at + wide] = jnp.where(upper, features[frame, high - 1], features[frame, 0])
        at += wide
    found = measured([features[f].astype(F32).reshape(size.cells, LANES) for f in range(FRAMES)])
    stats[...] = found
    for copy in copies[FRAMES:]:
        copy.wait()
    for frame in range(FRAMES):
        for row in range(2):
            edge = jnp.where(upper, out_grad[frame, high - 2 + row], out_grad[frame, row])
            pay[at : at + wide] = edge
            at += wide
    fill = jnp.zeros((pay.shape[0] - at - PARTS, LANES), F32)
    pay[at:] = jnp.concatenate([split3(found), fill], 0).astype(BF16)
    take_columns(size, ((features, 1), (out_grad, 2)), flat)


def slots_body(size, rims, across, place, flat, got, stats, slots, work):
    wide, high = size.wide, size.high
    upper = place[0] == 0
    work[...] = flat[...]
    at = base = 0
    for rim in rims:
        for j in range(rim):
            for frame in range(FRAMES):
                for row in range(rim):
                    start = base + (frame * rim + row) * wide
                    for side, col in ((0, j), (1, wide - rim + j)):
                        cell = start - start % 16 + 16 * ((start % 16 + col) // 16)
                        tile = got[cell : cell + 16].astype(F32)
                        edge = tile[start + col - cell : start + col - cell + 1]
                        nothing = jnp.zeros_like(edge)
                        top, bottom = at + row, at + rim + high + row
                        work[side, top : top + 1] = jnp.where(upper, nothing, edge)
                        work[side, bottom : bottom + 1] = jnp.where(upper, edge, nothing)
                at += size.stride(rim)
        base += FRAMES * rim * wide
    parts = split3(merged(stats[...], join3(got[base : base + PARTS]), size.cells))
    work[0, at : at + PARTS] = parts
    work[1, at : at + PARTS] = parts
    for peer in range(across):
        slots[peer] = jnp.where(peer > place[1], work[1], work[0]).astype(BF16)


def sides(place, across, got, first, count):
    left = got[jnp.maximum(place[1] - 1, 0), first : first + count].astype(F32)
    right = got[jnp.minimum(place[1] + 1, across - 1), first : first + count].astype(F32)
    nothing = jnp.zeros_like(left)
    left = jnp.where(place[1] > 0, left, nothing)
    right = jnp.where(place[1] < across - 1, right, nothing)
    return left, right


def padded_frame(size, own, top, bottom, left, right, frame):
    high, wide = size.high, size.wide
    frame[1 : high + 1, 1 : wide + 1] = own
    frame[0:1, 1 : wide + 1] = top[None]
    frame[high + 1 : high + 2, 1 : wide + 1] = bottom[None]
    tall = high + 2
    frame[:, 0:1] = left[:tall].reshape(tall, 1, LANES)
    frame[:, wide + 1 : wide + 2] = right[:tall].reshape(tall, 1, LANES)


def put_frame(size, frame, index, out):
    wide, tall, step = size.wide, size.tall(), size.stride(1)
    flat = frame[:, 1 : wide + 1].reshape(tall * wide, LANES)
    out[index * tall * wide : (index + 1) * tall * wide] = flat.astype(BF16)
    fill = jnp.zeros((step - tall, LANES), F32)
    left = frame[:, 0:1].reshape(tall, LANES)
    right = frame[:, wide + 1 : wide + 2].reshape(tall, LANES)
    return jnp.concatenate([left, fill], 0), jnp.concatenate([right, fill], 0)


def put_sides(out, first, blocks):
    fill = out.shape[0] - first - sum(b.shape[0] for b in blocks)
    if fill:
        blocks = [*blocks, jnp.zeros((fill, LANES), F32)]
    out[first:] = jnp.concatenate(blocks, 0).astype(BF16)


def act_first_body(
    size, across, place, features, out_grad, row_got, col_got, act, grad, norm, frame
):
    high, wide = size.high, size.wide
    at = FRAMES * size.stride(1) + 2 * FRAMES * size.stride(2)
    blocks = [join3(col_got[peer, at : at + PARTS]) for peer in range(across)]
    found = concluded(blocks, 2 * size.cells)
    norm[...] = found
    step = size.stride(1)
    left_all, right_all = sides(place, across, col_got, 0, FRAMES * step)
    ok = in_frame((size.tall(), size.broad(), LANES), place, across, size, 1)
    lefts, rights = [], []
    frame[...] = jnp.zeros_like(frame)
    for f in range(FRAMES):
        top, bottom = rim_rows(place, row_got[f * wide : (f + 1) * wide].astype(F32))
        padded_frame(
            size,
            features[f].astype(F32),
            top,
            bottom,
            left_all[f * step : (f + 1) * step],
            right_all[f * step : (f + 1) * step],
            frame,
        )
        normed = (frame[...] - found[f : f + 1][None]) * found[FRAMES + f : FRAMES + f + 1][None]
        frame[...] = jnp.where(ok, normed * logistic(normed), 0.0)
        left, right = put_frame(size, frame, f, act)
        lefts.append(left)
        rights.append(right)
    put_sides(act, size.main(1), lefts + rights)

    tall = high + 4
    for f in range(FRAMES):
        start = f * tall * wide
        for row in range(2):
            first = FRAMES * wide + (f * 2 + row) * wide
            top, bottom = rim_rows(place, row_got[first : first + wide])
            grad[start + row * wide : start + (row + 1) * wide] = top
            below = start + (high + 2 + row) * wide
            grad[below : below + wide] = bottom
        grad[start + 2 * wide : start + (high + 2) * wide] = out_grad[f].reshape(
            size.cells, LANES
        )
    left, right = sides(
        place, across, col_got, FRAMES * step, 2 * FRAMES * size.stride(2)
    )
    put_sides(grad, size.main(2), [left, right])


def spread_columns(size, rim, trim, wo, block, index, dst, at, frame):
    wide, high = size.wide, size.high
    tall, step = high + 2 * rim, size.stride(rim)
    main = block[index * tall * wide : (index + 1) * tall * wide].astype(F32)
    main = main.reshape(tall, wide, LANES)
    cut = rim - trim
    tall_out = tall - 2 * cut
    frame[:, trim : trim + wide] = main[cut : cut + tall_out]
    first = size.main(rim)
    edges = block[first:].astype(F32)
    for j in range(2 * rim):
        col = j - cut if j < rim else j - rim + trim + wide
        if j < cut or (j >= rim and j - rim >= trim):
            continue
        start = (j * FRAMES + index) * step
        edge = edges[start + cut : start + cut + tall_out]
        frame[:, col : col + 1] = edge.reshape(tall_out, 1, LANES)
    for c in range(3):
        dst[at, :, :, c * LANES : (c + 1) * LANES] = frame[:, c : c + wo].astype(BF16)


def spread_all(size, rim, trim, wo, near, far, dst, frame):
    filled = size.wide + 2 * trim
    if frame.shape[1] > filled:
        frame[:, filled:] = jnp.zeros((frame.shape[0], frame.shape[1] - filled, LANES), F32)
    for f in range(dst.shape[0]):
        block = near if f < FRAMES else far
        spread_columns(size, rim, trim, wo, block, f % FRAMES, dst, f, frame)


def tap_dot(x, kernel, turned):
    ho, wo = x.shape[1] - 2, x.shape[2]
    count = ho * wo
    span = 9 * LANES

    def cells(f):
        return jnp.concatenate(
            [x[f, b : b + ho].reshape(count, 3 * LANES) for b in range(3)], 1
        )

    def taps(a):
        if not turned:
            return kernel[a * span : (a + 1) * span]
        last = (3 - a) * 9 - 1
        return jnp.concatenate(
            [kernel[(last - k) * LANES : (last - k + 1) * LANES] for k in range(9)], 1
        )

    dims = (((1,), (1 if turned else 0,)), ((), ()))

    def dot(f, *times):
        weights = [taps(a) for a in times]
        if len(weights) > 1:
            weights = [jnp.concatenate(weights, 0 if turned else 1)]
        return lax.dot_general(cells(f), weights[0], dims, preferred_element_type=F32)

    return dot


def convolved(x, kernel, turned):
    dot = tap_dot(x, kernel, turned)
    both = dot(1, 1, 0) + dot(2, 2, 1)
    return both[:, :LANES] + dot(0, 0), both[:, LANES:] + dot(3, 2)


def conv_scratch(size, trim, wo, frames=2 * FRAMES):
    tall = size.high + 2 * trim
    return [((frames, tall, wo, 3 * LANES), BF16), ((tall, up(wo + 2, 8), LANES), F32)]


def hidden_own_body(size, own, kernel, sums, x, frame):
    spread_all(size, 1, 1, size.wide, own, None, x, frame)
    dot = tap_dot(x, kernel, False)
    both = dot(0, 2, 1)
    sums[0] = both[:, :LANES]
    sums[1] = both[:, LANES:] + dot(1, 2)


def hidden_body(size, across, place, before, sums, kernel, hidden, slots, x, frame, flat):
    high, wide = size.high, size.wide
    spread_all(size, 1, 1, wide, before, None, x, frame)
    dot = tap_dot(x, kernel, False)
    both = dot(1, 1, 0)
    sums = (sums[0] + both[:, :LANES] + dot(0, 0), sums[1] + both[:, LANES:])
    rounded = [s.astype(BF16) for s in sums]
    for f in range(FRAMES):
        hidden[f] = rounded[f].reshape(high, wide, LANES)
    span = span_second(size)
    found = split3(measured([r.astype(F32) for r in rounded]))
    take_columns(size, ((hidden, 1),), flat)
    upper = place[0] == 0
    edges = [jnp.where(upper, r[size.cells - wide :], r[:wide]).astype(F32) for r in rounded]
    fill = jnp.zeros((span - FRAMES * wide, LANES), F32)
    edges = jnp.concatenate([*edges, fill] if fill.shape[0] else edges, 0)
    rest = jnp.zeros((slots.shape[1] - span - PARTS, LANES), F32)
    for peer in range(slots.shape[0]):
        col = peer % across
        side = jnp.where(col > place[1], flat[1], flat[0])
        content = jnp.where(col == place[1], edges, side)
        slots[peer] = jnp.concatenate([content, found, rest], 0).astype(BF16)


def grad_act_body(size, near, far, kernel_far, out, x, frame, kernel, sems):
    wo = x.shape[2]
    copy = pltpu.make_async_copy(kernel_far, kernel, sems.at[0])
    copy.start()
    spread_all(size, 2, 2, wo, near, far, x, frame)
    copy.wait()
    sums = convolved(x, kernel, True)
    for f in range(FRAMES):
        out[f] = sums[f].reshape(size.tall(), wo, LANES)[:, : size.broad()]


def crossed_sides(size, place, across, got):
    step, high = size.stride(1), size.high
    count = FRAMES * step
    upper = place[0] == 0
    row = lax.broadcasted_iota(jnp.int32, (count, LANES), 0)
    found = []
    for at, there in (
        (jnp.maximum(place[1] - 1, 0), place[1] > 0),
        (jnp.minimum(place[1] + 1, across - 1), place[1] < across - 1),
    ):
        block = got[place[0] * across + at, 0:count].astype(F32)
        cross = got[(1 - place[0]) * across + at, 0:count].astype(F32)
        for f in range(FRAMES):
            above = jnp.where(upper, 0.0, cross[f * step + high : f * step + high + 1])
            below = jnp.where(upper, cross[f * step + 1 : f * step + 2], 0.0)
            block = jnp.where(row == f * step, above, block)
            block = jnp.where(row == f * step + high + 1, below, block)
        found.append(jnp.where(there, block, 0.0))
    return found


def span_second(size):
    return up(max(FRAMES * size.wide, FRAMES * size.stride(1)), 16)


def sums_second_body(size, across, hidden, got, grad_act, norm, slots):
    high, wide = size.high, size.wide
    at = span_second(size)
    blocks = [join3(got[peer, at : at + PARTS]) for peer in range(got.shape[0])]
    found = concluded(blocks, size.cells)
    norm[...] = found
    firsts, seconds = [], []
    for f in range(FRAMES):
        own = hidden[f].astype(F32)
        normed = (own - found[f : f + 1][None]) * found[FRAMES + f : FRAMES + f + 1][None]
        sigmoid = logistic(normed)
        grad = grad_act[f, 1 : high + 1, 1 : wide + 1]
        grad = grad * sigmoid * (1.0 + normed * (1.0 - sigmoid))
        grad, normed = grad.reshape(size.cells, LANES), normed.reshape(size.cells, LANES)
        firsts.append(jnp.sum(grad, 0, keepdims=True))
        seconds.append(jnp.sum(grad * normed, 0, keepdims=True))
    sums = stat_block(firsts, seconds)
    for peer in range(slots.shape[0]):
        slots[peer] = sums


def act_second_body(
    size, across, place, hidden, got, grad_act, norm, act, q_far, z_far, frame, q, z, sems
):
    wide = size.wide
    step = size.stride(1)
    left_all, right_all = crossed_sides(size, place, across, got)
    ok = in_frame((size.tall(), size.broad(), LANES), place, across, size, 1)
    lefts, rights, copies = [], [], []
    frame[...] = jnp.zeros_like(frame)
    facing = (1 - place[0]) * across + place[1]
    for f in range(FRAMES):
        top, bottom = rim_rows(place, got[facing, f * wide : (f + 1) * wide].astype(F32))
        padded_frame(
            size,
            hidden[f].astype(F32),
            top,
            bottom,
            left_all[f * step : (f + 1) * step],
            right_all[f * step : (f + 1) * step],
            frame,
        )
        normed = (frame[...] - norm[f : f + 1][None]) * norm[FRAMES + f : FRAMES + f + 1][None]
        sigmoid = logistic(normed)
        frame[...] = jnp.where(ok, normed * sigmoid, 0.0)
        left, right = put_frame(size, frame, f, act)
        lefts.append(left)
        rights.append(right)
        z[f] = normed
        q[f] = grad_act[f] * sigmoid * (1.0 + normed * (1.0 - sigmoid))
        for k, (source, target) in enumerate(((q, q_far), (z, z_far))):
            copy = pltpu.make_async_copy(source.at[f], target.at[f], sems.at[2 * f + k])
            copy.start()
            copies.append(copy)
    put_sides(act, size.main(1), lefts + rights)
    for copy in copies:
        copy.wait()


def hidden_grad(size, across, place, q, z, got, norm, out, frame, arrive):
    peers = got.shape[0]
    total = got[0]
    for peer in range(1, peers):
        total = total + got[peer]
    means = lane_totals(total) / (size.cells * peers * (LANES // GROUPS))
    ok = in_frame((size.tall(), size.broad(), LANES), place, across, size, 1)
    lefts, rights = [], []
    for f in range(FRAMES):
        first, second = means[f : f + 1][None], means[FRAMES + f : FRAMES + f + 1][None]
        inv = norm[FRAMES + f : FRAMES + f + 1][None]
        arrive(f)
        frame[...] = jnp.where(ok, inv * (q[f] - first - z[f] * second), 0.0)
        left, right = put_frame(size, frame, f, out)
        lefts.append(left)
        rights.append(right)
    put_sides(out, size.main(1), lefts + rights)


def own_cells(size, block, f):
    start = (f * size.tall() + 1) * size.wide
    return block[start : start + size.cells]


def turned_cells(size, block, out):
    for f in range(FRAMES):
        cells = own_cells(size, block, f).astype(F32).T.astype(BF16)
        out[f * LANES : (f + 1) * LANES] = cells


def tap_sums(x, turned, b):
    ho, wo = x.shape[1] - 2, x.shape[2]

    def cells(f):
        return x[f, b : b + ho].reshape(ho * wo, 3 * LANES)

    def dot(one, two):
        return jnp.dot(one, two, preferred_element_type=F32)

    low = dot(turned[...], cells(1))
    high = dot(turned[...], cells(2))
    return (
        dot(turned[:LANES], cells(0)) + low[LANES:],
        low[:LANES] + high[LANES:],
        high[:LANES] + dot(turned[LANES:], cells(3)),
    )


def second_term_body(size, near, far, act, out_far, x, frame, turned, out, sems):
    spread_all(size, 2, 1, size.wide, near, far, x, frame)
    turned_cells(size, act, turned)
    span = 3 * LANES
    copies = []
    for b in range(3):
        for a, total in enumerate(tap_sums(x, turned, b)):
            for c in range(3):
                tap = ((2 - a) * 3 + 2 - b) * 3 + 2 - c
                rows = slice(tap * LANES, (tap + 1) * LANES)
                out[rows] = total[:, c * LANES : (c + 1) * LANES]
            rows = pl.ds(((2 - a) * 3 + 2 - b) * span, span)
            copy = pltpu.make_async_copy(out.at[rows], out_far.at[rows], sems.at[3 * b + a])
            copy.start()
            copies.append(copy)
    for copy in copies:
        copy.wait()


def first_term_body(
    size,
    across,
    place,
    got,
    norm,
    q_far,
    z_far,
    near_far,
    own_far,
    second_far,
    both,
    give,
    grad_far,
    x,
    frame,
    turned,
    grad,
    near,
    own,
    q,
    z,
    sems,
):
    pairs = [(q_far.at[f], q.at[f]) for f in range(FRAMES)]
    pairs += [(z_far.at[f], z.at[f]) for f in range(FRAMES)]
    pairs += [(near_far, near), (own_far, own)]
    copies = [
        pltpu.make_async_copy(source, target, sems.at[k])
        for k, (source, target) in enumerate(pairs)
    ]
    for k in (0, FRAMES, 1, FRAMES + 1, 2 * FRAMES, 2 * FRAMES + 1):
        copies[k].start()
    upper = place[0] == 0
    fetched = pltpu.make_async_copy(second_far, both.at[1], sems.at[len(pairs) + 1])
    fetched.start()

    def arrive(f):
        copies[f].wait()
        copies[FRAMES + f].wait()

    hidden_grad(size, across, place, q, z, got, norm, grad, frame, arrive)
    sent = pltpu.make_async_copy(grad, grad_far, sems.at[len(pairs)])
    sent.start()
    turned_cells(size, grad, turned)
    for copy in copies[2 * FRAMES :]:
        copy.wait()
    spread_all(size, 1, 1, size.wide, near, own, x, frame)
    fetched.wait()

    @pl.when(upper)
    def _():
        give[...] = both[1].astype(BF16)

    for b in range(3):
        for a, total in enumerate(tap_sums(x, turned, b)):
            rows = slice((a * 3 + b) * 3 * LANES, (a * 3 + b + 1) * 3 * LANES)
            both[0, rows] = total.T

    @pl.when(jnp.logical_not(upper))
    def _():
        give[...] = both[0].astype(BF16)

    sent.wait()


def result_body(size, near, far, kernel, features, out, x, frame):
    spread_all(size, 1, 1, size.wide, near, far, x, frame)
    sums = convolved(x, kernel, False)
    for f in range(FRAMES):
        total = features[f].astype(F32) + sums[f].reshape(size.high, size.wide, LANES)
        out[f] = total.astype(BF16)


def back_first_body(size, near, far, kernel, features, norm, q, sums, x, frame):
    spread_all(size, 1, 1, size.wide, near, far, x, frame)
    grads = convolved(x, kernel, True)
    firsts, seconds = [], []
    for f in range(FRAMES):
        values = features[f].astype(F32).reshape(size.cells, LANES)
        normed = (values - norm[f : f + 1]) * norm[FRAMES + f : FRAMES + f + 1]
        sigmoid = logistic(normed)
        grad = grads[f] * sigmoid * (1.0 + normed * (1.0 - sigmoid))
        q[f] = grad
        firsts.append(jnp.sum(grad, 0, keepdims=True))
        seconds.append(jnp.sum(grad * normed, 0, keepdims=True))
    sums[...] = stat_block(firsts, seconds)


def feature_grad_body(size, peers, features, out_grad, norm, q, got, out):
    total = join3(got[0])
    for peer in range(1, got.shape[0]):
        total = total + join3(got[peer])
    means = lane_totals(total) / (size.cells * peers * (LANES // GROUPS))
    for f in range(FRAMES):
        values = features[f].astype(F32).reshape(size.cells, LANES)
        inv = norm[FRAMES + f : FRAMES + f + 1]
        normed = (values - norm[f : f + 1]) * inv
        grad = inv * (q[f] - means[f : f + 1] - normed * means[FRAMES + f : FRAMES + f + 1])
        grad = out_grad[f].astype(F32) + grad.reshape(size.high, size.wide, LANES)
        out[f] = grad.astype(BF16)


def row_swap(values):
    return lax.ppermute(values, "row", [(0, 1), (1, 0)])


def later(values, by):
    peers = lax.axis_size("tm")
    pairs = [(i, i + by) for i in range(peers) if 0 <= i + by < peers]
    return lax.ppermute(values, "tm", pairs)


def sum_parts(stat):
    high = lax.reduce_precision(stat, 8, 7)
    rest = stat - high
    middle = lax.reduce_precision(rest, 8, 7)
    return jnp.concatenate([high, middle, rest - middle], 0).astype(BF16)


def total_of(got):
    total = got[0].astype(F32)
    for peer in range(1, got.shape[0]):
        total = total + got[peer].astype(F32)
    return total


def joined_body(place, both, got, out):
    share = out.shape[1]
    for peer in range(out.shape[0]):
        rows = slice(peer * share, (peer + 1) * share)
        out[peer] = (both[place[0], rows] + got[rows].astype(F32)).astype(BF16)


def shared_body(got, out, flat):
    rows, share = got.shape[1], out.shape[1]
    if flat.shape[0] > rows:
        flat[rows:] = jnp.zeros((flat.shape[0] - rows, LANES), F32)
    flat[:rows] = total_of(got)
    for peer in range(out.shape[0]):
        out[peer] = flat[peer * share : (peer + 1) * share].astype(BF16)


def finished_body(factor, got, out):
    total = (total_of(got) * factor).astype(BF16)
    for peer in range(out.shape[0]):
        out[peer] = total


def placed_body(rows, swapped, *refs):
    block, first, second, sems = refs[0], *refs[-3:]
    place = here()

    def move(target):
        copies = [
            pltpu.make_async_copy(
                block.at[peer, pl.ds(0, rows)], target.at[pl.ds(peer * rows, rows)], sems.at[peer]
            )
            for peer in range(block.shape[0])
        ]
        for copy in copies:
            copy.start()
        for copy in copies:
            copy.wait()

    @pl.when(place[0] == swapped)
    def _():
        move(first)

    @pl.when(place[0] != swapped)
    def _():
        move(second)


def deliver(block, swapped, rows, so_far):
    anywhere = pl.BlockSpec(memory_space=pl.ANY)
    shape = (rows * block.shape[0], LANES)
    return pl.pallas_call(
        functools.partial(placed_body, rows, swapped),
        out_shape=[jax.ShapeDtypeStruct(shape, BF16)] * 2,
        in_specs=[anywhere] * (1 + len(so_far)),
        out_specs=[anywhere, anywhere],
        input_output_aliases={1 + k: k for k in range(len(so_far))},
        scratch_shapes=[pltpu.SemaphoreType.DMA((block.shape[0],))],
        compiler_params=pltpu.CompilerParams(vmem_limit_bytes=1 << 20),
    )(block, *so_far)


def on_device(features, conv_first, conv_second, out_grad):
    frames, high, wide, chans = features.shape
    assert frames == FRAMES and chans == LANES and lax.axis_size("row") == 2
    size = Sizes(high, wide)
    across = lax.axis_size("col")
    peers = 2 * across
    factor = 1.0 / math.sqrt(size.cells * FRAMES * lax.axis_size("tm") * peers)
    taps = conv_first.shape
    first = conv_first.reshape(-1, LANES)
    second = conv_second.reshape(-1, LANES)
    work = 2 * first.size * size.cells * FRAMES
    part = functools.partial
    stat = ((STATS, LANES), F32)
    tall, broad = size.tall(), size.broad()
    frame = ((tall, broad, LANES), F32)

    edge = up(3 * FRAMES * wide + PARTS, 16)
    lines = up(FRAMES * size.stride(1) + 2 * FRAMES * size.stride(2) + PARTS, 16)
    flat = ((2, lines, LANES), F32)
    pay, stats, cols, features_near, grad_near = call(
        part(start_body, size),
        [((edge, LANES), BF16), stat, flat, (features.shape, BF16), (features.shape, BF16)],
        [features, out_grad],
        placed=True,
        far=2,
        sems=2 * FRAMES,
    )
    row_got = row_swap(pay)
    (slots,) = call(
        part(slots_body, size, (1, 2), across),
        [((across, lines, LANES), BF16)],
        [cols, row_got, stats],
        [flat],
        placed=True,
    )
    col_got = lax.all_to_all(slots, "col", 0, 0)
    block = ((size.rows(1), LANES), BF16)
    act_first, grad, norm_first = call(
        part(act_first_body, size, across),
        [block, ((size.rows(2), LANES), BF16), stat],
        [features_near, grad_near, row_got, col_got],
        [frame],
        placed=True,
    )
    grad_after = later(grad, -1)
    act_before = later(act_first, 1)

    edge = up(FRAMES * wide + PARTS, 16)
    (sums,) = call(
        part(hidden_own_body, size),
        [((FRAMES, size.cells, LANES), F32)],
        [act_first, first],
        conv_scratch(size, 1, wide, FRAMES),
        mib=12,
        flops=work // 2,
    )
    span = span_second(size)
    hidden, slots = call(
        part(hidden_body, size, across),
        [(features.shape, BF16), ((peers, up(span + PARTS, 16), LANES), BF16)],
        [act_before, sums, first],
        [*conv_scratch(size, 1, wide, FRAMES), ((2, span, LANES), F32)],
        placed=True,
        mib=12,
        flops=2 * work,
    )
    got = lax.all_to_all(slots, ("row", "col"), 0, 0)
    (grad_act,) = call(
        part(grad_act_body, size),
        [((FRAMES, tall, broad, LANES), F32)],
        [grad, grad_after, second],
        [*conv_scratch(size, 2, up(wide + 2, 16)), (second.shape, BF16)],
        far=1,
        sems=1,
        mib=18,
        flops=2 * work,
    )
    field = ((FRAMES, tall, broad, LANES), F32)
    norm_second, slots = call(
        part(sums_second_body, size, across),
        [stat, ((peers, STATS, LANES), F32)],
        [hidden, got, grad_act],
    )
    act_second, q, z = call(
        part(act_second_body, size, across),
        [block, field, field],
        [hidden, got, grad_act, norm_second],
        [frame, field, field],
        placed=True,
        sems=2 * FRAMES,
        beside=True,
        out_far=2,
    )
    got = lax.all_to_all(slots, ("row", "col"), 0, 0)
    turned = ((FRAMES * LANES, size.cells), BF16)
    (second_term,) = call(
        part(second_term_body, size),
        [(first.shape, F32)],
        [grad, grad_after, act_second],
        [*conv_scratch(size, 1, wide), turned, (first.shape, F32)],
        sems=9,
        mib=16,
        beside=True,
        out_far=1,
    )
    both, give, grad_second = call(
        part(first_term_body, size, across),
        [((2, *first.shape), F32), (first.shape, BF16), block],
        [got, norm_second, q, z, act_before, act_first, second_term],
        [*conv_scratch(size, 1, wide), turned, *[block] * 3, field, field],
        placed=True,
        far=5,
        sems=2 * FRAMES + 4,
        mib=20,
        flops=work,
        out_far=1,
    )
    give, late_grad, late_act = lax.optimization_barrier((give, grad_second, act_second))
    act_second_before = later(late_act, 1)
    grad_second_after = later(late_grad, -1)

    along = lax.axis_size("tm")
    rows = first.shape[0]
    by_col = rows // across
    (slots,) = call(
        joined_body,
        [((across, by_col, LANES), BF16)],
        [both, row_swap(give)],
        placed=True,
    )
    slots = lax.all_to_all(slots, "col", 0, 0)
    share = up(by_col, 16 * along) // along
    (slots,) = call(
        shared_body,
        [((along, share, LANES), BF16)],
        [slots],
        [((along * share, LANES), F32)],
    )
    got = lax.all_to_all(slots, "tm", 0, 0)
    (result,) = call(
        part(result_body, size),
        [(features.shape, BF16)],
        [act_second_before, act_second, second, features],
        conv_scratch(size, 1, wide),
        mib=14,
        flops=work,
    )
    q, sums = call(
        part(back_first_body, size),
        [((FRAMES, size.cells, LANES), F32), stat],
        [grad_second, grad_second_after, first, features, norm_first],
        conv_scratch(size, 1, wide),
        mib=14,
        flops=work,
    )
    got, result, q = lax.optimization_barrier((got, result, q))
    (slots,) = call(part(finished_body, factor), [((along, share, LANES), BF16)], [got])
    done = lax.all_to_all(slots, "tm", 0, 0).reshape(-1, LANES)[:by_col]
    parts = sum_parts(sums + row_swap(sums))
    parts = jnp.pad(parts, ((0, -parts.shape[0] % 16), (0, 0)))
    done = jnp.concatenate([done, parts], 0)
    mine = lax.all_to_all(jnp.broadcast_to(done[None], (across, *done.shape)), "col", 0, 0)
    theirs = row_swap(mine)
    so_far = deliver(mine, 0, by_col, [])
    first_grad, second_grad = deliver(theirs, 1, by_col, so_far)
    (feature_grad,) = call(
        part(feature_grad_body, size, peers),
        [(features.shape, BF16)],
        [features, out_grad, norm_first, q, mine[:, by_col:]],
    )
    return (result, feature_grad, first_grad.reshape(taps), second_grad.reshape(taps))


def solution(mesh):
    in_specs = (P("tm", "row", "col", None), P(), P(), P("tm", "row", "col", None))
    out_specs = (P("tm", "row", "col", None), P("tm", "row", "col", None), P(), P())
    return jax.shard_map(
        on_device, mesh=mesh, in_specs=in_specs, out_specs=out_specs, check_vma=False
    )
```

```python
import functools
import math

import jax
import jax.numpy as jnp
from jax import lax
from jax.experimental import pallas as pl
from jax.experimental.pallas import tpu as pltpu
from jax.sharding import PartitionSpec as P

GROUPS = 32
EPSILON = 1e-06
F32 = jnp.float32
BF16 = jnp.bfloat16
LANES = 128
FRAMES = 2
STATS = 8
PARTS = 3 * STATS


def up(count, step):
    return -(-count // step) * step


class Sizes:
    def __init__(self, high, wide):
        self.high, self.wide = high, wide
        self.cells = high * wide

    def stride(self, rim):
        return up(self.high + 2 * rim, 8)

    def main(self, rim):
        return FRAMES * (self.high + 2 * rim) * self.wide

    def rows(self, rim):
        return up(self.main(rim) + 2 * rim * FRAMES * self.stride(rim), 16)

    def tall(self):
        return self.high + 2

    def broad(self):
        return up(self.wide + 2, 8)


def here():
    return lax.axis_index("row"), lax.axis_index("col")


def call(body, outs, args, scratch=(), placed=False, far=0, sems=0, mib=8, flops=0, beside=False, out_far=0):
    inner = body
    if placed:
        body = lambda *refs: inner(here(), *refs)
    specs = [pl.BlockSpec(memory_space=pltpu.VMEM)] * (len(args) - far)
    specs += [pl.BlockSpec(memory_space=pltpu.HBM)] * far
    near = len(args) - far
    args = [*args[:near], *(pltpu.with_memory_space_constraint(a, pltpu.HBM) for a in args[near:])]
    scratches = [pltpu.VMEM(shape, dtype) for shape, dtype in scratch]
    if sems:
        scratches.append(pltpu.SemaphoreType.DMA((sems,)))
    shapes = [jax.ShapeDtypeStruct(shape, dtype) for shape, dtype in outs]
    kept = len(outs) - out_far
    moved = sum(math.prod(a.shape) * a.dtype.itemsize for a in [*args, *shapes])
    moved = 0 if beside else moved
    return pl.pallas_call(
        body,
        out_shape=shapes[:kept] + [pltpu.HBM(o.shape, o.dtype) for o in shapes[kept:]],
        in_specs=specs,
        out_specs=[pl.BlockSpec(memory_space=pltpu.VMEM)] * kept
        + [pl.BlockSpec(memory_space=pltpu.HBM)] * out_far,
        scratch_shapes=scratches,
        cost_estimate=pl.CostEstimate(flops=flops, bytes_accessed=moved, transcendentals=0),
        compiler_params=pltpu.CompilerParams(vmem_limit_bytes=mib << 20),
    )(*args)


def logistic(values):
    return 0.5 * jnp.tanh(0.5 * values) + 0.5


def lane_totals(stat):
    lane = lax.broadcasted_iota(jnp.int32, stat.shape, 1)
    step = 1
    while step < LANES // GROUPS:
        ahead = pltpu.roll(stat, LANES - step, 1)
        behind = pltpu.roll(stat, step, 1)
        stat = stat + jnp.where((lane // step) % 2 == 0, ahead, behind)
        step *= 2
    return stat


def split3(stat):
    high = stat.astype(BF16).astype(F32)
    rest = stat - high
    middle = rest.astype(BF16).astype(F32)
    return jnp.concatenate([high, middle, rest - middle], 0)


def join3(parts):
    parts = parts.astype(F32)
    return parts[:STATS] + (parts[STATS : 2 * STATS] + parts[2 * STATS : PARTS])


def stat_block(first, second):
    rest = jnp.zeros((STATS - 2 * FRAMES, LANES), F32)
    return jnp.concatenate([*first, *second, rest], 0)


def measured(frames):
    means, squares = [], []
    for frame in frames:
        mean = jnp.sum(frame, 0, keepdims=True) / frame.shape[0]
        centred = frame - mean
        means.append(mean)
        squares.append(jnp.sum(centred * centred, 0, keepdims=True))
    return stat_block(means, squares)


def merged(one, two, cells):
    delta = one - two
    extra = (0.5 * cells) * delta * delta
    mean = 0.5 * (one[:FRAMES] + two[:FRAMES])
    square = one[FRAMES : 2 * FRAMES] + two[FRAMES : 2 * FRAMES] + extra[:FRAMES]
    return jnp.concatenate([mean, square, jnp.zeros((STATS - 2 * FRAMES, LANES), F32)], 0)


def concluded(blocks, cells):
    per_group = LANES // GROUPS
    mean = sum(blocks[1:], blocks[0])[:FRAMES]
    mean = lane_totals(mean) / (len(blocks) * per_group)
    total = jnp.zeros((FRAMES, LANES), F32)
    for block in blocks:
        off = block[:FRAMES] - mean
        total = total + block[FRAMES : 2 * FRAMES] + cells * off * off
    spread = lane_totals(total) / (cells * len(blocks) * per_group)
    rest = jnp.zeros((STATS - 2 * FRAMES, LANES), F32)
    return jnp.concatenate([mean, lax.rsqrt(spread + EPSILON), rest], 0)


def rim_rows(place, got):
    upper = place[0] == 0
    nothing = jnp.zeros_like(got)
    return jnp.where(upper, nothing, got), jnp.where(upper, got, nothing)


def in_frame(shape, place, across, size, rim):
    row = lax.broadcasted_iota(jnp.int32, shape, 0)
    col = lax.broadcasted_iota(jnp.int32, shape, 1)
    top = jnp.where(place[0] == 0, rim, 0)
    bottom = jnp.where(place[0] == 0, size.high + 2 * rim, size.high + rim)
    left = jnp.where(place[1] == 0, rim, 0)
    right = jnp.where(place[1] == across - 1, size.wide + rim, size.wide + 2 * rim)
    return (row >= top) & (row < bottom) & (col >= left) & (col < right)


def take_columns(size, arrays, flat):
    flat[...] = jnp.zeros_like(flat)
    at = 0
    for array, rim in arrays:
        for j in range(rim):
            for frame in range(FRAMES):
                for side, col in ((0, j), (1, size.wide - rim + j)):
                    rows = array[frame, :, col : col + 1].astype(F32)
                    rows = rows.reshape(size.high, LANES)
                    flat[side, at + rim : at + rim + size.high] = rows
                at += size.stride(rim)


def start_body(
    size, place, features_far, grad_far, pay, stats, flat, features, out_grad, sems
):
    high, wide = size.high, size.wide
    upper = place[0] == 0
    copies = [
        pltpu.make_async_copy(source.at[f], target.at[f], sems.at[FRAMES * k + f])
        for k, (source, target) in enumerate(((features_far, features), (grad_far, out_grad)))
        for f in range(FRAMES)
    ]
    for copy in copies:
        copy.start()
    for copy in copies[:FRAMES]:
        copy.wait()
    at = 0
    for frame in range(FRAMES):
        pay[at : at + wide] = jnp.where(upper, features[frame, high - 1], features[frame, 0])
        at += wide
    found = measured([features[f].astype(F32).reshape(size.cells, LANES) for f in range(FRAMES)])
    stats[...] = found
    for copy in copies[FRAMES:]:
        copy.wait()
    for frame in range(FRAMES):
        for row in range(2):
            edge = jnp.where(upper, out_grad[frame, high - 2 + row], out_grad[frame, row])
            pay[at : at + wide] = edge
            at += wide
    fill = jnp.zeros((pay.shape[0] - at - PARTS, LANES), F32)
    pay[at:] = jnp.concatenate([split3(found), fill], 0).astype(BF16)
    take_columns(size, ((features, 1), (out_grad, 2)), flat)


def slots_body(size, rims, across, place, flat, got, stats, slots, work):
    wide, high = size.wide, size.high
    upper = place[0] == 0
    work[...] = flat[...]
    at = base = 0
    for rim in rims:
        for j in range(rim):
            for frame in range(FRAMES):
                for row in range(rim):
                    start = base + (frame * rim + row) * wide
                    for side, col in ((0, j), (1, wide - rim + j)):
                        cell = start - start % 16 + 16 * ((start % 16 + col) // 16)
                        tile = got[cell : cell + 16].astype(F32)
                        edge = tile[start + col - cell : start + col - cell + 1]
                        nothing = jnp.zeros_like(edge)
                        top, bottom = at + row, at + rim + high + row
                        work[side, top : top + 1] = jnp.where(upper, nothing, edge)
                        work[side, bottom : bottom + 1] = jnp.where(upper, edge, nothing)
                at += size.stride(rim)
        base += FRAMES * rim * wide
    parts = split3(merged(stats[...], join3(got[base : base + PARTS]), size.cells))
    work[0, at : at + PARTS] = parts
    work[1, at : at + PARTS] = parts
    for peer in range(across):
        slots[peer] = jnp.where(peer > place[1], work[1], work[0]).astype(BF16)


def sides(place, across, got, first, count):
    left = got[jnp.maximum(place[1] - 1, 0), first : first + count].astype(F32)
    right = got[jnp.minimum(place[1] + 1, across - 1), first : first + count].astype(F32)
    nothing = jnp.zeros_like(left)
    left = jnp.where(place[1] > 0, left, nothing)
    right = jnp.where(place[1] < across - 1, right, nothing)
    return left, right


def padded_frame(size, own, top, bottom, left, right, frame):
    high, wide = size.high, size.wide
    frame[1 : high + 1, 1 : wide + 1] = own
    frame[0:1, 1 : wide + 1] = top[None]
    frame[high + 1 : high + 2, 1 : wide + 1] = bottom[None]
    tall = high + 2
    frame[:, 0:1] = left[:tall].reshape(tall, 1, LANES)
    frame[:, wide + 1 : wide + 2] = right[:tall].reshape(tall, 1, LANES)


def put_frame(size, frame, index, out):
    wide, tall, step = size.wide, size.tall(), size.stride(1)
    flat = frame[:, 1 : wide + 1].reshape(tall * wide, LANES)
    out[index * tall * wide : (index + 1) * tall * wide] = flat.astype(BF16)
    fill = jnp.zeros((step - tall, LANES), F32)
    left = frame[:, 0:1].reshape(tall, LANES)
    right = frame[:, wide + 1 : wide + 2].reshape(tall, LANES)
    return jnp.concatenate([left, fill], 0), jnp.concatenate([right, fill], 0)


def put_sides(out, first, blocks):
    fill = out.shape[0] - first - sum(b.shape[0] for b in blocks)
    if fill:
        blocks = [*blocks, jnp.zeros((fill, LANES), F32)]
    out[first:] = jnp.concatenate(blocks, 0).astype(BF16)


def act_first_body(
    size, across, place, features, out_grad, row_got, col_got, act, grad, norm, frame
):
    high, wide = size.high, size.wide
    at = FRAMES * size.stride(1) + 2 * FRAMES * size.stride(2)
    blocks = [join3(col_got[peer, at : at + PARTS]) for peer in range(across)]
    found = concluded(blocks, 2 * size.cells)
    norm[...] = found
    step = size.stride(1)
    left_all, right_all = sides(place, across, col_got, 0, FRAMES * step)
    ok = in_frame((size.tall(), size.broad(), LANES), place, across, size, 1)
    lefts, rights = [], []
    frame[...] = jnp.zeros_like(frame)
    for f in range(FRAMES):
        top, bottom = rim_rows(place, row_got[f * wide : (f + 1) * wide].astype(F32))
        padded_frame(
            size,
            features[f].astype(F32),
            top,
            bottom,
            left_all[f * step : (f + 1) * step],
            right_all[f * step : (f + 1) * step],
            frame,
        )
        normed = (frame[...] - found[f : f + 1][None]) * found[FRAMES + f : FRAMES + f + 1][None]
        frame[...] = jnp.where(ok, normed * logistic(normed), 0.0)
        left, right = put_frame(size, frame, f, act)
        lefts.append(left)
        rights.append(right)
    put_sides(act, size.main(1), lefts + rights)

    tall = high + 4
    for f in range(FRAMES):
        start = f * tall * wide
        for row in range(2):
            first = FRAMES * wide + (f * 2 + row) * wide
            top, bottom = rim_rows(place, row_got[first : first + wide])
            grad[start + row * wide : start + (row + 1) * wide] = top
            below = start + (high + 2 + row) * wide
            grad[below : below + wide] = bottom
        grad[start + 2 * wide : start + (high + 2) * wide] = out_grad[f].reshape(
            size.cells, LANES
        )
    left, right = sides(
        place, across, col_got, FRAMES * step, 2 * FRAMES * size.stride(2)
    )
    put_sides(grad, size.main(2), [left, right])


def spread_columns(size, rim, trim, wo, block, index, dst, at, frame):
    wide, high = size.wide, size.high
    tall, step = high + 2 * rim, size.stride(rim)
    main = block[index * tall * wide : (index + 1) * tall * wide].astype(F32)
    main = main.reshape(tall, wide, LANES)
    cut = rim - trim
    tall_out = tall - 2 * cut
    frame[:, trim : trim + wide] = main[cut : cut + tall_out]
    first = size.main(rim)
    edges = block[first:].astype(F32)
    for j in range(2 * rim):
        col = j - cut if j < rim else j - rim + trim + wide
        if j < cut or (j >= rim and j - rim >= trim):
            continue
        start = (j * FRAMES + index) * step
        edge = edges[start + cut : start + cut + tall_out]
        frame[:, col : col + 1] = edge.reshape(tall_out, 1, LANES)
    for c in range(3):
        dst[at, :, :, c * LANES : (c + 1) * LANES] = frame[:, c : c + wo].astype(BF16)


def spread_all(size, rim, trim, wo, near, far, dst, frame):
    filled = size.wide + 2 * trim
    if frame.shape[1] > filled:
        frame[:, filled:] = jnp.zeros((frame.shape[0], frame.shape[1] - filled, LANES), F32)
    for f in range(dst.shape[0]):
        block = near if f < FRAMES else far
        spread_columns(size, rim, trim, wo, block, f % FRAMES, dst, f, frame)


def tap_dot(x, kernel, turned):
    ho, wo = x.shape[1] - 2, x.shape[2]
    count = ho * wo
    span = 9 * LANES

    def cells(f):
        return jnp.concatenate(
            [x[f, b : b + ho].reshape(count, 3 * LANES) for b in range(3)], 1
        )

    def taps(a):
        if not turned:
            return kernel[a * span : (a + 1) * span]
        last = (3 - a) * 9 - 1
        return jnp.concatenate(
            [kernel[(last - k) * LANES : (last - k + 1) * LANES] for k in range(9)], 1
        )

    dims = (((1,), (1 if turned else 0,)), ((), ()))

    def dot(f, *times):
        weights = [taps(a) for a in times]
        if len(weights) > 1:
            weights = [jnp.concatenate(weights, 0 if turned else 1)]
        return lax.dot_general(cells(f), weights[0], dims, preferred_element_type=F32)

    return dot


def convolved(x, kernel, turned):
    dot = tap_dot(x, kernel, turned)
    both = dot(1, 1, 0) + dot(2, 2, 1)
    return both[:, :LANES] + dot(0, 0), both[:, LANES:] + dot(3, 2)


def conv_scratch(size, trim, wo, frames=2 * FRAMES):
    tall = size.high + 2 * trim
    return [((frames, tall, wo, 3 * LANES), BF16), ((tall, up(wo + 2, 8), LANES), F32)]


def hidden_own_body(size, own, kernel, sums, x, frame):
    spread_all(size, 1, 1, size.wide, own, None, x, frame)
    dot = tap_dot(x, kernel, False)
    both = dot(0, 2, 1)
    sums[0] = both[:, :LANES]
    sums[1] = both[:, LANES:] + dot(1, 2)


def hidden_body(size, across, place, before, sums, kernel, hidden, slots, x, frame, flat):
    high, wide = size.high, size.wide
    spread_all(size, 1, 1, wide, before, None, x, frame)
    dot = tap_dot(x, kernel, False)
    both = dot(1, 1, 0)
    sums = (sums[0] + both[:, :LANES] + dot(0, 0), sums[1] + both[:, LANES:])
    rounded = [s.astype(BF16) for s in sums]
    for f in range(FRAMES):
        hidden[f] = rounded[f].reshape(high, wide, LANES)
    span = span_second(size)
    found = split3(measured([r.astype(F32) for r in rounded]))
    take_columns(size, ((hidden, 1),), flat)
    upper = place[0] == 0
    edges = [jnp.where(upper, r[size.cells - wide :], r[:wide]).astype(F32) for r in rounded]
    fill = jnp.zeros((span - FRAMES * wide, LANES), F32)
    edges = jnp.concatenate([*edges, fill] if fill.shape[0] else edges, 0)
    rest = jnp.zeros((slots.shape[1] - span - PARTS, LANES), F32)
    for peer in range(slots.shape[0]):
        col = peer % across
        side = jnp.where(col > place[1], flat[1], flat[0])
        content = jnp.where(col == place[1], edges, side)
        slots[peer] = jnp.concatenate([content, found, rest], 0).astype(BF16)


def grad_act_body(size, near, far, kernel_far, out, x, frame, kernel, sems):
    wo = x.shape[2]
    copy = pltpu.make_async_copy(kernel_far, kernel, sems.at[0])
    copy.start()
    spread_all(size, 2, 2, wo, near, far, x, frame)
    copy.wait()
    sums = convolved(x, kernel, True)
    for f in range(FRAMES):
        out[f] = sums[f].reshape(size.tall(), wo, LANES)[:, : size.broad()]


def crossed_sides(size, place, across, got):
    step, high = size.stride(1), size.high
    count = FRAMES * step
    upper = place[0] == 0
    row = lax.broadcasted_iota(jnp.int32, (count, LANES), 0)
    found = []
    for at, there in (
        (jnp.maximum(place[1] - 1, 0), place[1] > 0),
        (jnp.minimum(place[1] + 1, across - 1), place[1] < across - 1),
    ):
        block = got[place[0] * across + at, 0:count].astype(F32)
        cross = got[(1 - place[0]) * across + at, 0:count].astype(F32)
        for f in range(FRAMES):
            above = jnp.where(upper, 0.0, cross[f * step + high : f * step + high + 1])
            below = jnp.where(upper, cross[f * step + 1 : f * step + 2], 0.0)
            block = jnp.where(row == f * step, above, block)
            block = jnp.where(row == f * step + high + 1, below, block)
        found.append(jnp.where(there, block, 0.0))
    return found


def span_second(size):
    return up(max(FRAMES * size.wide, FRAMES * size.stride(1)), 16)


def sums_second_body(size, across, hidden, got, grad_act, norm, slots):
    high, wide = size.high, size.wide
    at = span_second(size)
    blocks = [join3(got[peer, at : at + PARTS]) for peer in range(got.shape[0])]
    found = concluded(blocks, size.cells)
    norm[...] = found
    firsts, seconds = [], []
    for f in range(FRAMES):
        own = hidden[f].astype(F32)
        normed = (own - found[f : f + 1][None]) * found[FRAMES + f : FRAMES + f + 1][None]
        sigmoid = logistic(normed)
        grad = grad_act[f, 1 : high + 1, 1 : wide + 1]
        grad = grad * sigmoid * (1.0 + normed * (1.0 - sigmoid))
        grad, normed = grad.reshape(size.cells, LANES), normed.reshape(size.cells, LANES)
        firsts.append(jnp.sum(grad, 0, keepdims=True))
        seconds.append(jnp.sum(grad * normed, 0, keepdims=True))
    sums = stat_block(firsts, seconds)
    for peer in range(slots.shape[0]):
        slots[peer] = sums


def act_second_body(
    size, across, place, hidden, got, grad_act, norm, act, q_far, z_far, frame, q, z, sems
):
    wide = size.wide
    step = size.stride(1)
    left_all, right_all = crossed_sides(size, place, across, got)
    ok = in_frame((size.tall(), size.broad(), LANES), place, across, size, 1)
    lefts, rights, copies = [], [], []
    frame[...] = jnp.zeros_like(frame)
    facing = (1 - place[0]) * across + place[1]
    for f in range(FRAMES):
        top, bottom = rim_rows(place, got[facing, f * wide : (f + 1) * wide].astype(F32))
        padded_frame(
            size,
            hidden[f].astype(F32),
            top,
            bottom,
            left_all[f * step : (f + 1) * step],
            right_all[f * step : (f + 1) * step],
            frame,
        )
        normed = (frame[...] - norm[f : f + 1][None]) * norm[FRAMES + f : FRAMES + f + 1][None]
        sigmoid = logistic(normed)
        frame[...] = jnp.where(ok, normed * sigmoid, 0.0)
        left, right = put_frame(size, frame, f, act)
        lefts.append(left)
        rights.append(right)
        z[f] = normed
        q[f] = grad_act[f] * sigmoid * (1.0 + normed * (1.0 - sigmoid))
        for k, (source, target) in enumerate(((q, q_far), (z, z_far))):
            copy = pltpu.make_async_copy(source.at[f], target.at[f], sems.at[2 * f + k])
            copy.start()
            copies.append(copy)
    put_sides(act, size.main(1), lefts + rights)
    for copy in copies:
        copy.wait()


def hidden_grad(size, across, place, q, z, got, norm, out, frame, arrive):
    peers = got.shape[0]
    total = got[0]
    for peer in range(1, peers):
        total = total + got[peer]
    means = lane_totals(total) / (size.cells * peers * (LANES // GROUPS))
    ok = in_frame((size.tall(), size.broad(), LANES), place, across, size, 1)
    lefts, rights = [], []
    for f in range(FRAMES):
        first, second = means[f : f + 1][None], means[FRAMES + f : FRAMES + f + 1][None]
        inv = norm[FRAMES + f : FRAMES + f + 1][None]
        arrive(f)
        frame[...] = jnp.where(ok, inv * (q[f] - first - z[f] * second), 0.0)
        left, right = put_frame(size, frame, f, out)
        lefts.append(left)
        rights.append(right)
    put_sides(out, size.main(1), lefts + rights)


def own_cells(size, block, f):
    start = (f * size.tall() + 1) * size.wide
    return block[start : start + size.cells]


def turned_cells(size, block, out):
    for f in range(FRAMES):
        cells = own_cells(size, block, f).astype(F32).T.astype(BF16)
        out[f * LANES : (f + 1) * LANES] = cells


def tap_sums(x, turned, b):
    ho, wo = x.shape[1] - 2, x.shape[2]

    def cells(f):
        return x[f, b : b + ho].reshape(ho * wo, 3 * LANES)

    def dot(one, two):
        return jnp.dot(one, two, preferred_element_type=F32)

    low = dot(turned[...], cells(1))
    high = dot(turned[...], cells(2))
    return (
        dot(turned[:LANES], cells(0)) + low[LANES:],
        low[:LANES] + high[LANES:],
        high[:LANES] + dot(turned[LANES:], cells(3)),
    )


def second_term_body(size, near, far, act, out_far, x, frame, turned, out, sems):
    spread_all(size, 2, 1, size.wide, near, far, x, frame)
    turned_cells(size, act, turned)
    span = 3 * LANES
    copies = []
    for b in range(3):
        for a, total in enumerate(tap_sums(x, turned, b)):
            for c in range(3):
                tap = ((2 - a) * 3 + 2 - b) * 3 + 2 - c
                rows = slice(tap * LANES, (tap + 1) * LANES)
                out[rows] = total[:, c * LANES : (c + 1) * LANES]
            rows = pl.ds(((2 - a) * 3 + 2 - b) * span, span)
            copy = pltpu.make_async_copy(out.at[rows], out_far.at[rows], sems.at[3 * b + a])
            copy.start()
            copies.append(copy)
    for copy in copies:
        copy.wait()


def first_term_body(
    size,
    across,
    place,
    got,
    norm,
    q_far,
    z_far,
    near_far,
    own_far,
    second_far,
    both,
    give,
    grad_far,
    x,
    frame,
    turned,
    grad,
    near,
    own,
    q,
    z,
    sems,
):
    pairs = [(q_far.at[f], q.at[f]) for f in range(FRAMES)]
    pairs += [(z_far.at[f], z.at[f]) for f in range(FRAMES)]
    pairs += [(near_far, near), (own_far, own)]
    copies = [
        pltpu.make_async_copy(source, target, sems.at[k])
        for k, (source, target) in enumerate(pairs)
    ]
    for k in (0, FRAMES, 1, FRAMES + 1, 2 * FRAMES, 2 * FRAMES + 1):
        copies[k].start()
    upper = place[0] == 0
    fetched = pltpu.make_async_copy(second_far, both.at[1], sems.at[len(pairs) + 1])
    fetched.start()

    def arrive(f):
        copies[f].wait()
        copies[FRAMES + f].wait()

    hidden_grad(size, across, place, q, z, got, norm, grad, frame, arrive)
    sent = pltpu.make_async_copy(grad, grad_far, sems.at[len(pairs)])
    sent.start()
    turned_cells(size, grad, turned)
    for copy in copies[2 * FRAMES :]:
        copy.wait()
    spread_all(size, 1, 1, size.wide, near, own, x, frame)
    fetched.wait()

    @pl.when(upper)
    def _():
        give[...] = both[1].astype(BF16)

    for b in range(3):
        for a, total in enumerate(tap_sums(x, turned, b)):
            rows = slice((a * 3 + b) * 3 * LANES, (a * 3 + b + 1) * 3 * LANES)
            both[0, rows] = total.T

    @pl.when(jnp.logical_not(upper))
    def _():
        give[...] = both[0].astype(BF16)

    sent.wait()


def result_body(size, near, far, kernel, features, out, x, frame):
    spread_all(size, 1, 1, size.wide, near, far, x, frame)
    sums = convolved(x, kernel, False)
    for f in range(FRAMES):
        total = features[f].astype(F32) + sums[f].reshape(size.high, size.wide, LANES)
        out[f] = total.astype(BF16)


def back_first_body(size, near, far, kernel, features, norm, q, sums, x, frame):
    spread_all(size, 1, 1, size.wide, near, far, x, frame)
    grads = convolved(x, kernel, True)
    firsts, seconds = [], []
    for f in range(FRAMES):
        values = features[f].astype(F32).reshape(size.cells, LANES)
        normed = (values - norm[f : f + 1]) * norm[FRAMES + f : FRAMES + f + 1]
        sigmoid = logistic(normed)
        grad = grads[f] * sigmoid * (1.0 + normed * (1.0 - sigmoid))
        q[f] = grad
        firsts.append(jnp.sum(grad, 0, keepdims=True))
        seconds.append(jnp.sum(grad * normed, 0, keepdims=True))
    sums[...] = stat_block(firsts, seconds)


def feature_grad_body(size, peers, features, out_grad, norm, q, got, out):
    total = join3(got[0])
    for peer in range(1, got.shape[0]):
        total = total + join3(got[peer])
    means = lane_totals(total) / (size.cells * peers * (LANES // GROUPS))
    for f in range(FRAMES):
        values = features[f].astype(F32).reshape(size.cells, LANES)
        inv = norm[FRAMES + f : FRAMES + f + 1]
        normed = (values - norm[f : f + 1]) * inv
        grad = inv * (q[f] - means[f : f + 1] - normed * means[FRAMES + f : FRAMES + f + 1])
        grad = out_grad[f].astype(F32) + grad.reshape(size.high, size.wide, LANES)
        out[f] = grad.astype(BF16)


def row_swap(values):
    return lax.ppermute(values, "row", [(0, 1), (1, 0)])


def later(values, by):
    peers = lax.axis_size("tm")
    pairs = [(i, i + by) for i in range(peers) if 0 <= i + by < peers]
    return lax.ppermute(values, "tm", pairs)


def sum_parts(stat):
    high = lax.reduce_precision(stat, 8, 7)
    rest = stat - high
    middle = lax.reduce_precision(rest, 8, 7)
    return jnp.concatenate([high, middle, rest - middle], 0).astype(BF16)


def total_of(got):
    total = got[0].astype(F32)
    for peer in range(1, got.shape[0]):
        total = total + got[peer].astype(F32)
    return total


def joined_body(place, both, got, out):
    share = out.shape[1]
    for peer in range(out.shape[0]):
        rows = slice(peer * share, (peer + 1) * share)
        out[peer] = (both[place[0], rows] + got[rows].astype(F32)).astype(BF16)


def shared_body(got, out, flat):
    rows, share = got.shape[1], out.shape[1]
    if flat.shape[0] > rows:
        flat[rows:] = jnp.zeros((flat.shape[0] - rows, LANES), F32)
    flat[:rows] = total_of(got)
    for peer in range(out.shape[0]):
        out[peer] = flat[peer * share : (peer + 1) * share].astype(BF16)


def finished_body(factor, got, out):
    total = (total_of(got) * factor).astype(BF16)
    for peer in range(out.shape[0]):
        out[peer] = total


def placed_body(rows, swapped, *refs):
    block, first, second, sems = refs[0], *refs[-3:]
    half = rows // 2
    place = here()

    def move(target):
        copies = [
            pltpu.make_async_copy(
                block.at[peer, pl.ds(part * half, half)],
                target.at[pl.ds(peer * rows + part * half, half)],
                sems.at[2 * peer + part],
            )
            for peer in range(block.shape[0])
            for part in range(2)
        ]
        for copy in copies:
            copy.start()
        for copy in copies:
            copy.wait()

    @pl.when(place[0] == swapped)
    def _():
        move(first)

    @pl.when(place[0] != swapped)
    def _():
        move(second)


def deliver(block, swapped, rows, so_far):
    anywhere = pl.BlockSpec(memory_space=pl.ANY)
    shape = (rows * block.shape[0], LANES)
    return pl.pallas_call(
        functools.partial(placed_body, rows, swapped),
        out_shape=[jax.ShapeDtypeStruct(shape, BF16)] * 2,
        in_specs=[anywhere] * (1 + len(so_far)),
        out_specs=[anywhere, anywhere],
        input_output_aliases={1 + k: k for k in range(len(so_far))},
        scratch_shapes=[pltpu.SemaphoreType.DMA((2 * block.shape[0],))],
        compiler_params=pltpu.CompilerParams(vmem_limit_bytes=1 << 20),
    )(block, *so_far)


def on_device(features, conv_first, conv_second, out_grad):
    frames, high, wide, chans = features.shape
    assert frames == FRAMES and chans == LANES and lax.axis_size("row") == 2
    size = Sizes(high, wide)
    across = lax.axis_size("col")
    peers = 2 * across
    factor = 1.0 / math.sqrt(size.cells * FRAMES * lax.axis_size("tm") * peers)
    taps = conv_first.shape
    first = conv_first.reshape(-1, LANES)
    second = conv_second.reshape(-1, LANES)
    work = 2 * first.size * size.cells * FRAMES
    part = functools.partial
    stat = ((STATS, LANES), F32)
    tall, broad = size.tall(), size.broad()
    frame = ((tall, broad, LANES), F32)

    edge = up(3 * FRAMES * wide + PARTS, 16)
    lines = up(FRAMES * size.stride(1) + 2 * FRAMES * size.stride(2) + PARTS, 16)
    flat = ((2, lines, LANES), F32)
    pay, stats, cols, features_near, grad_near = call(
        part(start_body, size),
        [((edge, LANES), BF16), stat, flat, (features.shape, BF16), (features.shape, BF16)],
        [features, out_grad],
        placed=True,
        far=2,
        sems=2 * FRAMES,
    )
    row_got = row_swap(pay)
    (slots,) = call(
        part(slots_body, size, (1, 2), across),
        [((across, lines, LANES), BF16)],
        [cols, row_got, stats],
        [flat],
        placed=True,
    )
    col_got = lax.all_to_all(slots, "col", 0, 0)
    block = ((size.rows(1), LANES), BF16)
    act_first, grad, norm_first = call(
        part(act_first_body, size, across),
        [block, ((size.rows(2), LANES), BF16), stat],
        [features_near, grad_near, row_got, col_got],
        [frame],
        placed=True,
    )
    grad_after = later(grad, -1)
    act_before = later(act_first, 1)

    edge = up(FRAMES * wide + PARTS, 16)
    (sums,) = call(
        part(hidden_own_body, size),
        [((FRAMES, size.cells, LANES), F32)],
        [act_first, first],
        conv_scratch(size, 1, wide, FRAMES),
        mib=12,
        flops=work // 2,
    )
    span = span_second(size)
    hidden, slots = call(
        part(hidden_body, size, across),
        [(features.shape, BF16), ((peers, up(span + PARTS, 16), LANES), BF16)],
        [act_before, sums, first],
        [*conv_scratch(size, 1, wide, FRAMES), ((2, span, LANES), F32)],
        placed=True,
        mib=12,
        flops=2 * work,
    )
    got = lax.all_to_all(slots, ("row", "col"), 0, 0)
    (grad_act,) = call(
        part(grad_act_body, size),
        [((FRAMES, tall, broad, LANES), F32)],
        [grad, grad_after, second],
        [*conv_scratch(size, 2, up(wide + 2, 16)), (second.shape, BF16)],
        far=1,
        sems=1,
        mib=18,
        flops=2 * work,
    )
    field = ((FRAMES, tall, broad, LANES), F32)
    norm_second, slots = call(
        part(sums_second_body, size, across),
        [stat, ((peers, STATS, LANES), F32)],
        [hidden, got, grad_act],
    )
    act_second, q, z = call(
        part(act_second_body, size, across),
        [block, field, field],
        [hidden, got, grad_act, norm_second],
        [frame, field, field],
        placed=True,
        sems=2 * FRAMES,
        beside=True,
        out_far=2,
    )
    got = lax.all_to_all(slots, ("row", "col"), 0, 0)
    turned = ((FRAMES * LANES, size.cells), BF16)
    (second_term,) = call(
        part(second_term_body, size),
        [(first.shape, F32)],
        [grad, grad_after, act_second],
        [*conv_scratch(size, 1, wide), turned, (first.shape, F32)],
        sems=9,
        mib=16,
        beside=True,
        out_far=1,
    )
    both, give, grad_second = call(
        part(first_term_body, size, across),
        [((2, *first.shape), F32), (first.shape, BF16), block],
        [got, norm_second, q, z, act_before, act_first, second_term],
        [*conv_scratch(size, 1, wide), turned, *[block] * 3, field, field],
        placed=True,
        far=5,
        sems=2 * FRAMES + 4,
        mib=20,
        flops=work,
        out_far=1,
    )
    give, late_grad, late_act = lax.optimization_barrier((give, grad_second, act_second))
    act_second_before = later(late_act, 1)
    grad_second_after = later(late_grad, -1)

    along = lax.axis_size("tm")
    rows = first.shape[0]
    by_col = rows // across
    (slots,) = call(
        joined_body,
        [((across, by_col, LANES), BF16)],
        [both, row_swap(give)],
        placed=True,
    )
    slots = lax.all_to_all(slots, "col", 0, 0)
    slots, grad_second_after = lax.optimization_barrier((slots, grad_second_after))
    share = up(by_col, 16 * along) // along
    (slots,) = call(
        shared_body,
        [((along, share, LANES), BF16)],
        [slots],
        [((along * share, LANES), F32)],
    )
    got = lax.all_to_all(slots, "tm", 0, 0)
    (result,) = call(
        part(result_body, size),
        [(features.shape, BF16)],
        [act_second_before, act_second, second, features],
        conv_scratch(size, 1, wide),
        mib=14,
        flops=work,
    )
    q, sums = call(
        part(back_first_body, size),
        [((FRAMES, size.cells, LANES), F32), stat],
        [grad_second, grad_second_after, first, features, norm_first],
        conv_scratch(size, 1, wide),
        mib=14,
        flops=work,
    )
    got, result = lax.optimization_barrier((got, result))
    (slots,) = call(part(finished_body, factor), [((along, share, LANES), BF16)], [got])
    done = lax.all_to_all(slots, "tm", 0, 0).reshape(-1, LANES)[:by_col]
    parts = sum_parts(sums + row_swap(sums))
    parts = jnp.pad(parts, ((0, -parts.shape[0] % 16), (0, 0)))
    done = jnp.concatenate([done, parts], 0)
    mine = lax.all_to_all(jnp.broadcast_to(done[None], (across, *done.shape)), "col", 0, 0)
    theirs = row_swap(mine)
    so_far = deliver(mine, 0, by_col, [])
    first_grad, second_grad = deliver(theirs, 1, by_col, so_far)
    (feature_grad,) = call(
        part(feature_grad_body, size, peers),
        [(features.shape, BF16)],
        [features, out_grad, norm_first, q, mine[:, by_col:]],
    )
    return (result, feature_grad, first_grad.reshape(taps), second_grad.reshape(taps))


def solution(mesh):
    in_specs = (P("tm", "row", "col", None), P(), P(), P("tm", "row", "col", None))
    out_specs = (P("tm", "row", "col", None), P("tm", "row", "col", None), P(), P())
    return jax.shard_map(
        on_device, mesh=mesh, in_specs=in_specs, out_specs=out_specs, check_vma=False
    )
```
